32 devices in a mesh: seq: 16 (over z, x, core), head: 2 (over y).
Axes of the slice: x: 2, y: 2, z: 4, core: 2. Of those that a mesh axis runs over, the one named last changes fastest.
Arguments:
- tokens_in: bfloat16 [4096, 1024], P(('seq', 'head')), may hold values from -6 to 6
- mixer_norm: bfloat16 [1024], P(('seq', 'head')), may hold values from 0.5 to 1.5
- mix_weight: bfloat16 [1024, 5120], P(('seq', 'head')), may hold values from -0.1875 to 0.1875
- head_gates: bfloat16 [1024, 24], P(('seq', 'head')), may hold values from -0.1875 to 0.1875
- conv_taps: bfloat16 [4, 5120], P(None, ('seq', 'head')), may hold values from -3 to 3
- decay_log: float32 [8], replicated, may hold values from -11 to -1
- decay_bias: float32 [8], replicated, may hold values from -3 to 2
- gate_weight: bfloat16 [1024, 1024], P(('seq', 'head')), may hold values from -0.1875 to 0.1875
- out_norm: float32 [128], replicated, may hold values from 0.5 to 1.5
- out_weight: bfloat16 [1024, 1024], P(('seq', 'head')), may hold values from -0.1875 to 0.1875
- feed_norm: bfloat16 [1024], P(('seq', 'head')), may hold values from 0.5 to 1.5
- up_weight: bfloat16 [1024, 5632], P(('seq', 'head')), may hold values from -0.1875 to 0.1875
- down_weight: bfloat16 [2816, 1024], P(('seq', 'head')), may hold values from -0.109375 to 0.109375
- doc_lengths: int32 [4], replicated, may hold values from 1 to 2048, 4096 in all
- out_grad: bfloat16 [4096, 1024], P(('seq', 'head')), may hold values from -6 to 6
Outputs:
- layer_out: bfloat16 [4096, 1024], P(('seq', 'head'))
- grad_tokens: bfloat16 [4096, 1024], P(('seq', 'head'))
- grad_mixer_norm: float32 [1024], P(('seq', 'head'))
- grad_mix_weight: float32 [1024, 5120], P(('seq', 'head'))
- grad_head_gates: float32 [1024, 24], P(('seq', 'head'))
- grad_conv_taps: float32 [4, 5120], P(None, ('seq', 'head'))
- grad_decay_log: float32 [8], replicated
- grad_decay_bias: float32 [8], replicated
- grad_gate_weight: float32 [1024, 1024], P(('seq', 'head'))
- grad_out_norm: float32 [128], replicated
- grad_out_weight: float32 [1024, 1024], P(('seq', 'head'))
- grad_feed_norm: float32 [1024], P(('seq', 'head'))
- grad_up_weight: float32 [1024, 5632], P(('seq', 'head'))
- grad_down_weight: float32 [2816, 1024], P(('seq', 'head'))
The draws below stay inside these ranges and needn't reach their ends.
Inputs may be any that keep to these rules, and one draw needn't show every extreme that they name: `doc_lengths`: the lengths sum to 4096; the longest is exactly 2048.
All inputs are finite; a program needn't handle non-finite values.
Results may differ from the reference program's by a relative error of at most 0.018.
Values may be sent and summed in bfloat16 or wider, within the bound.
A program may use at most 256 MiB of HBM per device.

```python
import math
import jax
import jax.numpy as jnp
import numpy as np
from jax import lax

D = 1024
HEADS = 8
DK = 128
FF = 2816
STEPS = 2
CONV = 4
BLOCK = 64
TOKENS = 4096
DOC_MAX = 2048
DOCS = 4


def level_of(own_key, extent, shards, low, high):
    factor_of = 1.0
    for axis_at, blocks in shards:
        heights = jax.random.uniform(jax.random.fold_in(jax.random.fold_in(own_key, 6), axis_at), (blocks,), jnp.float32, low / len(shards), high / len(shards))
        factor_of = factor_of * jnp.repeat(jnp.exp(heights), extent[axis_at] // blocks).reshape((-1,) + (1,) * (len(extent) - 1 - axis_at))
    return factor_of


def split_up(count, total, limit, slope):
    portions = [(1 << 20) // math.isqrt(standing ** slope) + 1 for standing in range(2, count + 1)]
    rest, holding = total - limit - (count - 1), [1] * (count - 1)
    while rest > 0:
        movable = [i for i in range(count - 1) if holding[i] < limit]
        mass, remaining = sum([portions[i] for i in movable]), rest
        for i in movable:
            more = min(limit - holding[i], max(1, remaining * portions[i] // mass), rest)
            holding[i] = holding[i] + more
            rest = rest - more
    return np.array([limit] + holding)


def uneven(own_key, amount, total, bound, lean):
    if amount == 2:
        one = jax.random.randint(own_key, (), max(1, total - bound), min(bound, total - 1) + 1)
        return jnp.stack([one, total - one])
    lengths = jnp.asarray(split_up(amount, total, bound, lean), jnp.int32)
    pairs = (amount - 1) // 2
    donor, taker = lengths[1:1 + 2 * pairs:2], lengths[2:2 + 2 * pairs:2]
    margin = jnp.minimum(donor - 1, bound - taker)
    moved = jax.random.randint(jax.random.fold_in(own_key, 1), (pairs,), 0, 1 << 20) % (margin + 1)
    lengths = lengths.at[1:1 + 2 * pairs:2].set(donor - moved).at[2:2 + 2 * pairs:2].set(taker + moved)
    return lengths[jax.random.permutation(jax.random.fold_in(own_key, 2), amount)]


def centred(own_key, shape, spread, most, cuts=(), held_as=jnp.bfloat16):
    values = jax.random.normal(own_key, shape, jnp.float32) * spread
    if len(cuts) > 0:
        values = level_of(own_key, shape, cuts, -0.22, 0.18) * values
    return jnp.clip(values, min=-most, max=most).astype(held_as)


def setup_inputs(seed: int = 0) -> dict:
    streams_of = jax.random.split(jax.random.key(seed), 16)
    tokens_in = centred(streams_of[0], (TOKENS, D), 1.0, 6.0, ((0, 32),))
    mixer_norm = jnp.clip(1.0 + 0.1 * jax.random.normal(streams_of[1], (D,), jnp.float32), 0.5, 1.5).astype(jnp.bfloat16)
    mix_weight = centred(streams_of[2], (D, HEADS * (1 + 2 * STEPS) * DK), D ** -0.5, 0.1875, ((0, 32),))
    head_gates = centred(streams_of[3], (D, HEADS * (STEPS + 1)), D ** -0.5, 0.1875, ((0, 32),))
    conv_taps = centred(streams_of[4], (CONV, HEADS * (1 + 2 * STEPS) * DK), 0.5, 3.0, ((1, 32),))
    decay_log = jnp.clip(jax.random.uniform(streams_of[5], (HEADS,), jnp.float32, -11.0, -1.0), -11.0, -1.0)
    decay_bias = jnp.clip(jax.random.uniform(streams_of[6], (HEADS,), jnp.float32, -3.0, 2.0), -3.0, 2.0)
    gate_weight = centred(streams_of[7], (D, D), D ** -0.5, 0.1875, ((0, 32),))
    out_norm = jnp.clip(1.0 + 0.1 * jax.random.normal(streams_of[8], (DK,), jnp.float32), 0.5, 1.5)
    out_weight = centred(streams_of[9], (D, D), D ** -0.5, 0.1875, ((0, 32),))
    feed_norm = jnp.clip(1.0 + 0.1 * jax.random.normal(streams_of[10], (D,), jnp.float32), 0.5, 1.5).astype(jnp.bfloat16)
    up_weight = centred(streams_of[11], (D, 2 * FF), D ** -0.5, 0.1875, ((0, 32),))
    down_weight = centred(streams_of[12], (FF, D), FF ** -0.5, 0.109375, ((0, 32),))
    doc_lengths = uneven(streams_of[13], DOCS, TOKENS, DOC_MAX, 2).astype(jnp.int32)
    out_grad = centred(streams_of[14], (TOKENS, D), 1.0, 6.0, ((0, 32),))
    return dict(tokens_in=tokens_in, mixer_norm=mixer_norm, mix_weight=mix_weight, head_gates=head_gates, conv_taps=conv_taps, decay_log=decay_log, decay_bias=decay_bias, gate_weight=gate_weight, out_norm=out_norm, out_weight=out_weight, feed_norm=feed_norm, up_weight=up_weight, down_weight=down_weight, doc_lengths=doc_lengths, out_grad=out_grad)


EPS = 1e-06
HIGH_ACCURACY = lax.Precision.HIGHEST

@jax.custom_vjp
def low(v):
    return lax.optimization_barrier(v.astype(jnp.bfloat16)).astype(jnp.float32)

@jax.custom_vjp
def low_back(v):
    return v

def low_keep(v):
    return (low(v), None)

def low_pass(kept, grad):
    return (grad,)

def back_keep(v):
    return (v, None)

def back_low(kept, grad):
    return (low(grad),)
low.defvjp(low_keep, low_pass)
low_back.defvjp(back_keep, back_low)

def matmul(first_mat, second_mat):
    return jnp.dot(first_mat, second_mat, precision=HIGH_ACCURACY, preferred_element_type=jnp.float32)

def rms_norm(values, scale_gain):
    return values * lax.rsqrt(lax.optimization_barrier(jnp.mean(values * values, axis=-1, keepdims=True)) + EPS) * scale_gain

def unit_norm(values):
    return values * lax.rsqrt(lax.optimization_barrier(jnp.sum(values * values, axis=-1, keepdims=True)) + EPS)

def token_step(current_state, inputs):
    query_rows, key_rows, value_rows, beta_rows, decays = inputs
    current_state = decays[:, None, None] * current_state
    for step_index in range(STEPS):
        current_key = key_rows[step_index]
        retrieved_values = jnp.einsum('xb,xbm->xm', current_key, current_state, precision=HIGH_ACCURACY)
        update = value_rows[step_index] - retrieved_values
        current_state = current_state + beta_rows[step_index][:, None, None] * current_key[:, :, None] * update[:, None, :]
    layer_output = jnp.einsum('xb,xbm->xm', query_rows, current_state, precision=HIGH_ACCURACY)
    return (current_state, layer_output)

def block_scan(current_state, inputs):
    return lax.scan(token_step, current_state, inputs)

def layer(tokens_in, mixer_norm, mix_weight, head_gates, conv_taps, decay_log, decay_bias, gate_weight, out_norm, out_weight, feed_norm, up_weight, down_weight, starts_flag, doc_begin):
    positions = jnp.arange(TOKENS, dtype=jnp.int32)
    normed_one = low(rms_norm(tokens_in, mixer_norm))
    projected = low_back(low(matmul(normed_one, mix_weight)))
    scalars = low_back(low(matmul(normed_one, head_gates)))
    out_gate = low_back(matmul(normed_one, gate_weight))
    padded = jnp.concatenate([jnp.zeros((CONV - 1, projected.shape[1]), jnp.float32), projected], 0)
    convolved = jnp.zeros_like(projected)
    for tap_index in range(CONV):
        live = (positions - (CONV - 1) + tap_index >= doc_begin).astype(jnp.float32)
        convolved = convolved + conv_taps[tap_index] * padded[tap_index:tap_index + TOKENS] * live[:, None]
    activated = jax.nn.silu(convolved).reshape(TOKENS, HEADS, 1 + 2 * STEPS, DK)
    query_rows = unit_norm(activated[:, :, 0])
    key_rows = jnp.transpose(unit_norm(activated[:, :, 1:1 + STEPS]), (0, 2, 1, 3))
    value_rows = jnp.transpose(activated[:, :, 1 + STEPS:], (0, 2, 1, 3))
    scalars = scalars.reshape(TOKENS, HEADS, STEPS + 1)
    beta_rows = jnp.transpose(jax.nn.sigmoid(scalars[:, :, :STEPS]), (0, 2, 1))
    decays = jnp.exp(-jnp.exp(decay_log) * jax.nn.softplus(scalars[:, :, STEPS] + decay_bias)) * (1.0 - starts_flag)[:, None]
    blocks = TOKENS // BLOCK
    inputs = (query_rows.reshape(blocks, BLOCK, HEADS, DK), key_rows.reshape(blocks, BLOCK, STEPS, HEADS, DK), value_rows.reshape(blocks, BLOCK, STEPS, HEADS, DK), beta_rows.reshape(blocks, BLOCK, STEPS, HEADS), decays.reshape(blocks, BLOCK, HEADS))
    start_state = jnp.zeros((HEADS, DK, DK), jnp.float32)
    final_state, outputs = lax.scan(jax.checkpoint(block_scan), start_state, inputs)
    mixer_result = low_back(low(outputs.reshape(TOKENS, HEADS, DK)))
    gated = rms_norm(mixer_result, out_norm) * jax.nn.silu(out_gate.reshape(TOKENS, HEADS, DK))
    gated_rows = low(gated.reshape(TOKENS, D))
    branch_out = low_back(matmul(gated_rows, out_weight))
    middle = tokens_in + branch_out
    normed_two = low(rms_norm(middle, feed_norm))
    gate_up = low_back(matmul(normed_two, up_weight))
    hidden = low(jax.nn.silu(gate_up[:, :FF]) * gate_up[:, FF:])
    return middle + low_back(matmul(hidden, down_weight))

def reference(tokens_in, mixer_norm, mix_weight, head_gates, conv_taps, decay_log, decay_bias, gate_weight, out_norm, out_weight, feed_norm, up_weight, down_weight, doc_lengths, out_grad):
    starts = (jnp.cumsum(doc_lengths) - doc_lengths).astype(jnp.int32)
    flag_ints = jnp.zeros((TOKENS,), jnp.int32).at[starts].set(1)
    doc_index = (jnp.cumsum(flag_ints) - 1).astype(jnp.int32)
    doc_begin = starts[doc_index]
    starts_flag = flag_ints.astype(jnp.float32)
    params = tuple((item.astype(jnp.float32) for item in (tokens_in, mixer_norm, mix_weight, head_gates, conv_taps, decay_log, decay_bias, gate_weight, out_norm, out_weight, feed_norm, up_weight, down_weight)))
    result, pullback = jax.vjp(lambda *weights: layer(*weights, starts_flag, doc_begin), *params)
    grads = pullback(out_grad.astype(jnp.float32))
    return (result.astype(jnp.bfloat16), grads[0].astype(jnp.bfloat16), grads[1], grads[2], grads[3], grads[4], grads[5], grads[6], grads[7], grads[8], grads[9], grads[10], grads[11], grads[12])
```

```python
import jax
import jax.numpy as jnp
import numpy as np
from jax import lax
from jax.sharding import Mesh
from jax.sharding import PartitionSpec as P

D = 1024
HEADS = 8
DK = 128
FF = 2816
STEPS = 2
CONV = 4
BLOCK = 64
PROJ = (1 + 2 * STEPS) * DK
WIDE = DK + PROJ + STEPS + 1

EPS = 1e-06
HIGH_ACCURACY = lax.Precision.HIGHEST

GROUP = ("sl", "hd")
ALL = ("sh", "sl", "hd")


def from_behind(shard, axis, by):
    peers = lax.axis_size(axis)
    pairs = [(i, i + by) for i in range(peers) if 0 <= i + by < peers]
    return lax.ppermute(shard, axis, pairs)


def carried_in(shard, axis, join, neutral, backward):
    count = lax.axis_size(axis)
    place = lax.axis_index(axis)
    ahead = count - 1 - place if backward else place
    gathered = jax.tree.map(
        lambda a, kind: lax.all_gather(a.astype(kind), axis), shard, (jnp.bfloat16, jnp.bfloat16)
    )
    state = jax.tree.map(lambda a, e: jnp.zeros_like(a) + jnp.asarray(e, a.dtype), shard, neutral)

    def one(turn, state):
        source = count - 1 - turn if backward else turn
        return join(
            state,
            jax.tree.map(
                lambda a, own: lax.dynamic_index_in_dim(a, source, 0, False).astype(own.dtype),
                gathered,
                shard,
            ),
        )

    return lax.fori_loop(0, ahead, one, state)


def rms_norm(values, scale_gain):
    return values * lax.rsqrt(jnp.mean(values * values, axis=-1, keepdims=True) + EPS) * scale_gain


def unit_norm(values):
    return values * lax.rsqrt(jnp.sum(values * values, axis=-1, keepdims=True) + EPS)


def bf_product(first_mat, second_mat):
    return jnp.dot(first_mat, second_mat, preferred_element_type=jnp.float32)


def hi(spec, *arrays):
    return jnp.einsum(spec, *arrays, precision=HIGH_ACCURACY)


def compose(early_pair, late_pair):
    early_mat, early_add = early_pair
    late_mat, late_add = late_pair
    joined = hi("hij,hjk->hik", late_mat, early_mat)
    shifted = hi("hij,hjk->hik", late_mat, early_add) + late_add
    return (joined, shifted)


def gate_norm(values, out_gate, scale_gain):
    return rms_norm(values, scale_gain) * jax.nn.silu(out_gate)


def swiglu(gate_up):
    half = gate_up.shape[1] // 2
    return jax.nn.silu(gate_up[:, :half]) * gate_up[:, half:]


def rows_to_heads(block):
    groups = lax.axis_size("sh")
    count = groups * HEADS
    got = []
    for turn in range(groups):
        pairs = [(j, ((j % groups + turn) % groups) * HEADS + j // groups) for j in range(count)]
        got.append(lax.ppermute(block, ALL, pairs))
    stacked = jnp.stack(got)
    order = (lax.axis_index("sh") - jnp.arange(groups)) % groups
    taken = jnp.take(stacked, order, axis=0)
    return taken.reshape((groups * block.shape[0],) + block.shape[1:])


def heads_to_rows(partial):
    groups = lax.axis_size("sh")
    count = groups * HEADS
    pieces = partial.reshape((groups, partial.shape[0] // groups) + partial.shape[1:])
    place = lax.axis_index("sh")
    total = None
    for turn in range(groups):
        pairs = [
            (g * HEADS + t, t * groups + (g + turn) % groups)
            for g in range(groups)
            for t in range(HEADS)
        ]
        piece = lax.dynamic_index_in_dim(pieces, (place + turn) % groups, 0, False)
        moved = lax.ppermute(piece, ALL, pairs)
        total = moved if total is None else total + moved
    return total


def columns_to_heads(local_cols):
    per_head = jnp.transpose(local_cols, (1, 0, 2))
    mine = lax.all_to_all(per_head, GROUP, 0, 0, tiled=True)
    mine = mine.reshape(-1, mine.shape[-1])
    return lax.all_gather(mine, "sh", axis=0, tiled=True)


def heads_to_columns(partial):
    summed = lax.psum_scatter(
        partial.astype(jnp.bfloat16), "sh", scatter_dimension=0, tiled=True
    )
    summed = summed.reshape(HEADS, -1, summed.shape[-1])
    back = lax.all_to_all(summed, GROUP, 0, 0, tiled=True)
    return jnp.transpose(back, (1, 0, 2)).astype(jnp.float32)


def group_gather(rows):
    return lax.all_gather(rows, GROUP, axis=0, tiled=True)


def group_scatter(partial):
    low = partial.astype(jnp.bfloat16)
    return lax.psum_scatter(low, GROUP, scatter_dimension=0, tiled=True).astype(jnp.float32)


def masked_power_inverse(system):
    size = system.shape[-1]
    places = jnp.arange(size)
    base = 8
    inside = (places[:, None] // base == places[None, :] // base) & (
        places[:, None] > places[None, :]
    )
    step = -(system * inside.astype(system.dtype))
    eye = jnp.eye(size, dtype=system.dtype)
    result = eye + step
    for _ in range(2):
        step = hi("bij,bjk->bik", step, step)
        result = result + hi("bij,bjk->bik", result, step)
    width = base
    while width < size:
        across = (places[:, None] // (2 * width) == places[None, :] // (2 * width)) & (
            places[:, None] // width != places[None, :] // width
        )
        lower_left = system * across.astype(system.dtype)
        result = result - hi("bij,bjk->bik", result, hi("bij,bjk->bik", lower_left, result))
        width = 2 * width
    return result


@jax.custom_vjp
def unit_lower_inverse(system):
    return masked_power_inverse(system)


def inverse_keep(system):
    inverse = masked_power_inverse(system)
    return inverse, inverse


def inverse_back(inverse, grad):
    turned = jnp.swapaxes(inverse, -1, -2)
    return (-hi("bij,bjk->bik", turned, hi("bij,bjk->bik", grad, turned)),)


unit_lower_inverse.defvjp(inverse_keep, inverse_back)


def block_mixer(query_rows, key_rows, value_rows, beta_rows, log_decay, starts_flag):
    pseudo = key_rows.shape[0]
    span = STEPS * BLOCK
    blocks = pseudo // span
    queries = query_rows.reshape(blocks, BLOCK, DK)
    keys = key_rows.reshape(blocks, span, DK)
    values = value_rows.reshape(blocks, span, DK)
    betas = beta_rows.reshape(blocks, span)
    decays = log_decay.reshape(blocks, span)
    flags = starts_flag.reshape(blocks, span)
    places = jnp.arange(span)
    lower = places[:, None] >= places[None, :]
    strict = (places[:, None] > places[None, :]).astype(jnp.float32)
    identity = jnp.eye(span, dtype=jnp.float32)
    eye_key = jnp.eye(DK, dtype=jnp.float32)

    summed = jnp.cumsum(decays, axis=1)
    segment = jnp.cumsum(flags, axis=1)
    same_doc = (segment[:, :, None] == segment[:, None, :]) & lower
    decay_ratio = jnp.exp(
        jnp.where(same_doc, summed[:, :, None] - summed[:, None, :], 0.0)
    ) * same_doc.astype(jnp.float32)
    from_start = jnp.exp(summed) * (segment == 0.0).astype(jnp.float32)
    key_key = hi("bik,bjk->bij", keys, keys)
    system = identity + betas[:, :, None] * decay_ratio * key_key * strict
    right_side = jnp.concatenate(
        [betas[:, :, None] * values, (betas * from_start)[:, :, None] * keys], 2
    )
    solved = hi("bij,bjk->bik", unit_lower_inverse(system), right_side)
    fresh = solved[:, :, :DK]
    carried = solved[:, :, DK:]
    last_keys = keys * decay_ratio[:, -1, :, None]
    transfer = from_start[:, -1, None, None] * eye_key - hi("bsi,bsj->bij", last_keys, carried)
    offset = hi("bsi,bsj->bij", last_keys, fresh)
    query_key = hi("bqk,bsk->bqs", queries, keys) * decay_ratio[:, STEPS - 1 :: STEPS]
    frame = from_start[:, STEPS - 1 :: STEPS, None] * queries - hi(
        "bqs,bsj->bqj", query_key, carried
    )
    direct = hi("bqs,bsj->bqj", query_key, fresh)

    def advance(state, maps):
        block_transfer, block_offset = maps
        state_mat, state_add = state
        new_mat = hi("ij,jk->ik", block_transfer, state_mat)
        new_add = hi("ij,jk->ik", block_transfer, state_add) + block_offset
        return (new_mat, new_add), (state_mat, state_add)

    (final_mat, final_add), (mats, adds) = lax.scan(
        advance, (eye_key, jnp.zeros((DK, DK), jnp.float32)), (transfer, offset)
    )
    query_frame = hi("bqi,bij->bqj", frame, mats)
    partial = hi("bqi,bij->bqj", frame, adds) + direct
    return (
        query_frame.reshape(blocks * BLOCK, DK),
        partial.reshape(blocks * BLOCK, DK),
        final_mat[None],
        final_add[None],
    )


def local(
    tokens_in,
    mixer_norm,
    mix_weight,
    head_gates,
    conv_taps,
    decay_log,
    decay_bias,
    gate_weight,
    out_norm,
    out_weight,
    feed_norm,
    up_weight,
    down_weight,
    doc_lengths,
    out_grad,
):
    row_count = tokens_in.shape[0]
    weight_rows = mix_weight.shape[0]
    head = lax.axis_index("sl") * lax.axis_size("hd") + lax.axis_index("hd")
    length = row_count * HEADS

    head_cols = jnp.concatenate(
        [
            gate_weight.reshape(weight_rows, HEADS, DK),
            mix_weight.reshape(weight_rows, HEADS, PROJ),
            head_gates.reshape(weight_rows, HEADS, STEPS + 1),
            jnp.broadcast_to(mixer_norm[:, None, None], (weight_rows, HEADS, 1)),
        ],
        2,
    )
    head_wide = columns_to_heads(head_cols)
    head_full = head_wide[:, :WIDE]
    gain_one = head_wide[:, WIDE].astype(jnp.float32)
    half = FF // HEADS
    up_cols = jnp.concatenate(
        [
            up_weight[:, :FF].reshape(weight_rows, HEADS, half),
            up_weight[:, FF:].reshape(weight_rows, HEADS, half),
            jnp.broadcast_to(feed_norm[:, None, None], (weight_rows, HEADS, 1)),
        ],
        2,
    )
    up_wide = columns_to_heads(up_cols)
    up_full = up_wide[:, : 2 * half]
    gain_two = up_wide[:, 2 * half].astype(jnp.float32)
    out_full = rows_to_heads(out_weight)
    down_full = rows_to_heads(down_weight)
    conv_part = jnp.transpose(rows_to_heads(jnp.transpose(conv_taps))).astype(jnp.float32)

    x_float = tokens_in.astype(jnp.float32)
    normed_float, norm_one_back = jax.vjp(rms_norm, x_float, gain_one)
    normed_one = group_gather(normed_float.astype(jnp.bfloat16))
    head_out = bf_product(normed_one, head_full)
    out_gate = head_out[:, :DK]
    proj_head = head_out[:, DK : DK + PROJ].astype(jnp.bfloat16)
    scalar_rows = head_out[:, DK + PROJ :].astype(jnp.bfloat16).astype(jnp.float32)

    rim_rows = from_behind(proj_head[length - (CONV - 1) :], "sh", 1)
    padded = jnp.concatenate([rim_rows, proj_head], 0).astype(jnp.float32)
    starts = jnp.cumsum(doc_lengths) - doc_lengths
    positions = lax.axis_index("sh") * length + jnp.arange(length, dtype=jnp.int32)
    starts_flag = jnp.any(positions[:, None] == starts[None, :], 1).astype(jnp.float32)
    doc_begin = jnp.max(jnp.where(starts[None, :] <= positions[:, None], starts[None, :], 0), 1)
    tap_masks = [
        (positions - (CONV - 1) + tap_index >= doc_begin).astype(jnp.float32)
        for tap_index in range(CONV)
    ]
    pseudo_flag = jnp.concatenate(
        [starts_flag[:, None], jnp.zeros((length, STEPS - 1), jnp.float32)], 1
    ).reshape(-1)
    rate_log = lax.dynamic_index_in_dim(decay_log, head, 0, False)
    bias_part = lax.dynamic_index_in_dim(decay_bias, head, 0, False)

    def mixer_terms(padded, scalar_rows, conv_part, rate_log, bias_part):
        convolved = jnp.zeros_like(padded[CONV - 1 :])
        for tap_index in range(CONV):
            convolved = (
                convolved
                + conv_part[tap_index]
                * padded[tap_index : tap_index + length]
                * tap_masks[tap_index][:, None]
            )
        activated = jax.nn.silu(convolved).reshape(length, 1 + 2 * STEPS, DK)
        query_rows = unit_norm(activated[:, 0])
        key_rows = unit_norm(activated[:, 1 : 1 + STEPS]).reshape(STEPS * length, DK)
        value_rows = activated[:, 1 + STEPS :].reshape(STEPS * length, DK)
        beta_rows = jax.nn.sigmoid(scalar_rows[:, :STEPS]).reshape(STEPS * length)
        log_rate = -jnp.exp(rate_log) * jax.nn.softplus(scalar_rows[:, STEPS] + bias_part)
        log_decay = jnp.concatenate(
            [log_rate[:, None], jnp.zeros((length, STEPS - 1), jnp.float32)], 1
        ).reshape(STEPS * length)
        return block_mixer(query_rows, key_rows, value_rows, beta_rows, log_decay, pseudo_flag)

    (query_frame, partial_value_rows, transfer, offset), mixer_back = jax.vjp(
        mixer_terms, padded, scalar_rows, conv_part, rate_log, bias_part
    )
    identity = jnp.eye(DK, dtype=jnp.float32)[None]
    zeros_state = jnp.zeros((1, DK, DK), jnp.float32)
    prefix_map, incoming_state = carried_in(
        (transfer, offset), "sh", compose, (identity, zeros_state), False
    )
    mixer_result = partial_value_rows + hi("zy,yi->zi", query_frame, incoming_state[0])
    mixer_low = mixer_result.astype(jnp.bfloat16).astype(jnp.float32)
    gated, gate_back = jax.vjp(gate_norm, mixer_low, out_gate, out_norm)
    gated_rows = gated.astype(jnp.bfloat16)
    middle = x_float + group_scatter(bf_product(gated_rows, out_full))
    normed_mid, norm_two_back = jax.vjp(rms_norm, middle, gain_two)
    normed_two = group_gather(normed_mid.astype(jnp.bfloat16))
    gate_up = bf_product(normed_two, up_full)
    hidden_float, swiglu_back = jax.vjp(swiglu, gate_up)
    hidden = hidden_float.astype(jnp.bfloat16)
    layer_out = (middle + group_scatter(bf_product(hidden, down_full))).astype(jnp.bfloat16)

    grad_out = out_grad.astype(jnp.float32)
    grad_rows = group_gather(out_grad)
    grad_hidden = bf_product(grad_rows, down_full.T)
    grad_down = heads_to_rows(bf_product(hidden.T, grad_rows))
    (grad_gate_up,) = swiglu_back(grad_hidden)
    grad_gate_up = grad_gate_up.astype(jnp.bfloat16)
    grad_normed_two = group_scatter(bf_product(grad_gate_up, up_full.T))
    grad_mid_norm, grad_gain_two = norm_two_back(grad_normed_two)
    grad_up_cols = heads_to_columns(
        jnp.concatenate([bf_product(normed_two.T, grad_gate_up), grad_gain_two[:, None]], 1)
    )
    grad_up = jnp.concatenate(
        [
            grad_up_cols[:, :, :half].reshape(weight_rows, FF),
            grad_up_cols[:, :, half : 2 * half].reshape(weight_rows, FF),
        ],
        1,
    )
    grad_middle = grad_out + grad_mid_norm
    grad_branch = group_gather(grad_middle.astype(jnp.bfloat16))
    grad_gated = bf_product(grad_branch, out_full.T)
    grad_outw = heads_to_rows(bf_product(gated_rows.T, grad_branch))
    grad_mixer, grad_gate, grad_out_norm = gate_back(grad_gated)
    grad_gate = grad_gate.astype(jnp.bfloat16)
    head_gradients = grad_mixer.astype(jnp.bfloat16).astype(jnp.float32)
    local_adjoint = hi("dc,dr->cr", query_frame, head_gradients)[None]
    transfer_turned = jnp.transpose(transfer, (0, 2, 1))
    later_map, state_gradient = carried_in(
        (transfer_turned, local_adjoint), "sh", compose, (identity, zeros_state), True
    )
    basis_gradient = hi("nu,wu->nw", head_gradients, incoming_state[0])
    transfer_gradient = hi("tnf,tmf->tnm", state_gradient, incoming_state)
    grad_padded, grad_scalars, grad_conv, grad_rate, grad_bias = mixer_back(
        (basis_gradient, head_gradients, transfer_gradient, state_gradient)
    )
    rim_grad = from_behind(grad_padded[: CONV - 1], "sh", -1)
    own_grad = grad_padded[CONV - 1 :]
    grad_proj = jnp.concatenate(
        [own_grad[: length - (CONV - 1)], own_grad[length - (CONV - 1) :] + rim_grad], 0
    )
    grad_head = jnp.concatenate(
        [grad_gate, grad_proj.astype(jnp.bfloat16), grad_scalars.astype(jnp.bfloat16)], 1
    )
    grad_normed_one = group_scatter(bf_product(grad_head, head_full.T))
    grad_x_norm, grad_gain_one = norm_one_back(grad_normed_one)
    grad_head_cols = heads_to_columns(
        jnp.concatenate([bf_product(normed_one.T, grad_head), grad_gain_one[:, None]], 1)
    )
    grad_gatew = grad_head_cols[:, :, :DK].reshape(weight_rows, D)
    grad_mixw = grad_head_cols[:, :, DK : DK + PROJ].reshape(weight_rows, HEADS * PROJ)
    grad_gatesw = grad_head_cols[:, :, DK + PROJ : WIDE].reshape(
        weight_rows, HEADS * (STEPS + 1)
    )
    grad_tokens = (grad_middle + grad_x_norm).astype(jnp.bfloat16)
    conv_grad = jnp.transpose(heads_to_rows(jnp.transpose(grad_conv)))
    one_hot = (jnp.arange(HEADS) == head).astype(jnp.float32)
    small_sums = lax.psum(
        jnp.concatenate([one_hot * grad_rate, one_hot * grad_bias, grad_out_norm]), ALL
    )
    return (
        layer_out,
        grad_tokens,
        jnp.sum(grad_head_cols[:, :, WIDE], 1),
        grad_mixw,
        grad_gatesw,
        conv_grad,
        small_sums[:HEADS],
        small_sums[HEADS : 2 * HEADS],
        grad_gatew,
        small_sums[2 * HEADS :],
        grad_outw,
        jnp.sum(grad_up_cols[:, :, 2 * half], 1),
        grad_up,
        grad_down,
    )


def solution(mesh):
    seq = mesh.shape["seq"]
    across = mesh.shape["head"]
    inner = HEADS // across
    grid = Mesh(
        np.asarray(mesh.devices).reshape(seq // inner, inner, across), ("sh", "sl", "hd")
    )
    rows = P(ALL, None)
    flat = P(ALL)
    return jax.shard_map(
        local,
        mesh=grid,
        in_specs=(
            rows,
            flat,
            rows,
            rows,
            P(None, ALL),
            P(),
            P(),
            rows,
            P(),
            rows,
            flat,
            rows,
            rows,
            P(),
            rows,
        ),
        out_specs=(
            rows,
            rows,
            flat,
            rows,
            rows,
            P(None, ALL),
            P(),
            P(),
            rows,
            P(),
            rows,
            flat,
            rows,
            rows,
        ),
        check_vma=False,
    )
```

```python
import jax
import jax.numpy as jnp
import numpy as np
from jax import lax
from jax.experimental import pallas as pl
from jax.experimental.pallas import tpu as pltpu
from jax.sharding import Mesh
from jax.sharding import PartitionSpec as P

D = 1024
HEADS = 8
DK = 128
FF = 2816
STEPS = 2
CONV = 4
BLOCK = 64
PROJ = (1 + 2 * STEPS) * DK
WIDE = DK + PROJ + STEPS + 1

EPS = 1e-06
HIGH_ACCURACY = lax.Precision.HIGHEST

GROUP = ("sl", "hd")
ALL = ("sh", "sl", "hd")


def from_behind(shard, axis, by):
    peers = lax.axis_size(axis)
    pairs = [(i, i + by) for i in range(peers) if 0 <= i + by < peers]
    return lax.ppermute(shard, axis, pairs)


def carried_in(shard, axis, join, neutral, backward):
    count = lax.axis_size(axis)
    place = lax.axis_index(axis)
    ahead = count - 1 - place if backward else place
    both = lax.all_gather(jnp.stack(shard).astype(jnp.bfloat16), axis)
    gathered = (both[:, 0], both[:, 1])
    state = jax.tree.map(lambda a, e: jnp.zeros_like(a) + jnp.asarray(e, a.dtype), shard, neutral)

    def one(turn, state):
        source = count - 1 - turn if backward else turn
        return join(
            state,
            jax.tree.map(
                lambda a, own: lax.dynamic_index_in_dim(a, source, 0, False).astype(own.dtype),
                gathered,
                shard,
            ),
        )

    return lax.fori_loop(0, ahead, one, state)


def flat_place():
    return (
        lax.axis_index("sh") * lax.axis_size("sl") + lax.axis_index("sl")
    ) * lax.axis_size("hd") + lax.axis_index("hd")


def device_of(index):
    inner = lax.axis_size("sl") * lax.axis_size("hd")
    return (index // inner, (index // lax.axis_size("hd")) % lax.axis_size("sl"), index % lax.axis_size("hd"))


def sum_kernel(count, own_ref, out_ref, slots, send_sems, recv_sems):
    me = flat_place()
    barrier = pltpu.get_barrier_semaphore()

    def greet(index, carry):
        @pl.when(index != me)
        def _():
            pl.semaphore_signal(
                barrier, inc=1, device_id=device_of(index), device_id_type=pl.DeviceIdType.MESH
            )

        return carry

    lax.fori_loop(0, count, greet, 0)
    pl.semaphore_wait(barrier, count - 1)

    def copy_to(index):
        return pltpu.make_async_remote_copy(
            src_ref=own_ref,
            dst_ref=slots.at[me],
            send_sem=send_sems.at[index],
            recv_sem=recv_sems.at[me],
            device_id=device_of(index),
            device_id_type=pl.DeviceIdType.MESH,
        )

    def copy_from(index):
        return pltpu.make_async_remote_copy(
            src_ref=own_ref,
            dst_ref=slots.at[index],
            send_sem=send_sems.at[index],
            recv_sem=recv_sems.at[index],
            device_id=device_of(index),
            device_id_type=pl.DeviceIdType.MESH,
        )

    def send(index, carry):
        @pl.when(index != me)
        def _():
            copy_to(index).start()

        return carry

    lax.fori_loop(0, count, send, 0)
    slots[me] = own_ref[...]

    def finish(index, carry):
        @pl.when(index != me)
        def _():
            copy_to(index).wait_send()
            copy_from(index).wait_recv()

        return carry

    lax.fori_loop(0, count, finish, 0)
    out_ref[...] = jnp.sum(slots[...], axis=0)


def all_sum(vector):
    count = lax.axis_size("sh") * lax.axis_size("sl") * lax.axis_size("hd")
    size = vector.shape[0]
    lanes = 128
    tile = 8 * lanes
    padded = -(-size // tile) * tile
    block = jnp.pad(vector, (0, padded - size)).reshape(padded // lanes, lanes)
    total = pl.pallas_call(
        lambda *refs: sum_kernel(count, *refs),
        out_shape=jax.ShapeDtypeStruct(block.shape, jnp.float32),
        in_specs=[pl.BlockSpec(memory_space=pltpu.VMEM)],
        out_specs=pl.BlockSpec(memory_space=pltpu.VMEM),
        scratch_shapes=[
            pltpu.VMEM((count,) + block.shape, jnp.float32),
            pltpu.SemaphoreType.DMA((count,)),
            pltpu.SemaphoreType.DMA((count,)),
        ],
        compiler_params=pltpu.CompilerParams(collective_id=0, has_side_effects=True),
    )(block)
    return total.reshape(-1)[:size]


def rms_norm(values, scale_gain):
    return values * lax.rsqrt(jnp.mean(values * values, axis=-1, keepdims=True) + EPS) * scale_gain


def unit_norm(values):
    return values * lax.rsqrt(jnp.sum(values * values, axis=-1, keepdims=True) + EPS)


def bf_product(first_mat, second_mat):
    return jnp.dot(first_mat, second_mat, preferred_element_type=jnp.float32)


def hi(spec, *arrays):
    return jnp.einsum(spec, *arrays, precision=HIGH_ACCURACY)


def compose(early_pair, late_pair):
    early_mat, early_add = early_pair
    late_mat, late_add = late_pair
    joined = hi("hij,hjk->hik", late_mat, early_mat)
    shifted = hi("hij,hjk->hik", late_mat, early_add) + late_add
    return (joined, shifted)


def gate_norm(values, out_gate, scale_gain):
    return rms_norm(values, scale_gain) * jax.nn.silu(out_gate)


def swiglu(gate_up):
    half = gate_up.shape[1] // 2
    return jax.nn.silu(gate_up[:, :half]) * gate_up[:, half:]


def rows_to_heads(block):
    groups = lax.axis_size("sh")
    count = groups * HEADS
    got = []
    for turn in range(groups):
        pairs = [(j, ((j % groups + turn) % groups) * HEADS + j // groups) for j in range(count)]
        got.append(lax.ppermute(block, ALL, pairs))
    stacked = jnp.stack(got)
    order = (lax.axis_index("sh") - jnp.arange(groups)) % groups
    taken = jnp.take(stacked, order, axis=0)
    return taken.reshape((groups * block.shape[0],) + block.shape[1:])


def heads_to_rows(partial):
    groups = lax.axis_size("sh")
    count = groups * HEADS
    pieces = partial.reshape((groups, partial.shape[0] // groups) + partial.shape[1:])
    place = lax.axis_index("sh")
    total = None
    for turn in range(groups):
        pairs = [
            (g * HEADS + t, t * groups + (g + turn) % groups)
            for g in range(groups)
            for t in range(HEADS)
        ]
        piece = lax.dynamic_index_in_dim(pieces, (place + turn) % groups, 0, False)
        moved = lax.ppermute(piece, ALL, pairs)
        total = moved if total is None else total + moved
    return total


def columns_to_heads(local_cols):
    per_head = jnp.transpose(local_cols, (1, 0, 2))
    mine = lax.all_to_all(per_head, GROUP, 0, 0, tiled=True)
    mine = mine.reshape(-1, mine.shape[-1])
    return lax.all_gather(mine, "sh", axis=0, tiled=True)


def heads_to_columns(partial):
    summed = lax.psum_scatter(
        partial.astype(jnp.bfloat16), "sh", scatter_dimension=0, tiled=True
    )
    summed = summed.reshape(HEADS, -1, summed.shape[-1])
    back = lax.all_to_all(summed, GROUP, 0, 0, tiled=True)
    return jnp.transpose(back, (1, 0, 2)).astype(jnp.float32)


def group_gather(rows):
    return lax.all_gather(rows, GROUP, axis=0, tiled=True)


def group_scatter(partial):
    low = partial.astype(jnp.bfloat16)
    return lax.psum_scatter(low, GROUP, scatter_dimension=0, tiled=True).astype(jnp.float32)


def masked_power_inverse(system):
    size = system.shape[-1]
    places = jnp.arange(size)
    base = 8
    inside = (places[:, None] // base == places[None, :] // base) & (
        places[:, None] > places[None, :]
    )
    step = -(system * inside.astype(system.dtype))
    eye = jnp.eye(size, dtype=system.dtype)
    result = eye + step
    for _ in range(2):
        step = hi("bij,bjk->bik", step, step)
        result = result + hi("bij,bjk->bik", result, step)
    width = base
    while width < size:
        across = (places[:, None] // (2 * width) == places[None, :] // (2 * width)) & (
            places[:, None] // width != places[None, :] // width
        )
        lower_left = system * across.astype(system.dtype)
        result = result - hi("bij,bjk->bik", result, hi("bij,bjk->bik", lower_left, result))
        width = 2 * width
    return result


@jax.custom_vjp
def unit_lower_inverse(system):
    return masked_power_inverse(system)


def inverse_keep(system):
    inverse = masked_power_inverse(system)
    return inverse, inverse


def inverse_back(inverse, grad):
    turned = jnp.swapaxes(inverse, -1, -2)
    return (-hi("bij,bjk->bik", turned, hi("bij,bjk->bik", grad, turned)),)


unit_lower_inverse.defvjp(inverse_keep, inverse_back)


def block_mixer(query_rows, key_rows, value_rows, beta_rows, log_decay, starts_flag):
    pseudo = key_rows.shape[0]
    span = STEPS * BLOCK
    blocks = pseudo // span
    queries = query_rows.reshape(blocks, BLOCK, DK)
    keys = key_rows.reshape(blocks, span, DK)
    values = value_rows.reshape(blocks, span, DK)
    betas = beta_rows.reshape(blocks, span)
    decays = log_decay.reshape(blocks, span)
    flags = starts_flag.reshape(blocks, span)
    places = jnp.arange(span)
    lower = places[:, None] >= places[None, :]
    strict = (places[:, None] > places[None, :]).astype(jnp.float32)
    identity = jnp.eye(span, dtype=jnp.float32)
    eye_key = jnp.eye(DK, dtype=jnp.float32)

    summed = jnp.cumsum(decays, axis=1)
    segment = jnp.cumsum(flags, axis=1)
    same_doc = (segment[:, :, None] == segment[:, None, :]) & lower
    decay_ratio = jnp.exp(
        jnp.where(same_doc, summed[:, :, None] - summed[:, None, :], 0.0)
    ) * same_doc.astype(jnp.float32)
    from_start = jnp.exp(summed) * (segment == 0.0).astype(jnp.float32)
    key_key = hi("bik,bjk->bij", keys, keys)
    system = identity + betas[:, :, None] * decay_ratio * key_key * strict
    right_side = jnp.concatenate(
        [betas[:, :, None] * values, (betas * from_start)[:, :, None] * keys], 2
    )
    solved = hi("bij,bjk->bik", unit_lower_inverse(system), right_side)
    fresh = solved[:, :, :DK]
    carried = solved[:, :, DK:]
    last_keys = keys * decay_ratio[:, -1, :, None]
    transfer = from_start[:, -1, None, None] * eye_key - hi("bsi,bsj->bij", last_keys, carried)
    offset = hi("bsi,bsj->bij", last_keys, fresh)
    query_key = hi("bqk,bsk->bqs", queries, keys) * decay_ratio[:, STEPS - 1 :: STEPS]
    frame = from_start[:, STEPS - 1 :: STEPS, None] * queries - hi(
        "bqs,bsj->bqj", query_key, carried
    )
    direct = hi("bqs,bsj->bqj", query_key, fresh)

    state = jnp.concatenate([eye_key, jnp.zeros((DK, DK), jnp.float32)], 1)
    states = []
    for index in range(blocks):
        states.append(state)
        state = hi("ij,jk->ik", transfer[index], state) + jnp.concatenate(
            [jnp.zeros((DK, DK), jnp.float32), offset[index]], 1
        )
    states = jnp.stack(states)
    mats = states[:, :, :DK]
    adds = states[:, :, DK:]
    final_mat = state[:, :DK]
    final_add = state[:, DK:]
    query_frame = hi("bqi,bij->bqj", frame, mats)
    partial = hi("bqi,bij->bqj", frame, adds) + direct
    return (
        query_frame.reshape(blocks * BLOCK, DK),
        partial.reshape(blocks * BLOCK, DK),
        final_mat[None],
        final_add[None],
    )


def local(
    tokens_in,
    mixer_norm,
    mix_weight,
    head_gates,
    conv_taps,
    decay_log,
    decay_bias,
    gate_weight,
    out_norm,
    out_weight,
    feed_norm,
    up_weight,
    down_weight,
    doc_lengths,
    out_grad,
):
    row_count = tokens_in.shape[0]
    weight_rows = mix_weight.shape[0]
    head = lax.axis_index("sl") * lax.axis_size("hd") + lax.axis_index("hd")
    length = row_count * HEADS

    head_cols = jnp.concatenate(
        [
            gate_weight.reshape(weight_rows, HEADS, DK),
            mix_weight.reshape(weight_rows, HEADS, PROJ),
            head_gates.reshape(weight_rows, HEADS, STEPS + 1),
            jnp.broadcast_to(mixer_norm[:, None, None], (weight_rows, HEADS, 1)),
        ],
        2,
    )
    head_wide = columns_to_heads(head_cols)
    head_full = head_wide[:, :WIDE]
    gain_one = head_wide[:, WIDE].astype(jnp.float32)
    half = FF // HEADS
    up_cols = jnp.concatenate(
        [
            up_weight[:, :FF].reshape(weight_rows, HEADS, half),
            up_weight[:, FF:].reshape(weight_rows, HEADS, half),
            jnp.broadcast_to(feed_norm[:, None, None], (weight_rows, HEADS, 1)),
        ],
        2,
    )
    up_wide = columns_to_heads(up_cols)
    up_full = up_wide[:, : 2 * half]
    gain_two = up_wide[:, 2 * half].astype(jnp.float32)
    out_full = rows_to_heads(out_weight)
    down_full = rows_to_heads(down_weight)
    conv_part = jnp.transpose(rows_to_heads(jnp.transpose(conv_taps))).astype(jnp.float32)

    x_float = tokens_in.astype(jnp.float32)
    normed_float, norm_one_back = jax.vjp(rms_norm, x_float, gain_one)
    normed_one = group_gather(normed_float.astype(jnp.bfloat16))
    head_out = bf_product(normed_one, head_full)
    out_gate = head_out[:, :DK]
    proj_head = head_out[:, DK : DK + PROJ].astype(jnp.bfloat16)
    scalar_rows = head_out[:, DK + PROJ :].astype(jnp.bfloat16).astype(jnp.float32)

    rim_rows = from_behind(proj_head[length - (CONV - 1) :], "sh", 1)
    padded = jnp.concatenate([rim_rows, proj_head], 0).astype(jnp.float32)
    starts = jnp.cumsum(doc_lengths) - doc_lengths
    positions = lax.axis_index("sh") * length + jnp.arange(length, dtype=jnp.int32)
    starts_flag = jnp.any(positions[:, None] == starts[None, :], 1).astype(jnp.float32)
    doc_begin = jnp.max(jnp.where(starts[None, :] <= positions[:, None], starts[None, :], 0), 1)
    tap_masks = [
        (positions - (CONV - 1) + tap_index >= doc_begin).astype(jnp.float32)
        for tap_index in range(CONV)
    ]
    pseudo_flag = jnp.concatenate(
        [starts_flag[:, None], jnp.zeros((length, STEPS - 1), jnp.float32)], 1
    ).reshape(-1)
    rate_log = lax.dynamic_index_in_dim(decay_log, head, 0, False)
    bias_part = lax.dynamic_index_in_dim(decay_bias, head, 0, False)

    def mixer_terms(padded, scalar_rows, conv_part, rate_log, bias_part):
        convolved = jnp.zeros_like(padded[CONV - 1 :])
        for tap_index in range(CONV):
            convolved = (
                convolved
                + conv_part[tap_index]
                * padded[tap_index : tap_index + length]
                * tap_masks[tap_index][:, None]
            )
        activated = jax.nn.silu(convolved).reshape(length, 1 + 2 * STEPS, DK)
        query_rows = unit_norm(activated[:, 0])
        key_rows = unit_norm(activated[:, 1 : 1 + STEPS]).reshape(STEPS * length, DK)
        value_rows = activated[:, 1 + STEPS :].reshape(STEPS * length, DK)
        beta_rows = jax.nn.sigmoid(scalar_rows[:, :STEPS]).reshape(STEPS * length)
        log_rate = -jnp.exp(rate_log) * jax.nn.softplus(scalar_rows[:, STEPS] + bias_part)
        log_decay = jnp.concatenate(
            [log_rate[:, None], jnp.zeros((length, STEPS - 1), jnp.float32)], 1
        ).reshape(STEPS * length)
        return block_mixer(query_rows, key_rows, value_rows, beta_rows, log_decay, pseudo_flag)

    (query_frame, partial_value_rows, transfer, offset), mixer_back = jax.vjp(
        mixer_terms, padded, scalar_rows, conv_part, rate_log, bias_part
    )
    identity = jnp.eye(DK, dtype=jnp.float32)[None]
    zeros_state = jnp.zeros((1, DK, DK), jnp.float32)
    prefix_map, incoming_state = carried_in(
        (transfer, offset), "sh", compose, (identity, zeros_state), False
    )
    mixer_result = partial_value_rows + hi("zy,yi->zi", query_frame, incoming_state[0])
    mixer_low = mixer_result.astype(jnp.bfloat16).astype(jnp.float32)
    gated, gate_back = jax.vjp(gate_norm, mixer_low, out_gate, out_norm)
    gated_rows = gated.astype(jnp.bfloat16)
    middle = x_float + group_scatter(bf_product(gated_rows, out_full))
    normed_mid, norm_two_back = jax.vjp(rms_norm, middle, gain_two)
    normed_two = group_gather(normed_mid.astype(jnp.bfloat16))
    gate_up = bf_product(normed_two, up_full)
    hidden_float, swiglu_back = jax.vjp(swiglu, gate_up)
    hidden = hidden_float.astype(jnp.bfloat16)
    layer_out = (middle + group_scatter(bf_product(hidden, down_full))).astype(jnp.bfloat16)

    grad_out = out_grad.astype(jnp.float32)
    grad_rows = group_gather(out_grad)
    grad_hidden = bf_product(grad_rows, down_full.T)
    grad_down = heads_to_rows(bf_product(hidden.T, grad_rows))
    (grad_gate_up,) = swiglu_back(grad_hidden)
    grad_gate_up = grad_gate_up.astype(jnp.bfloat16)
    grad_normed_two = group_scatter(bf_product(grad_gate_up, up_full.T))
    grad_mid_norm, grad_gain_two = norm_two_back(grad_normed_two)
    grad_up_cols = heads_to_columns(
        jnp.concatenate([bf_product(normed_two.T, grad_gate_up), grad_gain_two[:, None]], 1)
    )
    grad_up = jnp.concatenate(
        [
            grad_up_cols[:, :, :half].reshape(weight_rows, FF),
            grad_up_cols[:, :, half : 2 * half].reshape(weight_rows, FF),
        ],
        1,
    )
    grad_middle = grad_out + grad_mid_norm
    grad_branch = group_gather(grad_middle.astype(jnp.bfloat16))
    grad_gated = bf_product(grad_branch, out_full.T)
    grad_outw = heads_to_rows(bf_product(gated_rows.T, grad_branch))
    grad_mixer, grad_gate, grad_out_norm = gate_back(grad_gated)
    grad_gate = grad_gate.astype(jnp.bfloat16)
    head_gradients = grad_mixer.astype(jnp.bfloat16).astype(jnp.float32)
    local_adjoint = hi("dc,dr->cr", query_frame, head_gradients)[None]
    transfer_turned = jnp.transpose(transfer, (0, 2, 1))
    later_map, state_gradient = carried_in(
        (transfer_turned, local_adjoint), "sh", compose, (identity, zeros_state), True
    )
    basis_gradient = hi("nu,wu->nw", head_gradients, incoming_state[0])
    transfer_gradient = hi("tnf,tmf->tnm", state_gradient, incoming_state)
    grad_padded, grad_scalars, grad_conv, grad_rate, grad_bias = mixer_back(
        (basis_gradient, head_gradients, transfer_gradient, state_gradient)
    )
    rim_grad = from_behind(grad_padded[: CONV - 1], "sh", -1)
    own_grad = grad_padded[CONV - 1 :]
    grad_proj = jnp.concatenate(
        [own_grad[: length - (CONV - 1)], own_grad[length - (CONV - 1) :] + rim_grad], 0
    )
    grad_head = jnp.concatenate(
        [grad_gate, grad_proj.astype(jnp.bfloat16), grad_scalars.astype(jnp.bfloat16)], 1
    )
    grad_normed_one = group_scatter(bf_product(grad_head, head_full.T))
    grad_x_norm, grad_gain_one = norm_one_back(grad_normed_one)
    grad_head_cols = heads_to_columns(
        jnp.concatenate([bf_product(normed_one.T, grad_head), grad_gain_one[:, None]], 1)
    )
    grad_gatew = grad_head_cols[:, :, :DK].reshape(weight_rows, D)
    grad_mixw = grad_head_cols[:, :, DK : DK + PROJ].reshape(weight_rows, HEADS * PROJ)
    grad_gatesw = grad_head_cols[:, :, DK + PROJ : WIDE].reshape(
        weight_rows, HEADS * (STEPS + 1)
    )
    grad_tokens = (grad_middle + grad_x_norm).astype(jnp.bfloat16)
    conv_grad = jnp.transpose(heads_to_rows(jnp.transpose(grad_conv)))
    one_hot = (jnp.arange(HEADS) == head).astype(jnp.float32)
    small_sums = all_sum(
        jnp.concatenate([one_hot * grad_rate, one_hot * grad_bias, grad_out_norm])
    )
    return (
        layer_out,
        grad_tokens,
        jnp.sum(grad_head_cols[:, :, WIDE], 1),
        grad_mixw,
        grad_gatesw,
        conv_grad,
        small_sums[:HEADS],
        small_sums[HEADS : 2 * HEADS],
        grad_gatew,
        small_sums[2 * HEADS :],
        grad_outw,
        jnp.sum(grad_up_cols[:, :, 2 * half], 1),
        grad_up,
        grad_down,
    )


def solution(mesh):
    seq = mesh.shape["seq"]
    across = mesh.shape["head"]
    inner = HEADS // across
    grid = Mesh(
        np.asarray(mesh.devices).reshape(seq // inner, inner, across), ("sh", "sl", "hd")
    )
    rows = P(ALL, None)
    flat = P(ALL)
    return jax.shard_map(
        local,
        mesh=grid,
        in_specs=(
            rows,
            flat,
            rows,
            rows,
            P(None, ALL),
            P(),
            P(),
            rows,
            P(),
            rows,
            flat,
            rows,
            rows,
            P(),
            rows,
        ),
        out_specs=(
            rows,
            rows,
            flat,
            rows,
            rows,
            P(None, ALL),
            P(),
            P(),
            rows,
            P(),
            rows,
            flat,
            rows,
            rows,
        ),
        check_vma=False,
    )
```

```python
import jax
import jax.numpy as jnp
import numpy as np
from jax import lax
from jax.experimental import pallas as pl
from jax.experimental.pallas import tpu as pltpu
from jax.sharding import Mesh
from jax.sharding import PartitionSpec as P

D = 1024
HEADS = 8
DK = 128
FF = 2816
STEPS = 2
CONV = 4
BLOCK = 64
PROJ = (1 + 2 * STEPS) * DK
WIDE = DK + PROJ + STEPS + 1

EPS = 1e-06
HIGH_ACCURACY = lax.Precision.HIGHEST

GROUP = ("sl", "hd")
ALL = ("sh", "sl", "hd")


def from_behind(shard, axis, by):
    peers = lax.axis_size(axis)
    pairs = [(i, i + by) for i in range(peers) if 0 <= i + by < peers]
    return lax.ppermute(shard, axis, pairs)


def carried_in(shard, axis, join, neutral, backward):
    count = lax.axis_size(axis)
    place = lax.axis_index(axis)
    ahead = count - 1 - place if backward else place
    both = lax.all_gather(jnp.stack(shard).astype(jnp.bfloat16), axis)
    gathered = (both[:, 0], both[:, 1])
    state = jax.tree.map(lambda a, e: jnp.zeros_like(a) + jnp.asarray(e, a.dtype), shard, neutral)

    def one(turn, state):
        source = count - 1 - turn if backward else turn
        return join(
            state,
            jax.tree.map(
                lambda a, own: lax.dynamic_index_in_dim(a, source, 0, False).astype(own.dtype),
                gathered,
                shard,
            ),
        )

    return lax.fori_loop(0, ahead, one, state)


def flat_place():
    return (
        lax.axis_index("sh") * lax.axis_size("sl") + lax.axis_index("sl")
    ) * lax.axis_size("hd") + lax.axis_index("hd")


def device_of(index):
    inner = lax.axis_size("sl") * lax.axis_size("hd")
    return (index // inner, (index // lax.axis_size("hd")) % lax.axis_size("sl"), index % lax.axis_size("hd"))


def sum_kernel(count, own_ref, out_ref, slots, send_sems, recv_sems):
    me = flat_place()
    barrier = pltpu.get_barrier_semaphore()

    def greet(index, carry):
        @pl.when(index != me)
        def _():
            pl.semaphore_signal(
                barrier, inc=1, device_id=device_of(index), device_id_type=pl.DeviceIdType.MESH
            )

        return carry

    lax.fori_loop(0, count, greet, 0)
    pl.semaphore_wait(barrier, count - 1)

    def copy_to(index):
        return pltpu.make_async_remote_copy(
            src_ref=own_ref,
            dst_ref=slots.at[me],
            send_sem=send_sems.at[index],
            recv_sem=recv_sems.at[me],
            device_id=device_of(index),
            device_id_type=pl.DeviceIdType.MESH,
        )

    def copy_from(index):
        return pltpu.make_async_remote_copy(
            src_ref=own_ref,
            dst_ref=slots.at[index],
            send_sem=send_sems.at[index],
            recv_sem=recv_sems.at[index],
            device_id=device_of(index),
            device_id_type=pl.DeviceIdType.MESH,
        )

    def send(index, carry):
        @pl.when(index != me)
        def _():
            copy_to(index).start()

        return carry

    lax.fori_loop(0, count, send, 0)
    slots[me] = own_ref[...]

    def finish(index, carry):
        @pl.when(index != me)
        def _():
            copy_to(index).wait_send()
            copy_from(index).wait_recv()

        return carry

    lax.fori_loop(0, count, finish, 0)
    out_ref[...] = jnp.sum(slots[...], axis=0)


def all_sum(vector):
    count = lax.axis_size("sh") * lax.axis_size("sl") * lax.axis_size("hd")
    size = vector.shape[0]
    lanes = 128
    tile = 8 * lanes
    padded = -(-size // tile) * tile
    block = jnp.pad(vector, (0, padded - size)).reshape(padded // lanes, lanes)
    total = pl.pallas_call(
        lambda *refs: sum_kernel(count, *refs),
        out_shape=jax.ShapeDtypeStruct(block.shape, jnp.float32),
        in_specs=[pl.BlockSpec(memory_space=pltpu.VMEM)],
        out_specs=pl.BlockSpec(memory_space=pltpu.VMEM),
        scratch_shapes=[
            pltpu.VMEM((count,) + block.shape, jnp.float32),
            pltpu.SemaphoreType.DMA((count,)),
            pltpu.SemaphoreType.DMA((count,)),
        ],
        compiler_params=pltpu.CompilerParams(collective_id=0, has_side_effects=True),
    )(block)
    return total.reshape(-1)[:size]


def rms_norm(values, scale_gain):
    return values * lax.rsqrt(jnp.mean(values * values, axis=-1, keepdims=True) + EPS) * scale_gain


def unit_norm(values):
    return values * lax.rsqrt(jnp.sum(values * values, axis=-1, keepdims=True) + EPS)


def bf_product(first_mat, second_mat):
    return jnp.dot(first_mat, second_mat, preferred_element_type=jnp.float32)


def hi(spec, *arrays):
    return jnp.einsum(spec, *arrays, precision=HIGH_ACCURACY)


def compose(early_pair, late_pair):
    early_mat, early_add = early_pair
    late_mat, late_add = late_pair
    joined = hi("hij,hjk->hik", late_mat, early_mat)
    shifted = hi("hij,hjk->hik", late_mat, early_add) + late_add
    return (joined, shifted)


def gate_norm(values, out_gate, scale_gain):
    return rms_norm(values, scale_gain) * jax.nn.silu(out_gate)


def swiglu(gate_up):
    half = gate_up.shape[1] // 2
    return jax.nn.silu(gate_up[:, :half]) * gate_up[:, half:]


def rows_to_heads(block):
    groups = lax.axis_size("sh")
    count = groups * HEADS
    got = []
    for turn in range(groups):
        pairs = [(j, ((j % groups + turn) % groups) * HEADS + j // groups) for j in range(count)]
        got.append(lax.ppermute(block, ALL, pairs))
    stacked = jnp.stack(got)
    order = (lax.axis_index("sh") - jnp.arange(groups)) % groups
    taken = jnp.take(stacked, order, axis=0)
    return taken.reshape((groups * block.shape[0],) + block.shape[1:])


def heads_to_rows(partial):
    groups = lax.axis_size("sh")
    count = groups * HEADS
    pieces = partial.reshape((groups, partial.shape[0] // groups) + partial.shape[1:])
    place = lax.axis_index("sh")
    total = None
    for turn in range(groups):
        pairs = [
            (g * HEADS + t, t * groups + (g + turn) % groups)
            for g in range(groups)
            for t in range(HEADS)
        ]
        piece = lax.dynamic_index_in_dim(pieces, (place + turn) % groups, 0, False)
        moved = lax.ppermute(piece, ALL, pairs)
        total = moved if total is None else total + moved
    return total


def columns_to_heads(local_cols):
    per_head = jnp.transpose(local_cols, (1, 0, 2))
    mine = lax.all_to_all(per_head, GROUP, 0, 0, tiled=True)
    mine = mine.reshape(-1, mine.shape[-1])
    return lax.all_gather(mine, "sh", axis=0, tiled=True)


def heads_to_columns(partial, direct=False):
    low = partial.astype(jnp.bfloat16)
    if direct:
        groups = lax.axis_size("sh")
        pieces = low.reshape((groups, low.shape[0] // groups) + low.shape[1:])
        moved = lax.all_to_all(pieces, "sh", 0, 0, tiled=True)
        summed = jnp.sum(moved.astype(jnp.float32), 0).astype(jnp.bfloat16)
    else:
        summed = lax.psum_scatter(low, "sh", scatter_dimension=0, tiled=True)
    summed = summed.reshape(HEADS, -1, summed.shape[-1])
    back = lax.all_to_all(summed, GROUP, 0, 0, tiled=True)
    return jnp.transpose(back, (1, 0, 2)).astype(jnp.float32)


def group_gather(rows):
    return lax.all_gather(rows, GROUP, axis=0, tiled=True)


def group_scatter(partial, direct=False):
    low = partial.astype(jnp.bfloat16)
    if direct:
        pieces = low.reshape((HEADS, low.shape[0] // HEADS) + low.shape[1:])
        moved = lax.all_to_all(pieces, GROUP, 0, 0, tiled=True)
        return jnp.sum(moved.astype(jnp.float32), 0)
    return lax.psum_scatter(low, GROUP, scatter_dimension=0, tiled=True).astype(jnp.float32)


def masked_power_inverse(system):
    size = system.shape[-1]
    places = jnp.arange(size)
    base = 8
    inside = (places[:, None] // base == places[None, :] // base) & (
        places[:, None] > places[None, :]
    )
    step = -(system * inside.astype(system.dtype))
    eye = jnp.eye(size, dtype=system.dtype)
    result = eye + step
    for _ in range(2):
        step = hi("bij,bjk->bik", step, step)
        result = result + hi("bij,bjk->bik", result, step)
    width = base
    while width < size:
        across = (places[:, None] // (2 * width) == places[None, :] // (2 * width)) & (
            places[:, None] // width != places[None, :] // width
        )
        lower_left = system * across.astype(system.dtype)
        result = result - hi("bij,bjk->bik", result, hi("bij,bjk->bik", lower_left, result))
        width = 2 * width
    return result


@jax.custom_vjp
def unit_lower_inverse(system):
    return masked_power_inverse(system)


def inverse_keep(system):
    inverse = masked_power_inverse(system)
    return inverse, inverse


def inverse_back(inverse, grad):
    turned = jnp.swapaxes(inverse, -1, -2)
    return (-hi("bij,bjk->bik", turned, hi("bij,bjk->bik", grad, turned)),)


unit_lower_inverse.defvjp(inverse_keep, inverse_back)


def block_mixer(query_rows, key_rows, value_rows, beta_rows, log_decay, starts_flag):
    pseudo = key_rows.shape[0]
    span = STEPS * BLOCK
    blocks = pseudo // span
    queries = query_rows.reshape(blocks, BLOCK, DK)
    keys = key_rows.reshape(blocks, span, DK)
    values = value_rows.reshape(blocks, span, DK)
    betas = beta_rows.reshape(blocks, span)
    decays = log_decay.reshape(blocks, span)
    flags = starts_flag.reshape(blocks, span)
    places = jnp.arange(span)
    lower = places[:, None] >= places[None, :]
    strict = (places[:, None] > places[None, :]).astype(jnp.float32)
    identity = jnp.eye(span, dtype=jnp.float32)
    eye_key = jnp.eye(DK, dtype=jnp.float32)

    summed = jnp.cumsum(decays, axis=1)
    segment = jnp.cumsum(flags, axis=1)
    same_doc = (segment[:, :, None] == segment[:, None, :]) & lower
    decay_ratio = jnp.exp(
        jnp.where(same_doc, summed[:, :, None] - summed[:, None, :], 0.0)
    ) * same_doc.astype(jnp.float32)
    from_start = jnp.exp(summed) * (segment == 0.0).astype(jnp.float32)
    key_key = hi("bik,bjk->bij", keys, keys)
    system = identity + betas[:, :, None] * decay_ratio * key_key * strict
    right_side = jnp.concatenate(
        [betas[:, :, None] * values, (betas * from_start)[:, :, None] * keys], 2
    )
    solved = hi("bij,bjk->bik", unit_lower_inverse(system), right_side)
    fresh = solved[:, :, :DK]
    carried = solved[:, :, DK:]
    last_keys = keys * decay_ratio[:, -1, :, None]
    transfer = from_start[:, -1, None, None] * eye_key - hi("bsi,bsj->bij", last_keys, carried)
    offset = hi("bsi,bsj->bij", last_keys, fresh)
    query_key = hi("bqk,bsk->bqs", queries, keys) * decay_ratio[:, STEPS - 1 :: STEPS]
    frame = from_start[:, STEPS - 1 :: STEPS, None] * queries - hi(
        "bqs,bsj->bqj", query_key, carried
    )
    direct = hi("bqs,bsj->bqj", query_key, fresh)

    state = jnp.concatenate([eye_key, jnp.zeros((DK, DK), jnp.float32)], 1)
    states = []
    for index in range(blocks):
        states.append(state)
        state = hi("ij,jk->ik", transfer[index], state) + jnp.concatenate(
            [jnp.zeros((DK, DK), jnp.float32), offset[index]], 1
        )
    states = jnp.stack(states)
    mats = states[:, :, :DK]
    adds = states[:, :, DK:]
    final_mat = state[:, :DK]
    final_add = state[:, DK:]
    query_frame = hi("bqi,bij->bqj", frame, mats)
    partial = hi("bqi,bij->bqj", frame, adds) + direct
    return (
        query_frame.reshape(blocks * BLOCK, DK),
        partial.reshape(blocks * BLOCK, DK),
        final_mat[None],
        final_add[None],
    )


def local(
    tokens_in,
    mixer_norm,
    mix_weight,
    head_gates,
    conv_taps,
    decay_log,
    decay_bias,
    gate_weight,
    out_norm,
    out_weight,
    feed_norm,
    up_weight,
    down_weight,
    doc_lengths,
    out_grad,
):
    row_count = tokens_in.shape[0]
    weight_rows = mix_weight.shape[0]
    head = lax.axis_index("sl") * lax.axis_size("hd") + lax.axis_index("hd")
    length = row_count * HEADS

    head_cols = jnp.concatenate(
        [
            gate_weight.reshape(weight_rows, HEADS, DK),
            mix_weight.reshape(weight_rows, HEADS, PROJ),
            head_gates.reshape(weight_rows, HEADS, STEPS + 1),
            jnp.broadcast_to(mixer_norm[:, None, None], (weight_rows, HEADS, 1)),
        ],
        2,
    )
    head_wide = columns_to_heads(head_cols)
    head_full = head_wide[:, :WIDE]
    gain_one = head_wide[:, WIDE].astype(jnp.float32)
    half = FF // HEADS
    up_cols = jnp.concatenate(
        [
            up_weight[:, :FF].reshape(weight_rows, HEADS, half),
            up_weight[:, FF:].reshape(weight_rows, HEADS, half),
            jnp.broadcast_to(feed_norm[:, None, None], (weight_rows, HEADS, 1)),
        ],
        2,
    )
    up_wide = columns_to_heads(up_cols)
    up_full = up_wide[:, : 2 * half]
    gain_two = up_wide[:, 2 * half].astype(jnp.float32)
    out_full = rows_to_heads(out_weight)
    down_full = rows_to_heads(down_weight)
    conv_part = jnp.transpose(rows_to_heads(jnp.transpose(conv_taps))).astype(jnp.float32)

    x_float = tokens_in.astype(jnp.float32)
    normed_float, norm_one_back = jax.vjp(rms_norm, x_float, gain_one)
    normed_one = group_gather(normed_float.astype(jnp.bfloat16))
    head_out = bf_product(normed_one, head_full)
    out_gate = head_out[:, :DK]
    proj_head = head_out[:, DK : DK + PROJ].astype(jnp.bfloat16)
    scalar_rows = head_out[:, DK + PROJ :].astype(jnp.bfloat16).astype(jnp.float32)

    rim_rows = from_behind(proj_head[length - (CONV - 1) :], "sh", 1)
    padded = jnp.concatenate([rim_rows, proj_head], 0).astype(jnp.float32)
    starts = jnp.cumsum(doc_lengths) - doc_lengths
    positions = lax.axis_index("sh") * length + jnp.arange(length, dtype=jnp.int32)
    starts_flag = jnp.any(positions[:, None] == starts[None, :], 1).astype(jnp.float32)
    doc_begin = jnp.max(jnp.where(starts[None, :] <= positions[:, None], starts[None, :], 0), 1)
    tap_masks = [
        (positions - (CONV - 1) + tap_index >= doc_begin).astype(jnp.float32)
        for tap_index in range(CONV)
    ]
    pseudo_flag = jnp.concatenate(
        [starts_flag[:, None], jnp.zeros((length, STEPS - 1), jnp.float32)], 1
    ).reshape(-1)
    rate_log = lax.dynamic_index_in_dim(decay_log, head, 0, False)
    bias_part = lax.dynamic_index_in_dim(decay_bias, head, 0, False)

    def mixer_terms(padded, scalar_rows, conv_part, rate_log, bias_part):
        convolved = jnp.zeros_like(padded[CONV - 1 :])
        for tap_index in range(CONV):
            convolved = (
                convolved
                + conv_part[tap_index]
                * padded[tap_index : tap_index + length]
                * tap_masks[tap_index][:, None]
            )
        activated = jax.nn.silu(convolved).reshape(length, 1 + 2 * STEPS, DK)
        query_rows = unit_norm(activated[:, 0])
        key_rows = unit_norm(activated[:, 1 : 1 + STEPS]).reshape(STEPS * length, DK)
        value_rows = activated[:, 1 + STEPS :].reshape(STEPS * length, DK)
        beta_rows = jax.nn.sigmoid(scalar_rows[:, :STEPS]).reshape(STEPS * length)
        log_rate = -jnp.exp(rate_log) * jax.nn.softplus(scalar_rows[:, STEPS] + bias_part)
        log_decay = jnp.concatenate(
            [log_rate[:, None], jnp.zeros((length, STEPS - 1), jnp.float32)], 1
        ).reshape(STEPS * length)
        return block_mixer(query_rows, key_rows, value_rows, beta_rows, log_decay, pseudo_flag)

    (query_frame, partial_value_rows, transfer, offset), mixer_back = jax.vjp(
        mixer_terms, padded, scalar_rows, conv_part, rate_log, bias_part
    )
    grad_rows = group_gather(out_grad)
    grad_rows, query_frame, partial_value_rows, transfer, offset = lax.optimization_barrier(
        (grad_rows, query_frame, partial_value_rows, transfer, offset)
    )
    identity = jnp.eye(DK, dtype=jnp.float32)[None]
    zeros_state = jnp.zeros((1, DK, DK), jnp.float32)
    prefix_map, incoming_state = carried_in(
        (transfer, offset), "sh", compose, (identity, zeros_state), False
    )
    mixer_result = partial_value_rows + hi("zy,yi->zi", query_frame, incoming_state[0])
    mixer_low = mixer_result.astype(jnp.bfloat16).astype(jnp.float32)
    gated, gate_back = jax.vjp(gate_norm, mixer_low, out_gate, out_norm)
    gated_rows = gated.astype(jnp.bfloat16)
    middle = x_float + group_scatter(bf_product(gated_rows, out_full))
    normed_mid, norm_two_back = jax.vjp(rms_norm, middle, gain_two)
    normed_two = group_gather(normed_mid.astype(jnp.bfloat16))
    gate_up = bf_product(normed_two, up_full)
    hidden_float, swiglu_back = jax.vjp(swiglu, gate_up)
    hidden = hidden_float.astype(jnp.bfloat16)
    feed_partial = bf_product(hidden, down_full)

    grad_out = out_grad.astype(jnp.float32)
    grad_hidden = bf_product(grad_rows, down_full.T)
    grad_down = heads_to_rows(bf_product(hidden.T, grad_rows))
    (grad_gate_up,) = swiglu_back(grad_hidden)
    grad_gate_up = grad_gate_up.astype(jnp.bfloat16)
    grad_normed_two = group_scatter(bf_product(grad_gate_up, up_full.T))
    grad_mid_norm, grad_gain_two = norm_two_back(grad_normed_two)
    grad_up_payload = jnp.concatenate(
        [bf_product(normed_two.T, grad_gate_up), grad_gain_two[:, None]], 1
    )
    grad_middle = grad_out + grad_mid_norm
    feed_partial, grad_up_payload, grad_branch_low = lax.optimization_barrier(
        (feed_partial, grad_up_payload, grad_middle.astype(jnp.bfloat16))
    )
    layer_out = (middle + group_scatter(feed_partial, True)).astype(jnp.bfloat16)
    grad_up_cols = heads_to_columns(grad_up_payload, True)
    grad_up = jnp.concatenate(
        [
            grad_up_cols[:, :, :half].reshape(weight_rows, FF),
            grad_up_cols[:, :, half : 2 * half].reshape(weight_rows, FF),
        ],
        1,
    )
    grad_branch = group_gather(grad_branch_low)
    grad_gated = bf_product(grad_branch, out_full.T)
    grad_outw = heads_to_rows(bf_product(gated_rows.T, grad_branch))
    grad_mixer, grad_gate, grad_out_norm = gate_back(grad_gated)
    grad_gate = grad_gate.astype(jnp.bfloat16)
    head_gradients = grad_mixer.astype(jnp.bfloat16).astype(jnp.float32)
    local_adjoint = hi("dc,dr->cr", query_frame, head_gradients)[None]
    transfer_turned = jnp.transpose(transfer, (0, 2, 1))
    later_map, state_gradient = carried_in(
        (transfer_turned, local_adjoint), "sh", compose, (identity, zeros_state), True
    )
    basis_gradient = hi("nu,wu->nw", head_gradients, incoming_state[0])
    transfer_gradient = hi("tnf,tmf->tnm", state_gradient, incoming_state)
    grad_padded, grad_scalars, grad_conv, grad_rate, grad_bias = mixer_back(
        (basis_gradient, head_gradients, transfer_gradient, state_gradient)
    )
    rim_grad = from_behind(grad_padded[: CONV - 1], "sh", -1)
    own_grad = grad_padded[CONV - 1 :]
    grad_proj = jnp.concatenate(
        [own_grad[: length - (CONV - 1)], own_grad[length - (CONV - 1) :] + rim_grad], 0
    )
    grad_head = jnp.concatenate(
        [grad_gate, grad_proj.astype(jnp.bfloat16), grad_scalars.astype(jnp.bfloat16)], 1
    )
    grad_normed_one = group_scatter(bf_product(grad_head, head_full.T), True)
    grad_x_norm, grad_gain_one = norm_one_back(grad_normed_one)
    grad_head_cols = heads_to_columns(
        jnp.concatenate([bf_product(normed_one.T, grad_head), grad_gain_one[:, None]], 1)
    )
    grad_gatew = grad_head_cols[:, :, :DK].reshape(weight_rows, D)
    grad_mixw = grad_head_cols[:, :, DK : DK + PROJ].reshape(weight_rows, HEADS * PROJ)
    grad_gatesw = grad_head_cols[:, :, DK + PROJ : WIDE].reshape(
        weight_rows, HEADS * (STEPS + 1)
    )
    grad_tokens = (grad_middle + grad_x_norm).astype(jnp.bfloat16)
    conv_grad = jnp.transpose(heads_to_rows(jnp.transpose(grad_conv)))
    one_hot = (jnp.arange(HEADS) == head).astype(jnp.float32)
    small_sums = all_sum(
        jnp.concatenate([one_hot * grad_rate, one_hot * grad_bias, grad_out_norm])
    )
    return (
        layer_out,
        grad_tokens,
        jnp.sum(grad_head_cols[:, :, WIDE], 1),
        grad_mixw,
        grad_gatesw,
        conv_grad,
        small_sums[:HEADS],
        small_sums[HEADS : 2 * HEADS],
        grad_gatew,
        small_sums[2 * HEADS :],
        grad_outw,
        jnp.sum(grad_up_cols[:, :, 2 * half], 1),
        grad_up,
        grad_down,
    )


def solution(mesh):
    seq = mesh.shape["seq"]
    across = mesh.shape["head"]
    inner = HEADS // across
    grid = Mesh(
        np.asarray(mesh.devices).reshape(seq // inner, inner, across), ("sh", "sl", "hd")
    )
    rows = P(ALL, None)
    flat = P(ALL)
    return jax.shard_map(
        local,
        mesh=grid,
        in_specs=(
            rows,
            flat,
            rows,
            rows,
            P(None, ALL),
            P(),
            P(),
            rows,
            P(),
            rows,
            flat,
            rows,
            rows,
            P(),
            rows,
        ),
        out_specs=(
            rows,
            rows,
            flat,
            rows,
            rows,
            P(None, ALL),
            P(),
            P(),
            rows,
            P(),
            rows,
            flat,
            rows,
            rows,
        ),
        check_vma=False,
    )
```

```python
import jax
import jax.numpy as jnp
import numpy as np
from jax import lax
from jax.experimental import pallas as pl
from jax.experimental.pallas import tpu as pltpu
from jax.sharding import Mesh
from jax.sharding import PartitionSpec as P

D = 1024
HEADS = 8
DK = 128
FF = 2816
STEPS = 2
CONV = 4
BLOCK = 64
PROJ = (1 + 2 * STEPS) * DK
WIDE = DK + PROJ + STEPS + 1

EPS = 1e-06
HIGH_ACCURACY = lax.Precision.HIGHEST

GROUP = ("sl", "hd")
ALL = ("sh", "sl", "hd")


def from_behind(shard, axis, by):
    peers = lax.axis_size(axis)
    pairs = [(i, i + by) for i in range(peers) if 0 <= i + by < peers]
    return lax.ppermute(shard, axis, pairs)


def carried_in(shard, axis, join, neutral, backward):
    count = lax.axis_size(axis)
    place = lax.axis_index(axis)
    ahead = count - 1 - place if backward else place
    both = lax.all_gather(jnp.stack(shard).astype(jnp.bfloat16), axis)
    gathered = (both[:, 0], both[:, 1])
    state = jax.tree.map(lambda a, e: jnp.zeros_like(a) + jnp.asarray(e, a.dtype), shard, neutral)

    def one(turn, state):
        source = count - 1 - turn if backward else turn
        return join(
            state,
            jax.tree.map(
                lambda a, own: lax.dynamic_index_in_dim(a, source, 0, False).astype(own.dtype),
                gathered,
                shard,
            ),
        )

    return lax.fori_loop(0, ahead, one, state)


def flat_place():
    return (
        lax.axis_index("sh") * lax.axis_size("sl") + lax.axis_index("sl")
    ) * lax.axis_size("hd") + lax.axis_index("hd")


def device_of(index):
    inner = lax.axis_size("sl") * lax.axis_size("hd")
    return (index // inner, (index // lax.axis_size("hd")) % lax.axis_size("sl"), index % lax.axis_size("hd"))


def sum_kernel(count, own_ref, out_ref, slots, send_sems, recv_sems):
    me = flat_place()
    barrier = pltpu.get_barrier_semaphore()

    def greet(index, carry):
        @pl.when(index != me)
        def _():
            pl.semaphore_signal(
                barrier, inc=1, device_id=device_of(index), device_id_type=pl.DeviceIdType.MESH
            )

        return carry

    lax.fori_loop(0, count, greet, 0)
    pl.semaphore_wait(barrier, count - 1)

    def copy_to(index):
        return pltpu.make_async_remote_copy(
            src_ref=own_ref,
            dst_ref=slots.at[me],
            send_sem=send_sems.at[index],
            recv_sem=recv_sems.at[me],
            device_id=device_of(index),
            device_id_type=pl.DeviceIdType.MESH,
        )

    def copy_from(index):
        return pltpu.make_async_remote_copy(
            src_ref=own_ref,
            dst_ref=slots.at[index],
            send_sem=send_sems.at[index],
            recv_sem=recv_sems.at[index],
            device_id=device_of(index),
            device_id_type=pl.DeviceIdType.MESH,
        )

    def send(index, carry):
        @pl.when(index != me)
        def _():
            copy_to(index).start()

        return carry

    lax.fori_loop(0, count, send, 0)
    slots[me] = own_ref[...]

    def finish(index, carry):
        @pl.when(index != me)
        def _():
            copy_to(index).wait_send()
            copy_from(index).wait_recv()

        return carry

    lax.fori_loop(0, count, finish, 0)
    out_ref[...] = jnp.sum(slots[...], axis=0)


def all_sum(vector):
    count = lax.axis_size("sh") * lax.axis_size("sl") * lax.axis_size("hd")
    size = vector.shape[0]
    lanes = 128
    tile = 8 * lanes
    padded = -(-size // tile) * tile
    block = jnp.pad(vector, (0, padded - size)).reshape(padded // lanes, lanes)
    total = pl.pallas_call(
        lambda *refs: sum_kernel(count, *refs),
        out_shape=jax.ShapeDtypeStruct(block.shape, jnp.float32),
        in_specs=[pl.BlockSpec(memory_space=pltpu.VMEM)],
        out_specs=pl.BlockSpec(memory_space=pltpu.VMEM),
        scratch_shapes=[
            pltpu.VMEM((count,) + block.shape, jnp.float32),
            pltpu.SemaphoreType.DMA((count,)),
            pltpu.SemaphoreType.DMA((count,)),
        ],
        compiler_params=pltpu.CompilerParams(collective_id=0, has_side_effects=True),
    )(block)
    return total.reshape(-1)[:size]


def rms_norm(values, scale_gain):
    return values * lax.rsqrt(jnp.mean(values * values, axis=-1, keepdims=True) + EPS) * scale_gain


def unit_norm(values):
    return values * lax.rsqrt(jnp.sum(values * values, axis=-1, keepdims=True) + EPS)


def bf_product(first_mat, second_mat):
    return jnp.dot(first_mat, second_mat, preferred_element_type=jnp.float32)


def hi(spec, *arrays):
    return jnp.einsum(spec, *arrays, precision=HIGH_ACCURACY)


def compose(early_pair, late_pair):
    early_mat, early_add = early_pair
    late_mat, late_add = late_pair
    joined = hi("hij,hjk->hik", late_mat, early_mat)
    shifted = hi("hij,hjk->hik", late_mat, early_add) + late_add
    return (joined, shifted)


def gate_norm(values, out_gate, scale_gain):
    return rms_norm(values, scale_gain) * jax.nn.silu(out_gate)


def swiglu(gate_up):
    half = gate_up.shape[1] // 2
    return jax.nn.silu(gate_up[:, :half]) * gate_up[:, half:]


def owner_pairs(inverse):
    groups = lax.axis_size("sh")
    pairs = [(g * HEADS + t, t * groups + g) for g in range(groups) for t in range(HEADS)]
    return [(b, a) for a, b in pairs] if inverse else pairs


def rows_to_heads(block):
    moved = lax.ppermute(block, ALL, owner_pairs(True))
    return lax.all_gather(moved, "sh", axis=0, tiled=True)


def heads_to_rows(partial):
    low = partial.astype(jnp.bfloat16)
    summed = lax.psum_scatter(low, "sh", scatter_dimension=0, tiled=True)
    return lax.ppermute(summed, ALL, owner_pairs(False)).astype(jnp.float32)


def columns_to_heads(local_cols):
    per_head = jnp.transpose(local_cols, (1, 0, 2))
    mine = lax.all_to_all(per_head, GROUP, 0, 0, tiled=True)
    mine = mine.reshape(-1, mine.shape[-1])
    return lax.all_gather(mine, "sh", axis=0, tiled=True)


def heads_to_columns(partial, direct=False):
    low = partial.astype(jnp.bfloat16)
    if direct:
        groups = lax.axis_size("sh")
        pieces = low.reshape((groups, low.shape[0] // groups) + low.shape[1:])
        moved = lax.all_to_all(pieces, "sh", 0, 0, tiled=True)
        summed = jnp.sum(moved.astype(jnp.float32), 0).astype(jnp.bfloat16)
    else:
        summed = lax.psum_scatter(low, "sh", scatter_dimension=0, tiled=True)
    summed = summed.reshape(HEADS, -1, summed.shape[-1])
    back = lax.all_to_all(summed, GROUP, 0, 0, tiled=True)
    return jnp.transpose(back, (1, 0, 2)).astype(jnp.float32)


def group_gather(rows):
    return lax.all_gather(rows, GROUP, axis=0, tiled=True)


def group_scatter(partial, direct=False):
    low = partial.astype(jnp.bfloat16)
    if direct:
        pieces = low.reshape((HEADS, low.shape[0] // HEADS) + low.shape[1:])
        moved = lax.all_to_all(pieces, GROUP, 0, 0, tiled=True)
        return jnp.sum(moved.astype(jnp.float32), 0)
    return lax.psum_scatter(low, GROUP, scatter_dimension=0, tiled=True).astype(jnp.float32)


def masked_power_inverse(system):
    size = system.shape[-1]
    places = jnp.arange(size)
    base = 8
    inside = (places[:, None] // base == places[None, :] // base) & (
        places[:, None] > places[None, :]
    )
    step = -(system * inside.astype(system.dtype))
    eye = jnp.eye(size, dtype=system.dtype)
    result = eye + step
    for _ in range(2):
        step = hi("bij,bjk->bik", step, step)
        result = result + hi("bij,bjk->bik", result, step)
    width = base
    while width < size:
        across = (places[:, None] // (2 * width) == places[None, :] // (2 * width)) & (
            places[:, None] // width != places[None, :] // width
        )
        lower_left = system * across.astype(system.dtype)
        result = result - hi("bij,bjk->bik", result, hi("bij,bjk->bik", lower_left, result))
        width = 2 * width
    return result


@jax.custom_vjp
def unit_lower_inverse(system):
    return masked_power_inverse(system)


def inverse_keep(system):
    inverse = masked_power_inverse(system)
    return inverse, inverse


def inverse_back(inverse, grad):
    turned = jnp.swapaxes(inverse, -1, -2)
    return (-hi("bij,bjk->bik", turned, hi("bij,bjk->bik", grad, turned)),)


unit_lower_inverse.defvjp(inverse_keep, inverse_back)


def block_mixer(query_rows, key_rows, value_rows, beta_rows, log_decay, starts_flag):
    pseudo = key_rows.shape[0]
    span = STEPS * BLOCK
    blocks = pseudo // span
    queries = query_rows.reshape(blocks, BLOCK, DK)
    keys = key_rows.reshape(blocks, span, DK)
    values = value_rows.reshape(blocks, span, DK)
    betas = beta_rows.reshape(blocks, span)
    decays = log_decay.reshape(blocks, span)
    flags = starts_flag.reshape(blocks, span)
    places = jnp.arange(span)
    lower = places[:, None] >= places[None, :]
    strict = (places[:, None] > places[None, :]).astype(jnp.float32)
    identity = jnp.eye(span, dtype=jnp.float32)
    eye_key = jnp.eye(DK, dtype=jnp.float32)

    summed = jnp.cumsum(decays, axis=1)
    segment = jnp.cumsum(flags, axis=1)
    same_doc = (segment[:, :, None] == segment[:, None, :]) & lower
    decay_ratio = jnp.exp(
        jnp.where(same_doc, summed[:, :, None] - summed[:, None, :], 0.0)
    ) * same_doc.astype(jnp.float32)
    from_start = jnp.exp(summed) * (segment == 0.0).astype(jnp.float32)
    key_key = hi("bik,bjk->bij", keys, keys)
    system = identity + betas[:, :, None] * decay_ratio * key_key * strict
    right_side = jnp.concatenate(
        [betas[:, :, None] * values, (betas * from_start)[:, :, None] * keys], 2
    )
    solved = hi("bij,bjk->bik", unit_lower_inverse(system), right_side)
    fresh = solved[:, :, :DK]
    carried = solved[:, :, DK:]
    last_keys = keys * decay_ratio[:, -1, :, None]
    transfer = from_start[:, -1, None, None] * eye_key - hi("bsi,bsj->bij", last_keys, carried)
    offset = hi("bsi,bsj->bij", last_keys, fresh)
    query_key = hi("bqk,bsk->bqs", queries, keys) * decay_ratio[:, STEPS - 1 :: STEPS]
    frame = from_start[:, STEPS - 1 :: STEPS, None] * queries - hi(
        "bqs,bsj->bqj", query_key, carried
    )
    direct = hi("bqs,bsj->bqj", query_key, fresh)

    state = jnp.concatenate([eye_key, jnp.zeros((DK, DK), jnp.float32)], 1)
    states = []
    for index in range(blocks):
        states.append(state)
        state = hi("ij,jk->ik", transfer[index], state) + jnp.concatenate(
            [jnp.zeros((DK, DK), jnp.float32), offset[index]], 1
        )
    states = jnp.stack(states)
    mats = states[:, :, :DK]
    adds = states[:, :, DK:]
    final_mat = state[:, :DK]
    final_add = state[:, DK:]
    query_frame = hi("bqi,bij->bqj", frame, mats)
    partial = hi("bqi,bij->bqj", frame, adds) + direct
    return (
        query_frame.reshape(blocks * BLOCK, DK),
        partial.reshape(blocks * BLOCK, DK),
        final_mat[None],
        final_add[None],
    )


def local(
    tokens_in,
    mixer_norm,
    mix_weight,
    head_gates,
    conv_taps,
    decay_log,
    decay_bias,
    gate_weight,
    out_norm,
    out_weight,
    feed_norm,
    up_weight,
    down_weight,
    doc_lengths,
    out_grad,
):
    row_count = tokens_in.shape[0]
    weight_rows = mix_weight.shape[0]
    head = lax.axis_index("sl") * lax.axis_size("hd") + lax.axis_index("hd")
    length = row_count * HEADS

    head_cols = jnp.concatenate(
        [
            gate_weight.reshape(weight_rows, HEADS, DK),
            mix_weight.reshape(weight_rows, HEADS, PROJ),
            head_gates.reshape(weight_rows, HEADS, STEPS + 1),
            jnp.broadcast_to(mixer_norm[:, None, None], (weight_rows, HEADS, 1)),
        ],
        2,
    )
    head_wide = columns_to_heads(head_cols)
    head_full = head_wide[:, :WIDE]
    gain_one = head_wide[:, WIDE].astype(jnp.float32)
    half = FF // HEADS
    up_cols = jnp.concatenate(
        [
            up_weight[:, :FF].reshape(weight_rows, HEADS, half),
            up_weight[:, FF:].reshape(weight_rows, HEADS, half),
            jnp.broadcast_to(feed_norm[:, None, None], (weight_rows, HEADS, 1)),
        ],
        2,
    )
    up_wide = columns_to_heads(up_cols)
    up_full = up_wide[:, : 2 * half]
    gain_two = up_wide[:, 2 * half].astype(jnp.float32)
    out_full = rows_to_heads(out_weight)
    down_full = rows_to_heads(down_weight)
    conv_part = jnp.transpose(rows_to_heads(jnp.transpose(conv_taps))).astype(jnp.float32)

    x_float = tokens_in.astype(jnp.float32)
    normed_float, norm_one_back = jax.vjp(rms_norm, x_float, gain_one)
    normed_one = group_gather(normed_float.astype(jnp.bfloat16))
    head_out = bf_product(normed_one, head_full)
    out_gate = head_out[:, :DK]
    proj_head = head_out[:, DK : DK + PROJ].astype(jnp.bfloat16)
    scalar_rows = head_out[:, DK + PROJ :].astype(jnp.bfloat16).astype(jnp.float32)

    rim_rows = from_behind(proj_head[length - (CONV - 1) :], "sh", 1)
    padded = jnp.concatenate([rim_rows, proj_head], 0).astype(jnp.float32)
    starts = jnp.cumsum(doc_lengths) - doc_lengths
    positions = lax.axis_index("sh") * length + jnp.arange(length, dtype=jnp.int32)
    starts_flag = jnp.any(positions[:, None] == starts[None, :], 1).astype(jnp.float32)
    doc_begin = jnp.max(jnp.where(starts[None, :] <= positions[:, None], starts[None, :], 0), 1)
    tap_masks = [
        (positions - (CONV - 1) + tap_index >= doc_begin).astype(jnp.float32)
        for tap_index in range(CONV)
    ]
    pseudo_flag = jnp.concatenate(
        [starts_flag[:, None], jnp.zeros((length, STEPS - 1), jnp.float32)], 1
    ).reshape(-1)
    rate_log = lax.dynamic_index_in_dim(decay_log, head, 0, False)
    bias_part = lax.dynamic_index_in_dim(decay_bias, head, 0, False)

    def mixer_terms(padded, scalar_rows, conv_part, rate_log, bias_part):
        convolved = jnp.zeros_like(padded[CONV - 1 :])
        for tap_index in range(CONV):
            convolved = (
                convolved
                + conv_part[tap_index]
                * padded[tap_index : tap_index + length]
                * tap_masks[tap_index][:, None]
            )
        activated = jax.nn.silu(convolved).reshape(length, 1 + 2 * STEPS, DK)
        query_rows = unit_norm(activated[:, 0])
        key_rows = unit_norm(activated[:, 1 : 1 + STEPS]).reshape(STEPS * length, DK)
        value_rows = activated[:, 1 + STEPS :].reshape(STEPS * length, DK)
        beta_rows = jax.nn.sigmoid(scalar_rows[:, :STEPS]).reshape(STEPS * length)
        log_rate = -jnp.exp(rate_log) * jax.nn.softplus(scalar_rows[:, STEPS] + bias_part)
        log_decay = jnp.concatenate(
            [log_rate[:, None], jnp.zeros((length, STEPS - 1), jnp.float32)], 1
        ).reshape(STEPS * length)
        return block_mixer(query_rows, key_rows, value_rows, beta_rows, log_decay, pseudo_flag)

    (query_frame, partial_value_rows, transfer, offset), mixer_back = jax.vjp(
        mixer_terms, padded, scalar_rows, conv_part, rate_log, bias_part
    )
    grad_rows = group_gather(out_grad)
    grad_rows, query_frame, partial_value_rows, transfer, offset = lax.optimization_barrier(
        (grad_rows, query_frame, partial_value_rows, transfer, offset)
    )
    identity = jnp.eye(DK, dtype=jnp.float32)[None]
    zeros_state = jnp.zeros((1, DK, DK), jnp.float32)
    prefix_map, incoming_state = carried_in(
        (transfer, offset), "sh", compose, (identity, zeros_state), False
    )
    mixer_result = partial_value_rows + hi("zy,yi->zi", query_frame, incoming_state[0])
    mixer_low = mixer_result.astype(jnp.bfloat16).astype(jnp.float32)
    gated, gate_back = jax.vjp(gate_norm, mixer_low, out_gate, out_norm)
    gated_rows = gated.astype(jnp.bfloat16)
    middle = x_float + group_scatter(bf_product(gated_rows, out_full))
    normed_mid, norm_two_back = jax.vjp(rms_norm, middle, gain_two)
    normed_two = group_gather(normed_mid.astype(jnp.bfloat16))
    gate_up = bf_product(normed_two, up_full)
    hidden_float, swiglu_back = jax.vjp(swiglu, gate_up)
    hidden = hidden_float.astype(jnp.bfloat16)
    feed_partial = bf_product(hidden, down_full)

    grad_out = out_grad.astype(jnp.float32)
    grad_hidden = bf_product(grad_rows, down_full.T)
    grad_down_partial = bf_product(hidden.T, grad_rows)
    (grad_gate_up,) = swiglu_back(grad_hidden)
    grad_gate_up = grad_gate_up.astype(jnp.bfloat16)
    grad_normed_two = group_scatter(bf_product(grad_gate_up, up_full.T))
    grad_mid_norm, grad_gain_two = norm_two_back(grad_normed_two)
    grad_up_payload = jnp.concatenate(
        [bf_product(normed_two.T, grad_gate_up), grad_gain_two[:, None]], 1
    )
    grad_middle = grad_out + grad_mid_norm
    feed_partial, grad_up_payload, grad_down_partial, grad_branch_low = lax.optimization_barrier(
        (feed_partial, grad_up_payload, grad_down_partial, grad_middle.astype(jnp.bfloat16))
    )
    grad_down = heads_to_rows(grad_down_partial)
    layer_out = (middle + group_scatter(feed_partial)).astype(jnp.bfloat16)
    grad_up_cols = heads_to_columns(grad_up_payload, True)
    grad_up = jnp.concatenate(
        [
            grad_up_cols[:, :, :half].reshape(weight_rows, FF),
            grad_up_cols[:, :, half : 2 * half].reshape(weight_rows, FF),
        ],
        1,
    )
    grad_branch = group_gather(grad_branch_low)
    grad_gated = bf_product(grad_branch, out_full.T)
    grad_outw = heads_to_rows(bf_product(gated_rows.T, grad_branch))
    grad_mixer, grad_gate, grad_out_norm = gate_back(grad_gated)
    grad_gate = grad_gate.astype(jnp.bfloat16)
    head_gradients = grad_mixer.astype(jnp.bfloat16).astype(jnp.float32)
    local_adjoint = hi("dc,dr->cr", query_frame, head_gradients)[None]
    transfer_turned = jnp.transpose(transfer, (0, 2, 1))
    later_map, state_gradient = carried_in(
        (transfer_turned, local_adjoint), "sh", compose, (identity, zeros_state), True
    )
    basis_gradient = hi("nu,wu->nw", head_gradients, incoming_state[0])
    transfer_gradient = hi("tnf,tmf->tnm", state_gradient, incoming_state)
    grad_padded, grad_scalars, grad_conv, grad_rate, grad_bias = mixer_back(
        (basis_gradient, head_gradients, transfer_gradient, state_gradient)
    )
    rim_grad = from_behind(grad_padded[: CONV - 1], "sh", -1)
    own_grad = grad_padded[CONV - 1 :]
    grad_proj = jnp.concatenate(
        [own_grad[: length - (CONV - 1)], own_grad[length - (CONV - 1) :] + rim_grad], 0
    )
    grad_head = jnp.concatenate(
        [grad_gate, grad_proj.astype(jnp.bfloat16), grad_scalars.astype(jnp.bfloat16)], 1
    )
    grad_normed_one = group_scatter(bf_product(grad_head, head_full.T), True)
    grad_x_norm, grad_gain_one = norm_one_back(grad_normed_one)
    grad_head_cols = heads_to_columns(
        jnp.concatenate([bf_product(normed_one.T, grad_head), grad_gain_one[:, None]], 1)
    )
    grad_gatew = grad_head_cols[:, :, :DK].reshape(weight_rows, D)
    grad_mixw = grad_head_cols[:, :, DK : DK + PROJ].reshape(weight_rows, HEADS * PROJ)
    grad_gatesw = grad_head_cols[:, :, DK + PROJ : WIDE].reshape(
        weight_rows, HEADS * (STEPS + 1)
    )
    grad_tokens = (grad_middle + grad_x_norm).astype(jnp.bfloat16)
    conv_grad = jnp.transpose(heads_to_rows(jnp.transpose(grad_conv)))
    one_hot = (jnp.arange(HEADS) == head).astype(jnp.float32)
    small_sums = all_sum(
        jnp.concatenate([one_hot * grad_rate, one_hot * grad_bias, grad_out_norm])
    )
    return (
        layer_out,
        grad_tokens,
        jnp.sum(grad_head_cols[:, :, WIDE], 1),
        grad_mixw,
        grad_gatesw,
        conv_grad,
        small_sums[:HEADS],
        small_sums[HEADS : 2 * HEADS],
        grad_gatew,
        small_sums[2 * HEADS :],
        grad_outw,
        jnp.sum(grad_up_cols[:, :, 2 * half], 1),
        grad_up,
        grad_down,
    )


def solution(mesh):
    seq = mesh.shape["seq"]
    across = mesh.shape["head"]
    inner = HEADS // across
    grid = Mesh(
        np.asarray(mesh.devices).reshape(seq // inner, inner, across), ("sh", "sl", "hd")
    )
    rows = P(ALL, None)
    flat = P(ALL)
    return jax.shard_map(
        local,
        mesh=grid,
        in_specs=(
            rows,
            flat,
            rows,
            rows,
            P(None, ALL),
            P(),
            P(),
            rows,
            P(),
            rows,
            flat,
            rows,
            rows,
            P(),
            rows,
        ),
        out_specs=(
            rows,
            rows,
            flat,
            rows,
            rows,
            P(None, ALL),
            P(),
            P(),
            rows,
            P(),
            rows,
            flat,
            rows,
            rows,
        ),
        check_vma=False,
    )
```

```python
import jax
import jax.numpy as jnp
import numpy as np
from jax import lax
from jax.experimental import pallas as pl
from jax.experimental.pallas import tpu as pltpu
from jax.sharding import Mesh
from jax.sharding import PartitionSpec as P

D = 1024
HEADS = 8
DK = 128
FF = 2816
STEPS = 2
CONV = 4
BLOCK = 64
PROJ = (1 + 2 * STEPS) * DK
WIDE = DK + PROJ + STEPS + 1

EPS = 1e-06
HIGH_ACCURACY = lax.Precision.HIGH

GROUP = ("sl", "hd")
ALL = ("sh", "sl", "hd")


def from_behind(shard, axis, by):
    peers = lax.axis_size(axis)
    pairs = [(i, i + by) for i in range(peers) if 0 <= i + by < peers]
    return lax.ppermute(shard, axis, pairs)


def carried_in(shard, axis, join, neutral, backward):
    count = lax.axis_size(axis)
    place = lax.axis_index(axis)
    ahead = count - 1 - place if backward else place
    both = lax.all_gather(jnp.stack(shard).astype(jnp.bfloat16), axis)
    gathered = (both[:, 0], both[:, 1])
    state = jax.tree.map(lambda a, e: jnp.zeros_like(a) + jnp.asarray(e, a.dtype), shard, neutral)

    def one(turn, state):
        source = count - 1 - turn if backward else turn
        return join(
            state,
            jax.tree.map(
                lambda a, own: lax.dynamic_index_in_dim(a, source, 0, False).astype(own.dtype),
                gathered,
                shard,
            ),
        )

    return lax.fori_loop(0, ahead, one, state)


def flat_place():
    return (
        lax.axis_index("sh") * lax.axis_size("sl") + lax.axis_index("sl")
    ) * lax.axis_size("hd") + lax.axis_index("hd")


def device_of(index):
    inner = lax.axis_size("sl") * lax.axis_size("hd")
    return (index // inner, (index // lax.axis_size("hd")) % lax.axis_size("sl"), index % lax.axis_size("hd"))


def sum_kernel(count, own_ref, out_ref, slots, send_sems, recv_sems):
    me = flat_place()
    barrier = pltpu.get_barrier_semaphore()

    def greet(index, carry):
        @pl.when(index != me)
        def _():
            pl.semaphore_signal(
                barrier, inc=1, device_id=device_of(index), device_id_type=pl.DeviceIdType.MESH
            )

        return carry

    lax.fori_loop(0, count, greet, 0)
    pl.semaphore_wait(barrier, count - 1)

    def copy_to(index):
        return pltpu.make_async_remote_copy(
            src_ref=own_ref,
            dst_ref=slots.at[me],
            send_sem=send_sems.at[index],
            recv_sem=recv_sems.at[me],
            device_id=device_of(index),
            device_id_type=pl.DeviceIdType.MESH,
        )

    def copy_from(index):
        return pltpu.make_async_remote_copy(
            src_ref=own_ref,
            dst_ref=slots.at[index],
            send_sem=send_sems.at[index],
            recv_sem=recv_sems.at[index],
            device_id=device_of(index),
            device_id_type=pl.DeviceIdType.MESH,
        )

    def send(index, carry):
        @pl.when(index != me)
        def _():
            copy_to(index).start()

        return carry

    lax.fori_loop(0, count, send, 0)
    slots[me] = own_ref[...]

    def finish(index, carry):
        @pl.when(index != me)
        def _():
            copy_to(index).wait_send()
            copy_from(index).wait_recv()

        return carry

    lax.fori_loop(0, count, finish, 0)
    out_ref[...] = jnp.sum(slots[...], axis=0)


def all_sum(vector):
    count = lax.axis_size("sh") * lax.axis_size("sl") * lax.axis_size("hd")
    size = vector.shape[0]
    lanes = 128
    tile = 8 * lanes
    padded = -(-size // tile) * tile
    block = jnp.pad(vector, (0, padded - size)).reshape(padded // lanes, lanes)
    total = pl.pallas_call(
        lambda *refs: sum_kernel(count, *refs),
        out_shape=jax.ShapeDtypeStruct(block.shape, jnp.float32),
        in_specs=[pl.BlockSpec(memory_space=pltpu.VMEM)],
        out_specs=pl.BlockSpec(memory_space=pltpu.VMEM),
        scratch_shapes=[
            pltpu.VMEM((count,) + block.shape, jnp.float32),
            pltpu.SemaphoreType.DMA((count,)),
            pltpu.SemaphoreType.DMA((count,)),
        ],
        compiler_params=pltpu.CompilerParams(collective_id=0, has_side_effects=True),
    )(block)
    return total.reshape(-1)[:size]


def rms_norm(values, scale_gain):
    return values * lax.rsqrt(jnp.mean(values * values, axis=-1, keepdims=True) + EPS) * scale_gain


def unit_norm(values):
    return values * lax.rsqrt(jnp.sum(values * values, axis=-1, keepdims=True) + EPS)


def bf_product(first_mat, second_mat):
    return jnp.dot(first_mat, second_mat, preferred_element_type=jnp.float32)


def hi(spec, *arrays):
    return jnp.einsum(spec, *arrays, precision=HIGH_ACCURACY)


def compose(early_pair, late_pair):
    early_mat, early_add = early_pair
    late_mat, late_add = late_pair
    joined = hi("hij,hjk->hik", late_mat, early_mat)
    shifted = hi("hij,hjk->hik", late_mat, early_add) + late_add
    return (joined, shifted)


def gate_norm(values, out_gate, scale_gain):
    return rms_norm(values, scale_gain) * jax.nn.silu(out_gate)


def swiglu(gate_up):
    half = gate_up.shape[1] // 2
    return jax.nn.silu(gate_up[:, :half]) * gate_up[:, half:]


def owner_pairs(inverse):
    groups = lax.axis_size("sh")
    pairs = [(g * HEADS + t, t * groups + g) for g in range(groups) for t in range(HEADS)]
    return [(b, a) for a, b in pairs] if inverse else pairs


def rows_to_heads(blocks):
    groups = lax.axis_size("sh")
    width = blocks[0].shape[1]
    used = sum(b.shape[0] for b in blocks)
    least = (1 << 20) // (groups * width * 2) + 1
    rows = -(-max(used, least) // 8) * 8
    packed = jnp.concatenate(
        list(blocks) + [jnp.zeros((rows - used, width), blocks[0].dtype)], 0
    )
    moved = lax.ppermute(packed, ALL, owner_pairs(True))
    full = lax.all_gather(moved, "sh", axis=0, tiled=False)
    parts = []
    first = 0
    for block in blocks:
        size = block.shape[0]
        parts.append(full[:, first : first + size].reshape(groups * size, width))
        first += size
    return parts


def heads_to_rows(partials):
    groups = lax.axis_size("sh")
    pieces = [
        p.astype(jnp.bfloat16).reshape((groups, p.shape[0] // groups) + p.shape[1:])
        for p in partials
    ]
    joined = jnp.concatenate(pieces, 1)
    joined = joined.reshape((-1,) + joined.shape[2:])
    summed = lax.psum_scatter(joined, "sh", scatter_dimension=0, tiled=True)
    moved = lax.ppermute(summed, ALL, owner_pairs(False)).astype(jnp.float32)
    parts = []
    first = 0
    for piece in pieces:
        size = piece.shape[1]
        parts.append(moved[first : first + size])
        first += size
    return parts


def columns_to_heads(local_cols):
    per_head = jnp.transpose(local_cols, (1, 0, 2))
    mine = lax.all_to_all(per_head, GROUP, 0, 0, tiled=True)
    mine = mine.reshape(-1, mine.shape[-1])
    return lax.all_gather(mine, "sh", axis=0, tiled=True)


def heads_to_columns(partial, direct=False):
    low = partial.astype(jnp.bfloat16)
    if direct:
        groups = lax.axis_size("sh")
        pieces = low.reshape((groups, low.shape[0] // groups) + low.shape[1:])
        moved = lax.all_to_all(pieces, "sh", 0, 0, tiled=True)
        summed = jnp.sum(moved.astype(jnp.float32), 0).astype(jnp.bfloat16)
    else:
        summed = lax.psum_scatter(low, "sh", scatter_dimension=0, tiled=True)
    summed = summed.reshape(HEADS, -1, summed.shape[-1])
    back = lax.all_to_all(summed, GROUP, 0, 0, tiled=True)
    return jnp.transpose(back, (1, 0, 2)).astype(jnp.float32)


def group_gather(rows):
    return lax.all_gather(rows, GROUP, axis=0, tiled=True)


def group_scatter(partial, direct=False):
    low = partial.astype(jnp.bfloat16)
    if direct:
        pieces = low.reshape((HEADS, low.shape[0] // HEADS) + low.shape[1:])
        moved = lax.all_to_all(pieces, GROUP, 0, 0, tiled=True)
        return jnp.sum(moved.astype(jnp.float32), 0)
    return lax.psum_scatter(low, GROUP, scatter_dimension=0, tiled=True).astype(jnp.float32)


def masked_power_inverse(system):
    size = system.shape[-1]
    places = jnp.arange(size)
    base = 8
    inside = (places[:, None] // base == places[None, :] // base) & (
        places[:, None] > places[None, :]
    )
    step = -(system * inside.astype(system.dtype))
    eye = jnp.eye(size, dtype=system.dtype)
    result = eye + step
    for _ in range(2):
        step = hi("bij,bjk->bik", step, step)
        result = result + hi("bij,bjk->bik", result, step)
    width = base
    while width < size:
        across = (places[:, None] // (2 * width) == places[None, :] // (2 * width)) & (
            places[:, None] // width != places[None, :] // width
        )
        lower_left = system * across.astype(system.dtype)
        result = result - hi("bij,bjk->bik", result, hi("bij,bjk->bik", lower_left, result))
        width = 2 * width
    return result


@jax.custom_vjp
def unit_lower_inverse(system):
    return masked_power_inverse(system)


def inverse_keep(system):
    inverse = masked_power_inverse(system)
    return inverse, inverse


def inverse_back(inverse, grad):
    turned = jnp.swapaxes(inverse, -1, -2)
    return (-hi("bij,bjk->bik", turned, hi("bij,bjk->bik", grad, turned)),)


unit_lower_inverse.defvjp(inverse_keep, inverse_back)


def block_mixer(query_rows, key_rows, value_rows, beta_rows, log_decay, starts_flag):
    pseudo = key_rows.shape[0]
    span = STEPS * BLOCK
    blocks = pseudo // span
    queries = query_rows.reshape(blocks, BLOCK, DK)
    keys = key_rows.reshape(blocks, span, DK)
    values = value_rows.reshape(blocks, span, DK)
    betas = beta_rows.reshape(blocks, span)
    decays = log_decay.reshape(blocks, span)
    flags = starts_flag.reshape(blocks, span)
    places = jnp.arange(span)
    lower = places[:, None] >= places[None, :]
    strict = (places[:, None] > places[None, :]).astype(jnp.float32)
    identity = jnp.eye(span, dtype=jnp.float32)
    eye_key = jnp.eye(DK, dtype=jnp.float32)

    summed = jnp.cumsum(decays, axis=1)
    segment = jnp.cumsum(flags, axis=1)
    same_doc = (segment[:, :, None] == segment[:, None, :]) & lower
    decay_ratio = jnp.exp(
        jnp.where(same_doc, summed[:, :, None] - summed[:, None, :], 0.0)
    ) * same_doc.astype(jnp.float32)
    from_start = jnp.exp(summed) * (segment == 0.0).astype(jnp.float32)
    key_key = hi("bik,bjk->bij", keys, keys)
    system = identity + betas[:, :, None] * decay_ratio * key_key * strict
    right_side = jnp.concatenate(
        [betas[:, :, None] * values, (betas * from_start)[:, :, None] * keys], 2
    )
    solved = hi("bij,bjk->bik", unit_lower_inverse(system), right_side)
    fresh = solved[:, :, :DK]
    carried = solved[:, :, DK:]
    last_keys = keys * decay_ratio[:, -1, :, None]
    transfer = from_start[:, -1, None, None] * eye_key - hi("bsi,bsj->bij", last_keys, carried)
    offset = hi("bsi,bsj->bij", last_keys, fresh)
    query_key = hi("bqk,bsk->bqs", queries, keys) * decay_ratio[:, STEPS - 1 :: STEPS]
    frame = from_start[:, STEPS - 1 :: STEPS, None] * queries - hi(
        "bqs,bsj->bqj", query_key, carried
    )
    direct = hi("bqs,bsj->bqj", query_key, fresh)

    state = jnp.concatenate([eye_key, jnp.zeros((DK, DK), jnp.float32)], 1)
    states = []
    for index in range(blocks):
        states.append(state)
        state = hi("ij,jk->ik", transfer[index], state) + jnp.concatenate(
            [jnp.zeros((DK, DK), jnp.float32), offset[index]], 1
        )
    states = jnp.stack(states)
    mats = states[:, :, :DK]
    adds = states[:, :, DK:]
    final_mat = state[:, :DK]
    final_add = state[:, DK:]
    query_frame = hi("bqi,bij->bqj", frame, mats)
    partial = hi("bqi,bij->bqj", frame, adds) + direct
    return (
        query_frame.reshape(blocks * BLOCK, DK),
        partial.reshape(blocks * BLOCK, DK),
        final_mat[None],
        final_add[None],
    )


def local(
    tokens_in,
    mixer_norm,
    mix_weight,
    head_gates,
    conv_taps,
    decay_log,
    decay_bias,
    gate_weight,
    out_norm,
    out_weight,
    feed_norm,
    up_weight,
    down_weight,
    doc_lengths,
    out_grad,
):
    row_count = tokens_in.shape[0]
    weight_rows = mix_weight.shape[0]
    head = lax.axis_index("sl") * lax.axis_size("hd") + lax.axis_index("hd")
    length = row_count * HEADS

    head_cols = jnp.concatenate(
        [
            gate_weight.reshape(weight_rows, HEADS, DK),
            mix_weight.reshape(weight_rows, HEADS, PROJ),
            head_gates.reshape(weight_rows, HEADS, STEPS + 1),
            jnp.broadcast_to(mixer_norm[:, None, None], (weight_rows, HEADS, 1)),
        ],
        2,
    )
    head_wide = columns_to_heads(head_cols)
    head_full = head_wide[:, :WIDE]
    gain_one = head_wide[:, WIDE].astype(jnp.float32)
    half = FF // HEADS
    up_cols = jnp.concatenate(
        [
            up_weight[:, :FF].reshape(weight_rows, HEADS, half),
            up_weight[:, FF:].reshape(weight_rows, HEADS, half),
            jnp.broadcast_to(feed_norm[:, None, None], (weight_rows, HEADS, 1)),
        ],
        2,
    )
    up_wide = columns_to_heads(up_cols)
    up_full = up_wide[:, : 2 * half]
    gain_two = up_wide[:, 2 * half].astype(jnp.float32)
    tap_width = conv_taps.shape[1]
    tap_row = jnp.pad(conv_taps.reshape(1, -1), ((0, 0), (0, D - CONV * tap_width)))
    out_full, down_full, tap_rows = rows_to_heads((out_weight, down_weight, tap_row))
    conv_part = jnp.transpose(
        tap_rows[:, : CONV * tap_width].reshape(-1, CONV, tap_width), (1, 0, 2)
    ).reshape(CONV, -1).astype(jnp.float32)

    x_float = tokens_in.astype(jnp.float32)
    normed_float, norm_one_back = jax.vjp(rms_norm, x_float, gain_one)
    normed_one = group_gather(normed_float.astype(jnp.bfloat16))
    head_out = bf_product(normed_one, head_full)
    out_gate = head_out[:, :DK]
    proj_head = head_out[:, DK : DK + PROJ].astype(jnp.bfloat16)
    scalar_rows = head_out[:, DK + PROJ :].astype(jnp.bfloat16).astype(jnp.float32)

    rim_rows = from_behind(proj_head[length - (CONV - 1) :], "sh", 1)
    padded = jnp.concatenate([rim_rows, proj_head], 0).astype(jnp.float32)
    starts = jnp.cumsum(doc_lengths) - doc_lengths
    positions = lax.axis_index("sh") * length + jnp.arange(length, dtype=jnp.int32)
    starts_flag = jnp.any(positions[:, None] == starts[None, :], 1).astype(jnp.float32)
    doc_begin = jnp.max(jnp.where(starts[None, :] <= positions[:, None], starts[None, :], 0), 1)
    tap_masks = [
        (positions - (CONV - 1) + tap_index >= doc_begin).astype(jnp.float32)
        for tap_index in range(CONV)
    ]
    pseudo_flag = jnp.concatenate(
        [starts_flag[:, None], jnp.zeros((length, STEPS - 1), jnp.float32)], 1
    ).reshape(-1)
    rate_log = lax.dynamic_index_in_dim(decay_log, head, 0, False)
    bias_part = lax.dynamic_index_in_dim(decay_bias, head, 0, False)

    def mixer_inputs(padded, scalar_rows, conv_part, rate_log, bias_part):
        convolved = jnp.zeros_like(padded[CONV - 1 :])
        for tap_index in range(CONV):
            convolved = (
                convolved
                + conv_part[tap_index]
                * padded[tap_index : tap_index + length]
                * tap_masks[tap_index][:, None]
            )
        activated = jax.nn.silu(convolved).reshape(length, 1 + 2 * STEPS, DK)
        query_rows = unit_norm(activated[:, 0])
        key_rows = unit_norm(activated[:, 1 : 1 + STEPS]).reshape(STEPS * length, DK)
        value_rows = activated[:, 1 + STEPS :].reshape(STEPS * length, DK)
        beta_rows = jax.nn.sigmoid(scalar_rows[:, :STEPS]).reshape(STEPS * length)
        log_rate = -jnp.exp(rate_log) * jax.nn.softplus(scalar_rows[:, STEPS] + bias_part)
        log_decay = jnp.concatenate(
            [log_rate[:, None], jnp.zeros((length, STEPS - 1), jnp.float32)], 1
        ).reshape(STEPS * length)
        return (query_rows, key_rows, value_rows, beta_rows, log_decay)

    def recurrence(query_rows, key_rows, value_rows, beta_rows, log_decay):
        return block_mixer(query_rows, key_rows, value_rows, beta_rows, log_decay, pseudo_flag)

    prepared, inputs_back = jax.vjp(
        mixer_inputs, padded, scalar_rows, conv_part, rate_log, bias_part
    )
    (query_frame, partial_value_rows, transfer, offset), recurrence_back = jax.vjp(
        recurrence, *prepared
    )
    grad_rows = group_gather(out_grad)
    grad_rows, query_frame, partial_value_rows, transfer, offset = lax.optimization_barrier(
        (grad_rows, query_frame, partial_value_rows, transfer, offset)
    )
    identity = jnp.eye(DK, dtype=jnp.float32)[None]
    zeros_state = jnp.zeros((1, DK, DK), jnp.float32)
    prefix_map, incoming_state = carried_in(
        (transfer, offset), "sh", compose, (identity, zeros_state), False
    )
    mixer_result = partial_value_rows + hi("zy,yi->zi", query_frame, incoming_state[0])
    mixer_low = mixer_result.astype(jnp.bfloat16).astype(jnp.float32)
    gated, gate_back = jax.vjp(gate_norm, mixer_low, out_gate, out_norm)
    gated_rows = gated.astype(jnp.bfloat16)
    middle = x_float + group_scatter(bf_product(gated_rows, out_full))
    normed_mid, norm_two_back = jax.vjp(rms_norm, middle, gain_two)
    normed_two = group_gather(normed_mid.astype(jnp.bfloat16))
    gate_up = bf_product(normed_two, up_full)
    hidden_float, swiglu_back = jax.vjp(swiglu, gate_up)
    hidden = hidden_float.astype(jnp.bfloat16)
    feed_partial = bf_product(hidden, down_full)

    grad_out = out_grad.astype(jnp.float32)
    grad_hidden = bf_product(grad_rows, down_full.T)
    grad_down_partial = bf_product(hidden.T, grad_rows)
    (grad_gate_up,) = swiglu_back(grad_hidden)
    grad_gate_up = grad_gate_up.astype(jnp.bfloat16)
    grad_normed_two = group_scatter(bf_product(grad_gate_up, up_full.T))
    grad_mid_norm, grad_gain_two = norm_two_back(grad_normed_two)
    grad_up_payload = jnp.concatenate(
        [bf_product(normed_two.T, grad_gate_up), grad_gain_two[:, None]], 1
    )
    grad_middle = grad_out + grad_mid_norm
    feed_partial, grad_up_payload, grad_down_partial, grad_branch_low = lax.optimization_barrier(
        (feed_partial, grad_up_payload, grad_down_partial, grad_middle.astype(jnp.bfloat16))
    )
    grad_up_cols = heads_to_columns(grad_up_payload, True)
    grad_up = jnp.concatenate(
        [
            grad_up_cols[:, :, :half].reshape(weight_rows, FF),
            grad_up_cols[:, :, half : 2 * half].reshape(weight_rows, FF),
        ],
        1,
    )
    grad_branch = group_gather(grad_branch_low)
    feed_partial, grad_down_partial, grad_branch = lax.optimization_barrier(
        (feed_partial, grad_down_partial, grad_branch)
    )
    feed_sum = group_scatter(feed_partial)
    grad_gated = bf_product(grad_branch, out_full.T)
    grad_down, grad_outw = heads_to_rows((grad_down_partial, bf_product(gated_rows.T, grad_branch)))
    grad_mixer, grad_gate, grad_out_norm = gate_back(grad_gated)
    grad_gate = grad_gate.astype(jnp.bfloat16)
    head_gradients = grad_mixer.astype(jnp.bfloat16).astype(jnp.float32)
    local_adjoint = hi("dc,dr->cr", query_frame, head_gradients)[None]
    transfer_turned = jnp.transpose(transfer, (0, 2, 1))
    later_map, state_gradient = carried_in(
        (transfer_turned, local_adjoint), "sh", compose, (identity, zeros_state), True
    )
    basis_gradient = hi("nu,wu->nw", head_gradients, incoming_state[0])
    transfer_gradient = hi("tnf,tmf->tnm", state_gradient, incoming_state)
    grad_prepared = recurrence_back(
        (basis_gradient, head_gradients, transfer_gradient, state_gradient)
    )
    grad_prepared, feed_sum, grad_up_cols, grad_down, grad_outw = lax.optimization_barrier(
        (grad_prepared, feed_sum, grad_up_cols, grad_down, grad_outw)
    )
    layer_out = (middle + feed_sum).astype(jnp.bfloat16)
    grad_padded, grad_scalars, grad_conv, grad_rate, grad_bias = inputs_back(grad_prepared)
    rim_grad = from_behind(grad_padded[: CONV - 1], "sh", -1)
    own_grad = grad_padded[CONV - 1 :]
    grad_proj = jnp.concatenate(
        [own_grad[: length - (CONV - 1)], own_grad[length - (CONV - 1) :] + rim_grad], 0
    )
    grad_head = jnp.concatenate(
        [grad_gate, grad_proj.astype(jnp.bfloat16), grad_scalars.astype(jnp.bfloat16)], 1
    )
    grad_normed_one = group_scatter(bf_product(grad_head, head_full.T), True)
    grad_x_norm, grad_gain_one = norm_one_back(grad_normed_one)
    grad_head_cols = heads_to_columns(
        jnp.concatenate([bf_product(normed_one.T, grad_head), grad_gain_one[:, None]], 1)
    )
    grad_gatew = grad_head_cols[:, :, :DK].reshape(weight_rows, D)
    grad_mixw = grad_head_cols[:, :, DK : DK + PROJ].reshape(weight_rows, HEADS * PROJ)
    grad_gatesw = grad_head_cols[:, :, DK + PROJ : WIDE].reshape(
        weight_rows, HEADS * (STEPS + 1)
    )
    grad_tokens = (grad_middle + grad_x_norm).astype(jnp.bfloat16)
    (conv_grad,) = heads_to_rows((jnp.transpose(grad_conv),))
    conv_grad = jnp.transpose(conv_grad)
    one_hot = (jnp.arange(HEADS) == head).astype(jnp.float32)
    small_sums = all_sum(
        jnp.concatenate([one_hot * grad_rate, one_hot * grad_bias, grad_out_norm])
    )
    return (
        layer_out,
        grad_tokens,
        jnp.sum(grad_head_cols[:, :, WIDE], 1),
        grad_mixw,
        grad_gatesw,
        conv_grad,
        small_sums[:HEADS],
        small_sums[HEADS : 2 * HEADS],
        grad_gatew,
        small_sums[2 * HEADS :],
        grad_outw,
        jnp.sum(grad_up_cols[:, :, 2 * half], 1),
        grad_up,
        grad_down,
    )


def solution(mesh):
    seq = mesh.shape["seq"]
    across = mesh.shape["head"]
    inner = HEADS // across
    grid = Mesh(
        np.asarray(mesh.devices).reshape(seq // inner, inner, across), ("sh", "sl", "hd")
    )
    rows = P(ALL, None)
    flat = P(ALL)
    return jax.shard_map(
        local,
        mesh=grid,
        in_specs=(
            rows,
            flat,
            rows,
            rows,
            P(None, ALL),
            P(),
            P(),
            rows,
            P(),
            rows,
            flat,
            rows,
            rows,
            P(),
            rows,
        ),
        out_specs=(
            rows,
            rows,
            flat,
            rows,
            rows,
            P(None, ALL),
            P(),
            P(),
            rows,
            P(),
            rows,
            flat,
            rows,
            rows,
        ),
        check_vma=False,
    )
```

```python
import jax
import jax.numpy as jnp
import numpy as np
from jax import lax
from jax.experimental import pallas as pl
from jax.experimental.pallas import tpu as pltpu
from jax.sharding import Mesh
from jax.sharding import PartitionSpec as P

D = 1024
HEADS = 8
DK = 128
FF = 2816
STEPS = 2
CONV = 4
BLOCK = 64
PROJ = (1 + 2 * STEPS) * DK
WIDE = DK + PROJ + STEPS + 1

EPS = 1e-06
HIGH_ACCURACY = lax.Precision.HIGH

GROUP = ("sl", "hd")
ALL = ("sh", "sl", "hd")


def from_behind(shard, axis, by):
    peers = lax.axis_size(axis)
    pairs = [(i, i + by) for i in range(peers) if 0 <= i + by < peers]
    return lax.ppermute(shard, axis, pairs)


def carried_in(shard, axis, join, neutral, backward):
    count = lax.axis_size(axis)
    place = lax.axis_index(axis)
    ahead = count - 1 - place if backward else place
    both = lax.all_gather(jnp.stack(shard).astype(jnp.bfloat16), axis)
    gathered = (both[:, 0], both[:, 1])
    state = jax.tree.map(lambda a, e: jnp.zeros_like(a) + jnp.asarray(e, a.dtype), shard, neutral)

    def one(turn, state):
        source = count - 1 - turn if backward else turn
        return join(
            state,
            jax.tree.map(
                lambda a, own: lax.dynamic_index_in_dim(a, source, 0, False).astype(own.dtype),
                gathered,
                shard,
            ),
        )

    return lax.fori_loop(0, ahead, one, state)


def flat_place():
    return (
        lax.axis_index("sh") * lax.axis_size("sl") + lax.axis_index("sl")
    ) * lax.axis_size("hd") + lax.axis_index("hd")


def device_of(index):
    inner = lax.axis_size("sl") * lax.axis_size("hd")
    return (index // inner, (index // lax.axis_size("hd")) % lax.axis_size("sl"), index % lax.axis_size("hd"))


def sum_kernel(count, own_ref, out_ref, slots, send_sems, recv_sems):
    me = flat_place()
    barrier = pltpu.get_barrier_semaphore()

    def greet(index, carry):
        @pl.when(index != me)
        def _():
            pl.semaphore_signal(
                barrier, inc=1, device_id=device_of(index), device_id_type=pl.DeviceIdType.MESH
            )

        return carry

    lax.fori_loop(0, count, greet, 0)
    pl.semaphore_wait(barrier, count - 1)

    def copy_to(index):
        return pltpu.make_async_remote_copy(
            src_ref=own_ref,
            dst_ref=slots.at[me],
            send_sem=send_sems.at[index],
            recv_sem=recv_sems.at[me],
            device_id=device_of(index),
            device_id_type=pl.DeviceIdType.MESH,
        )

    def copy_from(index):
        return pltpu.make_async_remote_copy(
            src_ref=own_ref,
            dst_ref=slots.at[index],
            send_sem=send_sems.at[index],
            recv_sem=recv_sems.at[index],
            device_id=device_of(index),
            device_id_type=pl.DeviceIdType.MESH,
        )

    def send(index, carry):
        @pl.when(index != me)
        def _():
            copy_to(index).start()

        return carry

    lax.fori_loop(0, count, send, 0)
    slots[me] = own_ref[...]

    def finish(index, carry):
        @pl.when(index != me)
        def _():
            copy_to(index).wait_send()
            copy_from(index).wait_recv()

        return carry

    lax.fori_loop(0, count, finish, 0)
    out_ref[...] = jnp.sum(slots[...], axis=0)


def all_sum(vector):
    count = lax.axis_size("sh") * lax.axis_size("sl") * lax.axis_size("hd")
    size = vector.shape[0]
    lanes = 128
    tile = 8 * lanes
    padded = -(-size // tile) * tile
    block = jnp.pad(vector, (0, padded - size)).reshape(padded // lanes, lanes)
    total = pl.pallas_call(
        lambda *refs: sum_kernel(count, *refs),
        out_shape=jax.ShapeDtypeStruct(block.shape, jnp.float32),
        in_specs=[pl.BlockSpec(memory_space=pltpu.VMEM)],
        out_specs=pl.BlockSpec(memory_space=pltpu.VMEM),
        scratch_shapes=[
            pltpu.VMEM((count,) + block.shape, jnp.float32),
            pltpu.SemaphoreType.DMA((count,)),
            pltpu.SemaphoreType.DMA((count,)),
        ],
        compiler_params=pltpu.CompilerParams(collective_id=0, has_side_effects=True),
    )(block)
    return total.reshape(-1)[:size]


def rms_norm(values, scale_gain):
    return values * lax.rsqrt(jnp.mean(values * values, axis=-1, keepdims=True) + EPS) * scale_gain


def unit_norm(values):
    return values * lax.rsqrt(jnp.sum(values * values, axis=-1, keepdims=True) + EPS)


def bf_product(first_mat, second_mat):
    return jnp.dot(first_mat, second_mat, preferred_element_type=jnp.float32)


def hi(spec, *arrays):
    return jnp.einsum(spec, *arrays, precision=HIGH_ACCURACY)


def compose(early_pair, late_pair):
    early_mat, early_add = early_pair
    late_mat, late_add = late_pair
    joined = hi("hij,hjk->hik", late_mat, early_mat)
    shifted = hi("hij,hjk->hik", late_mat, early_add) + late_add
    return (joined, shifted)


def gate_norm(values, out_gate, scale_gain):
    return rms_norm(values, scale_gain) * jax.nn.silu(out_gate)


def swiglu(gate_up):
    half = gate_up.shape[1] // 2
    return jax.nn.silu(gate_up[:, :half]) * gate_up[:, half:]


def owner_pairs(inverse):
    groups = lax.axis_size("sh")
    pairs = [(g * HEADS + t, t * groups + g) for g in range(groups) for t in range(HEADS)]
    return [(b, a) for a, b in pairs] if inverse else pairs


def rows_to_heads(blocks):
    groups = lax.axis_size("sh")
    width = blocks[0].shape[1]
    used = sum(b.shape[0] for b in blocks)
    least = (1 << 20) // (groups * width * 2) + 1
    rows = -(-max(used, least) // 8) * 8
    packed = jnp.concatenate(
        list(blocks) + [jnp.zeros((rows - used, width), blocks[0].dtype)], 0
    )
    moved = lax.ppermute(packed, ALL, owner_pairs(True))
    full = lax.all_gather(moved, "sh", axis=0, tiled=False)
    parts = []
    first = 0
    for block in blocks:
        size = block.shape[0]
        parts.append(full[:, first : first + size].reshape(groups * size, width))
        first += size
    return parts


def heads_to_rows(partials):
    groups = lax.axis_size("sh")
    pieces = [
        p.astype(jnp.bfloat16).reshape((groups, p.shape[0] // groups) + p.shape[1:])
        for p in partials
    ]
    joined = jnp.concatenate(pieces, 1)
    joined = joined.reshape((-1,) + joined.shape[2:])
    summed = lax.psum_scatter(joined, "sh", scatter_dimension=0, tiled=True)
    moved = lax.ppermute(summed, ALL, owner_pairs(False)).astype(jnp.float32)
    parts = []
    first = 0
    for piece in pieces:
        size = piece.shape[1]
        parts.append(moved[first : first + size])
        first += size
    return parts


def columns_to_heads(local_cols):
    per_head = jnp.transpose(local_cols, (1, 0, 2))
    mine = lax.all_to_all(per_head, GROUP, 0, 0, tiled=True)
    mine = mine.reshape(-1, mine.shape[-1])
    return lax.all_gather(mine, "sh", axis=0, tiled=True)


def heads_to_columns(partial, direct=False):
    low = partial.astype(jnp.bfloat16)
    if direct:
        groups = lax.axis_size("sh")
        pieces = low.reshape((groups, low.shape[0] // groups) + low.shape[1:])
        moved = lax.all_to_all(pieces, "sh", 0, 0, tiled=True)
        summed = jnp.sum(moved.astype(jnp.float32), 0).astype(jnp.bfloat16)
    else:
        summed = lax.psum_scatter(low, "sh", scatter_dimension=0, tiled=True)
    summed = summed.reshape(HEADS, -1, summed.shape[-1])
    back = lax.all_to_all(summed, GROUP, 0, 0, tiled=True)
    return jnp.transpose(back, (1, 0, 2)).astype(jnp.float32)


def group_gather(rows, direct=False):
    if direct:
        copies = jnp.broadcast_to(rows[None], (HEADS,) + rows.shape)
        moved = lax.all_to_all(copies, GROUP, 0, 0, tiled=True)
        return moved.reshape((-1,) + rows.shape[1:])
    return lax.all_gather(rows, GROUP, axis=0, tiled=True)


def group_scatter(partial, direct=False):
    low = partial.astype(jnp.bfloat16)
    if direct:
        pieces = low.reshape((HEADS, low.shape[0] // HEADS) + low.shape[1:])
        moved = lax.all_to_all(pieces, GROUP, 0, 0, tiled=True)
        return jnp.sum(moved.astype(jnp.float32), 0)
    return lax.psum_scatter(low, GROUP, scatter_dimension=0, tiled=True).astype(jnp.float32)


def masked_power_inverse(system):
    size = system.shape[-1]
    places = jnp.arange(size)
    base = 8
    inside = (places[:, None] // base == places[None, :] // base) & (
        places[:, None] > places[None, :]
    )
    step = -(system * inside.astype(system.dtype))
    eye = jnp.eye(size, dtype=system.dtype)
    result = eye + step
    for _ in range(2):
        step = hi("bij,bjk->bik", step, step)
        result = result + hi("bij,bjk->bik", result, step)
    width = base
    while width < size:
        across = (places[:, None] // (2 * width) == places[None, :] // (2 * width)) & (
            places[:, None] // width != places[None, :] // width
        )
        lower_left = system * across.astype(system.dtype)
        result = result - hi("bij,bjk->bik", result, hi("bij,bjk->bik", lower_left, result))
        width = 2 * width
    return result


@jax.custom_vjp
def unit_lower_inverse(system):
    return masked_power_inverse(system)


def inverse_keep(system):
    inverse = masked_power_inverse(system)
    return inverse, inverse


def inverse_back(inverse, grad):
    turned = jnp.swapaxes(inverse, -1, -2)
    return (-hi("bij,bjk->bik", turned, hi("bij,bjk->bik", grad, turned)),)


unit_lower_inverse.defvjp(inverse_keep, inverse_back)


def block_mixer(query_rows, key_rows, value_rows, beta_rows, log_decay, starts_flag):
    pseudo = key_rows.shape[0]
    span = STEPS * BLOCK
    blocks = pseudo // span
    queries = query_rows.reshape(blocks, BLOCK, DK)
    keys = key_rows.reshape(blocks, span, DK)
    values = value_rows.reshape(blocks, span, DK)
    betas = beta_rows.reshape(blocks, span)
    decays = log_decay.reshape(blocks, span)
    flags = starts_flag.reshape(blocks, span)
    places = jnp.arange(span)
    lower = places[:, None] >= places[None, :]
    strict = (places[:, None] > places[None, :]).astype(jnp.float32)
    identity = jnp.eye(span, dtype=jnp.float32)
    eye_key = jnp.eye(DK, dtype=jnp.float32)

    summed = jnp.cumsum(decays, axis=1)
    segment = jnp.cumsum(flags, axis=1)
    same_doc = (segment[:, :, None] == segment[:, None, :]) & lower
    decay_ratio = jnp.exp(
        jnp.where(same_doc, summed[:, :, None] - summed[:, None, :], 0.0)
    ) * same_doc.astype(jnp.float32)
    from_start = jnp.exp(summed) * (segment == 0.0).astype(jnp.float32)
    key_key = hi("bik,bjk->bij", keys, keys)
    system = identity + betas[:, :, None] * decay_ratio * key_key * strict
    right_side = jnp.concatenate(
        [betas[:, :, None] * values, (betas * from_start)[:, :, None] * keys], 2
    )
    solved = hi("bij,bjk->bik", unit_lower_inverse(system), right_side)
    fresh = solved[:, :, :DK]
    carried = solved[:, :, DK:]
    last_keys = keys * decay_ratio[:, -1, :, None]
    transfer = from_start[:, -1, None, None] * eye_key - hi("bsi,bsj->bij", last_keys, carried)
    offset = hi("bsi,bsj->bij", last_keys, fresh)
    query_key = hi("bqk,bsk->bqs", queries, keys) * decay_ratio[:, STEPS - 1 :: STEPS]
    frame = from_start[:, STEPS - 1 :: STEPS, None] * queries - hi(
        "bqs,bsj->bqj", query_key, carried
    )
    direct = hi("bqs,bsj->bqj", query_key, fresh)

    state = jnp.concatenate([eye_key, jnp.zeros((DK, DK), jnp.float32)], 1)
    states = []
    for index in range(blocks):
        states.append(state)
        state = hi("ij,jk->ik", transfer[index], state) + jnp.concatenate(
            [jnp.zeros((DK, DK), jnp.float32), offset[index]], 1
        )
    states = jnp.stack(states)
    mats = states[:, :, :DK]
    adds = states[:, :, DK:]
    final_mat = state[:, :DK]
    final_add = state[:, DK:]
    query_frame = hi("bqi,bij->bqj", frame, mats)
    partial = hi("bqi,bij->bqj", frame, adds) + direct
    return (
        query_frame.reshape(blocks * BLOCK, DK),
        partial.reshape(blocks * BLOCK, DK),
        final_mat[None],
        final_add[None],
    )


def local(
    tokens_in,
    mixer_norm,
    mix_weight,
    head_gates,
    conv_taps,
    decay_log,
    decay_bias,
    gate_weight,
    out_norm,
    out_weight,
    feed_norm,
    up_weight,
    down_weight,
    doc_lengths,
    out_grad,
):
    row_count = tokens_in.shape[0]
    weight_rows = mix_weight.shape[0]
    head = lax.axis_index("sl") * lax.axis_size("hd") + lax.axis_index("hd")
    length = row_count * HEADS

    head_cols = jnp.concatenate(
        [
            gate_weight.reshape(weight_rows, HEADS, DK),
            mix_weight.reshape(weight_rows, HEADS, PROJ),
            head_gates.reshape(weight_rows, HEADS, STEPS + 1),
            jnp.broadcast_to(mixer_norm[:, None, None], (weight_rows, HEADS, 1)),
        ],
        2,
    )
    head_wide = columns_to_heads(head_cols)
    head_full = head_wide[:, :WIDE]
    gain_one = head_wide[:, WIDE].astype(jnp.float32)
    half = FF // HEADS
    up_cols = jnp.concatenate(
        [
            up_weight[:, :FF].reshape(weight_rows, HEADS, half),
            up_weight[:, FF:].reshape(weight_rows, HEADS, half),
            jnp.broadcast_to(feed_norm[:, None, None], (weight_rows, HEADS, 1)),
        ],
        2,
    )
    up_wide = columns_to_heads(up_cols)
    up_full = up_wide[:, : 2 * half]
    gain_two = up_wide[:, 2 * half].astype(jnp.float32)
    tap_width = conv_taps.shape[1]
    tap_row = jnp.pad(conv_taps.reshape(1, -1), ((0, 0), (0, D - CONV * tap_width)))
    out_full, down_full, tap_rows = rows_to_heads((out_weight, down_weight, tap_row))
    conv_part = jnp.transpose(
        tap_rows[:, : CONV * tap_width].reshape(-1, CONV, tap_width), (1, 0, 2)
    ).reshape(CONV, -1).astype(jnp.float32)

    x_float = tokens_in.astype(jnp.float32)
    normed_float, norm_one_back = jax.vjp(rms_norm, x_float, gain_one)
    normed_one = group_gather(normed_float.astype(jnp.bfloat16), True)
    head_out = bf_product(normed_one, head_full)
    out_gate = head_out[:, :DK]
    proj_head = head_out[:, DK : DK + PROJ].astype(jnp.bfloat16)
    scalar_rows = head_out[:, DK + PROJ :].astype(jnp.bfloat16).astype(jnp.float32)

    rim_rows = from_behind(proj_head[length - (CONV - 1) :], "sh", 1)
    padded = jnp.concatenate([rim_rows, proj_head], 0).astype(jnp.float32)
    starts = jnp.cumsum(doc_lengths) - doc_lengths
    positions = lax.axis_index("sh") * length + jnp.arange(length, dtype=jnp.int32)
    starts_flag = jnp.any(positions[:, None] == starts[None, :], 1).astype(jnp.float32)
    doc_begin = jnp.max(jnp.where(starts[None, :] <= positions[:, None], starts[None, :], 0), 1)
    tap_masks = [
        (positions - (CONV - 1) + tap_index >= doc_begin).astype(jnp.float32)
        for tap_index in range(CONV)
    ]
    pseudo_flag = jnp.concatenate(
        [starts_flag[:, None], jnp.zeros((length, STEPS - 1), jnp.float32)], 1
    ).reshape(-1)
    rate_log = lax.dynamic_index_in_dim(decay_log, head, 0, False)
    bias_part = lax.dynamic_index_in_dim(decay_bias, head, 0, False)

    def mixer_inputs(padded, scalar_rows, conv_part, rate_log, bias_part):
        convolved = jnp.zeros_like(padded[CONV - 1 :])
        for tap_index in range(CONV):
            convolved = (
                convolved
                + conv_part[tap_index]
                * padded[tap_index : tap_index + length]
                * tap_masks[tap_index][:, None]
            )
        activated = jax.nn.silu(convolved).reshape(length, 1 + 2 * STEPS, DK)
        query_rows = unit_norm(activated[:, 0])
        key_rows = unit_norm(activated[:, 1 : 1 + STEPS]).reshape(STEPS * length, DK)
        value_rows = activated[:, 1 + STEPS :].reshape(STEPS * length, DK)
        beta_rows = jax.nn.sigmoid(scalar_rows[:, :STEPS]).reshape(STEPS * length)
        log_rate = -jnp.exp(rate_log) * jax.nn.softplus(scalar_rows[:, STEPS] + bias_part)
        log_decay = jnp.concatenate(
            [log_rate[:, None], jnp.zeros((length, STEPS - 1), jnp.float32)], 1
        ).reshape(STEPS * length)
        return (query_rows, key_rows, value_rows, beta_rows, log_decay)

    def recurrence(query_rows, key_rows, value_rows, beta_rows, log_decay):
        return block_mixer(query_rows, key_rows, value_rows, beta_rows, log_decay, pseudo_flag)

    prepared, inputs_back = jax.vjp(
        mixer_inputs, padded, scalar_rows, conv_part, rate_log, bias_part
    )
    (query_frame, partial_value_rows, transfer, offset), recurrence_back = jax.vjp(
        recurrence, *prepared
    )
    grad_rows = group_gather(out_grad)
    grad_rows, query_frame, partial_value_rows, transfer, offset = lax.optimization_barrier(
        (grad_rows, query_frame, partial_value_rows, transfer, offset)
    )
    identity = jnp.eye(DK, dtype=jnp.float32)[None]
    zeros_state = jnp.zeros((1, DK, DK), jnp.float32)
    prefix_map, incoming_state = carried_in(
        (transfer, offset), "sh", compose, (identity, zeros_state), False
    )
    mixer_result = partial_value_rows + hi("zy,yi->zi", query_frame, incoming_state[0])
    mixer_low = mixer_result.astype(jnp.bfloat16).astype(jnp.float32)
    gated, gate_back = jax.vjp(gate_norm, mixer_low, out_gate, out_norm)
    gated_rows = gated.astype(jnp.bfloat16)
    middle = x_float + group_scatter(bf_product(gated_rows, out_full))
    normed_mid, norm_two_back = jax.vjp(rms_norm, middle, gain_two)
    normed_two = group_gather(normed_mid.astype(jnp.bfloat16))
    gate_up = bf_product(normed_two, up_full)
    hidden_float, swiglu_back = jax.vjp(swiglu, gate_up)
    hidden = hidden_float.astype(jnp.bfloat16)
    feed_partial = bf_product(hidden, down_full)

    grad_out = out_grad.astype(jnp.float32)
    grad_hidden = bf_product(grad_rows, down_full.T)
    grad_down_partial = bf_product(hidden.T, grad_rows)
    (grad_gate_up,) = swiglu_back(grad_hidden)
    grad_gate_up = grad_gate_up.astype(jnp.bfloat16)
    grad_normed_two = group_scatter(bf_product(grad_gate_up, up_full.T))
    grad_mid_norm, grad_gain_two = norm_two_back(grad_normed_two)
    grad_up_payload = jnp.concatenate(
        [bf_product(normed_two.T, grad_gate_up), grad_gain_two[:, None]], 1
    )
    grad_middle = grad_out + grad_mid_norm
    feed_partial, grad_up_payload, grad_down_partial, grad_branch_low = lax.optimization_barrier(
        (feed_partial, grad_up_payload, grad_down_partial, grad_middle.astype(jnp.bfloat16))
    )
    grad_up_cols = heads_to_columns(grad_up_payload, True)
    grad_up = jnp.concatenate(
        [
            grad_up_cols[:, :, :half].reshape(weight_rows, FF),
            grad_up_cols[:, :, half : 2 * half].reshape(weight_rows, FF),
        ],
        1,
    )
    grad_branch = group_gather(grad_branch_low)
    feed_partial, grad_down_partial, grad_branch = lax.optimization_barrier(
        (feed_partial, grad_down_partial, grad_branch)
    )
    feed_sum = group_scatter(feed_partial)
    grad_gated = bf_product(grad_branch, out_full.T)
    grad_down, grad_outw = heads_to_rows((grad_down_partial, bf_product(gated_rows.T, grad_branch)))
    grad_mixer, grad_gate, grad_out_norm = gate_back(grad_gated)
    grad_gate = grad_gate.astype(jnp.bfloat16)
    head_gradients = grad_mixer.astype(jnp.bfloat16).astype(jnp.float32)
    local_adjoint = hi("dc,dr->cr", query_frame, head_gradients)[None]
    transfer_turned = jnp.transpose(transfer, (0, 2, 1))
    later_map, state_gradient = carried_in(
        (transfer_turned, local_adjoint), "sh", compose, (identity, zeros_state), True
    )
    basis_gradient = hi("nu,wu->nw", head_gradients, incoming_state[0])
    transfer_gradient = hi("tnf,tmf->tnm", state_gradient, incoming_state)
    grad_prepared = recurrence_back(
        (basis_gradient, head_gradients, transfer_gradient, state_gradient)
    )
    grad_prepared, feed_sum, grad_up_cols, grad_down, grad_outw = lax.optimization_barrier(
        (grad_prepared, feed_sum, grad_up_cols, grad_down, grad_outw)
    )
    layer_out = (middle + feed_sum).astype(jnp.bfloat16)
    grad_padded, grad_scalars, grad_conv, grad_rate, grad_bias = inputs_back(grad_prepared)
    rim_grad = from_behind(grad_padded[: CONV - 1], "sh", -1)
    own_grad = grad_padded[CONV - 1 :]
    grad_proj = jnp.concatenate(
        [own_grad[: length - (CONV - 1)], own_grad[length - (CONV - 1) :] + rim_grad], 0
    )
    grad_head = jnp.concatenate(
        [grad_gate, grad_proj.astype(jnp.bfloat16), grad_scalars.astype(jnp.bfloat16)], 1
    )
    grad_normed_one = group_scatter(bf_product(grad_head, head_full.T), True)
    grad_x_norm, grad_gain_one = norm_one_back(grad_normed_one)
    grad_head_cols = heads_to_columns(
        jnp.concatenate([bf_product(normed_one.T, grad_head), grad_gain_one[:, None]], 1)
    )
    grad_gatew = grad_head_cols[:, :, :DK].reshape(weight_rows, D)
    grad_mixw = grad_head_cols[:, :, DK : DK + PROJ].reshape(weight_rows, HEADS * PROJ)
    grad_gatesw = grad_head_cols[:, :, DK + PROJ : WIDE].reshape(
        weight_rows, HEADS * (STEPS + 1)
    )
    grad_tokens = (grad_middle + grad_x_norm).astype(jnp.bfloat16)
    (conv_grad,) = heads_to_rows((jnp.transpose(grad_conv),))
    conv_grad = jnp.transpose(conv_grad)
    one_hot = (jnp.arange(HEADS) == head).astype(jnp.float32)
    small_sums = all_sum(
        jnp.concatenate([one_hot * grad_rate, one_hot * grad_bias, grad_out_norm])
    )
    return (
        layer_out,
        grad_tokens,
        jnp.sum(grad_head_cols[:, :, WIDE], 1),
        grad_mixw,
        grad_gatesw,
        conv_grad,
        small_sums[:HEADS],
        small_sums[HEADS : 2 * HEADS],
        grad_gatew,
        small_sums[2 * HEADS :],
        grad_outw,
        jnp.sum(grad_up_cols[:, :, 2 * half], 1),
        grad_up,
        grad_down,
    )


def solution(mesh):
    seq = mesh.shape["seq"]
    across = mesh.shape["head"]
    inner = HEADS // across
    grid = Mesh(
        np.asarray(mesh.devices).reshape(seq // inner, inner, across), ("sh", "sl", "hd")
    )
    rows = P(ALL, None)
    flat = P(ALL)
    return jax.shard_map(
        local,
        mesh=grid,
        in_specs=(
            rows,
            flat,
            rows,
            rows,
            P(None, ALL),
            P(),
            P(),
            rows,
            P(),
            rows,
            flat,
            rows,
            rows,
            P(),
            rows,
        ),
        out_specs=(
            rows,
            rows,
            flat,
            rows,
            rows,
            P(None, ALL),
            P(),
            P(),
            rows,
            P(),
            rows,
            flat,
            rows,
            rows,
        ),
        check_vma=False,
    )
```

```python
import jax
import jax.numpy as jnp
import numpy as np
from jax import lax
from jax.experimental import pallas as pl
from jax.experimental.pallas import tpu as pltpu
from jax.sharding import Mesh
from jax.sharding import PartitionSpec as P

D = 1024
HEADS = 8
DK = 128
FF = 2816
STEPS = 2
CONV = 4
BLOCK = 64
PROJ = (1 + 2 * STEPS) * DK
WIDE = DK + PROJ + STEPS + 1

EPS = 1e-06
HIGH_ACCURACY = lax.Precision.HIGH

GROUP = ("sl", "hd")
ALL = ("sh", "sl", "hd")


def from_behind(shard, axis, by):
    peers = lax.axis_size(axis)
    pairs = [(i, i + by) for i in range(peers) if 0 <= i + by < peers]
    return lax.ppermute(shard, axis, pairs)


def carried_in(shard, axis, join, neutral, backward):
    count = lax.axis_size(axis)
    place = lax.axis_index(axis)
    ahead = count - 1 - place if backward else place
    both = lax.all_gather(jnp.stack(shard).astype(jnp.bfloat16), axis)
    gathered = (both[:, 0], both[:, 1])
    state = jax.tree.map(lambda a, e: jnp.zeros_like(a) + jnp.asarray(e, a.dtype), shard, neutral)

    def one(turn, state):
        source = count - 1 - turn if backward else turn
        return join(
            state,
            jax.tree.map(
                lambda a, own: lax.dynamic_index_in_dim(a, source, 0, False).astype(own.dtype),
                gathered,
                shard,
            ),
        )

    return lax.fori_loop(0, ahead, one, state)


def flat_place():
    return (
        lax.axis_index("sh") * lax.axis_size("sl") + lax.axis_index("sl")
    ) * lax.axis_size("hd") + lax.axis_index("hd")


def device_of(index):
    inner = lax.axis_size("sl") * lax.axis_size("hd")
    return (index // inner, (index // lax.axis_size("hd")) % lax.axis_size("sl"), index % lax.axis_size("hd"))


def sum_kernel(count, own_ref, out_ref, slots, send_sems, recv_sems):
    me = flat_place()
    barrier = pltpu.get_barrier_semaphore()

    def greet(index, carry):
        @pl.when(index != me)
        def _():
            pl.semaphore_signal(
                barrier, inc=1, device_id=device_of(index), device_id_type=pl.DeviceIdType.MESH
            )

        return carry

    lax.fori_loop(0, count, greet, 0)
    pl.semaphore_wait(barrier, count - 1)

    def copy_to(index):
        return pltpu.make_async_remote_copy(
            src_ref=own_ref,
            dst_ref=slots.at[me],
            send_sem=send_sems.at[index],
            recv_sem=recv_sems.at[me],
            device_id=device_of(index),
            device_id_type=pl.DeviceIdType.MESH,
        )

    def copy_from(index):
        return pltpu.make_async_remote_copy(
            src_ref=own_ref,
            dst_ref=slots.at[index],
            send_sem=send_sems.at[index],
            recv_sem=recv_sems.at[index],
            device_id=device_of(index),
            device_id_type=pl.DeviceIdType.MESH,
        )

    def send(index, carry):
        @pl.when(index != me)
        def _():
            copy_to(index).start()

        return carry

    lax.fori_loop(0, count, send, 0)
    slots[me] = own_ref[...]

    def finish(index, carry):
        @pl.when(index != me)
        def _():
            copy_to(index).wait_send()
            copy_from(index).wait_recv()

        return carry

    lax.fori_loop(0, count, finish, 0)
    out_ref[...] = jnp.sum(slots[...], axis=0)


def all_sum(vector):
    count = lax.axis_size("sh") * lax.axis_size("sl") * lax.axis_size("hd")
    size = vector.shape[0]
    lanes = 128
    tile = 8 * lanes
    padded = -(-size // tile) * tile
    block = jnp.pad(vector, (0, padded - size)).reshape(padded // lanes, lanes)
    total = pl.pallas_call(
        lambda *refs: sum_kernel(count, *refs),
        out_shape=jax.ShapeDtypeStruct(block.shape, jnp.float32),
        in_specs=[pl.BlockSpec(memory_space=pltpu.VMEM)],
        out_specs=pl.BlockSpec(memory_space=pltpu.VMEM),
        scratch_shapes=[
            pltpu.VMEM((count,) + block.shape, jnp.float32),
            pltpu.SemaphoreType.DMA((count,)),
            pltpu.SemaphoreType.DMA((count,)),
        ],
        compiler_params=pltpu.CompilerParams(collective_id=0, has_side_effects=True),
    )(block)
    return total.reshape(-1)[:size]


def rms_norm(values, scale_gain):
    return values * lax.rsqrt(jnp.mean(values * values, axis=-1, keepdims=True) + EPS) * scale_gain


def unit_norm(values):
    return values * lax.rsqrt(jnp.sum(values * values, axis=-1, keepdims=True) + EPS)


def bf_product(first_mat, second_mat):
    return jnp.dot(first_mat, second_mat, preferred_element_type=jnp.float32)


def hi(spec, *arrays):
    return jnp.einsum(spec, *arrays, precision=HIGH_ACCURACY)


def compose(early_pair, late_pair):
    early_mat, early_add = early_pair
    late_mat, late_add = late_pair
    joined = hi("hij,hjk->hik", late_mat, early_mat)
    shifted = hi("hij,hjk->hik", late_mat, early_add) + late_add
    return (joined, shifted)


def gate_norm(values, out_gate, scale_gain):
    return rms_norm(values, scale_gain) * jax.nn.silu(out_gate)


def swiglu(gate_up):
    half = gate_up.shape[1] // 2
    return jax.nn.silu(gate_up[:, :half]) * gate_up[:, half:]


def owner_pairs(inverse):
    groups = lax.axis_size("sh")
    pairs = [(g * HEADS + t, t * groups + g) for g in range(groups) for t in range(HEADS)]
    return [(b, a) for a, b in pairs] if inverse else pairs


def rows_to_heads(blocks):
    groups = lax.axis_size("sh")
    width = blocks[0].shape[1]
    used = sum(b.shape[0] for b in blocks)
    least = (1 << 20) // (groups * width * 2) + 1
    rows = -(-max(used, least) // 8) * 8
    packed = jnp.concatenate(
        list(blocks) + [jnp.zeros((rows - used, width), blocks[0].dtype)], 0
    )
    moved = lax.ppermute(packed, ALL, owner_pairs(True))
    full = lax.all_gather(moved, "sh", axis=0, tiled=False)
    parts = []
    first = 0
    for block in blocks:
        size = block.shape[0]
        parts.append(full[:, first : first + size].reshape(groups * size, width))
        first += size
    return parts


def heads_to_rows(partials, columns=None):
    groups = lax.axis_size("sh")
    pieces = [
        p.astype(jnp.bfloat16).reshape((groups, p.shape[0] // groups) + p.shape[1:])
        for p in partials
    ]
    joined = jnp.concatenate(pieces, 1)
    shape = joined.shape[1:]
    flat = joined.reshape(groups, -1)
    if columns is not None:
        flat = jnp.concatenate([flat, columns.astype(jnp.bfloat16).reshape(groups, -1)], 1)
    summed = lax.psum_scatter(flat, "sh", scatter_dimension=0, tiled=True)[0]
    size = shape[0] * shape[1]
    rows = summed[:size].reshape(shape)
    moved = lax.ppermute(rows, ALL, owner_pairs(False)).astype(jnp.float32)
    extra = []
    if columns is not None:
        block = summed[size:].reshape(HEADS, -1, columns.shape[-1])
        back = lax.all_to_all(block, GROUP, 0, 0, tiled=True)
        extra = [jnp.transpose(back, (1, 0, 2)).astype(jnp.float32)]
    parts = []
    first = 0
    for piece in pieces:
        size = piece.shape[1]
        parts.append(moved[first : first + size])
        first += size
    return parts + extra


def columns_to_heads(local_cols):
    per_head = jnp.transpose(local_cols, (1, 0, 2))
    mine = lax.all_to_all(per_head, GROUP, 0, 0, tiled=True)
    mine = mine.reshape(-1, mine.shape[-1])
    return lax.all_gather(mine, "sh", axis=0, tiled=True)


def heads_to_columns(partial, direct=False):
    low = partial.astype(jnp.bfloat16)
    if direct:
        groups = lax.axis_size("sh")
        pieces = low.reshape((groups, low.shape[0] // groups) + low.shape[1:])
        moved = lax.all_to_all(pieces, "sh", 0, 0, tiled=True)
        summed = jnp.sum(moved.astype(jnp.float32), 0).astype(jnp.bfloat16)
    else:
        summed = lax.psum_scatter(low, "sh", scatter_dimension=0, tiled=True)
    summed = summed.reshape(HEADS, -1, summed.shape[-1])
    back = lax.all_to_all(summed, GROUP, 0, 0, tiled=True)
    return jnp.transpose(back, (1, 0, 2)).astype(jnp.float32)


def group_gather(rows, direct=False):
    if direct:
        copies = jnp.broadcast_to(rows[None], (HEADS,) + rows.shape)
        moved = lax.all_to_all(copies, GROUP, 0, 0, tiled=True)
        return moved.reshape((-1,) + rows.shape[1:])
    return lax.all_gather(rows, GROUP, axis=0, tiled=True)


def group_scatter(partial, direct=False):
    low = partial.astype(jnp.bfloat16)
    if direct:
        pieces = low.reshape((HEADS, low.shape[0] // HEADS) + low.shape[1:])
        moved = lax.all_to_all(pieces, GROUP, 0, 0, tiled=True)
        return jnp.sum(moved.astype(jnp.float32), 0)
    return lax.psum_scatter(low, GROUP, scatter_dimension=0, tiled=True).astype(jnp.float32)


def masked_power_inverse(system):
    size = system.shape[-1]
    places = jnp.arange(size)
    base = 8
    inside = (places[:, None] // base == places[None, :] // base) & (
        places[:, None] > places[None, :]
    )
    step = -(system * inside.astype(system.dtype))
    eye = jnp.eye(size, dtype=system.dtype)
    result = eye + step
    for _ in range(2):
        step = hi("bij,bjk->bik", step, step)
        result = result + hi("bij,bjk->bik", result, step)
    width = base
    while width < size:
        across = (places[:, None] // (2 * width) == places[None, :] // (2 * width)) & (
            places[:, None] // width != places[None, :] // width
        )
        lower_left = system * across.astype(system.dtype)
        result = result - hi("bij,bjk->bik", result, hi("bij,bjk->bik", lower_left, result))
        width = 2 * width
    return result


@jax.custom_vjp
def unit_lower_inverse(system):
    return masked_power_inverse(system)


def inverse_keep(system):
    inverse = masked_power_inverse(system)
    return inverse, inverse


def inverse_back(inverse, grad):
    turned = jnp.swapaxes(inverse, -1, -2)
    return (-hi("bij,bjk->bik", turned, hi("bij,bjk->bik", grad, turned)),)


unit_lower_inverse.defvjp(inverse_keep, inverse_back)


def block_mixer(query_rows, key_rows, value_rows, beta_rows, log_decay, starts_flag):
    pseudo = key_rows.shape[0]
    span = STEPS * BLOCK
    blocks = pseudo // span
    queries = query_rows.reshape(blocks, BLOCK, DK)
    keys = key_rows.reshape(blocks, span, DK)
    values = value_rows.reshape(blocks, span, DK)
    betas = beta_rows.reshape(blocks, span)
    decays = log_decay.reshape(blocks, span)
    flags = starts_flag.reshape(blocks, span)
    places = jnp.arange(span)
    lower = places[:, None] >= places[None, :]
    strict = (places[:, None] > places[None, :]).astype(jnp.float32)
    identity = jnp.eye(span, dtype=jnp.float32)
    eye_key = jnp.eye(DK, dtype=jnp.float32)

    summed = jnp.cumsum(decays, axis=1)
    segment = jnp.cumsum(flags, axis=1)
    same_doc = (segment[:, :, None] == segment[:, None, :]) & lower
    decay_ratio = jnp.exp(
        jnp.where(same_doc, summed[:, :, None] - summed[:, None, :], 0.0)
    ) * same_doc.astype(jnp.float32)
    from_start = jnp.exp(summed) * (segment == 0.0).astype(jnp.float32)
    key_key = hi("bik,bjk->bij", keys, keys)
    system = identity + betas[:, :, None] * decay_ratio * key_key * strict
    right_side = jnp.concatenate(
        [betas[:, :, None] * values, (betas * from_start)[:, :, None] * keys], 2
    )
    solved = hi("bij,bjk->bik", unit_lower_inverse(system), right_side)
    fresh = solved[:, :, :DK]
    carried = solved[:, :, DK:]
    last_keys = keys * decay_ratio[:, -1, :, None]
    transfer = from_start[:, -1, None, None] * eye_key - hi("bsi,bsj->bij", last_keys, carried)
    offset = hi("bsi,bsj->bij", last_keys, fresh)
    query_key = hi("bqk,bsk->bqs", queries, keys) * decay_ratio[:, STEPS - 1 :: STEPS]
    frame = from_start[:, STEPS - 1 :: STEPS, None] * queries - hi(
        "bqs,bsj->bqj", query_key, carried
    )
    direct = hi("bqs,bsj->bqj", query_key, fresh)

    state = jnp.concatenate([eye_key, jnp.zeros((DK, DK), jnp.float32)], 1)
    states = []
    for index in range(blocks):
        states.append(state)
        state = hi("ij,jk->ik", transfer[index], state) + jnp.concatenate(
            [jnp.zeros((DK, DK), jnp.float32), offset[index]], 1
        )
    states = jnp.stack(states)
    mats = states[:, :, :DK]
    adds = states[:, :, DK:]
    final_mat = state[:, :DK]
    final_add = state[:, DK:]
    query_frame = hi("bqi,bij->bqj", frame, mats)
    partial = hi("bqi,bij->bqj", frame, adds) + direct
    return (
        query_frame.reshape(blocks * BLOCK, DK),
        partial.reshape(blocks * BLOCK, DK),
        final_mat[None],
        final_add[None],
    )


def local(
    tokens_in,
    mixer_norm,
    mix_weight,
    head_gates,
    conv_taps,
    decay_log,
    decay_bias,
    gate_weight,
    out_norm,
    out_weight,
    feed_norm,
    up_weight,
    down_weight,
    doc_lengths,
    out_grad,
):
    row_count = tokens_in.shape[0]
    weight_rows = mix_weight.shape[0]
    head = lax.axis_index("sl") * lax.axis_size("hd") + lax.axis_index("hd")
    length = row_count * HEADS

    head_cols = jnp.concatenate(
        [
            gate_weight.reshape(weight_rows, HEADS, DK),
            mix_weight.reshape(weight_rows, HEADS, PROJ),
            head_gates.reshape(weight_rows, HEADS, STEPS + 1),
            jnp.broadcast_to(mixer_norm[:, None, None], (weight_rows, HEADS, 1)),
        ],
        2,
    )
    head_wide = columns_to_heads(head_cols)
    head_full = head_wide[:, :WIDE]
    gain_one = head_wide[:, WIDE].astype(jnp.float32)
    half = FF // HEADS
    up_cols = jnp.concatenate(
        [
            up_weight[:, :FF].reshape(weight_rows, HEADS, half),
            up_weight[:, FF:].reshape(weight_rows, HEADS, half),
            jnp.broadcast_to(feed_norm[:, None, None], (weight_rows, HEADS, 1)),
        ],
        2,
    )
    up_wide = columns_to_heads(up_cols)
    up_full = up_wide[:, : 2 * half]
    gain_two = up_wide[:, 2 * half].astype(jnp.float32)
    tap_width = conv_taps.shape[1]
    tap_row = jnp.pad(conv_taps.reshape(1, -1), ((0, 0), (0, D - CONV * tap_width)))
    out_full, down_full, tap_rows = rows_to_heads((out_weight, down_weight, tap_row))
    conv_part = jnp.transpose(
        tap_rows[:, : CONV * tap_width].reshape(-1, CONV, tap_width), (1, 0, 2)
    ).reshape(CONV, -1).astype(jnp.float32)

    x_float = tokens_in.astype(jnp.float32)
    normed_float, norm_one_back = jax.vjp(rms_norm, x_float, gain_one)
    normed_one = group_gather(normed_float.astype(jnp.bfloat16), True)
    head_out = bf_product(normed_one, head_full)
    out_gate = head_out[:, :DK]
    proj_head = head_out[:, DK : DK + PROJ].astype(jnp.bfloat16)
    scalar_rows = head_out[:, DK + PROJ :].astype(jnp.bfloat16).astype(jnp.float32)

    rim_rows = from_behind(proj_head[length - (CONV - 1) :], "sh", 1)
    padded = jnp.concatenate([rim_rows, proj_head], 0).astype(jnp.float32)
    starts = jnp.cumsum(doc_lengths) - doc_lengths
    positions = lax.axis_index("sh") * length + jnp.arange(length, dtype=jnp.int32)
    starts_flag = jnp.any(positions[:, None] == starts[None, :], 1).astype(jnp.float32)
    doc_begin = jnp.max(jnp.where(starts[None, :] <= positions[:, None], starts[None, :], 0), 1)
    tap_masks = [
        (positions - (CONV - 1) + tap_index >= doc_begin).astype(jnp.float32)
        for tap_index in range(CONV)
    ]
    pseudo_flag = jnp.concatenate(
        [starts_flag[:, None], jnp.zeros((length, STEPS - 1), jnp.float32)], 1
    ).reshape(-1)
    rate_log = lax.dynamic_index_in_dim(decay_log, head, 0, False)
    bias_part = lax.dynamic_index_in_dim(decay_bias, head, 0, False)

    def mixer_inputs(padded, scalar_rows, conv_part, rate_log, bias_part):
        convolved = jnp.zeros_like(padded[CONV - 1 :])
        for tap_index in range(CONV):
            convolved = (
                convolved
                + conv_part[tap_index]
                * padded[tap_index : tap_index + length]
                * tap_masks[tap_index][:, None]
            )
        activated = jax.nn.silu(convolved).reshape(length, 1 + 2 * STEPS, DK)
        query_rows = unit_norm(activated[:, 0])
        key_rows = unit_norm(activated[:, 1 : 1 + STEPS]).reshape(STEPS * length, DK)
        value_rows = activated[:, 1 + STEPS :].reshape(STEPS * length, DK)
        beta_rows = jax.nn.sigmoid(scalar_rows[:, :STEPS]).reshape(STEPS * length)
        log_rate = -jnp.exp(rate_log) * jax.nn.softplus(scalar_rows[:, STEPS] + bias_part)
        log_decay = jnp.concatenate(
            [log_rate[:, None], jnp.zeros((length, STEPS - 1), jnp.float32)], 1
        ).reshape(STEPS * length)
        return (query_rows, key_rows, value_rows, beta_rows, log_decay)

    def recurrence(query_rows, key_rows, value_rows, beta_rows, log_decay):
        return block_mixer(query_rows, key_rows, value_rows, beta_rows, log_decay, pseudo_flag)

    prepared, inputs_back = jax.vjp(
        mixer_inputs, padded, scalar_rows, conv_part, rate_log, bias_part
    )
    (query_frame, partial_value_rows, transfer, offset), recurrence_back = jax.vjp(
        recurrence, *prepared
    )
    grad_rows = group_gather(out_grad)
    grad_rows, query_frame, partial_value_rows, transfer, offset = lax.optimization_barrier(
        (grad_rows, query_frame, partial_value_rows, transfer, offset)
    )
    identity = jnp.eye(DK, dtype=jnp.float32)[None]
    zeros_state = jnp.zeros((1, DK, DK), jnp.float32)
    prefix_map, incoming_state = carried_in(
        (transfer, offset), "sh", compose, (identity, zeros_state), False
    )
    mixer_result = partial_value_rows + hi("zy,yi->zi", query_frame, incoming_state[0])
    mixer_low = mixer_result.astype(jnp.bfloat16).astype(jnp.float32)
    gated, gate_back = jax.vjp(gate_norm, mixer_low, out_gate, out_norm)
    gated_rows = gated.astype(jnp.bfloat16)
    middle = x_float + group_scatter(bf_product(gated_rows, out_full))
    normed_mid, norm_two_back = jax.vjp(rms_norm, middle, gain_two)
    normed_two = group_gather(normed_mid.astype(jnp.bfloat16))
    gate_up = bf_product(normed_two, up_full)
    hidden_float, swiglu_back = jax.vjp(swiglu, gate_up)
    hidden = hidden_float.astype(jnp.bfloat16)
    feed_partial = bf_product(hidden, down_full)

    grad_out = out_grad.astype(jnp.float32)
    grad_hidden = bf_product(grad_rows, down_full.T)
    grad_down_partial = bf_product(hidden.T, grad_rows)
    (grad_gate_up,) = swiglu_back(grad_hidden)
    grad_gate_up = grad_gate_up.astype(jnp.bfloat16)
    grad_normed_two = group_scatter(bf_product(grad_gate_up, up_full.T))
    grad_mid_norm, grad_gain_two = norm_two_back(grad_normed_two)
    grad_up_payload = jnp.concatenate(
        [bf_product(normed_two.T, grad_gate_up), grad_gain_two[:, None]], 1
    )
    grad_middle = grad_out + grad_mid_norm
    feed_partial, grad_up_payload, grad_down_partial, grad_branch_low = lax.optimization_barrier(
        (feed_partial, grad_up_payload, grad_down_partial, grad_middle.astype(jnp.bfloat16))
    )
    grad_branch = group_gather(grad_branch_low)
    feed_partial, grad_down_partial, grad_branch = lax.optimization_barrier(
        (feed_partial, grad_down_partial, grad_branch)
    )
    feed_sum = group_scatter(feed_partial)
    grad_gated = bf_product(grad_branch, out_full.T)
    grad_down, grad_outw, grad_up_cols = heads_to_rows(
        (grad_down_partial, bf_product(gated_rows.T, grad_branch)), grad_up_payload
    )
    grad_mixer, grad_gate, grad_out_norm = gate_back(grad_gated)
    grad_gate = grad_gate.astype(jnp.bfloat16)
    head_gradients = grad_mixer.astype(jnp.bfloat16).astype(jnp.float32)
    local_adjoint = hi("dc,dr->cr", query_frame, head_gradients)[None]
    transfer_turned = jnp.transpose(transfer, (0, 2, 1))
    later_map, state_gradient = carried_in(
        (transfer_turned, local_adjoint), "sh", compose, (identity, zeros_state), True
    )
    basis_gradient = hi("nu,wu->nw", head_gradients, incoming_state[0])
    transfer_gradient = hi("tnf,tmf->tnm", state_gradient, incoming_state)
    grad_prepared = recurrence_back(
        (basis_gradient, head_gradients, transfer_gradient, state_gradient)
    )
    grad_prepared, feed_sum, grad_up_cols, grad_down, grad_outw = lax.optimization_barrier(
        (grad_prepared, feed_sum, grad_up_cols, grad_down, grad_outw)
    )
    layer_out = (middle + feed_sum).astype(jnp.bfloat16)
    grad_padded, grad_scalars, grad_conv, grad_rate, grad_bias = inputs_back(grad_prepared)
    rim_grad = from_behind(grad_padded[: CONV - 1], "sh", -1)
    own_grad = grad_padded[CONV - 1 :]
    grad_proj = jnp.concatenate(
        [own_grad[: length - (CONV - 1)], own_grad[length - (CONV - 1) :] + rim_grad], 0
    )
    grad_head = jnp.concatenate(
        [grad_gate, grad_proj.astype(jnp.bfloat16), grad_scalars.astype(jnp.bfloat16)], 1
    )
    grad_normed_one = group_scatter(bf_product(grad_head, head_full.T), True)
    grad_x_norm, grad_gain_one = norm_one_back(grad_normed_one)
    grad_head_cols = heads_to_columns(
        jnp.concatenate([bf_product(normed_one.T, grad_head), grad_gain_one[:, None]], 1)
    )
    grad_gatew = grad_head_cols[:, :, :DK].reshape(weight_rows, D)
    grad_mixw = grad_head_cols[:, :, DK : DK + PROJ].reshape(weight_rows, HEADS * PROJ)
    grad_gatesw = grad_head_cols[:, :, DK + PROJ : WIDE].reshape(
        weight_rows, HEADS * (STEPS + 1)
    )
    grad_tokens = (grad_middle + grad_x_norm).astype(jnp.bfloat16)
    grad_up = jnp.concatenate(
        [
            grad_up_cols[:, :, :half].reshape(weight_rows, FF),
            grad_up_cols[:, :, half : 2 * half].reshape(weight_rows, FF),
        ],
        1,
    )
    (conv_grad,) = heads_to_rows((jnp.transpose(grad_conv),))
    conv_grad = jnp.transpose(conv_grad)
    one_hot = (jnp.arange(HEADS) == head).astype(jnp.float32)
    small_sums = all_sum(
        jnp.concatenate([one_hot * grad_rate, one_hot * grad_bias, grad_out_norm])
    )
    return (
        layer_out,
        grad_tokens,
        jnp.sum(grad_head_cols[:, :, WIDE], 1),
        grad_mixw,
        grad_gatesw,
        conv_grad,
        small_sums[:HEADS],
        small_sums[HEADS : 2 * HEADS],
        grad_gatew,
        small_sums[2 * HEADS :],
        grad_outw,
        jnp.sum(grad_up_cols[:, :, 2 * half], 1),
        grad_up,
        grad_down,
    )


def solution(mesh):
    seq = mesh.shape["seq"]
    across = mesh.shape["head"]
    inner = HEADS // across
    grid = Mesh(
        np.asarray(mesh.devices).reshape(seq // inner, inner, across), ("sh", "sl", "hd")
    )
    rows = P(ALL, None)
    flat = P(ALL)
    return jax.shard_map(
        local,
        mesh=grid,
        in_specs=(
            rows,
            flat,
            rows,
            rows,
            P(None, ALL),
            P(),
            P(),
            rows,
            P(),
            rows,
            flat,
            rows,
            rows,
            P(),
            rows,
        ),
        out_specs=(
            rows,
            rows,
            flat,
            rows,
            rows,
            P(None, ALL),
            P(),
            P(),
            rows,
            P(),
            rows,
            flat,
            rows,
            rows,
        ),
        check_vma=False,
    )
```

```python
import jax
import jax.numpy as jnp
import numpy as np
from jax import lax
from jax.experimental import pallas as pl
from jax.experimental.pallas import tpu as pltpu
from jax.sharding import Mesh
from jax.sharding import PartitionSpec as P

D = 1024
HEADS = 8
DK = 128
FF = 2816
STEPS = 2
CONV = 4
BLOCK = 64
PROJ = (1 + 2 * STEPS) * DK
WIDE = DK + PROJ + STEPS + 1

EPS = 1e-06
HIGH_ACCURACY = lax.Precision.HIGH

GROUP = ("sl", "hd")
ALL = ("sh", "sl", "hd")


def from_behind(shard, axis, by):
    peers = lax.axis_size(axis)
    pairs = [(i, i + by) for i in range(peers) if 0 <= i + by < peers]
    return lax.ppermute(shard, axis, pairs)


def carried_in(shard, axis, join, neutral, backward):
    count = lax.axis_size(axis)
    place = lax.axis_index(axis)
    ahead = count - 1 - place if backward else place
    both = lax.all_gather(jnp.stack(shard).astype(jnp.bfloat16), axis)
    gathered = (both[:, 0], both[:, 1])
    state = jax.tree.map(lambda a, e: jnp.zeros_like(a) + jnp.asarray(e, a.dtype), shard, neutral)

    def one(turn, state):
        source = count - 1 - turn if backward else turn
        return join(
            state,
            jax.tree.map(
                lambda a, own: lax.dynamic_index_in_dim(a, source, 0, False).astype(own.dtype),
                gathered,
                shard,
            ),
        )

    return lax.fori_loop(0, ahead, one, state)


def flat_place():
    return (
        lax.axis_index("sh") * lax.axis_size("sl") + lax.axis_index("sl")
    ) * lax.axis_size("hd") + lax.axis_index("hd")


def device_of(index):
    inner = lax.axis_size("sl") * lax.axis_size("hd")
    return (index // inner, (index // lax.axis_size("hd")) % lax.axis_size("sl"), index % lax.axis_size("hd"))


def sum_kernel(count, own_ref, out_ref, slots, send_sems, recv_sems):
    me = flat_place()
    barrier = pltpu.get_barrier_semaphore()

    def greet(index, carry):
        @pl.when(index != me)
        def _():
            pl.semaphore_signal(
                barrier, inc=1, device_id=device_of(index), device_id_type=pl.DeviceIdType.MESH
            )

        return carry

    lax.fori_loop(0, count, greet, 0)
    pl.semaphore_wait(barrier, count - 1)

    def copy_to(index):
        return pltpu.make_async_remote_copy(
            src_ref=own_ref,
            dst_ref=slots.at[me],
            send_sem=send_sems.at[index],
            recv_sem=recv_sems.at[me],
            device_id=device_of(index),
            device_id_type=pl.DeviceIdType.MESH,
        )

    def copy_from(index):
        return pltpu.make_async_remote_copy(
            src_ref=own_ref,
            dst_ref=slots.at[index],
            send_sem=send_sems.at[index],
            recv_sem=recv_sems.at[index],
            device_id=device_of(index),
            device_id_type=pl.DeviceIdType.MESH,
        )

    def send(index, carry):
        @pl.when(index != me)
        def _():
            copy_to(index).start()

        return carry

    lax.fori_loop(0, count, send, 0)
    slots[me] = own_ref[...]

    def finish(index, carry):
        @pl.when(index != me)
        def _():
            copy_to(index).wait_send()
            copy_from(index).wait_recv()

        return carry

    lax.fori_loop(0, count, finish, 0)
    out_ref[...] = jnp.sum(slots[...], axis=0)


def all_sum(vector):
    count = lax.axis_size("sh") * lax.axis_size("sl") * lax.axis_size("hd")
    size = vector.shape[0]
    lanes = 128
    tile = 8 * lanes
    padded = -(-size // tile) * tile
    block = jnp.pad(vector, (0, padded - size)).reshape(padded // lanes, lanes)
    total = pl.pallas_call(
        lambda *refs: sum_kernel(count, *refs),
        out_shape=jax.ShapeDtypeStruct(block.shape, jnp.float32),
        in_specs=[pl.BlockSpec(memory_space=pltpu.VMEM)],
        out_specs=pl.BlockSpec(memory_space=pltpu.VMEM),
        scratch_shapes=[
            pltpu.VMEM((count,) + block.shape, jnp.float32),
            pltpu.SemaphoreType.DMA((count,)),
            pltpu.SemaphoreType.DMA((count,)),
        ],
        compiler_params=pltpu.CompilerParams(collective_id=0, has_side_effects=True),
    )(block)
    return total.reshape(-1)[:size]


def rms_norm(values, scale_gain):
    return values * lax.rsqrt(jnp.mean(values * values, axis=-1, keepdims=True) + EPS) * scale_gain


def unit_norm(values):
    return values * lax.rsqrt(jnp.sum(values * values, axis=-1, keepdims=True) + EPS)


def bf_product(first_mat, second_mat):
    return jnp.dot(first_mat, second_mat, preferred_element_type=jnp.float32)


def hi(spec, *arrays):
    return jnp.einsum(spec, *arrays, precision=HIGH_ACCURACY)


def compose(early_pair, late_pair):
    early_mat, early_add = early_pair
    late_mat, late_add = late_pair
    joined = hi("hij,hjk->hik", late_mat, early_mat)
    shifted = hi("hij,hjk->hik", late_mat, early_add) + late_add
    return (joined, shifted)


def gate_norm(values, out_gate, scale_gain):
    return rms_norm(values, scale_gain) * jax.nn.silu(out_gate)


def swiglu(gate_up):
    half = gate_up.shape[1] // 2
    return jax.nn.silu(gate_up[:, :half]) * gate_up[:, half:]


def owner_pairs(inverse):
    groups = lax.axis_size("sh")
    pairs = [(g * HEADS + t, t * groups + g) for g in range(groups) for t in range(HEADS)]
    return [(b, a) for a, b in pairs] if inverse else pairs


def rows_to_heads(blocks):
    groups = lax.axis_size("sh")
    width = blocks[0].shape[1]
    used = sum(b.shape[0] for b in blocks)
    least = (1 << 20) // (groups * width * 2) + 1
    rows = -(-max(used, least) // 8) * 8
    packed = jnp.concatenate(
        list(blocks) + [jnp.zeros((rows - used, width), blocks[0].dtype)], 0
    )
    moved = lax.ppermute(packed, ALL, owner_pairs(True))
    full = lax.all_gather(moved, "sh", axis=0, tiled=False)
    parts = []
    first = 0
    for block in blocks:
        size = block.shape[0]
        parts.append(full[:, first : first + size].reshape(groups * size, width))
        first += size
    return parts


def heads_to_rows(partials):
    groups = lax.axis_size("sh")
    pieces = [
        p.astype(jnp.bfloat16).reshape((groups, p.shape[0] // groups) + p.shape[1:])
        for p in partials
    ]
    joined = jnp.concatenate(pieces, 1)
    joined = joined.reshape((-1,) + joined.shape[2:])
    summed = lax.psum_scatter(joined, "sh", scatter_dimension=0, tiled=True)
    moved = lax.ppermute(summed, ALL, owner_pairs(False)).astype(jnp.float32)
    parts = []
    first = 0
    for piece in pieces:
        size = piece.shape[1]
        parts.append(moved[first : first + size])
        first += size
    return parts


def columns_to_heads(local_cols):
    per_head = jnp.transpose(local_cols, (1, 0, 2))
    mine = lax.all_to_all(per_head, GROUP, 0, 0, tiled=True)
    mine = mine.reshape(-1, mine.shape[-1])
    return lax.all_gather(mine, "sh", axis=0, tiled=True)


def heads_to_columns(partial, direct=False):
    low = partial.astype(jnp.bfloat16)
    if direct:
        groups = lax.axis_size("sh")
        pieces = low.reshape((groups, low.shape[0] // groups) + low.shape[1:])
        moved = lax.all_to_all(pieces, "sh", 0, 0, tiled=True)
        summed = jnp.sum(moved.astype(jnp.float32), 0).astype(jnp.bfloat16)
    else:
        summed = lax.psum_scatter(low, "sh", scatter_dimension=0, tiled=True)
    summed = summed.reshape(HEADS, -1, summed.shape[-1])
    back = lax.all_to_all(summed, GROUP, 0, 0, tiled=True)
    return jnp.transpose(back, (1, 0, 2)).astype(jnp.float32)


def group_gather(rows, direct=False):
    if direct:
        copies = jnp.broadcast_to(rows[None], (HEADS,) + rows.shape)
        moved = lax.all_to_all(copies, GROUP, 0, 0, tiled=True)
        return moved.reshape((-1,) + rows.shape[1:])
    return lax.all_gather(rows, GROUP, axis=0, tiled=True)


def group_scatter(partial, direct=False):
    low = partial.astype(jnp.bfloat16)
    if direct:
        pieces = low.reshape((HEADS, low.shape[0] // HEADS) + low.shape[1:])
        moved = lax.all_to_all(pieces, GROUP, 0, 0, tiled=True)
        return jnp.sum(moved.astype(jnp.float32), 0)
    return lax.psum_scatter(low, GROUP, scatter_dimension=0, tiled=True).astype(jnp.float32)


def masked_power_inverse(system):
    size = system.shape[-1]
    places = jnp.arange(size)
    base = 8
    inside = (places[:, None] // base == places[None, :] // base) & (
        places[:, None] > places[None, :]
    )
    step = -(system * inside.astype(system.dtype))
    eye = jnp.eye(size, dtype=system.dtype)
    result = eye + step
    for _ in range(2):
        step = hi("bij,bjk->bik", step, step)
        result = result + hi("bij,bjk->bik", result, step)
    width = base
    while width < size:
        across = (places[:, None] // (2 * width) == places[None, :] // (2 * width)) & (
            places[:, None] // width != places[None, :] // width
        )
        lower_left = system * across.astype(system.dtype)
        result = result - hi("bij,bjk->bik", result, hi("bij,bjk->bik", lower_left, result))
        width = 2 * width
    return result


@jax.custom_vjp
def unit_lower_inverse(system):
    return masked_power_inverse(system)


def inverse_keep(system):
    inverse = masked_power_inverse(system)
    return inverse, inverse


def inverse_back(inverse, grad):
    turned = jnp.swapaxes(inverse, -1, -2)
    return (-hi("bij,bjk->bik", turned, hi("bij,bjk->bik", grad, turned)),)


unit_lower_inverse.defvjp(inverse_keep, inverse_back)


def block_mixer(query_rows, key_rows, value_rows, beta_rows, log_decay, starts_flag):
    pseudo = key_rows.shape[0]
    span = STEPS * BLOCK
    blocks = pseudo // span
    queries = query_rows.reshape(blocks, BLOCK, DK)
    keys = key_rows.reshape(blocks, span, DK)
    values = value_rows.reshape(blocks, span, DK)
    betas = beta_rows.reshape(blocks, span)
    decays = log_decay.reshape(blocks, span)
    flags = starts_flag.reshape(blocks, span)
    places = jnp.arange(span)
    lower = places[:, None] >= places[None, :]
    strict = (places[:, None] > places[None, :]).astype(jnp.float32)
    identity = jnp.eye(span, dtype=jnp.float32)
    eye_key = jnp.eye(DK, dtype=jnp.float32)

    summed = jnp.cumsum(decays, axis=1)
    segment = jnp.cumsum(flags, axis=1)
    same_doc = (segment[:, :, None] == segment[:, None, :]) & lower
    decay_ratio = jnp.exp(
        jnp.where(same_doc, summed[:, :, None] - summed[:, None, :], 0.0)
    ) * same_doc.astype(jnp.float32)
    from_start = jnp.exp(summed) * (segment == 0.0).astype(jnp.float32)
    key_key = hi("bik,bjk->bij", keys, keys)
    system = identity + betas[:, :, None] * decay_ratio * key_key * strict
    right_side = jnp.concatenate(
        [betas[:, :, None] * values, (betas * from_start)[:, :, None] * keys], 2
    )
    solved = hi("bij,bjk->bik", unit_lower_inverse(system), right_side)
    fresh = solved[:, :, :DK]
    carried = solved[:, :, DK:]
    last_keys = keys * decay_ratio[:, -1, :, None]
    transfer = from_start[:, -1, None, None] * eye_key - hi("bsi,bsj->bij", last_keys, carried)
    offset = hi("bsi,bsj->bij", last_keys, fresh)
    query_key = hi("bqk,bsk->bqs", queries, keys) * decay_ratio[:, STEPS - 1 :: STEPS]
    frame = from_start[:, STEPS - 1 :: STEPS, None] * queries - hi(
        "bqs,bsj->bqj", query_key, carried
    )
    direct = hi("bqs,bsj->bqj", query_key, fresh)

    state = jnp.concatenate([eye_key, jnp.zeros((DK, DK), jnp.float32)], 1)
    states = []
    for index in range(blocks):
        states.append(state)
        state = hi("ij,jk->ik", transfer[index], state) + jnp.concatenate(
            [jnp.zeros((DK, DK), jnp.float32), offset[index]], 1
        )
    states = jnp.stack(states)
    mats = states[:, :, :DK]
    adds = states[:, :, DK:]
    final_mat = state[:, :DK]
    final_add = state[:, DK:]
    query_frame = hi("bqi,bij->bqj", frame, mats)
    partial = hi("bqi,bij->bqj", frame, adds) + direct
    return (
        query_frame.reshape(blocks * BLOCK, DK),
        partial.reshape(blocks * BLOCK, DK),
        final_mat[None],
        final_add[None],
    )


def local(
    tokens_in,
    mixer_norm,
    mix_weight,
    head_gates,
    conv_taps,
    decay_log,
    decay_bias,
    gate_weight,
    out_norm,
    out_weight,
    feed_norm,
    up_weight,
    down_weight,
    doc_lengths,
    out_grad,
):
    row_count = tokens_in.shape[0]
    weight_rows = mix_weight.shape[0]
    head = lax.axis_index("sl") * lax.axis_size("hd") + lax.axis_index("hd")
    length = row_count * HEADS

    head_cols = jnp.concatenate(
        [
            gate_weight.reshape(weight_rows, HEADS, DK),
            mix_weight.reshape(weight_rows, HEADS, PROJ),
            head_gates.reshape(weight_rows, HEADS, STEPS + 1),
            jnp.broadcast_to(mixer_norm[:, None, None], (weight_rows, HEADS, 1)),
        ],
        2,
    )
    head_wide = columns_to_heads(head_cols)
    head_full = head_wide[:, :WIDE]
    gain_one = head_wide[:, WIDE].astype(jnp.float32)
    half = FF // HEADS
    up_cols = jnp.concatenate(
        [
            up_weight[:, :FF].reshape(weight_rows, HEADS, half),
            up_weight[:, FF:].reshape(weight_rows, HEADS, half),
            jnp.broadcast_to(feed_norm[:, None, None], (weight_rows, HEADS, 1)),
        ],
        2,
    )
    up_wide = columns_to_heads(up_cols)
    up_full = up_wide[:, : 2 * half]
    gain_two = up_wide[:, 2 * half].astype(jnp.float32)
    tap_width = conv_taps.shape[1]
    tap_row = jnp.pad(conv_taps.reshape(1, -1), ((0, 0), (0, D - CONV * tap_width)))
    out_full, down_full, tap_rows = rows_to_heads((out_weight, down_weight, tap_row))
    conv_part = jnp.transpose(
        tap_rows[:, : CONV * tap_width].reshape(-1, CONV, tap_width), (1, 0, 2)
    ).reshape(CONV, -1).astype(jnp.float32)

    x_float = tokens_in.astype(jnp.float32)
    normed_float, norm_one_back = jax.vjp(rms_norm, x_float, gain_one)
    normed_one = group_gather(normed_float.astype(jnp.bfloat16), True)
    tokens_all = group_gather(tokens_in, True)
    head_out = bf_product(normed_one, head_full)
    out_gate = head_out[:, :DK]
    proj_head = head_out[:, DK : DK + PROJ].astype(jnp.bfloat16)
    scalar_rows = head_out[:, DK + PROJ :].astype(jnp.bfloat16).astype(jnp.float32)

    rim_rows = from_behind(proj_head[length - (CONV - 1) :], "sh", 1)
    padded = jnp.concatenate([rim_rows, proj_head], 0).astype(jnp.float32)
    starts = jnp.cumsum(doc_lengths) - doc_lengths
    positions = lax.axis_index("sh") * length + jnp.arange(length, dtype=jnp.int32)
    starts_flag = jnp.any(positions[:, None] == starts[None, :], 1).astype(jnp.float32)
    doc_begin = jnp.max(jnp.where(starts[None, :] <= positions[:, None], starts[None, :], 0), 1)
    tap_masks = [
        (positions - (CONV - 1) + tap_index >= doc_begin).astype(jnp.float32)
        for tap_index in range(CONV)
    ]
    pseudo_flag = jnp.concatenate(
        [starts_flag[:, None], jnp.zeros((length, STEPS - 1), jnp.float32)], 1
    ).reshape(-1)
    rate_log = lax.dynamic_index_in_dim(decay_log, head, 0, False)
    bias_part = lax.dynamic_index_in_dim(decay_bias, head, 0, False)

    def mixer_inputs(padded, scalar_rows, conv_part, rate_log, bias_part):
        convolved = jnp.zeros_like(padded[CONV - 1 :])
        for tap_index in range(CONV):
            convolved = (
                convolved
                + conv_part[tap_index]
                * padded[tap_index : tap_index + length]
                * tap_masks[tap_index][:, None]
            )
        activated = jax.nn.silu(convolved).reshape(length, 1 + 2 * STEPS, DK)
        query_rows = unit_norm(activated[:, 0])
        key_rows = unit_norm(activated[:, 1 : 1 + STEPS]).reshape(STEPS * length, DK)
        value_rows = activated[:, 1 + STEPS :].reshape(STEPS * length, DK)
        beta_rows = jax.nn.sigmoid(scalar_rows[:, :STEPS]).reshape(STEPS * length)
        log_rate = -jnp.exp(rate_log) * jax.nn.softplus(scalar_rows[:, STEPS] + bias_part)
        log_decay = jnp.concatenate(
            [log_rate[:, None], jnp.zeros((length, STEPS - 1), jnp.float32)], 1
        ).reshape(STEPS * length)
        return (query_rows, key_rows, value_rows, beta_rows, log_decay)

    def recurrence(query_rows, key_rows, value_rows, beta_rows, log_decay):
        return block_mixer(query_rows, key_rows, value_rows, beta_rows, log_decay, pseudo_flag)

    prepared, inputs_back = jax.vjp(
        mixer_inputs, padded, scalar_rows, conv_part, rate_log, bias_part
    )
    (query_frame, partial_value_rows, transfer, offset), recurrence_back = jax.vjp(
        recurrence, *prepared
    )
    grad_rows = group_gather(out_grad)
    grad_rows, query_frame, partial_value_rows, transfer, offset = lax.optimization_barrier(
        (grad_rows, query_frame, partial_value_rows, transfer, offset)
    )
    identity = jnp.eye(DK, dtype=jnp.float32)[None]
    zeros_state = jnp.zeros((1, DK, DK), jnp.float32)
    prefix_map, incoming_state = carried_in(
        (transfer, offset), "sh", compose, (identity, zeros_state), False
    )
    mixer_result = partial_value_rows + hi("zy,yi->zi", query_frame, incoming_state[0])
    mixer_low = mixer_result.astype(jnp.bfloat16).astype(jnp.float32)
    gated, gate_back = jax.vjp(gate_norm, mixer_low, out_gate, out_norm)
    gated_rows = gated.astype(jnp.bfloat16)
    branch_all = lax.psum(bf_product(gated_rows, out_full).astype(jnp.bfloat16), GROUP)
    middle_all = tokens_all.astype(jnp.float32) + branch_all.astype(jnp.float32)
    middle = lax.dynamic_slice_in_dim(middle_all, head * row_count, row_count, 0)
    normed_two = rms_norm(middle_all, gain_two).astype(jnp.bfloat16)
    normed_mid, norm_two_back = jax.vjp(rms_norm, middle, gain_two)
    gate_up = bf_product(normed_two, up_full)
    hidden_float, swiglu_back = jax.vjp(swiglu, gate_up)
    hidden = hidden_float.astype(jnp.bfloat16)
    feed_partial = bf_product(hidden, down_full)

    grad_out = out_grad.astype(jnp.float32)
    grad_hidden = bf_product(grad_rows, down_full.T)
    grad_down_partial = bf_product(hidden.T, grad_rows)
    (grad_gate_up,) = swiglu_back(grad_hidden)
    grad_gate_up = grad_gate_up.astype(jnp.bfloat16)
    grad_normed_two = group_scatter(bf_product(grad_gate_up, up_full.T))
    grad_mid_norm, grad_gain_two = norm_two_back(grad_normed_two)
    grad_up_payload = jnp.concatenate(
        [bf_product(normed_two.T, grad_gate_up), grad_gain_two[:, None]], 1
    )
    grad_middle = grad_out + grad_mid_norm
    feed_partial, grad_up_payload, grad_down_partial, grad_branch_low = lax.optimization_barrier(
        (feed_partial, grad_up_payload, grad_down_partial, grad_middle.astype(jnp.bfloat16))
    )
    grad_up_cols = heads_to_columns(grad_up_payload, True)
    grad_up = jnp.concatenate(
        [
            grad_up_cols[:, :, :half].reshape(weight_rows, FF),
            grad_up_cols[:, :, half : 2 * half].reshape(weight_rows, FF),
        ],
        1,
    )
    grad_branch = group_gather(grad_branch_low)
    feed_partial, grad_down_partial, grad_branch = lax.optimization_barrier(
        (feed_partial, grad_down_partial, grad_branch)
    )
    feed_sum = group_scatter(feed_partial)
    grad_gated = bf_product(grad_branch, out_full.T)
    grad_down, grad_outw = heads_to_rows((grad_down_partial, bf_product(gated_rows.T, grad_branch)))
    grad_mixer, grad_gate, grad_out_norm = gate_back(grad_gated)
    grad_gate = grad_gate.astype(jnp.bfloat16)
    head_gradients = grad_mixer.astype(jnp.bfloat16).astype(jnp.float32)
    local_adjoint = hi("dc,dr->cr", query_frame, head_gradients)[None]
    transfer_turned = jnp.transpose(transfer, (0, 2, 1))
    later_map, state_gradient = carried_in(
        (transfer_turned, local_adjoint), "sh", compose, (identity, zeros_state), True
    )
    basis_gradient = hi("nu,wu->nw", head_gradients, incoming_state[0])
    transfer_gradient = hi("tnf,tmf->tnm", state_gradient, incoming_state)
    grad_prepared = recurrence_back(
        (basis_gradient, head_gradients, transfer_gradient, state_gradient)
    )
    grad_prepared, feed_sum, grad_up_cols, grad_down, grad_outw = lax.optimization_barrier(
        (grad_prepared, feed_sum, grad_up_cols, grad_down, grad_outw)
    )
    layer_out = (middle + feed_sum).astype(jnp.bfloat16)
    grad_padded, grad_scalars, grad_conv, grad_rate, grad_bias = inputs_back(grad_prepared)
    rim_grad = from_behind(grad_padded[: CONV - 1], "sh", -1)
    own_grad = grad_padded[CONV - 1 :]
    grad_proj = jnp.concatenate(
        [own_grad[: length - (CONV - 1)], own_grad[length - (CONV - 1) :] + rim_grad], 0
    )
    grad_head = jnp.concatenate(
        [grad_gate, grad_proj.astype(jnp.bfloat16), grad_scalars.astype(jnp.bfloat16)], 1
    )
    grad_normed_one = group_scatter(bf_product(grad_head, head_full.T), True)
    grad_x_norm, grad_gain_one = norm_one_back(grad_normed_one)
    grad_head_cols = heads_to_columns(
        jnp.concatenate([bf_product(normed_one.T, grad_head), grad_gain_one[:, None]], 1)
    )
    grad_gatew = grad_head_cols[:, :, :DK].reshape(weight_rows, D)
    grad_mixw = grad_head_cols[:, :, DK : DK + PROJ].reshape(weight_rows, HEADS * PROJ)
    grad_gatesw = grad_head_cols[:, :, DK + PROJ : WIDE].reshape(
        weight_rows, HEADS * (STEPS + 1)
    )
    grad_tokens = (grad_middle + grad_x_norm).astype(jnp.bfloat16)
    (conv_grad,) = heads_to_rows((jnp.transpose(grad_conv),))
    conv_grad = jnp.transpose(conv_grad)
    one_hot = (jnp.arange(HEADS) == head).astype(jnp.float32)
    small_sums = all_sum(
        jnp.concatenate([one_hot * grad_rate, one_hot * grad_bias, grad_out_norm])
    )
    return (
        layer_out,
        grad_tokens,
        jnp.sum(grad_head_cols[:, :, WIDE], 1),
        grad_mixw,
        grad_gatesw,
        conv_grad,
        small_sums[:HEADS],
        small_sums[HEADS : 2 * HEADS],
        grad_gatew,
        small_sums[2 * HEADS :],
        grad_outw,
        jnp.sum(grad_up_cols[:, :, 2 * half], 1),
        grad_up,
        grad_down,
    )


def solution(mesh):
    seq = mesh.shape["seq"]
    across = mesh.shape["head"]
    inner = HEADS // across
    grid = Mesh(
        np.asarray(mesh.devices).reshape(seq // inner, inner, across), ("sh", "sl", "hd")
    )
    rows = P(ALL, None)
    flat = P(ALL)
    return jax.shard_map(
        local,
        mesh=grid,
        in_specs=(
            rows,
            flat,
            rows,
            rows,
            P(None, ALL),
            P(),
            P(),
            rows,
            P(),
            rows,
            flat,
            rows,
            rows,
            P(),
            rows,
        ),
        out_specs=(
            rows,
            rows,
            flat,
            rows,
            rows,
            P(None, ALL),
            P(),
            P(),
            rows,
            P(),
            rows,
            flat,
            rows,
            rows,
        ),
        check_vma=False,
    )
```

```python
import jax
import jax.numpy as jnp
import numpy as np
from jax import lax
from jax.experimental import pallas as pl
from jax.experimental.pallas import tpu as pltpu
from jax.sharding import Mesh
from jax.sharding import PartitionSpec as P

D = 1024
HEADS = 8
DK = 128
FF = 2816
STEPS = 2
CONV = 4
BLOCK = 64
PROJ = (1 + 2 * STEPS) * DK
WIDE = DK + PROJ + STEPS + 1

EPS = 1e-06
HIGH_ACCURACY = lax.Precision.HIGH

GROUP = ("sl", "hd")
ALL = ("sh", "sl", "hd")


def from_behind(shard, axis, by):
    peers = lax.axis_size(axis)
    pairs = [(i, i + by) for i in range(peers) if 0 <= i + by < peers]
    return lax.ppermute(shard, axis, pairs)


def carried_in(shard, axis, join, neutral, backward):
    count = lax.axis_size(axis)
    place = lax.axis_index(axis)
    ahead = count - 1 - place if backward else place
    both = lax.all_gather(jnp.stack(shard).astype(jnp.bfloat16), axis)
    gathered = (both[:, 0], both[:, 1])
    state = jax.tree.map(lambda a, e: jnp.zeros_like(a) + jnp.asarray(e, a.dtype), shard, neutral)

    def one(turn, state):
        source = count - 1 - turn if backward else turn
        return join(
            state,
            jax.tree.map(
                lambda a, own: lax.dynamic_index_in_dim(a, source, 0, False).astype(own.dtype),
                gathered,
                shard,
            ),
        )

    return lax.fori_loop(0, ahead, one, state)


def flat_place():
    return (
        lax.axis_index("sh") * lax.axis_size("sl") + lax.axis_index("sl")
    ) * lax.axis_size("hd") + lax.axis_index("hd")


def device_of(index):
    inner = lax.axis_size("sl") * lax.axis_size("hd")
    return (index // inner, (index // lax.axis_size("hd")) % lax.axis_size("sl"), index % lax.axis_size("hd"))


def sum_kernel(count, own_ref, out_ref, slots, send_sems, recv_sems):
    me = flat_place()
    barrier = pltpu.get_barrier_semaphore()

    def greet(index, carry):
        @pl.when(index != me)
        def _():
            pl.semaphore_signal(
                barrier, inc=1, device_id=device_of(index), device_id_type=pl.DeviceIdType.MESH
            )

        return carry

    lax.fori_loop(0, count, greet, 0)
    pl.semaphore_wait(barrier, count - 1)

    def copy_to(index):
        return pltpu.make_async_remote_copy(
            src_ref=own_ref,
            dst_ref=slots.at[me],
            send_sem=send_sems.at[index],
            recv_sem=recv_sems.at[me],
            device_id=device_of(index),
            device_id_type=pl.DeviceIdType.MESH,
        )

    def copy_from(index):
        return pltpu.make_async_remote_copy(
            src_ref=own_ref,
            dst_ref=slots.at[index],
            send_sem=send_sems.at[index],
            recv_sem=recv_sems.at[index],
            device_id=device_of(index),
            device_id_type=pl.DeviceIdType.MESH,
        )

    def send(index, carry):
        @pl.when(index != me)
        def _():
            copy_to(index).start()

        return carry

    lax.fori_loop(0, count, send, 0)
    slots[me] = own_ref[...]

    def finish(index, carry):
        @pl.when(index != me)
        def _():
            copy_to(index).wait_send()
            copy_from(index).wait_recv()

        return carry

    lax.fori_loop(0, count, finish, 0)
    out_ref[...] = jnp.sum(slots[...], axis=0)


def all_sum(vector):
    count = lax.axis_size("sh") * lax.axis_size("sl") * lax.axis_size("hd")
    size = vector.shape[0]
    lanes = 128
    tile = 8 * lanes
    padded = -(-size // tile) * tile
    block = jnp.pad(vector, (0, padded - size)).reshape(padded // lanes, lanes)
    total = pl.pallas_call(
        lambda *refs: sum_kernel(count, *refs),
        out_shape=jax.ShapeDtypeStruct(block.shape, jnp.float32),
        in_specs=[pl.BlockSpec(memory_space=pltpu.VMEM)],
        out_specs=pl.BlockSpec(memory_space=pltpu.VMEM),
        scratch_shapes=[
            pltpu.VMEM((count,) + block.shape, jnp.float32),
            pltpu.SemaphoreType.DMA((count,)),
            pltpu.SemaphoreType.DMA((count,)),
        ],
        compiler_params=pltpu.CompilerParams(collective_id=0, has_side_effects=True),
    )(block)
    return total.reshape(-1)[:size]


def rms_norm(values, scale_gain):
    return values * lax.rsqrt(jnp.mean(values * values, axis=-1, keepdims=True) + EPS) * scale_gain


def unit_norm(values):
    return values * lax.rsqrt(jnp.sum(values * values, axis=-1, keepdims=True) + EPS)


def bf_product(first_mat, second_mat):
    return jnp.dot(first_mat, second_mat, preferred_element_type=jnp.float32)


def hi(spec, *arrays):
    return jnp.einsum(spec, *arrays, precision=HIGH_ACCURACY)


def compose(early_pair, late_pair):
    early_mat, early_add = early_pair
    late_mat, late_add = late_pair
    joined = hi("hij,hjk->hik", late_mat, early_mat)
    shifted = hi("hij,hjk->hik", late_mat, early_add) + late_add
    return (joined, shifted)


def gate_norm(values, out_gate, scale_gain):
    return rms_norm(values, scale_gain) * jax.nn.silu(out_gate)


def swiglu(gate_up):
    half = gate_up.shape[1] // 2
    return jax.nn.silu(gate_up[:, :half]) * gate_up[:, half:]


def owner_pairs(inverse):
    groups = lax.axis_size("sh")
    pairs = [(g * HEADS + t, t * groups + g) for g in range(groups) for t in range(HEADS)]
    return [(b, a) for a, b in pairs] if inverse else pairs


def rows_to_heads(blocks):
    groups = lax.axis_size("sh")
    width = blocks[0].shape[1]
    used = sum(b.shape[0] for b in blocks)
    least = (1 << 20) // (groups * width * 2) + 1
    rows = -(-max(used, least) // 8) * 8
    packed = jnp.concatenate(
        list(blocks) + [jnp.zeros((rows - used, width), blocks[0].dtype)], 0
    )
    moved = lax.ppermute(packed, ALL, owner_pairs(True))
    full = lax.all_gather(moved, "sh", axis=0, tiled=False)
    parts = []
    first = 0
    for block in blocks:
        size = block.shape[0]
        parts.append(full[:, first : first + size].reshape(groups * size, width))
        first += size
    return parts


def heads_to_rows(partials):
    groups = lax.axis_size("sh")
    pieces = [
        p.astype(jnp.bfloat16).reshape((groups, p.shape[0] // groups) + p.shape[1:])
        for p in partials
    ]
    joined = jnp.concatenate(pieces, 1)
    joined = joined.reshape((-1,) + joined.shape[2:])
    summed = lax.psum_scatter(joined, "sh", scatter_dimension=0, tiled=True)
    moved = lax.ppermute(summed, ALL, owner_pairs(False)).astype(jnp.float32)
    parts = []
    first = 0
    for piece in pieces:
        size = piece.shape[1]
        parts.append(moved[first : first + size])
        first += size
    return parts


def columns_to_heads_pair(first_cols, second_cols):
    split = first_cols.shape[-1]
    joined = jnp.transpose(jnp.concatenate([first_cols, second_cols], 2), (1, 0, 2))
    mine = lax.all_to_all(joined, GROUP, 0, 0, tiled=True)
    mine = mine.reshape(-1, mine.shape[-1])
    return (
        lax.all_gather(mine[:, :split], "sh", axis=0, tiled=True),
        lax.all_gather(mine[:, split:], "sh", axis=0, tiled=True),
    )


def columns_to_heads(local_cols):
    per_head = jnp.transpose(local_cols, (1, 0, 2))
    mine = lax.all_to_all(per_head, GROUP, 0, 0, tiled=True)
    mine = mine.reshape(-1, mine.shape[-1])
    return lax.all_gather(mine, "sh", axis=0, tiled=True)


def heads_to_columns(partial, direct=False):
    low = partial.astype(jnp.bfloat16)
    if direct:
        groups = lax.axis_size("sh")
        pieces = low.reshape((groups, low.shape[0] // groups) + low.shape[1:])
        moved = lax.all_to_all(pieces, "sh", 0, 0, tiled=True)
        summed = jnp.sum(moved.astype(jnp.float32), 0).astype(jnp.bfloat16)
    else:
        summed = lax.psum_scatter(low, "sh", scatter_dimension=0, tiled=True)
    summed = summed.reshape(HEADS, -1, summed.shape[-1])
    back = lax.all_to_all(summed, GROUP, 0, 0, tiled=True)
    return jnp.transpose(back, (1, 0, 2)).astype(jnp.float32)


def group_gather(rows, direct=False):
    if direct:
        copies = jnp.broadcast_to(rows[None], (HEADS,) + rows.shape)
        moved = lax.all_to_all(copies, GROUP, 0, 0, tiled=True)
        return moved.reshape((-1,) + rows.shape[1:])
    return lax.all_gather(rows, GROUP, axis=0, tiled=True)


def group_scatter(partial, direct=False):
    low = partial.astype(jnp.bfloat16)
    if direct:
        pieces = low.reshape((HEADS, low.shape[0] // HEADS) + low.shape[1:])
        moved = lax.all_to_all(pieces, GROUP, 0, 0, tiled=True)
        return jnp.sum(moved.astype(jnp.float32), 0)
    return lax.psum_scatter(low, GROUP, scatter_dimension=0, tiled=True).astype(jnp.float32)


def masked_power_inverse(system):
    size = system.shape[-1]
    places = jnp.arange(size)
    base = 8
    inside = (places[:, None] // base == places[None, :] // base) & (
        places[:, None] > places[None, :]
    )
    step = -(system * inside.astype(system.dtype))
    eye = jnp.eye(size, dtype=system.dtype)
    result = eye + step
    for _ in range(2):
        step = hi("bij,bjk->bik", step, step)
        result = result + hi("bij,bjk->bik", result, step)
    width = base
    while width < size:
        across = (places[:, None] // (2 * width) == places[None, :] // (2 * width)) & (
            places[:, None] // width != places[None, :] // width
        )
        lower_left = system * across.astype(system.dtype)
        result = result - hi("bij,bjk->bik", result, hi("bij,bjk->bik", lower_left, result))
        width = 2 * width
    return result


@jax.custom_vjp
def unit_lower_inverse(system):
    return masked_power_inverse(system)


def inverse_keep(system):
    inverse = masked_power_inverse(system)
    return inverse, inverse


def inverse_back(inverse, grad):
    turned = jnp.swapaxes(inverse, -1, -2)
    return (-hi("bij,bjk->bik", turned, hi("bij,bjk->bik", grad, turned)),)


unit_lower_inverse.defvjp(inverse_keep, inverse_back)


def block_mixer(query_rows, key_rows, value_rows, beta_rows, log_decay, starts_flag):
    pseudo = key_rows.shape[0]
    span = STEPS * BLOCK
    blocks = pseudo // span
    queries = query_rows.reshape(blocks, BLOCK, DK)
    keys = key_rows.reshape(blocks, span, DK)
    values = value_rows.reshape(blocks, span, DK)
    betas = beta_rows.reshape(blocks, span)
    decays = log_decay.reshape(blocks, span)
    flags = starts_flag.reshape(blocks, span)
    places = jnp.arange(span)
    lower = places[:, None] >= places[None, :]
    strict = (places[:, None] > places[None, :]).astype(jnp.float32)
    identity = jnp.eye(span, dtype=jnp.float32)
    eye_key = jnp.eye(DK, dtype=jnp.float32)

    summed = jnp.cumsum(decays, axis=1)
    segment = jnp.cumsum(flags, axis=1)
    same_doc = (segment[:, :, None] == segment[:, None, :]) & lower
    decay_ratio = jnp.exp(
        jnp.where(same_doc, summed[:, :, None] - summed[:, None, :], 0.0)
    ) * same_doc.astype(jnp.float32)
    from_start = jnp.exp(summed) * (segment == 0.0).astype(jnp.float32)
    key_key = hi("bik,bjk->bij", keys, keys)
    system = identity + betas[:, :, None] * decay_ratio * key_key * strict
    right_side = jnp.concatenate(
        [betas[:, :, None] * values, (betas * from_start)[:, :, None] * keys], 2
    )
    solved = hi("bij,bjk->bik", unit_lower_inverse(system), right_side)
    fresh = solved[:, :, :DK]
    carried = solved[:, :, DK:]
    last_keys = keys * decay_ratio[:, -1, :, None]
    transfer = from_start[:, -1, None, None] * eye_key - hi("bsi,bsj->bij", last_keys, carried)
    offset = hi("bsi,bsj->bij", last_keys, fresh)
    query_key = hi("bqk,bsk->bqs", queries, keys) * decay_ratio[:, STEPS - 1 :: STEPS]
    frame = from_start[:, STEPS - 1 :: STEPS, None] * queries - hi(
        "bqs,bsj->bqj", query_key, carried
    )
    direct = hi("bqs,bsj->bqj", query_key, fresh)

    state = jnp.concatenate([eye_key, jnp.zeros((DK, DK), jnp.float32)], 1)
    states = []
    for index in range(blocks):
        states.append(state)
        state = hi("ij,jk->ik", transfer[index], state) + jnp.concatenate(
            [jnp.zeros((DK, DK), jnp.float32), offset[index]], 1
        )
    states = jnp.stack(states)
    mats = states[:, :, :DK]
    adds = states[:, :, DK:]
    final_mat = state[:, :DK]
    final_add = state[:, DK:]
    query_frame = hi("bqi,bij->bqj", frame, mats)
    partial = hi("bqi,bij->bqj", frame, adds) + direct
    return (
        query_frame.reshape(blocks * BLOCK, DK),
        partial.reshape(blocks * BLOCK, DK),
        final_mat[None],
        final_add[None],
    )


def local(
    tokens_in,
    mixer_norm,
    mix_weight,
    head_gates,
    conv_taps,
    decay_log,
    decay_bias,
    gate_weight,
    out_norm,
    out_weight,
    feed_norm,
    up_weight,
    down_weight,
    doc_lengths,
    out_grad,
):
    row_count = tokens_in.shape[0]
    weight_rows = mix_weight.shape[0]
    head = lax.axis_index("sl") * lax.axis_size("hd") + lax.axis_index("hd")
    length = row_count * HEADS

    head_cols = jnp.concatenate(
        [
            gate_weight.reshape(weight_rows, HEADS, DK),
            mix_weight.reshape(weight_rows, HEADS, PROJ),
            head_gates.reshape(weight_rows, HEADS, STEPS + 1),
            jnp.broadcast_to(mixer_norm[:, None, None], (weight_rows, HEADS, 1)),
        ],
        2,
    )
    half = FF // HEADS
    up_cols = jnp.concatenate(
        [
            up_weight[:, :FF].reshape(weight_rows, HEADS, half),
            up_weight[:, FF:].reshape(weight_rows, HEADS, half),
            jnp.broadcast_to(feed_norm[:, None, None], (weight_rows, HEADS, 1)),
        ],
        2,
    )
    head_wide, up_wide = columns_to_heads_pair(head_cols, up_cols)
    head_full = head_wide[:, :WIDE]
    gain_one = head_wide[:, WIDE].astype(jnp.float32)
    up_full = up_wide[:, : 2 * half]
    gain_two = up_wide[:, 2 * half].astype(jnp.float32)
    tap_width = conv_taps.shape[1]
    tap_row = jnp.pad(conv_taps.reshape(1, -1), ((0, 0), (0, D - CONV * tap_width)))
    out_full, down_full, tap_rows = rows_to_heads((out_weight, down_weight, tap_row))
    conv_part = jnp.transpose(
        tap_rows[:, : CONV * tap_width].reshape(-1, CONV, tap_width), (1, 0, 2)
    ).reshape(CONV, -1).astype(jnp.float32)

    x_float = tokens_in.astype(jnp.float32)
    normed_float, norm_one_back = jax.vjp(rms_norm, x_float, gain_one)
    normed_one = group_gather(normed_float.astype(jnp.bfloat16), True)
    tokens_all = group_gather(tokens_in, True)
    head_out = bf_product(normed_one, head_full)
    out_gate = head_out[:, :DK]
    proj_head = head_out[:, DK : DK + PROJ].astype(jnp.bfloat16)
    scalar_rows = head_out[:, DK + PROJ :].astype(jnp.bfloat16).astype(jnp.float32)

    rim_rows = from_behind(proj_head[length - (CONV - 1) :], "sh", 1)
    padded = jnp.concatenate([rim_rows, proj_head], 0).astype(jnp.float32)
    starts = jnp.cumsum(doc_lengths) - doc_lengths
    positions = lax.axis_index("sh") * length + jnp.arange(length, dtype=jnp.int32)
    starts_flag = jnp.any(positions[:, None] == starts[None, :], 1).astype(jnp.float32)
    doc_begin = jnp.max(jnp.where(starts[None, :] <= positions[:, None], starts[None, :], 0), 1)
    tap_masks = [
        (positions - (CONV - 1) + tap_index >= doc_begin).astype(jnp.float32)
        for tap_index in range(CONV)
    ]
    pseudo_flag = jnp.concatenate(
        [starts_flag[:, None], jnp.zeros((length, STEPS - 1), jnp.float32)], 1
    ).reshape(-1)
    rate_log = lax.dynamic_index_in_dim(decay_log, head, 0, False)
    bias_part = lax.dynamic_index_in_dim(decay_bias, head, 0, False)

    def mixer_inputs(padded, scalar_rows, conv_part, rate_log, bias_part):
        convolved = jnp.zeros_like(padded[CONV - 1 :])
        for tap_index in range(CONV):
            convolved = (
                convolved
                + conv_part[tap_index]
                * padded[tap_index : tap_index + length]
                * tap_masks[tap_index][:, None]
            )
        activated = jax.nn.silu(convolved).reshape(length, 1 + 2 * STEPS, DK)
        query_rows = unit_norm(activated[:, 0])
        key_rows = unit_norm(activated[:, 1 : 1 + STEPS]).reshape(STEPS * length, DK)
        value_rows = activated[:, 1 + STEPS :].reshape(STEPS * length, DK)
        beta_rows = jax.nn.sigmoid(scalar_rows[:, :STEPS]).reshape(STEPS * length)
        log_rate = -jnp.exp(rate_log) * jax.nn.softplus(scalar_rows[:, STEPS] + bias_part)
        log_decay = jnp.concatenate(
            [log_rate[:, None], jnp.zeros((length, STEPS - 1), jnp.float32)], 1
        ).reshape(STEPS * length)
        return (query_rows, key_rows, value_rows, beta_rows, log_decay)

    def recurrence(query_rows, key_rows, value_rows, beta_rows, log_decay):
        return block_mixer(query_rows, key_rows, value_rows, beta_rows, log_decay, pseudo_flag)

    prepared, inputs_back = jax.vjp(
        mixer_inputs, padded, scalar_rows, conv_part, rate_log, bias_part
    )
    (query_frame, partial_value_rows, transfer, offset), recurrence_back = jax.vjp(
        recurrence, *prepared
    )
    grad_rows = group_gather(out_grad)
    grad_rows, query_frame, partial_value_rows, transfer, offset = lax.optimization_barrier(
        (grad_rows, query_frame, partial_value_rows, transfer, offset)
    )
    identity = jnp.eye(DK, dtype=jnp.float32)[None]
    zeros_state = jnp.zeros((1, DK, DK), jnp.float32)
    prefix_map, incoming_state = carried_in(
        (transfer, offset), "sh", compose, (identity, zeros_state), False
    )
    mixer_result = partial_value_rows + hi("zy,yi->zi", query_frame, incoming_state[0])
    mixer_low = mixer_result.astype(jnp.bfloat16).astype(jnp.float32)
    gated, gate_back = jax.vjp(gate_norm, mixer_low, out_gate, out_norm)
    gated_rows = gated.astype(jnp.bfloat16)
    branch_all = lax.psum(bf_product(gated_rows, out_full).astype(jnp.bfloat16), GROUP)
    middle_all = tokens_all.astype(jnp.float32) + branch_all.astype(jnp.float32)
    middle = lax.dynamic_slice_in_dim(middle_all, head * row_count, row_count, 0)
    normed_two = rms_norm(middle_all, gain_two).astype(jnp.bfloat16)
    normed_mid, norm_two_back = jax.vjp(rms_norm, middle, gain_two)
    gate_up = bf_product(normed_two, up_full)
    hidden_float, swiglu_back = jax.vjp(swiglu, gate_up)
    hidden = hidden_float.astype(jnp.bfloat16)
    feed_partial = bf_product(hidden, down_full)

    grad_out = out_grad.astype(jnp.float32)
    grad_hidden = bf_product(grad_rows, down_full.T)
    grad_down_partial = bf_product(hidden.T, grad_rows)
    (grad_gate_up,) = swiglu_back(grad_hidden)
    grad_gate_up = grad_gate_up.astype(jnp.bfloat16)
    grad_normed_two = group_scatter(bf_product(grad_gate_up, up_full.T))
    grad_mid_norm, grad_gain_two = norm_two_back(grad_normed_two)
    grad_up_payload = jnp.concatenate(
        [bf_product(normed_two.T, grad_gate_up), grad_gain_two[:, None]], 1
    )
    grad_middle = grad_out + grad_mid_norm
    feed_partial, grad_up_payload, grad_down_partial, grad_branch_low = lax.optimization_barrier(
        (feed_partial, grad_up_payload, grad_down_partial, grad_middle.astype(jnp.bfloat16))
    )
    grad_up_cols = heads_to_columns(grad_up_payload, True)
    grad_up = jnp.concatenate(
        [
            grad_up_cols[:, :, :half].reshape(weight_rows, FF),
            grad_up_cols[:, :, half : 2 * half].reshape(weight_rows, FF),
        ],
        1,
    )
    grad_branch = group_gather(grad_branch_low)
    feed_partial, grad_down_partial, grad_branch = lax.optimization_barrier(
        (feed_partial, grad_down_partial, grad_branch)
    )
    feed_sum = group_scatter(feed_partial)
    grad_gated = bf_product(grad_branch, out_full.T)
    grad_down, grad_outw = heads_to_rows((grad_down_partial, bf_product(gated_rows.T, grad_branch)))
    grad_mixer, grad_gate, grad_out_norm = gate_back(grad_gated)
    grad_gate = grad_gate.astype(jnp.bfloat16)
    head_gradients = grad_mixer.astype(jnp.bfloat16).astype(jnp.float32)
    local_adjoint = hi("dc,dr->cr", query_frame, head_gradients)[None]
    transfer_turned = jnp.transpose(transfer, (0, 2, 1))
    later_map, state_gradient = carried_in(
        (transfer_turned, local_adjoint), "sh", compose, (identity, zeros_state), True
    )
    basis_gradient = hi("nu,wu->nw", head_gradients, incoming_state[0])
    transfer_gradient = hi("tnf,tmf->tnm", state_gradient, incoming_state)
    grad_prepared = recurrence_back(
        (basis_gradient, head_gradients, transfer_gradient, state_gradient)
    )
    grad_prepared, feed_sum, grad_up_cols, grad_down, grad_outw = lax.optimization_barrier(
        (grad_prepared, feed_sum, grad_up_cols, grad_down, grad_outw)
    )
    layer_out = (middle + feed_sum).astype(jnp.bfloat16)
    grad_padded, grad_scalars, grad_conv, grad_rate, grad_bias = inputs_back(grad_prepared)
    rim_grad = from_behind(grad_padded[: CONV - 1], "sh", -1)
    own_grad = grad_padded[CONV - 1 :]
    grad_proj = jnp.concatenate(
        [own_grad[: length - (CONV - 1)], own_grad[length - (CONV - 1) :] + rim_grad], 0
    )
    grad_head = jnp.concatenate(
        [grad_gate, grad_proj.astype(jnp.bfloat16), grad_scalars.astype(jnp.bfloat16)], 1
    )
    grad_normed_one = group_scatter(bf_product(grad_head, head_full.T), True)
    grad_x_norm, grad_gain_one = norm_one_back(grad_normed_one)
    grad_head_cols = heads_to_columns(
        jnp.concatenate([bf_product(normed_one.T, grad_head), grad_gain_one[:, None]], 1)
    )
    grad_gatew = grad_head_cols[:, :, :DK].reshape(weight_rows, D)
    grad_mixw = grad_head_cols[:, :, DK : DK + PROJ].reshape(weight_rows, HEADS * PROJ)
    grad_gatesw = grad_head_cols[:, :, DK + PROJ : WIDE].reshape(
        weight_rows, HEADS * (STEPS + 1)
    )
    grad_tokens = (grad_middle + grad_x_norm).astype(jnp.bfloat16)
    (conv_grad,) = heads_to_rows((jnp.transpose(grad_conv),))
    conv_grad = jnp.transpose(conv_grad)
    one_hot = (jnp.arange(HEADS) == head).astype(jnp.float32)
    small_sums = all_sum(
        jnp.concatenate([one_hot * grad_rate, one_hot * grad_bias, grad_out_norm])
    )
    return (
        layer_out,
        grad_tokens,
        jnp.sum(grad_head_cols[:, :, WIDE], 1),
        grad_mixw,
        grad_gatesw,
        conv_grad,
        small_sums[:HEADS],
        small_sums[HEADS : 2 * HEADS],
        grad_gatew,
        small_sums[2 * HEADS :],
        grad_outw,
        jnp.sum(grad_up_cols[:, :, 2 * half], 1),
        grad_up,
        grad_down,
    )


def solution(mesh):
    seq = mesh.shape["seq"]
    across = mesh.shape["head"]
    inner = HEADS // across
    grid = Mesh(
        np.asarray(mesh.devices).reshape(seq // inner, inner, across), ("sh", "sl", "hd")
    )
    rows = P(ALL, None)
    flat = P(ALL)
    return jax.shard_map(
        local,
        mesh=grid,
        in_specs=(
            rows,
            flat,
            rows,
            rows,
            P(None, ALL),
            P(),
            P(),
            rows,
            P(),
            rows,
            flat,
            rows,
            rows,
            P(),
            rows,
        ),
        out_specs=(
            rows,
            rows,
            flat,
            rows,
            rows,
            P(None, ALL),
            P(),
            P(),
            rows,
            P(),
            rows,
            flat,
            rows,
            rows,
        ),
        check_vma=False,
    )
```

```python
import jax
import jax.numpy as jnp
import numpy as np
from jax import lax
from jax.experimental import pallas as pl
from jax.experimental.pallas import tpu as pltpu
from jax.sharding import Mesh
from jax.sharding import PartitionSpec as P

D = 1024
HEADS = 8
DK = 128
FF = 2816
STEPS = 2
CONV = 4
BLOCK = 64
PROJ = (1 + 2 * STEPS) * DK
WIDE = DK + PROJ + STEPS + 1

EPS = 1e-06
HIGH_ACCURACY = lax.Precision.HIGH

GROUP = ("sl", "hd")
ALL = ("sh", "sl", "hd")


def from_behind(shard, axis, by):
    peers = lax.axis_size(axis)
    pairs = [(i, i + by) for i in range(peers) if 0 <= i + by < peers]
    return lax.ppermute(shard, axis, pairs)


def carried_in(shard, axis, join, neutral, backward):
    count = lax.axis_size(axis)
    place = lax.axis_index(axis)
    ahead = count - 1 - place if backward else place
    both = lax.all_gather(jnp.stack(shard).astype(jnp.bfloat16), axis)
    gathered = (both[:, 0], both[:, 1])
    state = jax.tree.map(lambda a, e: jnp.zeros_like(a) + jnp.asarray(e, a.dtype), shard, neutral)

    def one(turn, state):
        source = count - 1 - turn if backward else turn
        return join(
            state,
            jax.tree.map(
                lambda a, own: lax.dynamic_index_in_dim(a, source, 0, False).astype(own.dtype),
                gathered,
                shard,
            ),
        )

    return lax.fori_loop(0, ahead, one, state)


def flat_place():
    return (
        lax.axis_index("sh") * lax.axis_size("sl") + lax.axis_index("sl")
    ) * lax.axis_size("hd") + lax.axis_index("hd")


def device_of(index):
    inner = lax.axis_size("sl") * lax.axis_size("hd")
    return (index // inner, (index // lax.axis_size("hd")) % lax.axis_size("sl"), index % lax.axis_size("hd"))


def sum_kernel(count, own_ref, out_ref, slots, send_sems, recv_sems):
    me = flat_place()
    barrier = pltpu.get_barrier_semaphore()

    def greet(index, carry):
        @pl.when(index != me)
        def _():
            pl.semaphore_signal(
                barrier, inc=1, device_id=device_of(index), device_id_type=pl.DeviceIdType.MESH
            )

        return carry

    lax.fori_loop(0, count, greet, 0)
    pl.semaphore_wait(barrier, count - 1)

    def copy_to(index):
        return pltpu.make_async_remote_copy(
            src_ref=own_ref,
            dst_ref=slots.at[me],
            send_sem=send_sems.at[index],
            recv_sem=recv_sems.at[me],
            device_id=device_of(index),
            device_id_type=pl.DeviceIdType.MESH,
        )

    def copy_from(index):
        return pltpu.make_async_remote_copy(
            src_ref=own_ref,
            dst_ref=slots.at[index],
            send_sem=send_sems.at[index],
            recv_sem=recv_sems.at[index],
            device_id=device_of(index),
            device_id_type=pl.DeviceIdType.MESH,
        )

    def send(index, carry):
        @pl.when(index != me)
        def _():
            copy_to(index).start()

        return carry

    lax.fori_loop(0, count, send, 0)
    slots[me] = own_ref[...]

    def finish(index, carry):
        @pl.when(index != me)
        def _():
            copy_to(index).wait_send()
            copy_from(index).wait_recv()

        return carry

    lax.fori_loop(0, count, finish, 0)
    out_ref[...] = jnp.sum(slots[...], axis=0)


def all_sum(vector):
    count = lax.axis_size("sh") * lax.axis_size("sl") * lax.axis_size("hd")
    size = vector.shape[0]
    lanes = 128
    tile = 8 * lanes
    padded = -(-size // tile) * tile
    block = jnp.pad(vector, (0, padded - size)).reshape(padded // lanes, lanes)
    total = pl.pallas_call(
        lambda *refs: sum_kernel(count, *refs),
        out_shape=jax.ShapeDtypeStruct(block.shape, jnp.float32),
        in_specs=[pl.BlockSpec(memory_space=pltpu.VMEM)],
        out_specs=pl.BlockSpec(memory_space=pltpu.VMEM),
        scratch_shapes=[
            pltpu.VMEM((count,) + block.shape, jnp.float32),
            pltpu.SemaphoreType.DMA((count,)),
            pltpu.SemaphoreType.DMA((count,)),
        ],
        compiler_params=pltpu.CompilerParams(collective_id=0, has_side_effects=True),
    )(block)
    return total.reshape(-1)[:size]


def rms_norm(values, scale_gain):
    return values * lax.rsqrt(jnp.mean(values * values, axis=-1, keepdims=True) + EPS) * scale_gain


def unit_norm(values):
    return values * lax.rsqrt(jnp.sum(values * values, axis=-1, keepdims=True) + EPS)


def bf_product(first_mat, second_mat):
    return jnp.dot(first_mat, second_mat, preferred_element_type=jnp.float32)


def hi(spec, *arrays):
    return jnp.einsum(spec, *arrays, precision=HIGH_ACCURACY)


def compose(early_pair, late_pair):
    early_mat, early_add = early_pair
    late_mat, late_add = late_pair
    joined = hi("hij,hjk->hik", late_mat, early_mat)
    shifted = hi("hij,hjk->hik", late_mat, early_add) + late_add
    return (joined, shifted)


def gate_norm(values, out_gate, scale_gain):
    return rms_norm(values, scale_gain) * jax.nn.silu(out_gate)


def swiglu(gate_up):
    half = gate_up.shape[1] // 2
    return jax.nn.silu(gate_up[:, :half]) * gate_up[:, half:]


def owner_pairs(inverse):
    groups = lax.axis_size("sh")
    pairs = [(g * HEADS + t, t * groups + g) for g in range(groups) for t in range(HEADS)]
    return [(b, a) for a, b in pairs] if inverse else pairs


def rows_to_heads(blocks):
    groups = lax.axis_size("sh")
    width = blocks[0].shape[1]
    used = sum(b.shape[0] for b in blocks)
    least = (1 << 20) // (groups * width * 2) + 1
    rows = -(-max(used, least) // 8) * 8
    packed = jnp.concatenate(
        list(blocks) + [jnp.zeros((rows - used, width), blocks[0].dtype)], 0
    )
    moved = lax.ppermute(packed, ALL, owner_pairs(True))
    full = lax.all_gather(moved, "sh", axis=0, tiled=False)
    parts = []
    first = 0
    for block in blocks:
        size = block.shape[0]
        parts.append(full[:, first : first + size].reshape(groups * size, width))
        first += size
    return parts


def heads_to_rows(partials):
    groups = lax.axis_size("sh")
    pieces = [
        p.astype(jnp.bfloat16).reshape((groups, p.shape[0] // groups) + p.shape[1:])
        for p in partials
    ]
    joined = jnp.concatenate(pieces, 1)
    joined = joined.reshape((-1,) + joined.shape[2:])
    summed = lax.psum_scatter(joined, "sh", scatter_dimension=0, tiled=True)
    moved = lax.ppermute(summed, ALL, owner_pairs(False)).astype(jnp.float32)
    parts = []
    first = 0
    for piece in pieces:
        size = piece.shape[1]
        parts.append(moved[first : first + size])
        first += size
    return parts


def columns_to_heads(local_cols):
    per_head = jnp.transpose(local_cols, (1, 0, 2))
    mine = lax.all_to_all(per_head, GROUP, 0, 0, tiled=True)
    mine = mine.reshape(-1, mine.shape[-1])
    return lax.all_gather(mine, "sh", axis=0, tiled=True)


def heads_to_columns(partial, direct=False):
    low = partial.astype(jnp.bfloat16)
    if direct:
        groups = lax.axis_size("sh")
        pieces = low.reshape((groups, low.shape[0] // groups) + low.shape[1:])
        moved = lax.all_to_all(pieces, "sh", 0, 0, tiled=True)
        summed = jnp.sum(moved.astype(jnp.float32), 0).astype(jnp.bfloat16)
    else:
        summed = lax.psum_scatter(low, "sh", scatter_dimension=0, tiled=True)
    summed = summed.reshape(HEADS, -1, summed.shape[-1])
    back = lax.all_to_all(summed, GROUP, 0, 0, tiled=True)
    return jnp.transpose(back, (1, 0, 2)).astype(jnp.float32)


def group_gather(rows, direct=False):
    if direct:
        copies = jnp.broadcast_to(rows[None], (HEADS,) + rows.shape)
        moved = lax.all_to_all(copies, GROUP, 0, 0, tiled=True)
        return moved.reshape((-1,) + rows.shape[1:])
    return lax.all_gather(rows, GROUP, axis=0, tiled=True)


def group_scatter(partial, direct=False):
    low = partial.astype(jnp.bfloat16)
    if direct:
        pieces = low.reshape((HEADS, low.shape[0] // HEADS) + low.shape[1:])
        moved = lax.all_to_all(pieces, GROUP, 0, 0, tiled=True)
        return jnp.sum(moved.astype(jnp.float32), 0)
    return lax.psum_scatter(low, GROUP, scatter_dimension=0, tiled=True).astype(jnp.float32)


def masked_power_inverse(system):
    size = system.shape[-1]
    places = jnp.arange(size)
    base = 8
    inside = (places[:, None] // base == places[None, :] // base) & (
        places[:, None] > places[None, :]
    )
    step = -(system * inside.astype(system.dtype))
    eye = jnp.eye(size, dtype=system.dtype)
    result = eye + step
    for _ in range(2):
        step = hi("bij,bjk->bik", step, step)
        result = result + hi("bij,bjk->bik", result, step)
    width = base
    while width < size:
        across = (places[:, None] // (2 * width) == places[None, :] // (2 * width)) & (
            places[:, None] // width != places[None, :] // width
        )
        lower_left = system * across.astype(system.dtype)
        result = result - hi("bij,bjk->bik", result, hi("bij,bjk->bik", lower_left, result))
        width = 2 * width
    return result


@jax.custom_vjp
def unit_lower_inverse(system):
    return masked_power_inverse(system)


def inverse_keep(system):
    inverse = masked_power_inverse(system)
    return inverse, inverse


def inverse_back(inverse, grad):
    turned = jnp.swapaxes(inverse, -1, -2)
    return (-hi("bij,bjk->bik", turned, hi("bij,bjk->bik", grad, turned)),)


unit_lower_inverse.defvjp(inverse_keep, inverse_back)


def block_mixer(query_rows, key_rows, value_rows, beta_rows, log_decay, starts_flag):
    pseudo = key_rows.shape[0]
    span = STEPS * BLOCK
    blocks = pseudo // span
    queries = query_rows.reshape(blocks, BLOCK, DK)
    keys = key_rows.reshape(blocks, span, DK)
    values = value_rows.reshape(blocks, span, DK)
    betas = beta_rows.reshape(blocks, span)
    decays = log_decay.reshape(blocks, span)
    flags = starts_flag.reshape(blocks, span)
    places = jnp.arange(span)
    lower = places[:, None] >= places[None, :]
    strict = (places[:, None] > places[None, :]).astype(jnp.float32)
    identity = jnp.eye(span, dtype=jnp.float32)
    eye_key = jnp.eye(DK, dtype=jnp.float32)

    summed = jnp.cumsum(decays, axis=1)
    segment = jnp.cumsum(flags, axis=1)
    same_doc = (segment[:, :, None] == segment[:, None, :]) & lower
    decay_ratio = jnp.exp(
        jnp.where(same_doc, summed[:, :, None] - summed[:, None, :], 0.0)
    ) * same_doc.astype(jnp.float32)
    from_start = jnp.exp(summed) * (segment == 0.0).astype(jnp.float32)
    key_key = hi("bik,bjk->bij", keys, keys)
    system = identity + betas[:, :, None] * decay_ratio * key_key * strict
    right_side = jnp.concatenate(
        [betas[:, :, None] * values, (betas * from_start)[:, :, None] * keys], 2
    )
    solved = hi("bij,bjk->bik", unit_lower_inverse(system), right_side)
    fresh = solved[:, :, :DK]
    carried = solved[:, :, DK:]
    last_keys = keys * decay_ratio[:, -1, :, None]
    transfer = from_start[:, -1, None, None] * eye_key - hi("bsi,bsj->bij", last_keys, carried)
    offset = hi("bsi,bsj->bij", last_keys, fresh)
    query_key = hi("bqk,bsk->bqs", queries, keys) * decay_ratio[:, STEPS - 1 :: STEPS]
    frame = from_start[:, STEPS - 1 :: STEPS, None] * queries - hi(
        "bqs,bsj->bqj", query_key, carried
    )
    direct = hi("bqs,bsj->bqj", query_key, fresh)

    state = jnp.concatenate([eye_key, jnp.zeros((DK, DK), jnp.float32)], 1)
    states = []
    for index in range(blocks):
        states.append(state)
        state = hi("ij,jk->ik", transfer[index], state) + jnp.concatenate(
            [jnp.zeros((DK, DK), jnp.float32), offset[index]], 1
        )
    states = jnp.stack(states)
    mats = states[:, :, :DK]
    adds = states[:, :, DK:]
    final_mat = state[:, :DK]
    final_add = state[:, DK:]
    query_frame = hi("bqi,bij->bqj", frame, mats)
    partial = hi("bqi,bij->bqj", frame, adds) + direct
    return (
        query_frame.reshape(blocks * BLOCK, DK),
        partial.reshape(blocks * BLOCK, DK),
        final_mat[None],
        final_add[None],
    )


def local(
    tokens_in,
    mixer_norm,
    mix_weight,
    head_gates,
    conv_taps,
    decay_log,
    decay_bias,
    gate_weight,
    out_norm,
    out_weight,
    feed_norm,
    up_weight,
    down_weight,
    doc_lengths,
    out_grad,
):
    row_count = tokens_in.shape[0]
    weight_rows = mix_weight.shape[0]
    head = lax.axis_index("sl") * lax.axis_size("hd") + lax.axis_index("hd")
    length = row_count * HEADS

    head_cols = jnp.concatenate(
        [
            gate_weight.reshape(weight_rows, HEADS, DK),
            mix_weight.reshape(weight_rows, HEADS, PROJ),
            head_gates.reshape(weight_rows, HEADS, STEPS + 1),
            jnp.broadcast_to(mixer_norm[:, None, None], (weight_rows, HEADS, 1)),
        ],
        2,
    )
    head_wide = columns_to_heads(head_cols)
    head_full = head_wide[:, :WIDE]
    gain_one = head_wide[:, WIDE].astype(jnp.float32)
    half = FF // HEADS
    up_cols = jnp.concatenate(
        [
            up_weight[:, :FF].reshape(weight_rows, HEADS, half),
            up_weight[:, FF:].reshape(weight_rows, HEADS, half),
            jnp.broadcast_to(feed_norm[:, None, None], (weight_rows, HEADS, 1)),
        ],
        2,
    )
    up_wide = columns_to_heads(up_cols)
    up_full = up_wide[:, : 2 * half]
    gain_two = up_wide[:, 2 * half].astype(jnp.float32)
    tap_width = conv_taps.shape[1]
    tap_row = jnp.pad(conv_taps.reshape(1, -1), ((0, 0), (0, D - CONV * tap_width)))
    out_full, down_full, tap_rows = rows_to_heads((out_weight, down_weight, tap_row))
    conv_part = jnp.transpose(
        tap_rows[:, : CONV * tap_width].reshape(-1, CONV, tap_width), (1, 0, 2)
    ).reshape(CONV, -1).astype(jnp.float32)

    x_float = tokens_in.astype(jnp.float32)
    normed_float, norm_one_back = jax.vjp(rms_norm, x_float, gain_one)
    normed_one = group_gather(normed_float.astype(jnp.bfloat16), True)
    tokens_all = group_gather(tokens_in, True)
    head_out = bf_product(normed_one, head_full)
    out_gate = head_out[:, :DK]
    proj_head = head_out[:, DK : DK + PROJ].astype(jnp.bfloat16)
    scalar_rows = head_out[:, DK + PROJ :].astype(jnp.bfloat16).astype(jnp.float32)

    rim_rows = from_behind(proj_head[length - (CONV - 1) :], "sh", 1)
    padded = jnp.concatenate([rim_rows, proj_head], 0).astype(jnp.float32)
    starts = jnp.cumsum(doc_lengths) - doc_lengths
    positions = lax.axis_index("sh") * length + jnp.arange(length, dtype=jnp.int32)
    starts_flag = jnp.any(positions[:, None] == starts[None, :], 1).astype(jnp.float32)
    doc_begin = jnp.max(jnp.where(starts[None, :] <= positions[:, None], starts[None, :], 0), 1)
    tap_masks = [
        (positions - (CONV - 1) + tap_index >= doc_begin).astype(jnp.float32)
        for tap_index in range(CONV)
    ]
    pseudo_flag = jnp.concatenate(
        [starts_flag[:, None], jnp.zeros((length, STEPS - 1), jnp.float32)], 1
    ).reshape(-1)
    rate_log = lax.dynamic_index_in_dim(decay_log, head, 0, False)
    bias_part = lax.dynamic_index_in_dim(decay_bias, head, 0, False)

    def mixer_inputs(padded, scalar_rows, conv_part, rate_log, bias_part):
        convolved = jnp.zeros_like(padded[CONV - 1 :])
        for tap_index in range(CONV):
            convolved = (
                convolved
                + conv_part[tap_index]
                * padded[tap_index : tap_index + length]
                * tap_masks[tap_index][:, None]
            )
        activated = jax.nn.silu(convolved).reshape(length, 1 + 2 * STEPS, DK)
        query_rows = unit_norm(activated[:, 0])
        key_rows = unit_norm(activated[:, 1 : 1 + STEPS]).reshape(STEPS * length, DK)
        value_rows = activated[:, 1 + STEPS :].reshape(STEPS * length, DK)
        beta_rows = jax.nn.sigmoid(scalar_rows[:, :STEPS]).reshape(STEPS * length)
        log_rate = -jnp.exp(rate_log) * jax.nn.softplus(scalar_rows[:, STEPS] + bias_part)
        log_decay = jnp.concatenate(
            [log_rate[:, None], jnp.zeros((length, STEPS - 1), jnp.float32)], 1
        ).reshape(STEPS * length)
        return (query_rows, key_rows, value_rows, beta_rows, log_decay)

    def recurrence(query_rows, key_rows, value_rows, beta_rows, log_decay):
        return block_mixer(query_rows, key_rows, value_rows, beta_rows, log_decay, pseudo_flag)

    prepared, inputs_back = jax.vjp(
        mixer_inputs, padded, scalar_rows, conv_part, rate_log, bias_part
    )
    (query_frame, partial_value_rows, transfer, offset), recurrence_back = jax.vjp(
        recurrence, *prepared
    )
    grad_rows = group_gather(out_grad)
    grad_rows, query_frame, partial_value_rows, transfer, offset = lax.optimization_barrier(
        (grad_rows, query_frame, partial_value_rows, transfer, offset)
    )
    identity = jnp.eye(DK, dtype=jnp.float32)[None]
    zeros_state = jnp.zeros((1, DK, DK), jnp.float32)
    prefix_map, incoming_state = carried_in(
        (transfer, offset), "sh", compose, (identity, zeros_state), False
    )
    mixer_result = partial_value_rows + hi("zy,yi->zi", query_frame, incoming_state[0])
    mixer_low = mixer_result.astype(jnp.bfloat16).astype(jnp.float32)
    gated, gate_back = jax.vjp(gate_norm, mixer_low, out_gate, out_norm)
    gated_rows = gated.astype(jnp.bfloat16)
    branch_all = lax.psum(bf_product(gated_rows, out_full).astype(jnp.bfloat16), GROUP)
    middle_all = tokens_all.astype(jnp.float32) + branch_all.astype(jnp.float32)
    middle = lax.dynamic_slice_in_dim(middle_all, head * row_count, row_count, 0)
    normed_two = rms_norm(middle_all, gain_two).astype(jnp.bfloat16)
    normed_mid, norm_two_back = jax.vjp(rms_norm, middle, gain_two)
    gate_up = bf_product(normed_two, up_full)
    hidden_float, swiglu_back = jax.vjp(swiglu, gate_up)
    hidden = hidden_float.astype(jnp.bfloat16)
    feed_partial = bf_product(hidden, down_full)

    grad_out = out_grad.astype(jnp.float32)
    grad_hidden = bf_product(grad_rows, down_full.T)
    grad_down_partial = bf_product(hidden.T, grad_rows)
    (grad_gate_up,) = swiglu_back(grad_hidden)
    grad_gate_up = grad_gate_up.astype(jnp.bfloat16)
    grad_normed_two = group_scatter(bf_product(grad_gate_up, up_full.T))
    grad_mid_norm, grad_gain_two = norm_two_back(grad_normed_two)
    grad_up_payload = jnp.concatenate(
        [bf_product(normed_two.T, grad_gate_up), grad_gain_two[:, None]], 1
    )
    grad_middle = grad_out + grad_mid_norm
    feed_partial, grad_up_payload, grad_down_partial, grad_branch_low = lax.optimization_barrier(
        (feed_partial, grad_up_payload, grad_down_partial, grad_middle.astype(jnp.bfloat16))
    )
    grad_up_cols = heads_to_columns(grad_up_payload, True)
    grad_up = jnp.concatenate(
        [
            grad_up_cols[:, :, :half].reshape(weight_rows, FF),
            grad_up_cols[:, :, half : 2 * half].reshape(weight_rows, FF),
        ],
        1,
    )
    grad_branch = group_gather(grad_branch_low)
    feed_partial, grad_down_partial, grad_branch = lax.optimization_barrier(
        (feed_partial, grad_down_partial, grad_branch)
    )
    feed_sum = group_scatter(feed_partial)
    grad_gated = bf_product(grad_branch, out_full.T)
    (grad_down,) = heads_to_rows((grad_down_partial,))
    grad_outw_partial = bf_product(gated_rows.T, grad_branch)
    grad_mixer, grad_gate, grad_out_norm = gate_back(grad_gated)
    grad_gate = grad_gate.astype(jnp.bfloat16)
    head_gradients = grad_mixer.astype(jnp.bfloat16).astype(jnp.float32)
    local_adjoint = hi("dc,dr->cr", query_frame, head_gradients)[None]
    transfer_turned = jnp.transpose(transfer, (0, 2, 1))
    later_map, state_gradient = carried_in(
        (transfer_turned, local_adjoint), "sh", compose, (identity, zeros_state), True
    )
    basis_gradient = hi("nu,wu->nw", head_gradients, incoming_state[0])
    transfer_gradient = hi("tnf,tmf->tnm", state_gradient, incoming_state)
    grad_prepared = recurrence_back(
        (basis_gradient, head_gradients, transfer_gradient, state_gradient)
    )
    grad_prepared, feed_sum, grad_up_cols, grad_down = lax.optimization_barrier(
        (grad_prepared, feed_sum, grad_up_cols, grad_down)
    )
    layer_out = (middle + feed_sum).astype(jnp.bfloat16)
    grad_padded, grad_scalars, grad_conv, grad_rate, grad_bias = inputs_back(grad_prepared)
    rim_grad = from_behind(grad_padded[: CONV - 1], "sh", -1)
    own_grad = grad_padded[CONV - 1 :]
    grad_proj = jnp.concatenate(
        [own_grad[: length - (CONV - 1)], own_grad[length - (CONV - 1) :] + rim_grad], 0
    )
    grad_head = jnp.concatenate(
        [grad_gate, grad_proj.astype(jnp.bfloat16), grad_scalars.astype(jnp.bfloat16)], 1
    )
    grad_normed_one = group_scatter(bf_product(grad_head, head_full.T), True)
    grad_x_norm, grad_gain_one = norm_one_back(grad_normed_one)
    grad_head_cols = heads_to_columns(
        jnp.concatenate([bf_product(normed_one.T, grad_head), grad_gain_one[:, None]], 1)
    )
    grad_gatew = grad_head_cols[:, :, :DK].reshape(weight_rows, D)
    grad_mixw = grad_head_cols[:, :, DK : DK + PROJ].reshape(weight_rows, HEADS * PROJ)
    grad_gatesw = grad_head_cols[:, :, DK + PROJ : WIDE].reshape(
        weight_rows, HEADS * (STEPS + 1)
    )
    grad_tokens = (grad_middle + grad_x_norm).astype(jnp.bfloat16)
    groups = lax.axis_size("sh")
    conv_rows = jnp.transpose(grad_conv.reshape(CONV, groups, tap_width), (1, 0, 2))
    conv_rows = jnp.pad(conv_rows.reshape(groups, CONV * tap_width), ((0, 0), (0, D - CONV * tap_width)))
    grad_outw, conv_row = heads_to_rows((grad_outw_partial, conv_rows))
    conv_grad = conv_row[0, : CONV * tap_width].reshape(CONV, tap_width)
    one_hot = (jnp.arange(HEADS) == head).astype(jnp.float32)
    small_sums = all_sum(
        jnp.concatenate([one_hot * grad_rate, one_hot * grad_bias, grad_out_norm])
    )
    return (
        layer_out,
        grad_tokens,
        jnp.sum(grad_head_cols[:, :, WIDE], 1),
        grad_mixw,
        grad_gatesw,
        conv_grad,
        small_sums[:HEADS],
        small_sums[HEADS : 2 * HEADS],
        grad_gatew,
        small_sums[2 * HEADS :],
        grad_outw,
        jnp.sum(grad_up_cols[:, :, 2 * half], 1),
        grad_up,
        grad_down,
    )


def solution(mesh):
    seq = mesh.shape["seq"]
    across = mesh.shape["head"]
    inner = HEADS // across
    grid = Mesh(
        np.asarray(mesh.devices).reshape(seq // inner, inner, across), ("sh", "sl", "hd")
    )
    rows = P(ALL, None)
    flat = P(ALL)
    return jax.shard_map(
        local,
        mesh=grid,
        in_specs=(
            rows,
            flat,
            rows,
            rows,
            P(None, ALL),
            P(),
            P(),
            rows,
            P(),
            rows,
            flat,
            rows,
            rows,
            P(),
            rows,
        ),
        out_specs=(
            rows,
            rows,
            flat,
            rows,
            rows,
            P(None, ALL),
            P(),
            P(),
            rows,
            P(),
            rows,
            flat,
            rows,
            rows,
        ),
        check_vma=False,
    )
```

```python
import jax
import jax.numpy as jnp
import numpy as np
from jax import lax
from jax.experimental import pallas as pl
from jax.experimental.pallas import tpu as pltpu
from jax.sharding import Mesh
from jax.sharding import PartitionSpec as P

D = 1024
HEADS = 8
DK = 128
FF = 2816
STEPS = 2
CONV = 4
BLOCK = 64
PROJ = (1 + 2 * STEPS) * DK
WIDE = DK + PROJ + STEPS + 1

EPS = 1e-06
HIGH_ACCURACY = lax.Precision.HIGH

GROUP = ("sl", "hd")
ALL = ("sh", "sl", "hd")


def from_behind(shard, axis, by):
    peers = lax.axis_size(axis)
    pairs = [(i, i + by) for i in range(peers) if 0 <= i + by < peers]
    return lax.ppermute(shard, axis, pairs)


def gather_kernel(count, own_ref, out_ref, slots, send_sems, recv_sems):
    me = lax.axis_index("sh")
    across = lax.axis_index("sl")
    inner = lax.axis_index("hd")
    barrier = pltpu.get_barrier_semaphore()

    def peer(index):
        return (index, across, inner)

    def greet(index, carry):
        @pl.when(index != me)
        def _():
            pl.semaphore_signal(
                barrier, inc=1, device_id=peer(index), device_id_type=pl.DeviceIdType.MESH
            )

        return carry

    lax.fori_loop(0, count, greet, 0)
    pl.semaphore_wait(barrier, count - 1)

    def copy_to(index):
        return pltpu.make_async_remote_copy(
            src_ref=own_ref,
            dst_ref=slots.at[me],
            send_sem=send_sems.at[index],
            recv_sem=recv_sems.at[me],
            device_id=peer(index),
            device_id_type=pl.DeviceIdType.MESH,
        )

    def copy_from(index):
        return pltpu.make_async_remote_copy(
            src_ref=own_ref,
            dst_ref=slots.at[index],
            send_sem=send_sems.at[index],
            recv_sem=recv_sems.at[index],
            device_id=peer(index),
            device_id_type=pl.DeviceIdType.MESH,
        )

    def send(index, carry):
        @pl.when(index != me)
        def _():
            copy_to(index).start()

        return carry

    lax.fori_loop(0, count, send, 0)
    slots[me] = own_ref[...]

    def finish(index, carry):
        @pl.when(index != me)
        def _():
            copy_to(index).wait_send()
            copy_from(index).wait_recv()

        return carry

    lax.fori_loop(0, count, finish, 0)
    out_ref[...] = slots[...]


def group_maps(block, ident):
    count = lax.axis_size("sh")
    return pl.pallas_call(
        lambda *refs: gather_kernel(count, *refs),
        out_shape=jax.ShapeDtypeStruct((count,) + block.shape, block.dtype),
        in_specs=[pl.BlockSpec(memory_space=pltpu.VMEM)],
        out_specs=pl.BlockSpec(memory_space=pltpu.VMEM),
        scratch_shapes=[
            pltpu.VMEM((count,) + block.shape, block.dtype),
            pltpu.SemaphoreType.DMA((count,)),
            pltpu.SemaphoreType.DMA((count,)),
        ],
        compiler_params=pltpu.CompilerParams(collective_id=ident, has_side_effects=True),
    )(block)


def carried_in(shard, axis, join, neutral, backward):
    count = lax.axis_size(axis)
    place = lax.axis_index(axis)
    ahead = count - 1 - place if backward else place
    both = group_maps(jnp.stack(shard).astype(jnp.bfloat16), 2 if backward else 1)
    gathered = (both[:, 0], both[:, 1])
    state = jax.tree.map(lambda a, e: jnp.zeros_like(a) + jnp.asarray(e, a.dtype), shard, neutral)

    def one(turn, state):
        source = count - 1 - turn if backward else turn
        return join(
            state,
            jax.tree.map(
                lambda a, own: lax.dynamic_index_in_dim(a, source, 0, False).astype(own.dtype),
                gathered,
                shard,
            ),
        )

    return lax.fori_loop(0, ahead, one, state)


def flat_place():
    return (
        lax.axis_index("sh") * lax.axis_size("sl") + lax.axis_index("sl")
    ) * lax.axis_size("hd") + lax.axis_index("hd")


def device_of(index):
    inner = lax.axis_size("sl") * lax.axis_size("hd")
    return (index // inner, (index // lax.axis_size("hd")) % lax.axis_size("sl"), index % lax.axis_size("hd"))


def sum_kernel(count, own_ref, out_ref, slots, send_sems, recv_sems):
    me = flat_place()
    barrier = pltpu.get_barrier_semaphore()

    def greet(index, carry):
        @pl.when(index != me)
        def _():
            pl.semaphore_signal(
                barrier, inc=1, device_id=device_of(index), device_id_type=pl.DeviceIdType.MESH
            )

        return carry

    lax.fori_loop(0, count, greet, 0)
    pl.semaphore_wait(barrier, count - 1)

    def copy_to(index):
        return pltpu.make_async_remote_copy(
            src_ref=own_ref,
            dst_ref=slots.at[me],
            send_sem=send_sems.at[index],
            recv_sem=recv_sems.at[me],
            device_id=device_of(index),
            device_id_type=pl.DeviceIdType.MESH,
        )

    def copy_from(index):
        return pltpu.make_async_remote_copy(
            src_ref=own_ref,
            dst_ref=slots.at[index],
            send_sem=send_sems.at[index],
            recv_sem=recv_sems.at[index],
            device_id=device_of(index),
            device_id_type=pl.DeviceIdType.MESH,
        )

    def send(index, carry):
        @pl.when(index != me)
        def _():
            copy_to(index).start()

        return carry

    lax.fori_loop(0, count, send, 0)
    slots[me] = own_ref[...]

    def finish(index, carry):
        @pl.when(index != me)
        def _():
            copy_to(index).wait_send()
            copy_from(index).wait_recv()

        return carry

    lax.fori_loop(0, count, finish, 0)
    out_ref[...] = jnp.sum(slots[...], axis=0)


def all_sum(vector):
    count = lax.axis_size("sh") * lax.axis_size("sl") * lax.axis_size("hd")
    size = vector.shape[0]
    lanes = 128
    tile = 8 * lanes
    padded = -(-size // tile) * tile
    block = jnp.pad(vector, (0, padded - size)).reshape(padded // lanes, lanes)
    total = pl.pallas_call(
        lambda *refs: sum_kernel(count, *refs),
        out_shape=jax.ShapeDtypeStruct(block.shape, jnp.float32),
        in_specs=[pl.BlockSpec(memory_space=pltpu.VMEM)],
        out_specs=pl.BlockSpec(memory_space=pltpu.VMEM),
        scratch_shapes=[
            pltpu.VMEM((count,) + block.shape, jnp.float32),
            pltpu.SemaphoreType.DMA((count,)),
            pltpu.SemaphoreType.DMA((count,)),
        ],
        compiler_params=pltpu.CompilerParams(collective_id=0, has_side_effects=True),
    )(block)
    return total.reshape(-1)[:size]


def rms_norm(values, scale_gain):
    return values * lax.rsqrt(jnp.mean(values * values, axis=-1, keepdims=True) + EPS) * scale_gain


def unit_norm(values):
    return values * lax.rsqrt(jnp.sum(values * values, axis=-1, keepdims=True) + EPS)


def bf_product(first_mat, second_mat):
    return jnp.dot(first_mat, second_mat, preferred_element_type=jnp.float32)


def hi(spec, *arrays):
    return jnp.einsum(spec, *arrays, precision=HIGH_ACCURACY)


def compose(early_pair, late_pair):
    early_mat, early_add = early_pair
    late_mat, late_add = late_pair
    joined = hi("hij,hjk->hik", late_mat, early_mat)
    shifted = hi("hij,hjk->hik", late_mat, early_add) + late_add
    return (joined, shifted)


def gate_norm(values, out_gate, scale_gain):
    return rms_norm(values, scale_gain) * jax.nn.silu(out_gate)


def swiglu(gate_up):
    half = gate_up.shape[1] // 2
    return jax.nn.silu(gate_up[:, :half]) * gate_up[:, half:]


def owner_pairs(inverse):
    groups = lax.axis_size("sh")
    pairs = [(g * HEADS + t, t * groups + g) for g in range(groups) for t in range(HEADS)]
    return [(b, a) for a, b in pairs] if inverse else pairs


def rows_to_heads(blocks):
    groups = lax.axis_size("sh")
    width = blocks[0].shape[1]
    used = sum(b.shape[0] for b in blocks)
    least = (1 << 20) // (groups * width * 2) + 1
    rows = -(-max(used, least) // 8) * 8
    packed = jnp.concatenate(
        list(blocks) + [jnp.zeros((rows - used, width), blocks[0].dtype)], 0
    )
    moved = lax.ppermute(packed, ALL, owner_pairs(True))
    full = lax.all_gather(moved, "sh", axis=0, tiled=False)
    parts = []
    first = 0
    for block in blocks:
        size = block.shape[0]
        parts.append(full[:, first : first + size].reshape(groups * size, width))
        first += size
    return parts


def heads_to_rows(partials):
    groups = lax.axis_size("sh")
    pieces = [
        p.astype(jnp.bfloat16).reshape((groups, p.shape[0] // groups) + p.shape[1:])
        for p in partials
    ]
    joined = jnp.concatenate(pieces, 1)
    joined = joined.reshape((-1,) + joined.shape[2:])
    summed = lax.psum_scatter(joined, "sh", scatter_dimension=0, tiled=True)
    moved = lax.ppermute(summed, ALL, owner_pairs(False)).astype(jnp.float32)
    parts = []
    first = 0
    for piece in pieces:
        size = piece.shape[1]
        parts.append(moved[first : first + size])
        first += size
    return parts


def columns_to_heads(local_cols):
    per_head = jnp.transpose(local_cols, (1, 0, 2))
    mine = lax.all_to_all(per_head, GROUP, 0, 0, tiled=True)
    mine = mine.reshape(-1, mine.shape[-1])
    return lax.all_gather(mine, "sh", axis=0, tiled=True)


def heads_to_columns(partial, direct=False):
    low = partial.astype(jnp.bfloat16)
    if direct:
        groups = lax.axis_size("sh")
        pieces = low.reshape((groups, low.shape[0] // groups) + low.shape[1:])
        moved = lax.all_to_all(pieces, "sh", 0, 0, tiled=True)
        summed = jnp.sum(moved.astype(jnp.float32), 0).astype(jnp.bfloat16)
    else:
        summed = lax.psum_scatter(low, "sh", scatter_dimension=0, tiled=True)
    summed = summed.reshape(HEADS, -1, summed.shape[-1])
    back = lax.all_to_all(summed, GROUP, 0, 0, tiled=True)
    return jnp.transpose(back, (1, 0, 2)).astype(jnp.float32)


def group_gather(rows, direct=False):
    if direct:
        copies = jnp.broadcast_to(rows[None], (HEADS,) + rows.shape)
        moved = lax.all_to_all(copies, GROUP, 0, 0, tiled=True)
        return moved.reshape((-1,) + rows.shape[1:])
    return lax.all_gather(rows, GROUP, axis=0, tiled=True)


def group_scatter(partial, direct=False):
    low = partial.astype(jnp.bfloat16)
    if direct:
        pieces = low.reshape((HEADS, low.shape[0] // HEADS) + low.shape[1:])
        moved = lax.all_to_all(pieces, GROUP, 0, 0, tiled=True)
        return jnp.sum(moved.astype(jnp.float32), 0)
    return lax.psum_scatter(low, GROUP, scatter_dimension=0, tiled=True).astype(jnp.float32)


def masked_power_inverse(system):
    size = system.shape[-1]
    places = jnp.arange(size)
    base = 8
    inside = (places[:, None] // base == places[None, :] // base) & (
        places[:, None] > places[None, :]
    )
    step = -(system * inside.astype(system.dtype))
    eye = jnp.eye(size, dtype=system.dtype)
    result = eye + step
    for _ in range(2):
        step = hi("bij,bjk->bik", step, step)
        result = result + hi("bij,bjk->bik", result, step)
    width = base
    while width < size:
        across = (places[:, None] // (2 * width) == places[None, :] // (2 * width)) & (
            places[:, None] // width != places[None, :] // width
        )
        lower_left = system * across.astype(system.dtype)
        result = result - hi("bij,bjk->bik", result, hi("bij,bjk->bik", lower_left, result))
        width = 2 * width
    return result


@jax.custom_vjp
def unit_lower_inverse(system):
    return masked_power_inverse(system)


def inverse_keep(system):
    inverse = masked_power_inverse(system)
    return inverse, inverse


def inverse_back(inverse, grad):
    turned = jnp.swapaxes(inverse, -1, -2)
    return (-hi("bij,bjk->bik", turned, hi("bij,bjk->bik", grad, turned)),)


unit_lower_inverse.defvjp(inverse_keep, inverse_back)


def block_mixer(query_rows, key_rows, value_rows, beta_rows, log_decay, starts_flag):
    pseudo = key_rows.shape[0]
    span = STEPS * BLOCK
    blocks = pseudo // span
    queries = query_rows.reshape(blocks, BLOCK, DK)
    keys = key_rows.reshape(blocks, span, DK)
    values = value_rows.reshape(blocks, span, DK)
    betas = beta_rows.reshape(blocks, span)
    decays = log_decay.reshape(blocks, span)
    flags = starts_flag.reshape(blocks, span)
    places = jnp.arange(span)
    lower = places[:, None] >= places[None, :]
    strict = (places[:, None] > places[None, :]).astype(jnp.float32)
    identity = jnp.eye(span, dtype=jnp.float32)
    eye_key = jnp.eye(DK, dtype=jnp.float32)

    summed = jnp.cumsum(decays, axis=1)
    segment = jnp.cumsum(flags, axis=1)
    same_doc = (segment[:, :, None] == segment[:, None, :]) & lower
    decay_ratio = jnp.exp(
        jnp.where(same_doc, summed[:, :, None] - summed[:, None, :], 0.0)
    ) * same_doc.astype(jnp.float32)
    from_start = jnp.exp(summed) * (segment == 0.0).astype(jnp.float32)
    key_key = hi("bik,bjk->bij", keys, keys)
    system = identity + betas[:, :, None] * decay_ratio * key_key * strict
    right_side = jnp.concatenate(
        [betas[:, :, None] * values, (betas * from_start)[:, :, None] * keys], 2
    )
    solved = hi("bij,bjk->bik", unit_lower_inverse(system), right_side)
    fresh = solved[:, :, :DK]
    carried = solved[:, :, DK:]
    last_keys = keys * decay_ratio[:, -1, :, None]
    transfer = from_start[:, -1, None, None] * eye_key - hi("bsi,bsj->bij", last_keys, carried)
    offset = hi("bsi,bsj->bij", last_keys, fresh)
    query_key = hi("bqk,bsk->bqs", queries, keys) * decay_ratio[:, STEPS - 1 :: STEPS]
    frame = from_start[:, STEPS - 1 :: STEPS, None] * queries - hi(
        "bqs,bsj->bqj", query_key, carried
    )
    direct = hi("bqs,bsj->bqj", query_key, fresh)

    state = jnp.concatenate([eye_key, jnp.zeros((DK, DK), jnp.float32)], 1)
    states = []
    for index in range(blocks):
        states.append(state)
        state = hi("ij,jk->ik", transfer[index], state) + jnp.concatenate(
            [jnp.zeros((DK, DK), jnp.float32), offset[index]], 1
        )
    states = jnp.stack(states)
    mats = states[:, :, :DK]
    adds = states[:, :, DK:]
    final_mat = state[:, :DK]
    final_add = state[:, DK:]
    query_frame = hi("bqi,bij->bqj", frame, mats)
    partial = hi("bqi,bij->bqj", frame, adds) + direct
    return (
        query_frame.reshape(blocks * BLOCK, DK),
        partial.reshape(blocks * BLOCK, DK),
        final_mat[None],
        final_add[None],
    )


def local(
    tokens_in,
    mixer_norm,
    mix_weight,
    head_gates,
    conv_taps,
    decay_log,
    decay_bias,
    gate_weight,
    out_norm,
    out_weight,
    feed_norm,
    up_weight,
    down_weight,
    doc_lengths,
    out_grad,
):
    row_count = tokens_in.shape[0]
    weight_rows = mix_weight.shape[0]
    head = lax.axis_index("sl") * lax.axis_size("hd") + lax.axis_index("hd")
    length = row_count * HEADS

    head_cols = jnp.concatenate(
        [
            gate_weight.reshape(weight_rows, HEADS, DK),
            mix_weight.reshape(weight_rows, HEADS, PROJ),
            head_gates.reshape(weight_rows, HEADS, STEPS + 1),
            jnp.broadcast_to(mixer_norm[:, None, None], (weight_rows, HEADS, 1)),
        ],
        2,
    )
    head_wide = columns_to_heads(head_cols)
    head_full = head_wide[:, :WIDE]
    gain_one = head_wide[:, WIDE].astype(jnp.float32)
    half = FF // HEADS
    up_cols = jnp.concatenate(
        [
            up_weight[:, :FF].reshape(weight_rows, HEADS, half),
            up_weight[:, FF:].reshape(weight_rows, HEADS, half),
            jnp.broadcast_to(feed_norm[:, None, None], (weight_rows, HEADS, 1)),
        ],
        2,
    )
    up_wide = columns_to_heads(up_cols)
    up_full = up_wide[:, : 2 * half]
    gain_two = up_wide[:, 2 * half].astype(jnp.float32)
    tap_width = conv_taps.shape[1]
    tap_row = jnp.pad(conv_taps.reshape(1, -1), ((0, 0), (0, D - CONV * tap_width)))
    out_full, down_full, tap_rows = rows_to_heads((out_weight, down_weight, tap_row))
    conv_part = jnp.transpose(
        tap_rows[:, : CONV * tap_width].reshape(-1, CONV, tap_width), (1, 0, 2)
    ).reshape(CONV, -1).astype(jnp.float32)

    x_float = tokens_in.astype(jnp.float32)
    normed_float, norm_one_back = jax.vjp(rms_norm, x_float, gain_one)
    normed_one = group_gather(normed_float.astype(jnp.bfloat16), True)
    tokens_all = group_gather(tokens_in, True)
    head_out = bf_product(normed_one, head_full)
    out_gate = head_out[:, :DK]
    proj_head = head_out[:, DK : DK + PROJ].astype(jnp.bfloat16)
    scalar_rows = head_out[:, DK + PROJ :].astype(jnp.bfloat16).astype(jnp.float32)

    rim_rows = from_behind(proj_head[length - (CONV - 1) :], "sh", 1)
    padded = jnp.concatenate([rim_rows, proj_head], 0).astype(jnp.float32)
    starts = jnp.cumsum(doc_lengths) - doc_lengths
    positions = lax.axis_index("sh") * length + jnp.arange(length, dtype=jnp.int32)
    starts_flag = jnp.any(positions[:, None] == starts[None, :], 1).astype(jnp.float32)
    doc_begin = jnp.max(jnp.where(starts[None, :] <= positions[:, None], starts[None, :], 0), 1)
    tap_masks = [
        (positions - (CONV - 1) + tap_index >= doc_begin).astype(jnp.float32)
        for tap_index in range(CONV)
    ]
    pseudo_flag = jnp.concatenate(
        [starts_flag[:, None], jnp.zeros((length, STEPS - 1), jnp.float32)], 1
    ).reshape(-1)
    rate_log = lax.dynamic_index_in_dim(decay_log, head, 0, False)
    bias_part = lax.dynamic_index_in_dim(decay_bias, head, 0, False)

    def mixer_inputs(padded, scalar_rows, conv_part, rate_log, bias_part):
        convolved = jnp.zeros_like(padded[CONV - 1 :])
        for tap_index in range(CONV):
            convolved = (
                convolved
                + conv_part[tap_index]
                * padded[tap_index : tap_index + length]
                * tap_masks[tap_index][:, None]
            )
        activated = jax.nn.silu(convolved).reshape(length, 1 + 2 * STEPS, DK)
        query_rows = unit_norm(activated[:, 0])
        key_rows = unit_norm(activated[:, 1 : 1 + STEPS]).reshape(STEPS * length, DK)
        value_rows = activated[:, 1 + STEPS :].reshape(STEPS * length, DK)
        beta_rows = jax.nn.sigmoid(scalar_rows[:, :STEPS]).reshape(STEPS * length)
        log_rate = -jnp.exp(rate_log) * jax.nn.softplus(scalar_rows[:, STEPS] + bias_part)
        log_decay = jnp.concatenate(
            [log_rate[:, None], jnp.zeros((length, STEPS - 1), jnp.float32)], 1
        ).reshape(STEPS * length)
        return (query_rows, key_rows, value_rows, beta_rows, log_decay)

    def recurrence(query_rows, key_rows, value_rows, beta_rows, log_decay):
        return block_mixer(query_rows, key_rows, value_rows, beta_rows, log_decay, pseudo_flag)

    prepared, inputs_back = jax.vjp(
        mixer_inputs, padded, scalar_rows, conv_part, rate_log, bias_part
    )
    (query_frame, partial_value_rows, transfer, offset), recurrence_back = jax.vjp(
        recurrence, *prepared
    )
    grad_rows = group_gather(out_grad)
    grad_rows, query_frame, partial_value_rows, transfer, offset = lax.optimization_barrier(
        (grad_rows, query_frame, partial_value_rows, transfer, offset)
    )
    identity = jnp.eye(DK, dtype=jnp.float32)[None]
    zeros_state = jnp.zeros((1, DK, DK), jnp.float32)
    prefix_map, incoming_state = carried_in(
        (transfer, offset), "sh", compose, (identity, zeros_state), False
    )
    mixer_result = partial_value_rows + hi("zy,yi->zi", query_frame, incoming_state[0])
    mixer_low = mixer_result.astype(jnp.bfloat16).astype(jnp.float32)
    gated, gate_back = jax.vjp(gate_norm, mixer_low, out_gate, out_norm)
    gated_rows = gated.astype(jnp.bfloat16)
    branch_all = lax.psum(bf_product(gated_rows, out_full).astype(jnp.bfloat16), GROUP)
    middle_all = tokens_all.astype(jnp.float32) + branch_all.astype(jnp.float32)
    middle = lax.dynamic_slice_in_dim(middle_all, head * row_count, row_count, 0)
    normed_two = rms_norm(middle_all, gain_two).astype(jnp.bfloat16)
    normed_mid, norm_two_back = jax.vjp(rms_norm, middle, gain_two)
    gate_up = bf_product(normed_two, up_full)
    hidden_float, swiglu_back = jax.vjp(swiglu, gate_up)
    hidden = hidden_float.astype(jnp.bfloat16)
    feed_partial = bf_product(hidden, down_full)

    grad_out = out_grad.astype(jnp.float32)
    grad_hidden = bf_product(grad_rows, down_full.T)
    grad_down_partial = bf_product(hidden.T, grad_rows)
    (grad_gate_up,) = swiglu_back(grad_hidden)
    grad_gate_up = grad_gate_up.astype(jnp.bfloat16)
    grad_normed_two = group_scatter(bf_product(grad_gate_up, up_full.T))
    grad_mid_norm, grad_gain_two = norm_two_back(grad_normed_two)
    grad_up_payload = jnp.concatenate(
        [bf_product(normed_two.T, grad_gate_up), grad_gain_two[:, None]], 1
    )
    grad_middle = grad_out + grad_mid_norm
    feed_partial, grad_up_payload, grad_down_partial, grad_branch_low = lax.optimization_barrier(
        (feed_partial, grad_up_payload, grad_down_partial, grad_middle.astype(jnp.bfloat16))
    )
    grad_up_cols = heads_to_columns(grad_up_payload, True)
    grad_up = jnp.concatenate(
        [
            grad_up_cols[:, :, :half].reshape(weight_rows, FF),
            grad_up_cols[:, :, half : 2 * half].reshape(weight_rows, FF),
        ],
        1,
    )
    grad_branch = group_gather(grad_branch_low)
    feed_partial, grad_down_partial, grad_branch = lax.optimization_barrier(
        (feed_partial, grad_down_partial, grad_branch)
    )
    feed_sum = group_scatter(feed_partial)
    grad_gated = bf_product(grad_branch, out_full.T)
    grad_down, grad_outw = heads_to_rows((grad_down_partial, bf_product(gated_rows.T, grad_branch)))
    grad_mixer, grad_gate, grad_out_norm = gate_back(grad_gated)
    grad_gate = grad_gate.astype(jnp.bfloat16)
    head_gradients = grad_mixer.astype(jnp.bfloat16).astype(jnp.float32)
    local_adjoint = hi("dc,dr->cr", query_frame, head_gradients)[None]
    transfer_turned = jnp.transpose(transfer, (0, 2, 1))
    later_map, state_gradient = carried_in(
        (transfer_turned, local_adjoint), "sh", compose, (identity, zeros_state), True
    )
    basis_gradient = hi("nu,wu->nw", head_gradients, incoming_state[0])
    transfer_gradient = hi("tnf,tmf->tnm", state_gradient, incoming_state)
    grad_prepared = recurrence_back(
        (basis_gradient, head_gradients, transfer_gradient, state_gradient)
    )
    grad_prepared, feed_sum, grad_up_cols, grad_down, grad_outw = lax.optimization_barrier(
        (grad_prepared, feed_sum, grad_up_cols, grad_down, grad_outw)
    )
    layer_out = (middle + feed_sum).astype(jnp.bfloat16)
    grad_padded, grad_scalars, grad_conv, grad_rate, grad_bias = inputs_back(grad_prepared)
    rim_grad = from_behind(grad_padded[: CONV - 1], "sh", -1)
    own_grad = grad_padded[CONV - 1 :]
    grad_proj = jnp.concatenate(
        [own_grad[: length - (CONV - 1)], own_grad[length - (CONV - 1) :] + rim_grad], 0
    )
    grad_head = jnp.concatenate(
        [grad_gate, grad_proj.astype(jnp.bfloat16), grad_scalars.astype(jnp.bfloat16)], 1
    )
    grad_normed_one = group_scatter(bf_product(grad_head, head_full.T), True)
    grad_x_norm, grad_gain_one = norm_one_back(grad_normed_one)
    grad_head_cols = heads_to_columns(
        jnp.concatenate([bf_product(normed_one.T, grad_head), grad_gain_one[:, None]], 1)
    )
    grad_gatew = grad_head_cols[:, :, :DK].reshape(weight_rows, D)
    grad_mixw = grad_head_cols[:, :, DK : DK + PROJ].reshape(weight_rows, HEADS * PROJ)
    grad_gatesw = grad_head_cols[:, :, DK + PROJ : WIDE].reshape(
        weight_rows, HEADS * (STEPS + 1)
    )
    grad_tokens = (grad_middle + grad_x_norm).astype(jnp.bfloat16)
    (conv_grad,) = heads_to_rows((jnp.transpose(grad_conv),))
    conv_grad = jnp.transpose(conv_grad)
    one_hot = (jnp.arange(HEADS) == head).astype(jnp.float32)
    small_sums = all_sum(
        jnp.concatenate([one_hot * grad_rate, one_hot * grad_bias, grad_out_norm])
    )
    return (
        layer_out,
        grad_tokens,
        jnp.sum(grad_head_cols[:, :, WIDE], 1),
        grad_mixw,
        grad_gatesw,
        conv_grad,
        small_sums[:HEADS],
        small_sums[HEADS : 2 * HEADS],
        grad_gatew,
        small_sums[2 * HEADS :],
        grad_outw,
        jnp.sum(grad_up_cols[:, :, 2 * half], 1),
        grad_up,
        grad_down,
    )


def solution(mesh):
    seq = mesh.shape["seq"]
    across = mesh.shape["head"]
    inner = HEADS // across
    grid = Mesh(
        np.asarray(mesh.devices).reshape(seq // inner, inner, across), ("sh", "sl", "hd")
    )
    rows = P(ALL, None)
    flat = P(ALL)
    return jax.shard_map(
        local,
        mesh=grid,
        in_specs=(
            rows,
            flat,
            rows,
            rows,
            P(None, ALL),
            P(),
            P(),
            rows,
            P(),
            rows,
            flat,
            rows,
            rows,
            P(),
            rows,
        ),
        out_specs=(
            rows,
            rows,
            flat,
            rows,
            rows,
            P(None, ALL),
            P(),
            P(),
            rows,
            P(),
            rows,
            flat,
            rows,
            rows,
        ),
        check_vma=False,
    )
```

```python
import jax
import jax.numpy as jnp
import numpy as np
from jax import lax
from jax.experimental import pallas as pl
from jax.experimental.pallas import tpu as pltpu
from jax.sharding import Mesh
from jax.sharding import PartitionSpec as P

D = 1024
HEADS = 8
DK = 128
FF = 2816
STEPS = 2
CONV = 4
BLOCK = 64
PROJ = (1 + 2 * STEPS) * DK
WIDE = DK + PROJ + STEPS + 1

EPS = 1e-06
HIGH_ACCURACY = lax.Precision.HIGH

GROUP = ("sl", "hd")
ALL = ("sh", "sl", "hd")


def from_behind(shard, axis, by):
    peers = lax.axis_size(axis)
    pairs = [(i, i + by) for i in range(peers) if 0 <= i + by < peers]
    return lax.ppermute(shard, axis, pairs)


def gather_kernel(count, own_ref, out_ref, slots, send_sems, recv_sems):
    me = lax.axis_index("sh")
    across = lax.axis_index("sl")
    inner = lax.axis_index("hd")
    barrier = pltpu.get_barrier_semaphore()

    def peer(index):
        return (index, across, inner)

    def greet(index, carry):
        @pl.when(index != me)
        def _():
            pl.semaphore_signal(
                barrier, inc=1, device_id=peer(index), device_id_type=pl.DeviceIdType.MESH
            )

        return carry

    lax.fori_loop(0, count, greet, 0)
    pl.semaphore_wait(barrier, count - 1)

    def copy_to(index):
        return pltpu.make_async_remote_copy(
            src_ref=own_ref,
            dst_ref=slots.at[me],
            send_sem=send_sems.at[index],
            recv_sem=recv_sems.at[me],
            device_id=peer(index),
            device_id_type=pl.DeviceIdType.MESH,
        )

    def copy_from(index):
        return pltpu.make_async_remote_copy(
            src_ref=own_ref,
            dst_ref=slots.at[index],
            send_sem=send_sems.at[index],
            recv_sem=recv_sems.at[index],
            device_id=peer(index),
            device_id_type=pl.DeviceIdType.MESH,
        )

    def send(index, carry):
        @pl.when(index != me)
        def _():
            copy_to(index).start()

        return carry

    lax.fori_loop(0, count, send, 0)
    slots[me] = own_ref[...]

    def finish(index, carry):
        @pl.when(index != me)
        def _():
            copy_to(index).wait_send()
            copy_from(index).wait_recv()

        return carry

    lax.fori_loop(0, count, finish, 0)
    out_ref[...] = slots[...]


def scatter_kernel(count, own_ref, out_ref, slots, send_sems, recv_sems):
    me = lax.axis_index("sh")
    across = lax.axis_index("sl")
    inner = lax.axis_index("hd")
    barrier = pltpu.get_barrier_semaphore()

    def peer(index):
        return (index, across, inner)

    def greet(index, carry):
        @pl.when(index != me)
        def _():
            pl.semaphore_signal(
                barrier, inc=1, device_id=peer(index), device_id_type=pl.DeviceIdType.MESH
            )

        return carry

    lax.fori_loop(0, count, greet, 0)
    pl.semaphore_wait(barrier, count - 1)

    def copy_to(index):
        return pltpu.make_async_remote_copy(
            src_ref=own_ref.at[index],
            dst_ref=slots.at[me],
            send_sem=send_sems.at[index],
            recv_sem=recv_sems.at[me],
            device_id=peer(index),
            device_id_type=pl.DeviceIdType.MESH,
        )

    def copy_from(index):
        return pltpu.make_async_remote_copy(
            src_ref=own_ref.at[index],
            dst_ref=slots.at[index],
            send_sem=send_sems.at[index],
            recv_sem=recv_sems.at[index],
            device_id=peer(index),
            device_id_type=pl.DeviceIdType.MESH,
        )

    def send(index, carry):
        @pl.when(index != me)
        def _():
            copy_to(index).start()

        return carry

    lax.fori_loop(0, count, send, 0)
    slots[me] = own_ref[me]

    def finish(index, carry):
        @pl.when(index != me)
        def _():
            copy_to(index).wait_send()
            copy_from(index).wait_recv()

        return carry

    lax.fori_loop(0, count, finish, 0)
    out_ref[...] = jnp.sum(slots[...].astype(jnp.float32), axis=0)


def group_sum_scatter(partial, ident):
    count = lax.axis_size("sh")
    pieces = partial.astype(jnp.bfloat16).reshape((count, partial.shape[0] // count) + partial.shape[1:])
    return pl.pallas_call(
        lambda *refs: scatter_kernel(count, *refs),
        out_shape=jax.ShapeDtypeStruct(pieces.shape[1:], jnp.float32),
        in_specs=[pl.BlockSpec(memory_space=pltpu.VMEM)],
        out_specs=pl.BlockSpec(memory_space=pltpu.VMEM),
        scratch_shapes=[
            pltpu.VMEM(pieces.shape, jnp.bfloat16),
            pltpu.SemaphoreType.DMA((count,)),
            pltpu.SemaphoreType.DMA((count,)),
        ],
        compiler_params=pltpu.CompilerParams(collective_id=ident, has_side_effects=True),
    )(pieces)


def reduce_kernel(count, own_ref, out_ref, slots, full, send_one, recv_one, send_two, recv_two):
    me = lax.axis_index("sl") * lax.axis_size("hd") + lax.axis_index("hd")
    place = lax.axis_index("sh")
    barrier = pltpu.get_barrier_semaphore()

    def peer(index):
        return (place, index // lax.axis_size("hd"), index % lax.axis_size("hd"))

    def greet(index, carry):
        @pl.when(index != me)
        def _():
            pl.semaphore_signal(
                barrier, inc=1, device_id=peer(index), device_id_type=pl.DeviceIdType.MESH
            )

        return carry

    lax.fori_loop(0, count, greet, 0)
    pl.semaphore_wait(barrier, count - 1)

    def part_to(index):
        return pltpu.make_async_remote_copy(
            src_ref=own_ref.at[index],
            dst_ref=slots.at[me],
            send_sem=send_one.at[index],
            recv_sem=recv_one.at[me],
            device_id=peer(index),
            device_id_type=pl.DeviceIdType.MESH,
        )

    def part_from(index):
        return pltpu.make_async_remote_copy(
            src_ref=own_ref.at[index],
            dst_ref=slots.at[index],
            send_sem=send_one.at[index],
            recv_sem=recv_one.at[index],
            device_id=peer(index),
            device_id_type=pl.DeviceIdType.MESH,
        )

    def sum_to(index):
        return pltpu.make_async_remote_copy(
            src_ref=full.at[me],
            dst_ref=full.at[me],
            send_sem=send_two.at[index],
            recv_sem=recv_two.at[me],
            device_id=peer(index),
            device_id_type=pl.DeviceIdType.MESH,
        )

    def sum_from(index):
        return pltpu.make_async_remote_copy(
            src_ref=full.at[index],
            dst_ref=full.at[index],
            send_sem=send_two.at[index],
            recv_sem=recv_two.at[index],
            device_id=peer(index),
            device_id_type=pl.DeviceIdType.MESH,
        )

    def send_parts(index, carry):
        @pl.when(index != me)
        def _():
            part_to(index).start()

        return carry

    lax.fori_loop(0, count, send_parts, 0)
    slots[me] = own_ref[me]

    def finish_parts(index, carry):
        @pl.when(index != me)
        def _():
            part_to(index).wait_send()
            part_from(index).wait_recv()

        return carry

    lax.fori_loop(0, count, finish_parts, 0)
    full[me] = jnp.sum(slots[...].astype(jnp.float32), axis=0).astype(full.dtype)

    def send_sums(index, carry):
        @pl.when(index != me)
        def _():
            sum_to(index).start()

        return carry

    lax.fori_loop(0, count, send_sums, 0)

    def finish_sums(index, carry):
        @pl.when(index != me)
        def _():
            sum_to(index).wait_send()
            sum_from(index).wait_recv()

        return carry

    lax.fori_loop(0, count, finish_sums, 0)
    out_ref[...] = full[...]


def group_all_sum(partial, ident):
    count = HEADS
    pieces = partial.astype(jnp.bfloat16).reshape((count, partial.shape[0] // count) + partial.shape[1:])
    total = pl.pallas_call(
        lambda *refs: reduce_kernel(count, *refs),
        out_shape=jax.ShapeDtypeStruct(pieces.shape, jnp.bfloat16),
        in_specs=[pl.BlockSpec(memory_space=pltpu.VMEM)],
        out_specs=pl.BlockSpec(memory_space=pltpu.VMEM),
        scratch_shapes=[
            pltpu.VMEM(pieces.shape, jnp.bfloat16),
            pltpu.VMEM(pieces.shape, jnp.bfloat16),
            pltpu.SemaphoreType.DMA((count,)),
            pltpu.SemaphoreType.DMA((count,)),
            pltpu.SemaphoreType.DMA((count,)),
            pltpu.SemaphoreType.DMA((count,)),
        ],
        compiler_params=pltpu.CompilerParams(collective_id=ident, has_side_effects=True),
    )(pieces)
    return total.reshape(partial.shape)


def group_maps(block, ident):
    count = lax.axis_size("sh")
    return pl.pallas_call(
        lambda *refs: gather_kernel(count, *refs),
        out_shape=jax.ShapeDtypeStruct((count,) + block.shape, block.dtype),
        in_specs=[pl.BlockSpec(memory_space=pltpu.VMEM)],
        out_specs=pl.BlockSpec(memory_space=pltpu.VMEM),
        scratch_shapes=[
            pltpu.VMEM((count,) + block.shape, block.dtype),
            pltpu.SemaphoreType.DMA((count,)),
            pltpu.SemaphoreType.DMA((count,)),
        ],
        compiler_params=pltpu.CompilerParams(collective_id=ident, has_side_effects=True),
    )(block)


def carried_in(shard, axis, join, neutral, backward):
    count = lax.axis_size(axis)
    place = lax.axis_index(axis)
    ahead = count - 1 - place if backward else place
    both = group_maps(jnp.stack(shard).astype(jnp.bfloat16), 2 if backward else 1)
    gathered = (both[:, 0], both[:, 1])
    state = jax.tree.map(lambda a, e: jnp.zeros_like(a) + jnp.asarray(e, a.dtype), shard, neutral)

    def one(turn, state):
        source = count - 1 - turn if backward else turn
        return join(
            state,
            jax.tree.map(
                lambda a, own: lax.dynamic_index_in_dim(a, source, 0, False).astype(own.dtype),
                gathered,
                shard,
            ),
        )

    return lax.fori_loop(0, ahead, one, state)


def flat_place():
    return (
        lax.axis_index("sh") * lax.axis_size("sl") + lax.axis_index("sl")
    ) * lax.axis_size("hd") + lax.axis_index("hd")


def device_of(index):
    inner = lax.axis_size("sl") * lax.axis_size("hd")
    return (index // inner, (index // lax.axis_size("hd")) % lax.axis_size("sl"), index % lax.axis_size("hd"))


def sum_kernel(count, own_ref, out_ref, slots, send_sems, recv_sems):
    me = flat_place()
    barrier = pltpu.get_barrier_semaphore()

    def greet(index, carry):
        @pl.when(index != me)
        def _():
            pl.semaphore_signal(
                barrier, inc=1, device_id=device_of(index), device_id_type=pl.DeviceIdType.MESH
            )

        return carry

    lax.fori_loop(0, count, greet, 0)
    pl.semaphore_wait(barrier, count - 1)

    def copy_to(index):
        return pltpu.make_async_remote_copy(
            src_ref=own_ref,
            dst_ref=slots.at[me],
            send_sem=send_sems.at[index],
            recv_sem=recv_sems.at[me],
            device_id=device_of(index),
            device_id_type=pl.DeviceIdType.MESH,
        )

    def copy_from(index):
        return pltpu.make_async_remote_copy(
            src_ref=own_ref,
            dst_ref=slots.at[index],
            send_sem=send_sems.at[index],
            recv_sem=recv_sems.at[index],
            device_id=device_of(index),
            device_id_type=pl.DeviceIdType.MESH,
        )

    def send(index, carry):
        @pl.when(index != me)
        def _():
            copy_to(index).start()

        return carry

    lax.fori_loop(0, count, send, 0)
    slots[me] = own_ref[...]

    def finish(index, carry):
        @pl.when(index != me)
        def _():
            copy_to(index).wait_send()
            copy_from(index).wait_recv()

        return carry

    lax.fori_loop(0, count, finish, 0)
    out_ref[...] = jnp.sum(slots[...], axis=0)


def all_sum(vector):
    count = lax.axis_size("sh") * lax.axis_size("sl") * lax.axis_size("hd")
    size = vector.shape[0]
    lanes = 128
    tile = 8 * lanes
    padded = -(-size // tile) * tile
    block = jnp.pad(vector, (0, padded - size)).reshape(padded // lanes, lanes)
    total = pl.pallas_call(
        lambda *refs: sum_kernel(count, *refs),
        out_shape=jax.ShapeDtypeStruct(block.shape, jnp.float32),
        in_specs=[pl.BlockSpec(memory_space=pltpu.VMEM)],
        out_specs=pl.BlockSpec(memory_space=pltpu.VMEM),
        scratch_shapes=[
            pltpu.VMEM((count,) + block.shape, jnp.float32),
            pltpu.SemaphoreType.DMA((count,)),
            pltpu.SemaphoreType.DMA((count,)),
        ],
        compiler_params=pltpu.CompilerParams(collective_id=0, has_side_effects=True),
    )(block)
    return total.reshape(-1)[:size]


def rms_norm(values, scale_gain):
    return values * lax.rsqrt(jnp.mean(values * values, axis=-1, keepdims=True) + EPS) * scale_gain


def unit_norm(values):
    return values * lax.rsqrt(jnp.sum(values * values, axis=-1, keepdims=True) + EPS)


def bf_product(first_mat, second_mat):
    return jnp.dot(first_mat, second_mat, preferred_element_type=jnp.float32)


def hi(spec, *arrays):
    return jnp.einsum(spec, *arrays, precision=HIGH_ACCURACY)


def compose(early_pair, late_pair):
    early_mat, early_add = early_pair
    late_mat, late_add = late_pair
    joined = hi("hij,hjk->hik", late_mat, early_mat)
    shifted = hi("hij,hjk->hik", late_mat, early_add) + late_add
    return (joined, shifted)


def gate_norm(values, out_gate, scale_gain):
    return rms_norm(values, scale_gain) * jax.nn.silu(out_gate)


def swiglu(gate_up):
    half = gate_up.shape[1] // 2
    return jax.nn.silu(gate_up[:, :half]) * gate_up[:, half:]


def owner_pairs(inverse):
    groups = lax.axis_size("sh")
    pairs = [(g * HEADS + t, t * groups + g) for g in range(groups) for t in range(HEADS)]
    return [(b, a) for a, b in pairs] if inverse else pairs


def rows_to_heads(blocks):
    groups = lax.axis_size("sh")
    width = blocks[0].shape[1]
    used = sum(b.shape[0] for b in blocks)
    least = (1 << 20) // (groups * width * 2) + 1
    rows = -(-max(used, least) // 8) * 8
    packed = jnp.concatenate(
        list(blocks) + [jnp.zeros((rows - used, width), blocks[0].dtype)], 0
    )
    moved = lax.ppermute(packed, ALL, owner_pairs(True))
    full = lax.all_gather(moved, "sh", axis=0, tiled=False)
    parts = []
    first = 0
    for block in blocks:
        size = block.shape[0]
        parts.append(full[:, first : first + size].reshape(groups * size, width))
        first += size
    return parts


def heads_to_rows(partials):
    groups = lax.axis_size("sh")
    pieces = [
        p.astype(jnp.bfloat16).reshape((groups, p.shape[0] // groups) + p.shape[1:])
        for p in partials
    ]
    joined = jnp.concatenate(pieces, 1)
    joined = joined.reshape((-1,) + joined.shape[2:])
    summed = lax.psum_scatter(joined, "sh", scatter_dimension=0, tiled=True)
    moved = lax.ppermute(summed, ALL, owner_pairs(False)).astype(jnp.float32)
    parts = []
    first = 0
    for piece in pieces:
        size = piece.shape[1]
        parts.append(moved[first : first + size])
        first += size
    return parts


def columns_to_heads(local_cols):
    per_head = jnp.transpose(local_cols, (1, 0, 2))
    mine = lax.all_to_all(per_head, GROUP, 0, 0, tiled=True)
    mine = mine.reshape(-1, mine.shape[-1])
    return lax.all_gather(mine, "sh", axis=0, tiled=True)


def heads_to_columns(partial, direct=False):
    low = partial.astype(jnp.bfloat16)
    if direct:
        summed = group_sum_scatter(low, 3).astype(jnp.bfloat16)
    else:
        summed = lax.psum_scatter(low, "sh", scatter_dimension=0, tiled=True)
    summed = summed.reshape(HEADS, -1, summed.shape[-1])
    back = lax.all_to_all(summed, GROUP, 0, 0, tiled=True)
    return jnp.transpose(back, (1, 0, 2)).astype(jnp.float32)


def group_gather(rows, direct=False):
    if direct:
        copies = jnp.broadcast_to(rows[None], (HEADS,) + rows.shape)
        moved = lax.all_to_all(copies, GROUP, 0, 0, tiled=True)
        return moved.reshape((-1,) + rows.shape[1:])
    return lax.all_gather(rows, GROUP, axis=0, tiled=True)


def group_scatter(partial, direct=False):
    low = partial.astype(jnp.bfloat16)
    if direct:
        pieces = low.reshape((HEADS, low.shape[0] // HEADS) + low.shape[1:])
        moved = lax.all_to_all(pieces, GROUP, 0, 0, tiled=True)
        return jnp.sum(moved.astype(jnp.float32), 0)
    return lax.psum_scatter(low, GROUP, scatter_dimension=0, tiled=True).astype(jnp.float32)


def masked_power_inverse(system):
    size = system.shape[-1]
    places = jnp.arange(size)
    base = 8
    inside = (places[:, None] // base == places[None, :] // base) & (
        places[:, None] > places[None, :]
    )
    step = -(system * inside.astype(system.dtype))
    eye = jnp.eye(size, dtype=system.dtype)
    result = eye + step
    for _ in range(2):
        step = hi("bij,bjk->bik", step, step)
        result = result + hi("bij,bjk->bik", result, step)
    width = base
    while width < size:
        across = (places[:, None] // (2 * width) == places[None, :] // (2 * width)) & (
            places[:, None] // width != places[None, :] // width
        )
        lower_left = system * across.astype(system.dtype)
        result = result - hi("bij,bjk->bik", result, hi("bij,bjk->bik", lower_left, result))
        width = 2 * width
    return result


@jax.custom_vjp
def unit_lower_inverse(system):
    return masked_power_inverse(system)


def inverse_keep(system):
    inverse = masked_power_inverse(system)
    return inverse, inverse


def inverse_back(inverse, grad):
    turned = jnp.swapaxes(inverse, -1, -2)
    return (-hi("bij,bjk->bik", turned, hi("bij,bjk->bik", grad, turned)),)


unit_lower_inverse.defvjp(inverse_keep, inverse_back)


def block_mixer(query_rows, key_rows, value_rows, beta_rows, log_decay, starts_flag):
    pseudo = key_rows.shape[0]
    span = STEPS * BLOCK
    blocks = pseudo // span
    queries = query_rows.reshape(blocks, BLOCK, DK)
    keys = key_rows.reshape(blocks, span, DK)
    values = value_rows.reshape(blocks, span, DK)
    betas = beta_rows.reshape(blocks, span)
    decays = log_decay.reshape(blocks, span)
    flags = starts_flag.reshape(blocks, span)
    places = jnp.arange(span)
    lower = places[:, None] >= places[None, :]
    strict = (places[:, None] > places[None, :]).astype(jnp.float32)
    identity = jnp.eye(span, dtype=jnp.float32)
    eye_key = jnp.eye(DK, dtype=jnp.float32)

    summed = jnp.cumsum(decays, axis=1)
    segment = jnp.cumsum(flags, axis=1)
    same_doc = (segment[:, :, None] == segment[:, None, :]) & lower
    decay_ratio = jnp.exp(
        jnp.where(same_doc, summed[:, :, None] - summed[:, None, :], 0.0)
    ) * same_doc.astype(jnp.float32)
    from_start = jnp.exp(summed) * (segment == 0.0).astype(jnp.float32)
    key_key = hi("bik,bjk->bij", keys, keys)
    system = identity + betas[:, :, None] * decay_ratio * key_key * strict
    right_side = jnp.concatenate(
        [betas[:, :, None] * values, (betas * from_start)[:, :, None] * keys], 2
    )
    solved = hi("bij,bjk->bik", unit_lower_inverse(system), right_side)
    fresh = solved[:, :, :DK]
    carried = solved[:, :, DK:]
    last_keys = keys * decay_ratio[:, -1, :, None]
    transfer = from_start[:, -1, None, None] * eye_key - hi("bsi,bsj->bij", last_keys, carried)
    offset = hi("bsi,bsj->bij", last_keys, fresh)
    query_key = hi("bqk,bsk->bqs", queries, keys) * decay_ratio[:, STEPS - 1 :: STEPS]
    frame = from_start[:, STEPS - 1 :: STEPS, None] * queries - hi(
        "bqs,bsj->bqj", query_key, carried
    )
    direct = hi("bqs,bsj->bqj", query_key, fresh)

    state = jnp.concatenate([eye_key, jnp.zeros((DK, DK), jnp.float32)], 1)
    states = []
    for index in range(blocks):
        states.append(state)
        state = hi("ij,jk->ik", transfer[index], state) + jnp.concatenate(
            [jnp.zeros((DK, DK), jnp.float32), offset[index]], 1
        )
    states = jnp.stack(states)
    mats = states[:, :, :DK]
    adds = states[:, :, DK:]
    final_mat = state[:, :DK]
    final_add = state[:, DK:]
    query_frame = hi("bqi,bij->bqj", frame, mats)
    partial = hi("bqi,bij->bqj", frame, adds) + direct
    return (
        query_frame.reshape(blocks * BLOCK, DK),
        partial.reshape(blocks * BLOCK, DK),
        final_mat[None],
        final_add[None],
    )


def local(
    tokens_in,
    mixer_norm,
    mix_weight,
    head_gates,
    conv_taps,
    decay_log,
    decay_bias,
    gate_weight,
    out_norm,
    out_weight,
    feed_norm,
    up_weight,
    down_weight,
    doc_lengths,
    out_grad,
):
    row_count = tokens_in.shape[0]
    weight_rows = mix_weight.shape[0]
    head = lax.axis_index("sl") * lax.axis_size("hd") + lax.axis_index("hd")
    length = row_count * HEADS

    head_cols = jnp.concatenate(
        [
            gate_weight.reshape(weight_rows, HEADS, DK),
            mix_weight.reshape(weight_rows, HEADS, PROJ),
            head_gates.reshape(weight_rows, HEADS, STEPS + 1),
            jnp.broadcast_to(mixer_norm[:, None, None], (weight_rows, HEADS, 1)),
        ],
        2,
    )
    head_wide = columns_to_heads(head_cols)
    head_full = head_wide[:, :WIDE]
    gain_one = head_wide[:, WIDE].astype(jnp.float32)
    half = FF // HEADS
    up_cols = jnp.concatenate(
        [
            up_weight[:, :FF].reshape(weight_rows, HEADS, half),
            up_weight[:, FF:].reshape(weight_rows, HEADS, half),
            jnp.broadcast_to(feed_norm[:, None, None], (weight_rows, HEADS, 1)),
        ],
        2,
    )
    up_wide = columns_to_heads(up_cols)
    up_full = up_wide[:, : 2 * half]
    gain_two = up_wide[:, 2 * half].astype(jnp.float32)
    tap_width = conv_taps.shape[1]
    tap_row = jnp.pad(conv_taps.reshape(1, -1), ((0, 0), (0, D - CONV * tap_width)))
    out_full, down_full, tap_rows = rows_to_heads((out_weight, down_weight, tap_row))
    conv_part = jnp.transpose(
        tap_rows[:, : CONV * tap_width].reshape(-1, CONV, tap_width), (1, 0, 2)
    ).reshape(CONV, -1).astype(jnp.float32)

    x_float = tokens_in.astype(jnp.float32)
    normed_float, norm_one_back = jax.vjp(rms_norm, x_float, gain_one)
    normed_one = group_gather(normed_float.astype(jnp.bfloat16), True)
    tokens_all = group_gather(tokens_in, True)
    head_out = bf_product(normed_one, head_full)
    out_gate = head_out[:, :DK]
    proj_head = head_out[:, DK : DK + PROJ].astype(jnp.bfloat16)
    scalar_rows = head_out[:, DK + PROJ :].astype(jnp.bfloat16).astype(jnp.float32)

    rim_rows = from_behind(proj_head[length - (CONV - 1) :], "sh", 1)
    padded = jnp.concatenate([rim_rows, proj_head], 0).astype(jnp.float32)
    starts = jnp.cumsum(doc_lengths) - doc_lengths
    positions = lax.axis_index("sh") * length + jnp.arange(length, dtype=jnp.int32)
    starts_flag = jnp.any(positions[:, None] == starts[None, :], 1).astype(jnp.float32)
    doc_begin = jnp.max(jnp.where(starts[None, :] <= positions[:, None], starts[None, :], 0), 1)
    tap_masks = [
        (positions - (CONV - 1) + tap_index >= doc_begin).astype(jnp.float32)
        for tap_index in range(CONV)
    ]
    pseudo_flag = jnp.concatenate(
        [starts_flag[:, None], jnp.zeros((length, STEPS - 1), jnp.float32)], 1
    ).reshape(-1)
    rate_log = lax.dynamic_index_in_dim(decay_log, head, 0, False)
    bias_part = lax.dynamic_index_in_dim(decay_bias, head, 0, False)

    def mixer_inputs(padded, scalar_rows, conv_part, rate_log, bias_part):
        convolved = jnp.zeros_like(padded[CONV - 1 :])
        for tap_index in range(CONV):
            convolved = (
                convolved
                + conv_part[tap_index]
                * padded[tap_index : tap_index + length]
                * tap_masks[tap_index][:, None]
            )
        activated = jax.nn.silu(convolved).reshape(length, 1 + 2 * STEPS, DK)
        query_rows = unit_norm(activated[:, 0])
        key_rows = unit_norm(activated[:, 1 : 1 + STEPS]).reshape(STEPS * length, DK)
        value_rows = activated[:, 1 + STEPS :].reshape(STEPS * length, DK)
        beta_rows = jax.nn.sigmoid(scalar_rows[:, :STEPS]).reshape(STEPS * length)
        log_rate = -jnp.exp(rate_log) * jax.nn.softplus(scalar_rows[:, STEPS] + bias_part)
        log_decay = jnp.concatenate(
            [log_rate[:, None], jnp.zeros((length, STEPS - 1), jnp.float32)], 1
        ).reshape(STEPS * length)
        return (query_rows, key_rows, value_rows, beta_rows, log_decay)

    def recurrence(query_rows, key_rows, value_rows, beta_rows, log_decay):
        return block_mixer(query_rows, key_rows, value_rows, beta_rows, log_decay, pseudo_flag)

    prepared, inputs_back = jax.vjp(
        mixer_inputs, padded, scalar_rows, conv_part, rate_log, bias_part
    )
    (query_frame, partial_value_rows, transfer, offset), recurrence_back = jax.vjp(
        recurrence, *prepared
    )
    grad_rows = group_gather(out_grad)
    grad_rows, query_frame, partial_value_rows, transfer, offset = lax.optimization_barrier(
        (grad_rows, query_frame, partial_value_rows, transfer, offset)
    )
    identity = jnp.eye(DK, dtype=jnp.float32)[None]
    zeros_state = jnp.zeros((1, DK, DK), jnp.float32)
    prefix_map, incoming_state = carried_in(
        (transfer, offset), "sh", compose, (identity, zeros_state), False
    )
    mixer_result = partial_value_rows + hi("zy,yi->zi", query_frame, incoming_state[0])
    mixer_low = mixer_result.astype(jnp.bfloat16).astype(jnp.float32)
    gated, gate_back = jax.vjp(gate_norm, mixer_low, out_gate, out_norm)
    gated_rows = gated.astype(jnp.bfloat16)
    branch_all = group_all_sum(bf_product(gated_rows, out_full), 4)
    middle_all = tokens_all.astype(jnp.float32) + branch_all.astype(jnp.float32)
    middle = lax.dynamic_slice_in_dim(middle_all, head * row_count, row_count, 0)
    normed_two = rms_norm(middle_all, gain_two).astype(jnp.bfloat16)
    normed_mid, norm_two_back = jax.vjp(rms_norm, middle, gain_two)
    gate_up = bf_product(normed_two, up_full)
    hidden_float, swiglu_back = jax.vjp(swiglu, gate_up)
    hidden = hidden_float.astype(jnp.bfloat16)
    feed_partial = bf_product(hidden, down_full)

    grad_out = out_grad.astype(jnp.float32)
    grad_hidden = bf_product(grad_rows, down_full.T)
    grad_down_partial = bf_product(hidden.T, grad_rows)
    (grad_gate_up,) = swiglu_back(grad_hidden)
    grad_gate_up = grad_gate_up.astype(jnp.bfloat16)
    grad_normed_two = group_scatter(bf_product(grad_gate_up, up_full.T))
    grad_mid_norm, grad_gain_two = norm_two_back(grad_normed_two)
    grad_up_payload = jnp.concatenate(
        [bf_product(normed_two.T, grad_gate_up), grad_gain_two[:, None]], 1
    )
    grad_middle = grad_out + grad_mid_norm
    feed_partial, grad_up_payload, grad_down_partial, grad_branch_low = lax.optimization_barrier(
        (feed_partial, grad_up_payload, grad_down_partial, grad_middle.astype(jnp.bfloat16))
    )
    grad_up_cols = heads_to_columns(grad_up_payload, True)
    grad_up = jnp.concatenate(
        [
            grad_up_cols[:, :, :half].reshape(weight_rows, FF),
            grad_up_cols[:, :, half : 2 * half].reshape(weight_rows, FF),
        ],
        1,
    )
    grad_branch = group_gather(grad_branch_low)
    feed_partial, grad_down_partial, grad_branch = lax.optimization_barrier(
        (feed_partial, grad_down_partial, grad_branch)
    )
    feed_sum = group_scatter(feed_partial)
    grad_gated = bf_product(grad_branch, out_full.T)
    grad_down, grad_outw = heads_to_rows((grad_down_partial, bf_product(gated_rows.T, grad_branch)))
    grad_mixer, grad_gate, grad_out_norm = gate_back(grad_gated)
    grad_gate = grad_gate.astype(jnp.bfloat16)
    head_gradients = grad_mixer.astype(jnp.bfloat16).astype(jnp.float32)
    local_adjoint = hi("dc,dr->cr", query_frame, head_gradients)[None]
    transfer_turned = jnp.transpose(transfer, (0, 2, 1))
    later_map, state_gradient = carried_in(
        (transfer_turned, local_adjoint), "sh", compose, (identity, zeros_state), True
    )
    basis_gradient = hi("nu,wu->nw", head_gradients, incoming_state[0])
    transfer_gradient = hi("tnf,tmf->tnm", state_gradient, incoming_state)
    grad_prepared = recurrence_back(
        (basis_gradient, head_gradients, transfer_gradient, state_gradient)
    )
    grad_prepared, feed_sum, grad_up_cols, grad_down, grad_outw = lax.optimization_barrier(
        (grad_prepared, feed_sum, grad_up_cols, grad_down, grad_outw)
    )
    layer_out = (middle + feed_sum).astype(jnp.bfloat16)
    grad_padded, grad_scalars, grad_conv, grad_rate, grad_bias = inputs_back(grad_prepared)
    rim_grad = from_behind(grad_padded[: CONV - 1], "sh", -1)
    own_grad = grad_padded[CONV - 1 :]
    grad_proj = jnp.concatenate(
        [own_grad[: length - (CONV - 1)], own_grad[length - (CONV - 1) :] + rim_grad], 0
    )
    grad_head = jnp.concatenate(
        [grad_gate, grad_proj.astype(jnp.bfloat16), grad_scalars.astype(jnp.bfloat16)], 1
    )
    grad_normed_one = group_scatter(bf_product(grad_head, head_full.T), True)
    grad_x_norm, grad_gain_one = norm_one_back(grad_normed_one)
    grad_head_cols = heads_to_columns(
        jnp.concatenate([bf_product(normed_one.T, grad_head), grad_gain_one[:, None]], 1)
    )
    grad_gatew = grad_head_cols[:, :, :DK].reshape(weight_rows, D)
    grad_mixw = grad_head_cols[:, :, DK : DK + PROJ].reshape(weight_rows, HEADS * PROJ)
    grad_gatesw = grad_head_cols[:, :, DK + PROJ : WIDE].reshape(
        weight_rows, HEADS * (STEPS + 1)
    )
    grad_tokens = (grad_middle + grad_x_norm).astype(jnp.bfloat16)
    (conv_grad,) = heads_to_rows((jnp.transpose(grad_conv),))
    conv_grad = jnp.transpose(conv_grad)
    one_hot = (jnp.arange(HEADS) == head).astype(jnp.float32)
    small_sums = all_sum(
        jnp.concatenate([one_hot * grad_rate, one_hot * grad_bias, grad_out_norm])
    )
    return (
        layer_out,
        grad_tokens,
        jnp.sum(grad_head_cols[:, :, WIDE], 1),
        grad_mixw,
        grad_gatesw,
        conv_grad,
        small_sums[:HEADS],
        small_sums[HEADS : 2 * HEADS],
        grad_gatew,
        small_sums[2 * HEADS :],
        grad_outw,
        jnp.sum(grad_up_cols[:, :, 2 * half], 1),
        grad_up,
        grad_down,
    )


def solution(mesh):
    seq = mesh.shape["seq"]
    across = mesh.shape["head"]
    inner = HEADS // across
    grid = Mesh(
        np.asarray(mesh.devices).reshape(seq // inner, inner, across), ("sh", "sl", "hd")
    )
    rows = P(ALL, None)
    flat = P(ALL)
    return jax.shard_map(
        local,
        mesh=grid,
        in_specs=(
            rows,
            flat,
            rows,
            rows,
            P(None, ALL),
            P(),
            P(),
            rows,
            P(),
            rows,
            flat,
            rows,
            rows,
            P(),
            rows,
        ),
        out_specs=(
            rows,
            rows,
            flat,
            rows,
            rows,
            P(None, ALL),
            P(),
            P(),
            rows,
            P(),
            rows,
            flat,
            rows,
            rows,
        ),
        check_vma=False,
    )
```

```python
import jax
import jax.numpy as jnp
import numpy as np
from jax import lax
from jax.experimental import pallas as pl
from jax.experimental.pallas import tpu as pltpu
from jax.sharding import Mesh
from jax.sharding import PartitionSpec as P

D = 1024
HEADS = 8
DK = 128
FF = 2816
STEPS = 2
CONV = 4
BLOCK = 64
PROJ = (1 + 2 * STEPS) * DK
WIDE = DK + PROJ + STEPS + 1

EPS = 1e-06
HIGH_ACCURACY = lax.Precision.HIGH

GROUP = ("sl", "hd")
ALL = ("sh", "sl", "hd")


def from_behind(shard, axis, by):
    peers = lax.axis_size(axis)
    pairs = [(i, i + by) for i in range(peers) if 0 <= i + by < peers]
    return lax.ppermute(shard, axis, pairs)


def gather_kernel(count, own_ref, out_ref, slots, send_sems, recv_sems):
    me = lax.axis_index("sh")
    across = lax.axis_index("sl")
    inner = lax.axis_index("hd")
    barrier = pltpu.get_barrier_semaphore()

    def peer(index):
        return (index, across, inner)

    def greet(index, carry):
        @pl.when(index != me)
        def _():
            pl.semaphore_signal(
                barrier, inc=1, device_id=peer(index), device_id_type=pl.DeviceIdType.MESH
            )

        return carry

    lax.fori_loop(0, count, greet, 0)
    pl.semaphore_wait(barrier, count - 1)

    def copy_to(index):
        return pltpu.make_async_remote_copy(
            src_ref=own_ref,
            dst_ref=slots.at[me],
            send_sem=send_sems.at[index],
            recv_sem=recv_sems.at[me],
            device_id=peer(index),
            device_id_type=pl.DeviceIdType.MESH,
        )

    def copy_from(index):
        return pltpu.make_async_remote_copy(
            src_ref=own_ref,
            dst_ref=slots.at[index],
            send_sem=send_sems.at[index],
            recv_sem=recv_sems.at[index],
            device_id=peer(index),
            device_id_type=pl.DeviceIdType.MESH,
        )

    def send(index, carry):
        @pl.when(index != me)
        def _():
            copy_to(index).start()

        return carry

    lax.fori_loop(0, count, send, 0)
    slots[me] = own_ref[...]

    def finish(index, carry):
        @pl.when(index != me)
        def _():
            copy_to(index).wait_send()
            copy_from(index).wait_recv()

        return carry

    lax.fori_loop(0, count, finish, 0)
    out_ref[...] = slots[...]


def scatter_kernel(count, own_ref, out_ref, slots, send_sems, recv_sems):
    me = lax.axis_index("sh")
    across = lax.axis_index("sl")
    inner = lax.axis_index("hd")
    barrier = pltpu.get_barrier_semaphore()

    def peer(index):
        return (index, across, inner)

    def greet(index, carry):
        @pl.when(index != me)
        def _():
            pl.semaphore_signal(
                barrier, inc=1, device_id=peer(index), device_id_type=pl.DeviceIdType.MESH
            )

        return carry

    lax.fori_loop(0, count, greet, 0)
    pl.semaphore_wait(barrier, count - 1)

    def copy_to(index):
        return pltpu.make_async_remote_copy(
            src_ref=own_ref.at[index],
            dst_ref=slots.at[me],
            send_sem=send_sems.at[index],
            recv_sem=recv_sems.at[me],
            device_id=peer(index),
            device_id_type=pl.DeviceIdType.MESH,
        )

    def copy_from(index):
        return pltpu.make_async_remote_copy(
            src_ref=own_ref.at[index],
            dst_ref=slots.at[index],
            send_sem=send_sems.at[index],
            recv_sem=recv_sems.at[index],
            device_id=peer(index),
            device_id_type=pl.DeviceIdType.MESH,
        )

    def send(index, carry):
        @pl.when(index != me)
        def _():
            copy_to(index).start()

        return carry

    lax.fori_loop(0, count, send, 0)
    slots[me] = own_ref[me]

    def finish(index, carry):
        @pl.when(index != me)
        def _():
            copy_to(index).wait_send()
            copy_from(index).wait_recv()

        return carry

    lax.fori_loop(0, count, finish, 0)
    out_ref[...] = jnp.sum(slots[...].astype(jnp.float32), axis=0)


def group_sum_scatter(partial, ident):
    count = lax.axis_size("sh")
    pieces = partial.astype(jnp.bfloat16).reshape((count, partial.shape[0] // count) + partial.shape[1:])
    return pl.pallas_call(
        lambda *refs: scatter_kernel(count, *refs),
        out_shape=jax.ShapeDtypeStruct(pieces.shape[1:], jnp.float32),
        in_specs=[pl.BlockSpec(memory_space=pltpu.VMEM)],
        out_specs=pl.BlockSpec(memory_space=pltpu.VMEM),
        scratch_shapes=[
            pltpu.VMEM(pieces.shape, jnp.bfloat16),
            pltpu.SemaphoreType.DMA((count,)),
            pltpu.SemaphoreType.DMA((count,)),
        ],
        compiler_params=pltpu.CompilerParams(collective_id=ident, has_side_effects=True),
    )(pieces)


def group_maps(block, ident):
    count = lax.axis_size("sh")
    return pl.pallas_call(
        lambda *refs: gather_kernel(count, *refs),
        out_shape=jax.ShapeDtypeStruct((count,) + block.shape, block.dtype),
        in_specs=[pl.BlockSpec(memory_space=pltpu.VMEM)],
        out_specs=pl.BlockSpec(memory_space=pltpu.VMEM),
        scratch_shapes=[
            pltpu.VMEM((count,) + block.shape, block.dtype),
            pltpu.SemaphoreType.DMA((count,)),
            pltpu.SemaphoreType.DMA((count,)),
        ],
        compiler_params=pltpu.CompilerParams(collective_id=ident, has_side_effects=True),
    )(block)


def carried_in(shard, axis, join, neutral, backward):
    count = lax.axis_size(axis)
    place = lax.axis_index(axis)
    ahead = count - 1 - place if backward else place
    both = group_maps(jnp.stack(shard).astype(jnp.bfloat16), 2 if backward else 1)
    gathered = (both[:, 0], both[:, 1])
    state = jax.tree.map(lambda a, e: jnp.zeros_like(a) + jnp.asarray(e, a.dtype), shard, neutral)

    def one(turn, state):
        source = count - 1 - turn if backward else turn
        return join(
            state,
            jax.tree.map(
                lambda a, own: lax.dynamic_index_in_dim(a, source, 0, False).astype(own.dtype),
                gathered,
                shard,
            ),
        )

    return lax.fori_loop(0, ahead, one, state)


def flat_place():
    return (
        lax.axis_index("sh") * lax.axis_size("sl") + lax.axis_index("sl")
    ) * lax.axis_size("hd") + lax.axis_index("hd")


def device_of(index):
    inner = lax.axis_size("sl") * lax.axis_size("hd")
    return (index // inner, (index // lax.axis_size("hd")) % lax.axis_size("sl"), index % lax.axis_size("hd"))


def sum_kernel(count, own_ref, out_ref, slots, send_sems, recv_sems):
    me = flat_place()
    barrier = pltpu.get_barrier_semaphore()

    def greet(index, carry):
        @pl.when(index != me)
        def _():
            pl.semaphore_signal(
                barrier, inc=1, device_id=device_of(index), device_id_type=pl.DeviceIdType.MESH
            )

        return carry

    lax.fori_loop(0, count, greet, 0)
    pl.semaphore_wait(barrier, count - 1)

    def copy_to(index):
        return pltpu.make_async_remote_copy(
            src_ref=own_ref,
            dst_ref=slots.at[me],
            send_sem=send_sems.at[index],
            recv_sem=recv_sems.at[me],
            device_id=device_of(index),
            device_id_type=pl.DeviceIdType.MESH,
        )

    def copy_from(index):
        return pltpu.make_async_remote_copy(
            src_ref=own_ref,
            dst_ref=slots.at[index],
            send_sem=send_sems.at[index],
            recv_sem=recv_sems.at[index],
            device_id=device_of(index),
            device_id_type=pl.DeviceIdType.MESH,
        )

    def send(index, carry):
        @pl.when(index != me)
        def _():
            copy_to(index).start()

        return carry

    lax.fori_loop(0, count, send, 0)
    slots[me] = own_ref[...]

    def finish(index, carry):
        @pl.when(index != me)
        def _():
            copy_to(index).wait_send()
            copy_from(index).wait_recv()

        return carry

    lax.fori_loop(0, count, finish, 0)
    out_ref[...] = jnp.sum(slots[...], axis=0)


def all_sum(vector):
    count = lax.axis_size("sh") * lax.axis_size("sl") * lax.axis_size("hd")
    size = vector.shape[0]
    lanes = 128
    tile = 8 * lanes
    padded = -(-size // tile) * tile
    block = jnp.pad(vector, (0, padded - size)).reshape(padded // lanes, lanes)
    total = pl.pallas_call(
        lambda *refs: sum_kernel(count, *refs),
        out_shape=jax.ShapeDtypeStruct(block.shape, jnp.float32),
        in_specs=[pl.BlockSpec(memory_space=pltpu.VMEM)],
        out_specs=pl.BlockSpec(memory_space=pltpu.VMEM),
        scratch_shapes=[
            pltpu.VMEM((count,) + block.shape, jnp.float32),
            pltpu.SemaphoreType.DMA((count,)),
            pltpu.SemaphoreType.DMA((count,)),
        ],
        compiler_params=pltpu.CompilerParams(collective_id=0, has_side_effects=True),
    )(block)
    return total.reshape(-1)[:size]


def rms_norm(values, scale_gain):
    return values * lax.rsqrt(jnp.mean(values * values, axis=-1, keepdims=True) + EPS) * scale_gain


def unit_norm(values):
    return values * lax.rsqrt(jnp.sum(values * values, axis=-1, keepdims=True) + EPS)


def bf_product(first_mat, second_mat):
    return jnp.dot(first_mat, second_mat, preferred_element_type=jnp.float32)


def hi(spec, *arrays):
    return jnp.einsum(spec, *arrays, precision=HIGH_ACCURACY)


def compose(early_pair, late_pair):
    early_mat, early_add = early_pair
    late_mat, late_add = late_pair
    joined = hi("hij,hjk->hik", late_mat, early_mat)
    shifted = hi("hij,hjk->hik", late_mat, early_add) + late_add
    return (joined, shifted)


def gate_norm(values, out_gate, scale_gain):
    return rms_norm(values, scale_gain) * jax.nn.silu(out_gate)


def swiglu(gate_up):
    half = gate_up.shape[1] // 2
    return jax.nn.silu(gate_up[:, :half]) * gate_up[:, half:]


def owner_pairs(inverse):
    groups = lax.axis_size("sh")
    pairs = [(g * HEADS + t, t * groups + g) for g in range(groups) for t in range(HEADS)]
    return [(b, a) for a, b in pairs] if inverse else pairs


def rows_to_heads(blocks):
    groups = lax.axis_size("sh")
    width = blocks[0].shape[1]
    used = sum(b.shape[0] for b in blocks)
    least = (1 << 20) // (groups * width * 2) + 1
    rows = -(-max(used, least) // 8) * 8
    packed = jnp.concatenate(
        list(blocks) + [jnp.zeros((rows - used, width), blocks[0].dtype)], 0
    )
    moved = lax.ppermute(packed, ALL, owner_pairs(True))
    full = lax.all_gather(moved, "sh", axis=0, tiled=False)
    parts = []
    first = 0
    for block in blocks:
        size = block.shape[0]
        parts.append(full[:, first : first + size].reshape(groups * size, width))
        first += size
    return parts


def heads_to_rows(partials):
    groups = lax.axis_size("sh")
    pieces = [
        p.astype(jnp.bfloat16).reshape((groups, p.shape[0] // groups) + p.shape[1:])
        for p in partials
    ]
    joined = jnp.concatenate(pieces, 1)
    joined = joined.reshape((-1,) + joined.shape[2:])
    summed = lax.psum_scatter(joined, "sh", scatter_dimension=0, tiled=True)
    moved = lax.ppermute(summed, ALL, owner_pairs(False)).astype(jnp.float32)
    parts = []
    first = 0
    for piece in pieces:
        size = piece.shape[1]
        parts.append(moved[first : first + size])
        first += size
    return parts


def columns_to_heads(local_cols):
    per_head = jnp.transpose(local_cols, (1, 0, 2))
    mine = lax.all_to_all(per_head, GROUP, 0, 0, tiled=True)
    mine = mine.reshape(-1, mine.shape[-1])
    return lax.all_gather(mine, "sh", axis=0, tiled=True)


def heads_to_columns(partial, direct=False):
    low = partial.astype(jnp.bfloat16)
    if direct:
        summed = group_sum_scatter(low, 3).astype(jnp.bfloat16)
    else:
        summed = lax.psum_scatter(low, "sh", scatter_dimension=0, tiled=True)
    summed = summed.reshape(HEADS, -1, summed.shape[-1])
    back = lax.all_to_all(summed, GROUP, 0, 0, tiled=True)
    return jnp.transpose(back, (1, 0, 2)).astype(jnp.float32)


def group_gather(rows, direct=False):
    if direct:
        copies = jnp.broadcast_to(rows[None], (HEADS,) + rows.shape)
        moved = lax.all_to_all(copies, GROUP, 0, 0, tiled=True)
        return moved.reshape((-1,) + rows.shape[1:])
    return lax.all_gather(rows, GROUP, axis=0, tiled=True)


def group_scatter(partial, direct=False):
    low = partial.astype(jnp.bfloat16)
    if direct:
        pieces = low.reshape((HEADS, low.shape[0] // HEADS) + low.shape[1:])
        moved = lax.all_to_all(pieces, GROUP, 0, 0, tiled=True)
        return jnp.sum(moved.astype(jnp.float32), 0)
    return lax.psum_scatter(low, GROUP, scatter_dimension=0, tiled=True).astype(jnp.float32)


def masked_power_inverse(system):
    size = system.shape[-1]
    places = jnp.arange(size)
    base = 8
    inside = (places[:, None] // base == places[None, :] // base) & (
        places[:, None] > places[None, :]
    )
    step = -(system * inside.astype(system.dtype))
    eye = jnp.eye(size, dtype=system.dtype)
    result = eye + step
    for _ in range(2):
        step = hi("bij,bjk->bik", step, step)
        result = result + hi("bij,bjk->bik", result, step)
    width = base
    while width < size:
        across = (places[:, None] // (2 * width) == places[None, :] // (2 * width)) & (
            places[:, None] // width != places[None, :] // width
        )
        lower_left = system * across.astype(system.dtype)
        result = result - hi("bij,bjk->bik", result, hi("bij,bjk->bik", lower_left, result))
        width = 2 * width
    return result


@jax.custom_vjp
def unit_lower_inverse(system):
    return masked_power_inverse(system)


def inverse_keep(system):
    inverse = masked_power_inverse(system)
    return inverse, inverse


def inverse_back(inverse, grad):
    turned = jnp.swapaxes(inverse, -1, -2)
    return (-hi("bij,bjk->bik", turned, hi("bij,bjk->bik", grad, turned)),)


unit_lower_inverse.defvjp(inverse_keep, inverse_back)


def block_mixer(query_rows, key_rows, value_rows, beta_rows, log_decay, starts_flag):
    pseudo = key_rows.shape[0]
    span = STEPS * BLOCK
    blocks = pseudo // span
    queries = query_rows.reshape(blocks, BLOCK, DK)
    keys = key_rows.reshape(blocks, span, DK)
    values = value_rows.reshape(blocks, span, DK)
    betas = beta_rows.reshape(blocks, span)
    decays = log_decay.reshape(blocks, span)
    flags = starts_flag.reshape(blocks, span)
    places = jnp.arange(span)
    lower = places[:, None] >= places[None, :]
    strict = (places[:, None] > places[None, :]).astype(jnp.float32)
    identity = jnp.eye(span, dtype=jnp.float32)
    eye_key = jnp.eye(DK, dtype=jnp.float32)

    summed = jnp.cumsum(decays, axis=1)
    segment = jnp.cumsum(flags, axis=1)
    same_doc = (segment[:, :, None] == segment[:, None, :]) & lower
    decay_ratio = jnp.exp(
        jnp.where(same_doc, summed[:, :, None] - summed[:, None, :], 0.0)
    ) * same_doc.astype(jnp.float32)
    from_start = jnp.exp(summed) * (segment == 0.0).astype(jnp.float32)
    key_key = hi("bik,bjk->bij", keys, keys)
    system = identity + betas[:, :, None] * decay_ratio * key_key * strict
    right_side = jnp.concatenate(
        [betas[:, :, None] * values, (betas * from_start)[:, :, None] * keys], 2
    )
    solved = hi("bij,bjk->bik", unit_lower_inverse(system), right_side)
    fresh = solved[:, :, :DK]
    carried = solved[:, :, DK:]
    last_keys = keys * decay_ratio[:, -1, :, None]
    transfer = from_start[:, -1, None, None] * eye_key - hi("bsi,bsj->bij", last_keys, carried)
    offset = hi("bsi,bsj->bij", last_keys, fresh)
    query_key = hi("bqk,bsk->bqs", queries, keys) * decay_ratio[:, STEPS - 1 :: STEPS]
    frame = from_start[:, STEPS - 1 :: STEPS, None] * queries - hi(
        "bqs,bsj->bqj", query_key, carried
    )
    direct = hi("bqs,bsj->bqj", query_key, fresh)

    state = jnp.concatenate([eye_key, jnp.zeros((DK, DK), jnp.float32)], 1)
    states = []
    for index in range(blocks):
        states.append(state)
        state = hi("ij,jk->ik", transfer[index], state) + jnp.concatenate(
            [jnp.zeros((DK, DK), jnp.float32), offset[index]], 1
        )
    states = jnp.stack(states)
    mats = states[:, :, :DK]
    adds = states[:, :, DK:]
    final_mat = state[:, :DK]
    final_add = state[:, DK:]
    query_frame = hi("bqi,bij->bqj", frame, mats)
    partial = hi("bqi,bij->bqj", frame, adds) + direct
    return (
        query_frame.reshape(blocks * BLOCK, DK),
        partial.reshape(blocks * BLOCK, DK),
        final_mat[None],
        final_add[None],
    )


def local(
    tokens_in,
    mixer_norm,
    mix_weight,
    head_gates,
    conv_taps,
    decay_log,
    decay_bias,
    gate_weight,
    out_norm,
    out_weight,
    feed_norm,
    up_weight,
    down_weight,
    doc_lengths,
    out_grad,
):
    row_count = tokens_in.shape[0]
    weight_rows = mix_weight.shape[0]
    head = lax.axis_index("sl") * lax.axis_size("hd") + lax.axis_index("hd")
    length = row_count * HEADS

    head_cols = jnp.concatenate(
        [
            gate_weight.reshape(weight_rows, HEADS, DK),
            mix_weight.reshape(weight_rows, HEADS, PROJ),
            head_gates.reshape(weight_rows, HEADS, STEPS + 1),
            jnp.broadcast_to(mixer_norm[:, None, None], (weight_rows, HEADS, 1)),
        ],
        2,
    )
    head_wide = columns_to_heads(head_cols)
    head_full = head_wide[:, :WIDE]
    gain_one = head_wide[:, WIDE].astype(jnp.float32)
    half = FF // HEADS
    up_cols = jnp.concatenate(
        [
            up_weight[:, :FF].reshape(weight_rows, HEADS, half),
            up_weight[:, FF:].reshape(weight_rows, HEADS, half),
            jnp.broadcast_to(feed_norm[:, None, None], (weight_rows, HEADS, 1)),
        ],
        2,
    )
    up_wide = columns_to_heads(up_cols)
    up_full = up_wide[:, : 2 * half]
    gain_two = up_wide[:, 2 * half].astype(jnp.float32)
    tap_width = conv_taps.shape[1]
    tap_row = jnp.pad(conv_taps.reshape(1, -1), ((0, 0), (0, D - CONV * tap_width)))
    out_full, down_full, tap_rows = rows_to_heads((out_weight, down_weight, tap_row))
    conv_part = jnp.transpose(
        tap_rows[:, : CONV * tap_width].reshape(-1, CONV, tap_width), (1, 0, 2)
    ).reshape(CONV, -1).astype(jnp.float32)

    x_float = tokens_in.astype(jnp.float32)
    normed_float, norm_one_back = jax.vjp(rms_norm, x_float, gain_one)
    normed_one = group_gather(normed_float.astype(jnp.bfloat16), True)
    head_out = bf_product(normed_one, head_full)
    out_gate = head_out[:, :DK]
    proj_head = head_out[:, DK : DK + PROJ].astype(jnp.bfloat16)
    scalar_rows = head_out[:, DK + PROJ :].astype(jnp.bfloat16).astype(jnp.float32)

    rim_rows = from_behind(proj_head[length - (CONV - 1) :], "sh", 1)
    padded = jnp.concatenate([rim_rows, proj_head], 0).astype(jnp.float32)
    starts = jnp.cumsum(doc_lengths) - doc_lengths
    positions = lax.axis_index("sh") * length + jnp.arange(length, dtype=jnp.int32)
    starts_flag = jnp.any(positions[:, None] == starts[None, :], 1).astype(jnp.float32)
    doc_begin = jnp.max(jnp.where(starts[None, :] <= positions[:, None], starts[None, :], 0), 1)
    tap_masks = [
        (positions - (CONV - 1) + tap_index >= doc_begin).astype(jnp.float32)
        for tap_index in range(CONV)
    ]
    pseudo_flag = jnp.concatenate(
        [starts_flag[:, None], jnp.zeros((length, STEPS - 1), jnp.float32)], 1
    ).reshape(-1)
    rate_log = lax.dynamic_index_in_dim(decay_log, head, 0, False)
    bias_part = lax.dynamic_index_in_dim(decay_bias, head, 0, False)

    def mixer_inputs(padded, scalar_rows, conv_part, rate_log, bias_part):
        convolved = jnp.zeros_like(padded[CONV - 1 :])
        for tap_index in range(CONV):
            convolved = (
                convolved
                + conv_part[tap_index]
                * padded[tap_index : tap_index + length]
                * tap_masks[tap_index][:, None]
            )
        activated = jax.nn.silu(convolved).reshape(length, 1 + 2 * STEPS, DK)
        query_rows = unit_norm(activated[:, 0])
        key_rows = unit_norm(activated[:, 1 : 1 + STEPS]).reshape(STEPS * length, DK)
        value_rows = activated[:, 1 + STEPS :].reshape(STEPS * length, DK)
        beta_rows = jax.nn.sigmoid(scalar_rows[:, :STEPS]).reshape(STEPS * length)
        log_rate = -jnp.exp(rate_log) * jax.nn.softplus(scalar_rows[:, STEPS] + bias_part)
        log_decay = jnp.concatenate(
            [log_rate[:, None], jnp.zeros((length, STEPS - 1), jnp.float32)], 1
        ).reshape(STEPS * length)
        return (query_rows, key_rows, value_rows, beta_rows, log_decay)

    def recurrence(query_rows, key_rows, value_rows, beta_rows, log_decay):
        return block_mixer(query_rows, key_rows, value_rows, beta_rows, log_decay, pseudo_flag)

    prepared, inputs_back = jax.vjp(
        mixer_inputs, padded, scalar_rows, conv_part, rate_log, bias_part
    )
    (query_frame, partial_value_rows, transfer, offset), recurrence_back = jax.vjp(
        recurrence, *prepared
    )
    grad_rows = group_gather(out_grad)
    grad_rows, query_frame, partial_value_rows, transfer, offset = lax.optimization_barrier(
        (grad_rows, query_frame, partial_value_rows, transfer, offset)
    )
    identity = jnp.eye(DK, dtype=jnp.float32)[None]
    zeros_state = jnp.zeros((1, DK, DK), jnp.float32)
    prefix_map, incoming_state = carried_in(
        (transfer, offset), "sh", compose, (identity, zeros_state), False
    )
    mixer_result = partial_value_rows + hi("zy,yi->zi", query_frame, incoming_state[0])
    mixer_low = mixer_result.astype(jnp.bfloat16).astype(jnp.float32)
    gated, gate_back = jax.vjp(gate_norm, mixer_low, out_gate, out_norm)
    gated_rows = gated.astype(jnp.bfloat16)
    middle = x_float + group_scatter(bf_product(gated_rows, out_full))
    normed_mid, norm_two_back = jax.vjp(rms_norm, middle, gain_two)
    normed_two = group_gather(normed_mid.astype(jnp.bfloat16))
    gate_up = bf_product(normed_two, up_full)
    hidden_float, swiglu_back = jax.vjp(swiglu, gate_up)
    hidden = hidden_float.astype(jnp.bfloat16)
    feed_partial = bf_product(hidden, down_full)

    grad_out = out_grad.astype(jnp.float32)
    grad_hidden = bf_product(grad_rows, down_full.T)
    grad_down_partial = bf_product(hidden.T, grad_rows)
    (grad_gate_up,) = swiglu_back(grad_hidden)
    grad_gate_up = grad_gate_up.astype(jnp.bfloat16)
    grad_normed_two = group_scatter(bf_product(grad_gate_up, up_full.T))
    grad_mid_norm, grad_gain_two = norm_two_back(grad_normed_two)
    grad_up_payload = jnp.concatenate(
        [bf_product(normed_two.T, grad_gate_up), grad_gain_two[:, None]], 1
    )
    grad_middle = grad_out + grad_mid_norm
    feed_partial, grad_up_payload, grad_down_partial, grad_branch_low = lax.optimization_barrier(
        (feed_partial, grad_up_payload, grad_down_partial, grad_middle.astype(jnp.bfloat16))
    )
    grad_up_cols = heads_to_columns(grad_up_payload, True)
    grad_up = jnp.concatenate(
        [
            grad_up_cols[:, :, :half].reshape(weight_rows, FF),
            grad_up_cols[:, :, half : 2 * half].reshape(weight_rows, FF),
        ],
        1,
    )
    grad_branch = group_gather(grad_branch_low)
    feed_partial, grad_down_partial, grad_branch = lax.optimization_barrier(
        (feed_partial, grad_down_partial, grad_branch)
    )
    feed_sum = group_scatter(feed_partial)
    grad_gated = bf_product(grad_branch, out_full.T)
    grad_down, grad_outw = heads_to_rows((grad_down_partial, bf_product(gated_rows.T, grad_branch)))
    grad_mixer, grad_gate, grad_out_norm = gate_back(grad_gated)
    grad_gate = grad_gate.astype(jnp.bfloat16)
    head_gradients = grad_mixer.astype(jnp.bfloat16).astype(jnp.float32)
    local_adjoint = hi("dc,dr->cr", query_frame, head_gradients)[None]
    transfer_turned = jnp.transpose(transfer, (0, 2, 1))
    later_map, state_gradient = carried_in(
        (transfer_turned, local_adjoint), "sh", compose, (identity, zeros_state), True
    )
    basis_gradient = hi("nu,wu->nw", head_gradients, incoming_state[0])
    transfer_gradient = hi("tnf,tmf->tnm", state_gradient, incoming_state)
    grad_prepared = recurrence_back(
        (basis_gradient, head_gradients, transfer_gradient, state_gradient)
    )
    grad_prepared, feed_sum, grad_up_cols, grad_down, grad_outw = lax.optimization_barrier(
        (grad_prepared, feed_sum, grad_up_cols, grad_down, grad_outw)
    )
    layer_out = (middle + feed_sum).astype(jnp.bfloat16)
    grad_padded, grad_scalars, grad_conv, grad_rate, grad_bias = inputs_back(grad_prepared)
    rim_grad = from_behind(grad_padded[: CONV - 1], "sh", -1)
    own_grad = grad_padded[CONV - 1 :]
    grad_proj = jnp.concatenate(
        [own_grad[: length - (CONV - 1)], own_grad[length - (CONV - 1) :] + rim_grad], 0
    )
    grad_head = jnp.concatenate(
        [grad_gate, grad_proj.astype(jnp.bfloat16), grad_scalars.astype(jnp.bfloat16)], 1
    )
    grad_normed_one = group_scatter(bf_product(grad_head, head_full.T), True)
    grad_x_norm, grad_gain_one = norm_one_back(grad_normed_one)
    grad_head_cols = heads_to_columns(
        jnp.concatenate([bf_product(normed_one.T, grad_head), grad_gain_one[:, None]], 1)
    )
    grad_gatew = grad_head_cols[:, :, :DK].reshape(weight_rows, D)
    grad_mixw = grad_head_cols[:, :, DK : DK + PROJ].reshape(weight_rows, HEADS * PROJ)
    grad_gatesw = grad_head_cols[:, :, DK + PROJ : WIDE].reshape(
        weight_rows, HEADS * (STEPS + 1)
    )
    grad_tokens = (grad_middle + grad_x_norm).astype(jnp.bfloat16)
    (conv_grad,) = heads_to_rows((jnp.transpose(grad_conv),))
    conv_grad = jnp.transpose(conv_grad)
    one_hot = (jnp.arange(HEADS) == head).astype(jnp.float32)
    small_sums = all_sum(
        jnp.concatenate([one_hot * grad_rate, one_hot * grad_bias, grad_out_norm])
    )
    return (
        layer_out,
        grad_tokens,
        jnp.sum(grad_head_cols[:, :, WIDE], 1),
        grad_mixw,
        grad_gatesw,
        conv_grad,
        small_sums[:HEADS],
        small_sums[HEADS : 2 * HEADS],
        grad_gatew,
        small_sums[2 * HEADS :],
        grad_outw,
        jnp.sum(grad_up_cols[:, :, 2 * half], 1),
        grad_up,
        grad_down,
    )


def solution(mesh):
    seq = mesh.shape["seq"]
    across = mesh.shape["head"]
    inner = HEADS // across
    grid = Mesh(
        np.asarray(mesh.devices).reshape(seq // inner, inner, across), ("sh", "sl", "hd")
    )
    rows = P(ALL, None)
    flat = P(ALL)
    return jax.shard_map(
        local,
        mesh=grid,
        in_specs=(
            rows,
            flat,
            rows,
            rows,
            P(None, ALL),
            P(),
            P(),
            rows,
            P(),
            rows,
            flat,
            rows,
            rows,
            P(),
            rows,
        ),
        out_specs=(
            rows,
            rows,
            flat,
            rows,
            rows,
            P(None, ALL),
            P(),
            P(),
            rows,
            P(),
            rows,
            flat,
            rows,
            rows,
        ),
        check_vma=False,
    )
```

```python
import jax
import jax.numpy as jnp
import numpy as np
from jax import lax
from jax.experimental import pallas as pl
from jax.experimental.pallas import tpu as pltpu
from jax.sharding import Mesh
from jax.sharding import PartitionSpec as P

D = 1024
HEADS = 8
DK = 128
FF = 2816
STEPS = 2
CONV = 4
BLOCK = 64
PROJ = (1 + 2 * STEPS) * DK
WIDE = DK + PROJ + STEPS + 1

EPS = 1e-06
HIGH_ACCURACY = lax.Precision.HIGH

GROUP = ("sl", "hd")
ALL = ("sh", "sl", "hd")


def from_behind(shard, axis, by):
    peers = lax.axis_size(axis)
    pairs = [(i, i + by) for i in range(peers) if 0 <= i + by < peers]
    return lax.ppermute(shard, axis, pairs)


def gather_kernel(count, own_ref, out_ref, slots, send_sems, recv_sems):
    me = lax.axis_index("sh")
    across = lax.axis_index("sl")
    inner = lax.axis_index("hd")
    barrier = pltpu.get_barrier_semaphore()

    def peer(index):
        return (index, across, inner)

    def greet(index, carry):
        @pl.when(index != me)
        def _():
            pl.semaphore_signal(
                barrier, inc=1, device_id=peer(index), device_id_type=pl.DeviceIdType.MESH
            )

        return carry

    lax.fori_loop(0, count, greet, 0)
    pl.semaphore_wait(barrier, count - 1)

    def copy_to(index):
        return pltpu.make_async_remote_copy(
            src_ref=own_ref,
            dst_ref=slots.at[me],
            send_sem=send_sems.at[index],
            recv_sem=recv_sems.at[me],
            device_id=peer(index),
            device_id_type=pl.DeviceIdType.MESH,
        )

    def copy_from(index):
        return pltpu.make_async_remote_copy(
            src_ref=own_ref,
            dst_ref=slots.at[index],
            send_sem=send_sems.at[index],
            recv_sem=recv_sems.at[index],
            device_id=peer(index),
            device_id_type=pl.DeviceIdType.MESH,
        )

    def send(index, carry):
        @pl.when(index != me)
        def _():
            copy_to(index).start()

        return carry

    lax.fori_loop(0, count, send, 0)
    slots[me] = own_ref[...]

    def finish(index, carry):
        @pl.when(index != me)
        def _():
            copy_to(index).wait_send()
            copy_from(index).wait_recv()

        return carry

    lax.fori_loop(0, count, finish, 0)
    out_ref[...] = slots[...]


def scatter_kernel(count, own_ref, out_ref, slots, send_sems, recv_sems):
    me = lax.axis_index("sh")
    across = lax.axis_index("sl")
    inner = lax.axis_index("hd")
    barrier = pltpu.get_barrier_semaphore()

    def peer(index):
        return (index, across, inner)

    def greet(index, carry):
        @pl.when(index != me)
        def _():
            pl.semaphore_signal(
                barrier, inc=1, device_id=peer(index), device_id_type=pl.DeviceIdType.MESH
            )

        return carry

    lax.fori_loop(0, count, greet, 0)
    pl.semaphore_wait(barrier, count - 1)

    def copy_to(index):
        return pltpu.make_async_remote_copy(
            src_ref=own_ref.at[index],
            dst_ref=slots.at[me],
            send_sem=send_sems.at[index],
            recv_sem=recv_sems.at[me],
            device_id=peer(index),
            device_id_type=pl.DeviceIdType.MESH,
        )

    def copy_from(index):
        return pltpu.make_async_remote_copy(
            src_ref=own_ref.at[index],
            dst_ref=slots.at[index],
            send_sem=send_sems.at[index],
            recv_sem=recv_sems.at[index],
            device_id=peer(index),
            device_id_type=pl.DeviceIdType.MESH,
        )

    def send(index, carry):
        @pl.when(index != me)
        def _():
            copy_to(index).start()

        return carry

    lax.fori_loop(0, count, send, 0)
    slots[me] = own_ref[me]

    def finish(index, carry):
        @pl.when(index != me)
        def _():
            copy_to(index).wait_send()
            copy_from(index).wait_recv()

        return carry

    lax.fori_loop(0, count, finish, 0)
    out_ref[...] = jnp.sum(slots[...].astype(jnp.float32), axis=0)


def group_sum_scatter(partial, ident):
    count = lax.axis_size("sh")
    pieces = partial.astype(jnp.bfloat16).reshape((count, partial.shape[0] // count) + partial.shape[1:])
    return pl.pallas_call(
        lambda *refs: scatter_kernel(count, *refs),
        out_shape=jax.ShapeDtypeStruct(pieces.shape[1:], jnp.float32),
        in_specs=[pl.BlockSpec(memory_space=pltpu.VMEM)],
        out_specs=pl.BlockSpec(memory_space=pltpu.VMEM),
        scratch_shapes=[
            pltpu.VMEM(pieces.shape, jnp.bfloat16),
            pltpu.SemaphoreType.DMA((count,)),
            pltpu.SemaphoreType.DMA((count,)),
        ],
        compiler_params=pltpu.CompilerParams(collective_id=ident, has_side_effects=True),
    )(pieces)


def group_maps(block, ident):
    count = lax.axis_size("sh")
    return pl.pallas_call(
        lambda *refs: gather_kernel(count, *refs),
        out_shape=jax.ShapeDtypeStruct((count,) + block.shape, block.dtype),
        in_specs=[pl.BlockSpec(memory_space=pltpu.VMEM)],
        out_specs=pl.BlockSpec(memory_space=pltpu.VMEM),
        scratch_shapes=[
            pltpu.VMEM((count,) + block.shape, block.dtype),
            pltpu.SemaphoreType.DMA((count,)),
            pltpu.SemaphoreType.DMA((count,)),
        ],
        compiler_params=pltpu.CompilerParams(collective_id=ident, has_side_effects=True),
    )(block)


def carried_in(shard, axis, join, neutral, backward):
    count = lax.axis_size(axis)
    place = lax.axis_index(axis)
    ahead = count - 1 - place if backward else place
    both = group_maps(jnp.stack(shard).astype(jnp.bfloat16), 2 if backward else 1)
    gathered = (both[:, 0], both[:, 1])
    state = jax.tree.map(lambda a, e: jnp.zeros_like(a) + jnp.asarray(e, a.dtype), shard, neutral)

    def one(turn, state):
        source = count - 1 - turn if backward else turn
        return join(
            state,
            jax.tree.map(
                lambda a, own: lax.dynamic_index_in_dim(a, source, 0, False).astype(own.dtype),
                gathered,
                shard,
            ),
        )

    return lax.fori_loop(0, ahead, one, state)


def flat_place():
    return (
        lax.axis_index("sh") * lax.axis_size("sl") + lax.axis_index("sl")
    ) * lax.axis_size("hd") + lax.axis_index("hd")


def device_of(index):
    inner = lax.axis_size("sl") * lax.axis_size("hd")
    return (index // inner, (index // lax.axis_size("hd")) % lax.axis_size("sl"), index % lax.axis_size("hd"))


def sum_kernel(count, own_ref, out_ref, slots, send_sems, recv_sems):
    me = flat_place()
    barrier = pltpu.get_barrier_semaphore()

    def greet(index, carry):
        @pl.when(index != me)
        def _():
            pl.semaphore_signal(
                barrier, inc=1, device_id=device_of(index), device_id_type=pl.DeviceIdType.MESH
            )

        return carry

    lax.fori_loop(0, count, greet, 0)
    pl.semaphore_wait(barrier, count - 1)

    def copy_to(index):
        return pltpu.make_async_remote_copy(
            src_ref=own_ref,
            dst_ref=slots.at[me],
            send_sem=send_sems.at[index],
            recv_sem=recv_sems.at[me],
            device_id=device_of(index),
            device_id_type=pl.DeviceIdType.MESH,
        )

    def copy_from(index):
        return pltpu.make_async_remote_copy(
            src_ref=own_ref,
            dst_ref=slots.at[index],
            send_sem=send_sems.at[index],
            recv_sem=recv_sems.at[index],
            device_id=device_of(index),
            device_id_type=pl.DeviceIdType.MESH,
        )

    def send(index, carry):
        @pl.when(index != me)
        def _():
            copy_to(index).start()

        return carry

    lax.fori_loop(0, count, send, 0)
    slots[me] = own_ref[...]

    def finish(index, carry):
        @pl.when(index != me)
        def _():
            copy_to(index).wait_send()
            copy_from(index).wait_recv()

        return carry

    lax.fori_loop(0, count, finish, 0)
    out_ref[...] = jnp.sum(slots[...], axis=0)


def all_sum(vector):
    count = lax.axis_size("sh") * lax.axis_size("sl") * lax.axis_size("hd")
    size = vector.shape[0]
    lanes = 128
    tile = 8 * lanes
    padded = -(-size // tile) * tile
    block = jnp.pad(vector, (0, padded - size)).reshape(padded // lanes, lanes)
    total = pl.pallas_call(
        lambda *refs: sum_kernel(count, *refs),
        out_shape=jax.ShapeDtypeStruct(block.shape, jnp.float32),
        in_specs=[pl.BlockSpec(memory_space=pltpu.VMEM)],
        out_specs=pl.BlockSpec(memory_space=pltpu.VMEM),
        scratch_shapes=[
            pltpu.VMEM((count,) + block.shape, jnp.float32),
            pltpu.SemaphoreType.DMA((count,)),
            pltpu.SemaphoreType.DMA((count,)),
        ],
        compiler_params=pltpu.CompilerParams(collective_id=0, has_side_effects=True),
    )(block)
    return total.reshape(-1)[:size]


def rms_norm(values, scale_gain):
    return values * lax.rsqrt(jnp.mean(values * values, axis=-1, keepdims=True) + EPS) * scale_gain


def unit_norm(values):
    return values * lax.rsqrt(jnp.sum(values * values, axis=-1, keepdims=True) + EPS)


def bf_product(first_mat, second_mat):
    return jnp.dot(first_mat, second_mat, preferred_element_type=jnp.float32)


def hi(spec, *arrays):
    return jnp.einsum(spec, *arrays, precision=HIGH_ACCURACY)


def compose(early_pair, late_pair):
    early_mat, early_add = early_pair
    late_mat, late_add = late_pair
    joined = hi("hij,hjk->hik", late_mat, early_mat)
    shifted = hi("hij,hjk->hik", late_mat, early_add) + late_add
    return (joined, shifted)


def gate_norm(values, out_gate, scale_gain):
    return rms_norm(values, scale_gain) * jax.nn.silu(out_gate)


def swiglu(gate_up):
    half = gate_up.shape[1] // 2
    return jax.nn.silu(gate_up[:, :half]) * gate_up[:, half:]


def owner_pairs(inverse):
    groups = lax.axis_size("sh")
    pairs = [(g * HEADS + t, t * groups + g) for g in range(groups) for t in range(HEADS)]
    return [(b, a) for a, b in pairs] if inverse else pairs


def rows_to_heads(blocks):
    groups = lax.axis_size("sh")
    width = blocks[0].shape[1]
    used = sum(b.shape[0] for b in blocks)
    least = (1 << 20) // (groups * width * 2) + 1
    rows = -(-max(used, least) // 8) * 8
    packed = jnp.concatenate(
        list(blocks) + [jnp.zeros((rows - used, width), blocks[0].dtype)], 0
    )
    moved = lax.ppermute(packed, ALL, owner_pairs(True))
    full = lax.all_gather(moved, "sh", axis=0, tiled=False)
    parts = []
    first = 0
    for block in blocks:
        size = block.shape[0]
        parts.append(full[:, first : first + size].reshape(groups * size, width))
        first += size
    return parts


def heads_to_rows(partials):
    groups = lax.axis_size("sh")
    pieces = [
        p.astype(jnp.bfloat16).reshape((groups, p.shape[0] // groups) + p.shape[1:])
        for p in partials
    ]
    joined = jnp.concatenate(pieces, 1)
    joined = joined.reshape((-1,) + joined.shape[2:])
    summed = lax.psum_scatter(joined, "sh", scatter_dimension=0, tiled=True)
    moved = lax.ppermute(summed, ALL, owner_pairs(False)).astype(jnp.float32)
    parts = []
    first = 0
    for piece in pieces:
        size = piece.shape[1]
        parts.append(moved[first : first + size])
        first += size
    return parts


def columns_to_heads(local_cols):
    per_head = jnp.transpose(local_cols, (1, 0, 2))
    mine = lax.all_to_all(per_head, GROUP, 0, 0, tiled=True)
    mine = mine.reshape(-1, mine.shape[-1])
    return lax.all_gather(mine, "sh", axis=0, tiled=True)


def heads_to_columns(partial, direct=False):
    low = partial.astype(jnp.bfloat16)
    if direct:
        summed = group_sum_scatter(low, 3).astype(jnp.bfloat16)
    else:
        summed = lax.psum_scatter(low, "sh", scatter_dimension=0, tiled=True)
    summed = summed.reshape(HEADS, -1, summed.shape[-1])
    back = lax.all_to_all(summed, GROUP, 0, 0, tiled=True)
    return jnp.transpose(back, (1, 0, 2)).astype(jnp.float32)


def group_gather(rows, direct=False):
    if direct:
        copies = jnp.broadcast_to(rows[None], (HEADS,) + rows.shape)
        moved = lax.all_to_all(copies, GROUP, 0, 0, tiled=True)
        return moved.reshape((-1,) + rows.shape[1:])
    return lax.all_gather(rows, GROUP, axis=0, tiled=True)


def group_scatter(partial, direct=False):
    low = partial.astype(jnp.bfloat16)
    if direct:
        pieces = low.reshape((HEADS, low.shape[0] // HEADS) + low.shape[1:])
        moved = lax.all_to_all(pieces, GROUP, 0, 0, tiled=True)
        return jnp.sum(moved.astype(jnp.float32), 0)
    return lax.psum_scatter(low, GROUP, scatter_dimension=0, tiled=True).astype(jnp.float32)


def masked_power_inverse(system):
    size = system.shape[-1]
    places = jnp.arange(size)
    base = 8
    inside = (places[:, None] // base == places[None, :] // base) & (
        places[:, None] > places[None, :]
    )
    step = -(system * inside.astype(system.dtype))
    eye = jnp.eye(size, dtype=system.dtype)
    result = eye + step
    for _ in range(2):
        step = hi("bij,bjk->bik", step, step)
        result = result + hi("bij,bjk->bik", result, step)
    width = base
    while width < size:
        across = (places[:, None] // (2 * width) == places[None, :] // (2 * width)) & (
            places[:, None] // width != places[None, :] // width
        )
        lower_left = system * across.astype(system.dtype)
        result = result - hi("bij,bjk->bik", result, hi("bij,bjk->bik", lower_left, result))
        width = 2 * width
    return result


@jax.custom_vjp
def unit_lower_inverse(system):
    return masked_power_inverse(system)


def inverse_keep(system):
    inverse = masked_power_inverse(system)
    return inverse, inverse


def inverse_back(inverse, grad):
    turned = jnp.swapaxes(inverse, -1, -2)
    return (-hi("bij,bjk->bik", turned, hi("bij,bjk->bik", grad, turned)),)


unit_lower_inverse.defvjp(inverse_keep, inverse_back)


def block_mixer(query_rows, key_rows, value_rows, beta_rows, log_decay, starts_flag):
    pseudo = key_rows.shape[0]
    span = STEPS * BLOCK
    blocks = pseudo // span
    queries = query_rows.reshape(blocks, BLOCK, DK)
    keys = key_rows.reshape(blocks, span, DK)
    values = value_rows.reshape(blocks, span, DK)
    betas = beta_rows.reshape(blocks, span)
    decays = log_decay.reshape(blocks, span)
    flags = starts_flag.reshape(blocks, span)
    places = jnp.arange(span)
    lower = places[:, None] >= places[None, :]
    strict = (places[:, None] > places[None, :]).astype(jnp.float32)
    identity = jnp.eye(span, dtype=jnp.float32)
    eye_key = jnp.eye(DK, dtype=jnp.float32)

    summed = jnp.cumsum(decays, axis=1)
    segment = jnp.cumsum(flags, axis=1)
    same_doc = (segment[:, :, None] == segment[:, None, :]) & lower
    decay_ratio = jnp.exp(
        jnp.where(same_doc, summed[:, :, None] - summed[:, None, :], 0.0)
    ) * same_doc.astype(jnp.float32)
    from_start = jnp.exp(summed) * (segment == 0.0).astype(jnp.float32)
    key_key = hi("bik,bjk->bij", keys, keys)
    system = identity + betas[:, :, None] * decay_ratio * key_key * strict
    right_side = jnp.concatenate(
        [betas[:, :, None] * values, (betas * from_start)[:, :, None] * keys], 2
    )
    solved = hi("bij,bjk->bik", unit_lower_inverse(system), right_side)
    fresh = solved[:, :, :DK]
    carried = solved[:, :, DK:]
    last_keys = keys * decay_ratio[:, -1, :, None]
    transfer = from_start[:, -1, None, None] * eye_key - hi("bsi,bsj->bij", last_keys, carried)
    offset = hi("bsi,bsj->bij", last_keys, fresh)
    query_key = hi("bqk,bsk->bqs", queries, keys) * decay_ratio[:, STEPS - 1 :: STEPS]
    frame = from_start[:, STEPS - 1 :: STEPS, None] * queries - hi(
        "bqs,bsj->bqj", query_key, carried
    )
    direct = hi("bqs,bsj->bqj", query_key, fresh)

    state = jnp.concatenate([eye_key, jnp.zeros((DK, DK), jnp.float32)], 1)
    states = []
    for index in range(blocks):
        states.append(state)
        state = hi("ij,jk->ik", transfer[index], state) + jnp.concatenate(
            [jnp.zeros((DK, DK), jnp.float32), offset[index]], 1
        )
    states = jnp.stack(states)
    mats = states[:, :, :DK]
    adds = states[:, :, DK:]
    final_mat = state[:, :DK]
    final_add = state[:, DK:]
    query_frame = hi("bqi,bij->bqj", frame, mats)
    partial = hi("bqi,bij->bqj", frame, adds) + direct
    return (
        query_frame.reshape(blocks * BLOCK, DK),
        partial.reshape(blocks * BLOCK, DK),
        final_mat[None],
        final_add[None],
    )


def local(
    tokens_in,
    mixer_norm,
    mix_weight,
    head_gates,
    conv_taps,
    decay_log,
    decay_bias,
    gate_weight,
    out_norm,
    out_weight,
    feed_norm,
    up_weight,
    down_weight,
    doc_lengths,
    out_grad,
):
    row_count = tokens_in.shape[0]
    weight_rows = mix_weight.shape[0]
    head = lax.axis_index("sl") * lax.axis_size("hd") + lax.axis_index("hd")
    length = row_count * HEADS

    head_cols = jnp.concatenate(
        [
            gate_weight.reshape(weight_rows, HEADS, DK),
            mix_weight.reshape(weight_rows, HEADS, PROJ),
            head_gates.reshape(weight_rows, HEADS, STEPS + 1),
            jnp.broadcast_to(mixer_norm[:, None, None], (weight_rows, HEADS, 1)),
        ],
        2,
    )
    head_wide = columns_to_heads(head_cols)
    head_full = head_wide[:, :WIDE]
    gain_one = head_wide[:, WIDE].astype(jnp.float32)
    half = FF // HEADS
    up_cols = jnp.concatenate(
        [
            up_weight[:, :FF].reshape(weight_rows, HEADS, half),
            up_weight[:, FF:].reshape(weight_rows, HEADS, half),
            jnp.broadcast_to(feed_norm[:, None, None], (weight_rows, HEADS, 1)),
        ],
        2,
    )
    up_wide = columns_to_heads(up_cols)
    up_full = up_wide[:, : 2 * half]
    gain_two = up_wide[:, 2 * half].astype(jnp.float32)
    tap_width = conv_taps.shape[1]
    tap_row = jnp.pad(conv_taps.reshape(1, -1), ((0, 0), (0, D - CONV * tap_width)))
    out_full, down_full, tap_rows = rows_to_heads((out_weight, down_weight, tap_row))
    conv_part = jnp.transpose(
        tap_rows[:, : CONV * tap_width].reshape(-1, CONV, tap_width), (1, 0, 2)
    ).reshape(CONV, -1).astype(jnp.float32)

    x_float = tokens_in.astype(jnp.float32)
    normed_float, norm_one_back = jax.vjp(rms_norm, x_float, gain_one)
    normed_one = group_gather(normed_float.astype(jnp.bfloat16), True)
    head_out = bf_product(normed_one, head_full)
    out_gate = head_out[:, :DK]
    proj_head = head_out[:, DK : DK + PROJ].astype(jnp.bfloat16)
    scalar_rows = head_out[:, DK + PROJ :].astype(jnp.bfloat16).astype(jnp.float32)

    rim_rows = from_behind(proj_head[length - (CONV - 1) :], "sh", 1)
    padded = jnp.concatenate([rim_rows, proj_head], 0).astype(jnp.float32)
    starts = jnp.cumsum(doc_lengths) - doc_lengths
    positions = lax.axis_index("sh") * length + jnp.arange(length, dtype=jnp.int32)
    starts_flag = jnp.any(positions[:, None] == starts[None, :], 1).astype(jnp.float32)
    doc_begin = jnp.max(jnp.where(starts[None, :] <= positions[:, None], starts[None, :], 0), 1)
    tap_masks = [
        (positions - (CONV - 1) + tap_index >= doc_begin).astype(jnp.float32)
        for tap_index in range(CONV)
    ]
    pseudo_flag = jnp.concatenate(
        [starts_flag[:, None], jnp.zeros((length, STEPS - 1), jnp.float32)], 1
    ).reshape(-1)
    rate_log = lax.dynamic_index_in_dim(decay_log, head, 0, False)
    bias_part = lax.dynamic_index_in_dim(decay_bias, head, 0, False)

    def mixer_inputs(padded, scalar_rows, conv_part, rate_log, bias_part):
        convolved = jnp.zeros_like(padded[CONV - 1 :])
        for tap_index in range(CONV):
            convolved = (
                convolved
                + conv_part[tap_index]
                * padded[tap_index : tap_index + length]
                * tap_masks[tap_index][:, None]
            )
        activated = jax.nn.silu(convolved).reshape(length, 1 + 2 * STEPS, DK)
        query_rows = unit_norm(activated[:, 0])
        key_rows = unit_norm(activated[:, 1 : 1 + STEPS]).reshape(STEPS * length, DK)
        value_rows = activated[:, 1 + STEPS :].reshape(STEPS * length, DK)
        beta_rows = jax.nn.sigmoid(scalar_rows[:, :STEPS]).reshape(STEPS * length)
        log_rate = -jnp.exp(rate_log) * jax.nn.softplus(scalar_rows[:, STEPS] + bias_part)
        log_decay = jnp.concatenate(
            [log_rate[:, None], jnp.zeros((length, STEPS - 1), jnp.float32)], 1
        ).reshape(STEPS * length)
        return (query_rows, key_rows, value_rows, beta_rows, log_decay)

    def recurrence(query_rows, key_rows, value_rows, beta_rows, log_decay):
        return block_mixer(query_rows, key_rows, value_rows, beta_rows, log_decay, pseudo_flag)

    prepared, inputs_back = jax.vjp(
        mixer_inputs, padded, scalar_rows, conv_part, rate_log, bias_part
    )
    (query_frame, partial_value_rows, transfer, offset), recurrence_back = jax.vjp(
        recurrence, *prepared
    )
    grad_rows = group_gather(out_grad)
    grad_rows, query_frame, partial_value_rows, transfer, offset = lax.optimization_barrier(
        (grad_rows, query_frame, partial_value_rows, transfer, offset)
    )
    identity = jnp.eye(DK, dtype=jnp.float32)[None]
    zeros_state = jnp.zeros((1, DK, DK), jnp.float32)
    prefix_map, incoming_state = carried_in(
        (transfer, offset), "sh", compose, (identity, zeros_state), False
    )
    mixer_result = partial_value_rows + hi("zy,yi->zi", query_frame, incoming_state[0])
    mixer_low = mixer_result.astype(jnp.bfloat16).astype(jnp.float32)
    gated, gate_back = jax.vjp(gate_norm, mixer_low, out_gate, out_norm)
    gated_rows = gated.astype(jnp.bfloat16)
    middle = x_float + group_scatter(bf_product(gated_rows, out_full), True)
    normed_mid, norm_two_back = jax.vjp(rms_norm, middle, gain_two)
    normed_two = group_gather(normed_mid.astype(jnp.bfloat16))
    gate_up = bf_product(normed_two, up_full)
    hidden_float, swiglu_back = jax.vjp(swiglu, gate_up)
    hidden = hidden_float.astype(jnp.bfloat16)
    feed_partial = bf_product(hidden, down_full)

    grad_out = out_grad.astype(jnp.float32)
    grad_hidden = bf_product(grad_rows, down_full.T)
    grad_down_partial = bf_product(hidden.T, grad_rows)
    (grad_gate_up,) = swiglu_back(grad_hidden)
    grad_gate_up = grad_gate_up.astype(jnp.bfloat16)
    grad_normed_two = group_scatter(bf_product(grad_gate_up, up_full.T))
    grad_mid_norm, grad_gain_two = norm_two_back(grad_normed_two)
    grad_up_payload = jnp.concatenate(
        [bf_product(normed_two.T, grad_gate_up), grad_gain_two[:, None]], 1
    )
    grad_middle = grad_out + grad_mid_norm
    feed_partial, grad_up_payload, grad_down_partial, grad_branch_low = lax.optimization_barrier(
        (feed_partial, grad_up_payload, grad_down_partial, grad_middle.astype(jnp.bfloat16))
    )
    grad_up_cols = heads_to_columns(grad_up_payload, True)
    grad_up = jnp.concatenate(
        [
            grad_up_cols[:, :, :half].reshape(weight_rows, FF),
            grad_up_cols[:, :, half : 2 * half].reshape(weight_rows, FF),
        ],
        1,
    )
    grad_branch = group_gather(grad_branch_low)
    feed_partial, grad_down_partial, grad_branch = lax.optimization_barrier(
        (feed_partial, grad_down_partial, grad_branch)
    )
    feed_sum = group_scatter(feed_partial)
    grad_gated = bf_product(grad_branch, out_full.T)
    grad_down, grad_outw = heads_to_rows((grad_down_partial, bf_product(gated_rows.T, grad_branch)))
    grad_mixer, grad_gate, grad_out_norm = gate_back(grad_gated)
    grad_gate = grad_gate.astype(jnp.bfloat16)
    head_gradients = grad_mixer.astype(jnp.bfloat16).astype(jnp.float32)
    local_adjoint = hi("dc,dr->cr", query_frame, head_gradients)[None]
    transfer_turned = jnp.transpose(transfer, (0, 2, 1))
    later_map, state_gradient = carried_in(
        (transfer_turned, local_adjoint), "sh", compose, (identity, zeros_state), True
    )
    basis_gradient = hi("nu,wu->nw", head_gradients, incoming_state[0])
    transfer_gradient = hi("tnf,tmf->tnm", state_gradient, incoming_state)
    grad_prepared = recurrence_back(
        (basis_gradient, head_gradients, transfer_gradient, state_gradient)
    )
    grad_prepared, feed_sum, grad_up_cols, grad_down, grad_outw = lax.optimization_barrier(
        (grad_prepared, feed_sum, grad_up_cols, grad_down, grad_outw)
    )
    layer_out = (middle + feed_sum).astype(jnp.bfloat16)
    grad_padded, grad_scalars, grad_conv, grad_rate, grad_bias = inputs_back(grad_prepared)
    rim_grad = from_behind(grad_padded[: CONV - 1], "sh", -1)
    own_grad = grad_padded[CONV - 1 :]
    grad_proj = jnp.concatenate(
        [own_grad[: length - (CONV - 1)], own_grad[length - (CONV - 1) :] + rim_grad], 0
    )
    grad_head = jnp.concatenate(
        [grad_gate, grad_proj.astype(jnp.bfloat16), grad_scalars.astype(jnp.bfloat16)], 1
    )
    grad_normed_one = group_scatter(bf_product(grad_head, head_full.T), True)
    grad_x_norm, grad_gain_one = norm_one_back(grad_normed_one)
    grad_head_cols = heads_to_columns(
        jnp.concatenate([bf_product(normed_one.T, grad_head), grad_gain_one[:, None]], 1)
    )
    grad_gatew = grad_head_cols[:, :, :DK].reshape(weight_rows, D)
    grad_mixw = grad_head_cols[:, :, DK : DK + PROJ].reshape(weight_rows, HEADS * PROJ)
    grad_gatesw = grad_head_cols[:, :, DK + PROJ : WIDE].reshape(
        weight_rows, HEADS * (STEPS + 1)
    )
    grad_tokens = (grad_middle + grad_x_norm).astype(jnp.bfloat16)
    (conv_grad,) = heads_to_rows((jnp.transpose(grad_conv),))
    conv_grad = jnp.transpose(conv_grad)
    one_hot = (jnp.arange(HEADS) == head).astype(jnp.float32)
    small_sums = all_sum(
        jnp.concatenate([one_hot * grad_rate, one_hot * grad_bias, grad_out_norm])
    )
    return (
        layer_out,
        grad_tokens,
        jnp.sum(grad_head_cols[:, :, WIDE], 1),
        grad_mixw,
        grad_gatesw,
        conv_grad,
        small_sums[:HEADS],
        small_sums[HEADS : 2 * HEADS],
        grad_gatew,
        small_sums[2 * HEADS :],
        grad_outw,
        jnp.sum(grad_up_cols[:, :, 2 * half], 1),
        grad_up,
        grad_down,
    )


def solution(mesh):
    seq = mesh.shape["seq"]
    across = mesh.shape["head"]
    inner = HEADS // across
    grid = Mesh(
        np.asarray(mesh.devices).reshape(seq // inner, inner, across), ("sh", "sl", "hd")
    )
    rows = P(ALL, None)
    flat = P(ALL)
    return jax.shard_map(
        local,
        mesh=grid,
        in_specs=(
            rows,
            flat,
            rows,
            rows,
            P(None, ALL),
            P(),
            P(),
            rows,
            P(),
            rows,
            flat,
            rows,
            rows,
            P(),
            rows,
        ),
        out_specs=(
            rows,
            rows,
            flat,
            rows,
            rows,
            P(None, ALL),
            P(),
            P(),
            rows,
            P(),
            rows,
            flat,
            rows,
            rows,
        ),
        check_vma=False,
    )
```

```python
import jax
import jax.numpy as jnp
import numpy as np
from jax import lax
from jax.experimental import pallas as pl
from jax.experimental.pallas import tpu as pltpu
from jax.sharding import Mesh
from jax.sharding import PartitionSpec as P

D = 1024
HEADS = 8
DK = 128
FF = 2816
STEPS = 2
CONV = 4
BLOCK = 64
PROJ = (1 + 2 * STEPS) * DK
WIDE = DK + PROJ + STEPS + 1

EPS = 1e-06
HIGH_ACCURACY = lax.Precision.HIGH

GROUP = ("sl", "hd")
ALL = ("sh", "sl", "hd")


def from_behind(shard, axis, by):
    peers = lax.axis_size(axis)
    pairs = [(i, i + by) for i in range(peers) if 0 <= i + by < peers]
    return lax.ppermute(shard, axis, pairs)


def gather_kernel(count, own_ref, out_ref, slots, send_sems, recv_sems):
    me = lax.axis_index("sh")
    across = lax.axis_index("sl")
    inner = lax.axis_index("hd")
    barrier = pltpu.get_barrier_semaphore()

    def peer(index):
        return (index, across, inner)

    def greet(index, carry):
        @pl.when(index != me)
        def _():
            pl.semaphore_signal(
                barrier, inc=1, device_id=peer(index), device_id_type=pl.DeviceIdType.MESH
            )

        return carry

    lax.fori_loop(0, count, greet, 0)
    pl.semaphore_wait(barrier, count - 1)

    def copy_to(index):
        return pltpu.make_async_remote_copy(
            src_ref=own_ref,
            dst_ref=slots.at[me],
            send_sem=send_sems.at[index],
            recv_sem=recv_sems.at[me],
            device_id=peer(index),
            device_id_type=pl.DeviceIdType.MESH,
        )

    def copy_from(index):
        return pltpu.make_async_remote_copy(
            src_ref=own_ref,
            dst_ref=slots.at[index],
            send_sem=send_sems.at[index],
            recv_sem=recv_sems.at[index],
            device_id=peer(index),
            device_id_type=pl.DeviceIdType.MESH,
        )

    def send(index, carry):
        @pl.when(index != me)
        def _():
            copy_to(index).start()

        return carry

    lax.fori_loop(0, count, send, 0)
    slots[me] = own_ref[...]

    def finish(index, carry):
        @pl.when(index != me)
        def _():
            copy_to(index).wait_send()
            copy_from(index).wait_recv()

        return carry

    lax.fori_loop(0, count, finish, 0)
    out_ref[...] = slots[...]


def scatter_kernel(count, own_ref, out_ref, slots, send_sems, recv_sems):
    me = lax.axis_index("sh")
    across = lax.axis_index("sl")
    inner = lax.axis_index("hd")
    barrier = pltpu.get_barrier_semaphore()

    def peer(index):
        return (index, across, inner)

    def greet(index, carry):
        @pl.when(index != me)
        def _():
            pl.semaphore_signal(
                barrier, inc=1, device_id=peer(index), device_id_type=pl.DeviceIdType.MESH
            )

        return carry

    lax.fori_loop(0, count, greet, 0)
    pl.semaphore_wait(barrier, count - 1)

    def copy_to(index):
        return pltpu.make_async_remote_copy(
            src_ref=own_ref.at[index],
            dst_ref=slots.at[me],
            send_sem=send_sems.at[index],
            recv_sem=recv_sems.at[me],
            device_id=peer(index),
            device_id_type=pl.DeviceIdType.MESH,
        )

    def copy_from(index):
        return pltpu.make_async_remote_copy(
            src_ref=own_ref.at[index],
            dst_ref=slots.at[index],
            send_sem=send_sems.at[index],
            recv_sem=recv_sems.at[index],
            device_id=peer(index),
            device_id_type=pl.DeviceIdType.MESH,
        )

    def send(index, carry):
        @pl.when(index != me)
        def _():
            copy_to(index).start()

        return carry

    lax.fori_loop(0, count, send, 0)
    slots[me] = own_ref[me]

    def finish(index, carry):
        @pl.when(index != me)
        def _():
            copy_to(index).wait_send()
            copy_from(index).wait_recv()

        return carry

    lax.fori_loop(0, count, finish, 0)
    out_ref[...] = jnp.sum(slots[...].astype(jnp.float32), axis=0)


def group_sum_scatter(partial, ident):
    count = lax.axis_size("sh")
    pieces = partial.astype(jnp.bfloat16).reshape((count, partial.shape[0] // count) + partial.shape[1:])
    return pl.pallas_call(
        lambda *refs: scatter_kernel(count, *refs),
        out_shape=jax.ShapeDtypeStruct(pieces.shape[1:], jnp.float32),
        in_specs=[pl.BlockSpec(memory_space=pltpu.VMEM)],
        out_specs=pl.BlockSpec(memory_space=pltpu.VMEM),
        scratch_shapes=[
            pltpu.VMEM(pieces.shape, jnp.bfloat16),
            pltpu.SemaphoreType.DMA((count,)),
            pltpu.SemaphoreType.DMA((count,)),
        ],
        compiler_params=pltpu.CompilerParams(collective_id=ident, has_side_effects=True),
    )(pieces)


def group_maps(block, ident):
    count = lax.axis_size("sh")
    return pl.pallas_call(
        lambda *refs: gather_kernel(count, *refs),
        out_shape=jax.ShapeDtypeStruct((count,) + block.shape, block.dtype),
        in_specs=[pl.BlockSpec(memory_space=pltpu.VMEM)],
        out_specs=pl.BlockSpec(memory_space=pltpu.VMEM),
        scratch_shapes=[
            pltpu.VMEM((count,) + block.shape, block.dtype),
            pltpu.SemaphoreType.DMA((count,)),
            pltpu.SemaphoreType.DMA((count,)),
        ],
        compiler_params=pltpu.CompilerParams(collective_id=ident, has_side_effects=True),
    )(block)


def carried_in(shard, axis, join, neutral, backward):
    count = lax.axis_size(axis)
    place = lax.axis_index(axis)
    ahead = count - 1 - place if backward else place
    both = group_maps(jnp.stack(shard).astype(jnp.bfloat16), 2 if backward else 1)
    gathered = (both[:, 0], both[:, 1])
    state = jax.tree.map(lambda a, e: jnp.zeros_like(a) + jnp.asarray(e, a.dtype), shard, neutral)

    def one(turn, state):
        source = count - 1 - turn if backward else turn
        return join(
            state,
            jax.tree.map(
                lambda a, own: lax.dynamic_index_in_dim(a, source, 0, False).astype(own.dtype),
                gathered,
                shard,
            ),
        )

    return lax.fori_loop(0, ahead, one, state)


def flat_place():
    return (
        lax.axis_index("sh") * lax.axis_size("sl") + lax.axis_index("sl")
    ) * lax.axis_size("hd") + lax.axis_index("hd")


def device_of(index):
    inner = lax.axis_size("sl") * lax.axis_size("hd")
    return (index // inner, (index // lax.axis_size("hd")) % lax.axis_size("sl"), index % lax.axis_size("hd"))


def sum_kernel(count, own_ref, out_ref, slots, send_sems, recv_sems):
    me = flat_place()
    barrier = pltpu.get_barrier_semaphore()

    def greet(index, carry):
        @pl.when(index != me)
        def _():
            pl.semaphore_signal(
                barrier, inc=1, device_id=device_of(index), device_id_type=pl.DeviceIdType.MESH
            )

        return carry

    lax.fori_loop(0, count, greet, 0)
    pl.semaphore_wait(barrier, count - 1)

    def copy_to(index):
        return pltpu.make_async_remote_copy(
            src_ref=own_ref,
            dst_ref=slots.at[me],
            send_sem=send_sems.at[index],
            recv_sem=recv_sems.at[me],
            device_id=device_of(index),
            device_id_type=pl.DeviceIdType.MESH,
        )

    def copy_from(index):
        return pltpu.make_async_remote_copy(
            src_ref=own_ref,
            dst_ref=slots.at[index],
            send_sem=send_sems.at[index],
            recv_sem=recv_sems.at[index],
            device_id=device_of(index),
            device_id_type=pl.DeviceIdType.MESH,
        )

    def send(index, carry):
        @pl.when(index != me)
        def _():
            copy_to(index).start()

        return carry

    lax.fori_loop(0, count, send, 0)
    slots[me] = own_ref[...]

    def finish(index, carry):
        @pl.when(index != me)
        def _():
            copy_to(index).wait_send()
            copy_from(index).wait_recv()

        return carry

    lax.fori_loop(0, count, finish, 0)
    out_ref[...] = jnp.sum(slots[...], axis=0)


def all_sum(vector):
    count = lax.axis_size("sh") * lax.axis_size("sl") * lax.axis_size("hd")
    size = vector.shape[0]
    lanes = 128
    tile = 8 * lanes
    padded = -(-size // tile) * tile
    block = jnp.pad(vector, (0, padded - size)).reshape(padded // lanes, lanes)
    total = pl.pallas_call(
        lambda *refs: sum_kernel(count, *refs),
        out_shape=jax.ShapeDtypeStruct(block.shape, jnp.float32),
        in_specs=[pl.BlockSpec(memory_space=pltpu.VMEM)],
        out_specs=pl.BlockSpec(memory_space=pltpu.VMEM),
        scratch_shapes=[
            pltpu.VMEM((count,) + block.shape, jnp.float32),
            pltpu.SemaphoreType.DMA((count,)),
            pltpu.SemaphoreType.DMA((count,)),
        ],
        compiler_params=pltpu.CompilerParams(collective_id=0, has_side_effects=True),
    )(block)
    return total.reshape(-1)[:size]


def rms_norm(values, scale_gain):
    return values * lax.rsqrt(jnp.mean(values * values, axis=-1, keepdims=True) + EPS) * scale_gain


def unit_norm(values):
    return values * lax.rsqrt(jnp.sum(values * values, axis=-1, keepdims=True) + EPS)


def bf_product(first_mat, second_mat):
    return jnp.dot(first_mat, second_mat, preferred_element_type=jnp.float32)


def hi(spec, *arrays):
    return jnp.einsum(spec, *arrays, precision=HIGH_ACCURACY)


def compose(early_pair, late_pair):
    early_mat, early_add = early_pair
    late_mat, late_add = late_pair
    joined = hi("hij,hjk->hik", late_mat, early_mat)
    shifted = hi("hij,hjk->hik", late_mat, early_add) + late_add
    return (joined, shifted)


def gate_norm(values, out_gate, scale_gain):
    return rms_norm(values, scale_gain) * jax.nn.silu(out_gate)


def swiglu(gate_up):
    half = gate_up.shape[1] // 2
    return jax.nn.silu(gate_up[:, :half]) * gate_up[:, half:]


def owner_pairs(inverse):
    groups = lax.axis_size("sh")
    pairs = [(g * HEADS + t, t * groups + g) for g in range(groups) for t in range(HEADS)]
    return [(b, a) for a, b in pairs] if inverse else pairs


def rows_to_heads(blocks):
    groups = lax.axis_size("sh")
    width = blocks[0].shape[1]
    used = sum(b.shape[0] for b in blocks)
    least = (1 << 20) // (groups * width * 2) + 1
    rows = -(-max(used, least) // 8) * 8
    packed = jnp.concatenate(
        list(blocks) + [jnp.zeros((rows - used, width), blocks[0].dtype)], 0
    )
    moved = lax.ppermute(packed, ALL, owner_pairs(True))
    full = lax.all_gather(moved, "sh", axis=0, tiled=False)
    parts = []
    first = 0
    for block in blocks:
        size = block.shape[0]
        parts.append(full[:, first : first + size].reshape(groups * size, width))
        first += size
    return parts


def heads_to_rows(partials):
    groups = lax.axis_size("sh")
    pieces = [
        p.astype(jnp.bfloat16).reshape((groups, p.shape[0] // groups) + p.shape[1:])
        for p in partials
    ]
    joined = jnp.concatenate(pieces, 1)
    joined = joined.reshape((-1,) + joined.shape[2:])
    summed = lax.psum_scatter(joined, "sh", scatter_dimension=0, tiled=True)
    moved = lax.ppermute(summed, ALL, owner_pairs(False)).astype(jnp.float32)
    parts = []
    first = 0
    for piece in pieces:
        size = piece.shape[1]
        parts.append(moved[first : first + size])
        first += size
    return parts


def columns_to_heads(local_cols):
    per_head = jnp.transpose(local_cols, (1, 0, 2))
    mine = lax.all_to_all(per_head, GROUP, 0, 0, tiled=True)
    mine = mine.reshape(-1, mine.shape[-1])
    return lax.all_gather(mine, "sh", axis=0, tiled=True)


def heads_to_columns(partial, direct=False):
    low = partial.astype(jnp.bfloat16)
    if direct:
        summed = group_sum_scatter(low, 3).astype(jnp.bfloat16)
    else:
        summed = lax.psum_scatter(low, "sh", scatter_dimension=0, tiled=True)
    summed = summed.reshape(HEADS, -1, summed.shape[-1])
    back = lax.all_to_all(summed, GROUP, 0, 0, tiled=True)
    return jnp.transpose(back, (1, 0, 2)).astype(jnp.float32)


def group_gather(rows, direct=False):
    if direct:
        copies = jnp.broadcast_to(rows[None], (HEADS,) + rows.shape)
        moved = lax.all_to_all(copies, GROUP, 0, 0, tiled=True)
        return moved.reshape((-1,) + rows.shape[1:])
    return lax.all_gather(rows, GROUP, axis=0, tiled=True)


def group_scatter(partial, direct=False):
    low = partial.astype(jnp.bfloat16)
    if direct:
        pieces = low.reshape((HEADS, low.shape[0] // HEADS) + low.shape[1:])
        moved = lax.all_to_all(pieces, GROUP, 0, 0, tiled=True)
        return jnp.sum(moved.astype(jnp.float32), 0)
    return lax.psum_scatter(low, GROUP, scatter_dimension=0, tiled=True).astype(jnp.float32)


def masked_power_inverse(system):
    size = system.shape[-1]
    places = jnp.arange(size)
    base = 8
    inside = (places[:, None] // base == places[None, :] // base) & (
        places[:, None] > places[None, :]
    )
    step = -(system * inside.astype(system.dtype))
    eye = jnp.eye(size, dtype=system.dtype)
    result = eye + step
    for _ in range(2):
        step = hi("bij,bjk->bik", step, step)
        result = result + hi("bij,bjk->bik", result, step)
    width = base
    while width < size:
        across = (places[:, None] // (2 * width) == places[None, :] // (2 * width)) & (
            places[:, None] // width != places[None, :] // width
        )
        lower_left = system * across.astype(system.dtype)
        result = result - hi("bij,bjk->bik", result, hi("bij,bjk->bik", lower_left, result))
        width = 2 * width
    return result


@jax.custom_vjp
def unit_lower_inverse(system):
    return masked_power_inverse(system)


def inverse_keep(system):
    inverse = masked_power_inverse(system)
    return inverse, inverse


def inverse_back(inverse, grad):
    turned = jnp.swapaxes(inverse, -1, -2)
    return (-hi("bij,bjk->bik", turned, hi("bij,bjk->bik", grad, turned)),)


unit_lower_inverse.defvjp(inverse_keep, inverse_back)


def block_mixer(query_rows, key_rows, value_rows, beta_rows, log_decay, starts_flag):
    pseudo = key_rows.shape[0]
    span = STEPS * BLOCK
    blocks = pseudo // span
    queries = query_rows.reshape(blocks, BLOCK, DK)
    keys = key_rows.reshape(blocks, span, DK)
    values = value_rows.reshape(blocks, span, DK)
    betas = beta_rows.reshape(blocks, span)
    decays = log_decay.reshape(blocks, span)
    flags = starts_flag.reshape(blocks, span)
    places = jnp.arange(span)
    lower = places[:, None] >= places[None, :]
    strict = (places[:, None] > places[None, :]).astype(jnp.float32)
    identity = jnp.eye(span, dtype=jnp.float32)
    eye_key = jnp.eye(DK, dtype=jnp.float32)

    summed = jnp.cumsum(decays, axis=1)
    segment = jnp.cumsum(flags, axis=1)
    same_doc = (segment[:, :, None] == segment[:, None, :]) & lower
    decay_ratio = jnp.exp(
        jnp.where(same_doc, summed[:, :, None] - summed[:, None, :], 0.0)
    ) * same_doc.astype(jnp.float32)
    from_start = jnp.exp(summed) * (segment == 0.0).astype(jnp.float32)
    key_key = hi("bik,bjk->bij", keys, keys)
    system = identity + betas[:, :, None] * decay_ratio * key_key * strict
    right_side = jnp.concatenate(
        [betas[:, :, None] * values, (betas * from_start)[:, :, None] * keys], 2
    )
    solved = hi("bij,bjk->bik", unit_lower_inverse(system), right_side)
    fresh = solved[:, :, :DK]
    carried = solved[:, :, DK:]
    last_keys = keys * decay_ratio[:, -1, :, None]
    transfer = from_start[:, -1, None, None] * eye_key - hi("bsi,bsj->bij", last_keys, carried)
    offset = hi("bsi,bsj->bij", last_keys, fresh)
    query_key = hi("bqk,bsk->bqs", queries, keys) * decay_ratio[:, STEPS - 1 :: STEPS]
    frame = from_start[:, STEPS - 1 :: STEPS, None] * queries - hi(
        "bqs,bsj->bqj", query_key, carried
    )
    direct = hi("bqs,bsj->bqj", query_key, fresh)

    state = jnp.concatenate([eye_key, jnp.zeros((DK, DK), jnp.float32)], 1)
    states = []
    for index in range(blocks):
        states.append(state)
        state = hi("ij,jk->ik", transfer[index], state) + jnp.concatenate(
            [jnp.zeros((DK, DK), jnp.float32), offset[index]], 1
        )
    states = jnp.stack(states)
    mats = states[:, :, :DK]
    adds = states[:, :, DK:]
    final_mat = state[:, :DK]
    final_add = state[:, DK:]
    query_frame = hi("bqi,bij->bqj", frame, mats)
    partial = hi("bqi,bij->bqj", frame, adds) + direct
    return (
        query_frame.reshape(blocks * BLOCK, DK),
        partial.reshape(blocks * BLOCK, DK),
        final_mat[None],
        final_add[None],
    )


def local(
    tokens_in,
    mixer_norm,
    mix_weight,
    head_gates,
    conv_taps,
    decay_log,
    decay_bias,
    gate_weight,
    out_norm,
    out_weight,
    feed_norm,
    up_weight,
    down_weight,
    doc_lengths,
    out_grad,
):
    row_count = tokens_in.shape[0]
    weight_rows = mix_weight.shape[0]
    head = lax.axis_index("sl") * lax.axis_size("hd") + lax.axis_index("hd")
    length = row_count * HEADS

    head_cols = jnp.concatenate(
        [
            gate_weight.reshape(weight_rows, HEADS, DK),
            mix_weight.reshape(weight_rows, HEADS, PROJ),
            head_gates.reshape(weight_rows, HEADS, STEPS + 1),
            jnp.broadcast_to(mixer_norm[:, None, None], (weight_rows, HEADS, 1)),
        ],
        2,
    )
    head_wide = columns_to_heads(head_cols)
    head_full = head_wide[:, :WIDE]
    gain_one = head_wide[:, WIDE].astype(jnp.float32)
    half = FF // HEADS
    up_cols = jnp.concatenate(
        [
            up_weight[:, :FF].reshape(weight_rows, HEADS, half),
            up_weight[:, FF:].reshape(weight_rows, HEADS, half),
            jnp.broadcast_to(feed_norm[:, None, None], (weight_rows, HEADS, 1)),
        ],
        2,
    )
    up_wide = columns_to_heads(up_cols)
    up_full = up_wide[:, : 2 * half]
    gain_two = up_wide[:, 2 * half].astype(jnp.float32)
    tap_width = conv_taps.shape[1]
    tap_row = jnp.pad(conv_taps.reshape(1, -1), ((0, 0), (0, D - CONV * tap_width)))
    out_full, down_full, tap_rows = rows_to_heads((out_weight, down_weight, tap_row))
    conv_part = jnp.transpose(
        tap_rows[:, : CONV * tap_width].reshape(-1, CONV, tap_width), (1, 0, 2)
    ).reshape(CONV, -1).astype(jnp.float32)

    x_float = tokens_in.astype(jnp.float32)
    normed_float, norm_one_back = jax.vjp(rms_norm, x_float, gain_one)
    normed_one = group_gather(normed_float.astype(jnp.bfloat16), True)
    head_out = bf_product(normed_one, head_full)
    out_gate = head_out[:, :DK]
    proj_head = head_out[:, DK : DK + PROJ].astype(jnp.bfloat16)
    scalar_rows = head_out[:, DK + PROJ :].astype(jnp.bfloat16).astype(jnp.float32)

    rim_rows = from_behind(proj_head[length - (CONV - 1) :], "sh", 1)
    padded = jnp.concatenate([rim_rows, proj_head], 0).astype(jnp.float32)
    starts = jnp.cumsum(doc_lengths) - doc_lengths
    positions = lax.axis_index("sh") * length + jnp.arange(length, dtype=jnp.int32)
    starts_flag = jnp.any(positions[:, None] == starts[None, :], 1).astype(jnp.float32)
    doc_begin = jnp.max(jnp.where(starts[None, :] <= positions[:, None], starts[None, :], 0), 1)
    tap_masks = [
        (positions - (CONV - 1) + tap_index >= doc_begin).astype(jnp.float32)
        for tap_index in range(CONV)
    ]
    pseudo_flag = jnp.concatenate(
        [starts_flag[:, None], jnp.zeros((length, STEPS - 1), jnp.float32)], 1
    ).reshape(-1)
    rate_log = lax.dynamic_index_in_dim(decay_log, head, 0, False)
    bias_part = lax.dynamic_index_in_dim(decay_bias, head, 0, False)

    def mixer_inputs(padded, scalar_rows, conv_part, rate_log, bias_part):
        convolved = jnp.zeros_like(padded[CONV - 1 :])
        for tap_index in range(CONV):
            convolved = (
                convolved
                + conv_part[tap_index]
                * padded[tap_index : tap_index + length]
                * tap_masks[tap_index][:, None]
            )
        activated = jax.nn.silu(convolved).reshape(length, 1 + 2 * STEPS, DK)
        query_rows = unit_norm(activated[:, 0])
        key_rows = unit_norm(activated[:, 1 : 1 + STEPS]).reshape(STEPS * length, DK)
        value_rows = activated[:, 1 + STEPS :].reshape(STEPS * length, DK)
        beta_rows = jax.nn.sigmoid(scalar_rows[:, :STEPS]).reshape(STEPS * length)
        log_rate = -jnp.exp(rate_log) * jax.nn.softplus(scalar_rows[:, STEPS] + bias_part)
        log_decay = jnp.concatenate(
            [log_rate[:, None], jnp.zeros((length, STEPS - 1), jnp.float32)], 1
        ).reshape(STEPS * length)
        return (query_rows, key_rows, value_rows, beta_rows, log_decay)

    def recurrence(query_rows, key_rows, value_rows, beta_rows, log_decay):
        return block_mixer(query_rows, key_rows, value_rows, beta_rows, log_decay, pseudo_flag)

    prepared, inputs_back = jax.vjp(
        mixer_inputs, padded, scalar_rows, conv_part, rate_log, bias_part
    )
    (query_frame, partial_value_rows, transfer, offset), recurrence_back = jax.vjp(
        recurrence, *prepared
    )
    grad_rows = group_gather(out_grad)
    grad_rows, query_frame, partial_value_rows, transfer, offset = lax.optimization_barrier(
        (grad_rows, query_frame, partial_value_rows, transfer, offset)
    )
    identity = jnp.eye(DK, dtype=jnp.float32)[None]
    zeros_state = jnp.zeros((1, DK, DK), jnp.float32)
    prefix_map, incoming_state = carried_in(
        (transfer, offset), "sh", compose, (identity, zeros_state), False
    )
    mixer_result = partial_value_rows + hi("zy,yi->zi", query_frame, incoming_state[0])
    mixer_low = mixer_result.astype(jnp.bfloat16).astype(jnp.float32)
    gated, gate_back = jax.vjp(gate_norm, mixer_low, out_gate, out_norm)
    gated_rows = gated.astype(jnp.bfloat16)
    middle = x_float + group_scatter(bf_product(gated_rows, out_full), True)
    normed_mid, norm_two_back = jax.vjp(rms_norm, middle, gain_two)
    normed_two = group_gather(normed_mid.astype(jnp.bfloat16), True)
    gate_up = bf_product(normed_two, up_full)
    hidden_float, swiglu_back = jax.vjp(swiglu, gate_up)
    hidden = hidden_float.astype(jnp.bfloat16)
    feed_partial = bf_product(hidden, down_full)

    grad_out = out_grad.astype(jnp.float32)
    grad_hidden = bf_product(grad_rows, down_full.T)
    grad_down_partial = bf_product(hidden.T, grad_rows)
    (grad_gate_up,) = swiglu_back(grad_hidden)
    grad_gate_up = grad_gate_up.astype(jnp.bfloat16)
    grad_normed_two = group_scatter(bf_product(grad_gate_up, up_full.T))
    grad_mid_norm, grad_gain_two = norm_two_back(grad_normed_two)
    grad_up_payload = jnp.concatenate(
        [bf_product(normed_two.T, grad_gate_up), grad_gain_two[:, None]], 1
    )
    grad_middle = grad_out + grad_mid_norm
    feed_partial, grad_up_payload, grad_down_partial, grad_branch_low = lax.optimization_barrier(
        (feed_partial, grad_up_payload, grad_down_partial, grad_middle.astype(jnp.bfloat16))
    )
    grad_up_cols = heads_to_columns(grad_up_payload, True)
    grad_up = jnp.concatenate(
        [
            grad_up_cols[:, :, :half].reshape(weight_rows, FF),
            grad_up_cols[:, :, half : 2 * half].reshape(weight_rows, FF),
        ],
        1,
    )
    grad_branch = group_gather(grad_branch_low)
    feed_partial, grad_down_partial, grad_branch = lax.optimization_barrier(
        (feed_partial, grad_down_partial, grad_branch)
    )
    feed_sum = group_scatter(feed_partial)
    grad_gated = bf_product(grad_branch, out_full.T)
    grad_down, grad_outw = heads_to_rows((grad_down_partial, bf_product(gated_rows.T, grad_branch)))
    grad_mixer, grad_gate, grad_out_norm = gate_back(grad_gated)
    grad_gate = grad_gate.astype(jnp.bfloat16)
    head_gradients = grad_mixer.astype(jnp.bfloat16).astype(jnp.float32)
    local_adjoint = hi("dc,dr->cr", query_frame, head_gradients)[None]
    transfer_turned = jnp.transpose(transfer, (0, 2, 1))
    later_map, state_gradient = carried_in(
        (transfer_turned, local_adjoint), "sh", compose, (identity, zeros_state), True
    )
    basis_gradient = hi("nu,wu->nw", head_gradients, incoming_state[0])
    transfer_gradient = hi("tnf,tmf->tnm", state_gradient, incoming_state)
    grad_prepared = recurrence_back(
        (basis_gradient, head_gradients, transfer_gradient, state_gradient)
    )
    grad_prepared, feed_sum, grad_up_cols, grad_down, grad_outw = lax.optimization_barrier(
        (grad_prepared, feed_sum, grad_up_cols, grad_down, grad_outw)
    )
    layer_out = (middle + feed_sum).astype(jnp.bfloat16)
    grad_padded, grad_scalars, grad_conv, grad_rate, grad_bias = inputs_back(grad_prepared)
    rim_grad = from_behind(grad_padded[: CONV - 1], "sh", -1)
    own_grad = grad_padded[CONV - 1 :]
    grad_proj = jnp.concatenate(
        [own_grad[: length - (CONV - 1)], own_grad[length - (CONV - 1) :] + rim_grad], 0
    )
    grad_head = jnp.concatenate(
        [grad_gate, grad_proj.astype(jnp.bfloat16), grad_scalars.astype(jnp.bfloat16)], 1
    )
    grad_normed_one = group_scatter(bf_product(grad_head, head_full.T), True)
    grad_x_norm, grad_gain_one = norm_one_back(grad_normed_one)
    grad_head_cols = heads_to_columns(
        jnp.concatenate([bf_product(normed_one.T, grad_head), grad_gain_one[:, None]], 1)
    )
    grad_gatew = grad_head_cols[:, :, :DK].reshape(weight_rows, D)
    grad_mixw = grad_head_cols[:, :, DK : DK + PROJ].reshape(weight_rows, HEADS * PROJ)
    grad_gatesw = grad_head_cols[:, :, DK + PROJ : WIDE].reshape(
        weight_rows, HEADS * (STEPS + 1)
    )
    grad_tokens = (grad_middle + grad_x_norm).astype(jnp.bfloat16)
    (conv_grad,) = heads_to_rows((jnp.transpose(grad_conv),))
    conv_grad = jnp.transpose(conv_grad)
    one_hot = (jnp.arange(HEADS) == head).astype(jnp.float32)
    small_sums = all_sum(
        jnp.concatenate([one_hot * grad_rate, one_hot * grad_bias, grad_out_norm])
    )
    return (
        layer_out,
        grad_tokens,
        jnp.sum(grad_head_cols[:, :, WIDE], 1),
        grad_mixw,
        grad_gatesw,
        conv_grad,
        small_sums[:HEADS],
        small_sums[HEADS : 2 * HEADS],
        grad_gatew,
        small_sums[2 * HEADS :],
        grad_outw,
        jnp.sum(grad_up_cols[:, :, 2 * half], 1),
        grad_up,
        grad_down,
    )


def solution(mesh):
    seq = mesh.shape["seq"]
    across = mesh.shape["head"]
    inner = HEADS // across
    grid = Mesh(
        np.asarray(mesh.devices).reshape(seq // inner, inner, across), ("sh", "sl", "hd")
    )
    rows = P(ALL, None)
    flat = P(ALL)
    return jax.shard_map(
        local,
        mesh=grid,
        in_specs=(
            rows,
            flat,
            rows,
            rows,
            P(None, ALL),
            P(),
            P(),
            rows,
            P(),
            rows,
            flat,
            rows,
            rows,
            P(),
            rows,
        ),
        out_specs=(
            rows,
            rows,
            flat,
            rows,
            rows,
            P(None, ALL),
            P(),
            P(),
            rows,
            P(),
            rows,
            flat,
            rows,
            rows,
        ),
        check_vma=False,
    )
```

```python
import jax
import jax.numpy as jnp
import numpy as np
from jax import lax
from jax.experimental import pallas as pl
from jax.experimental.pallas import tpu as pltpu
from jax.sharding import Mesh
from jax.sharding import PartitionSpec as P

D = 1024
HEADS = 8
DK = 128
FF = 2816
STEPS = 2
CONV = 4
BLOCK = 64
PROJ = (1 + 2 * STEPS) * DK
WIDE = DK + PROJ + STEPS + 1

EPS = 1e-06
HIGH_ACCURACY = lax.Precision.HIGH

GROUP = ("sl", "hd")
ALL = ("sh", "sl", "hd")


def from_behind(shard, axis, by):
    peers = lax.axis_size(axis)
    pairs = [(i, i + by) for i in range(peers) if 0 <= i + by < peers]
    return lax.ppermute(shard, axis, pairs)


def gather_kernel(count, own_ref, out_ref, slots, send_sems, recv_sems):
    me = lax.axis_index("sh")
    across = lax.axis_index("sl")
    inner = lax.axis_index("hd")
    barrier = pltpu.get_barrier_semaphore()

    def peer(index):
        return (index, across, inner)

    def greet(index, carry):
        @pl.when(index != me)
        def _():
            pl.semaphore_signal(
                barrier, inc=1, device_id=peer(index), device_id_type=pl.DeviceIdType.MESH
            )

        return carry

    lax.fori_loop(0, count, greet, 0)
    pl.semaphore_wait(barrier, count - 1)

    def copy_to(index):
        return pltpu.make_async_remote_copy(
            src_ref=own_ref,
            dst_ref=slots.at[me],
            send_sem=send_sems.at[index],
            recv_sem=recv_sems.at[me],
            device_id=peer(index),
            device_id_type=pl.DeviceIdType.MESH,
        )

    def copy_from(index):
        return pltpu.make_async_remote_copy(
            src_ref=own_ref,
            dst_ref=slots.at[index],
            send_sem=send_sems.at[index],
            recv_sem=recv_sems.at[index],
            device_id=peer(index),
            device_id_type=pl.DeviceIdType.MESH,
        )

    def send(index, carry):
        @pl.when(index != me)
        def _():
            copy_to(index).start()

        return carry

    lax.fori_loop(0, count, send, 0)
    slots[me] = own_ref[...]

    def finish(index, carry):
        @pl.when(index != me)
        def _():
            copy_to(index).wait_send()
            copy_from(index).wait_recv()

        return carry

    lax.fori_loop(0, count, finish, 0)
    out_ref[...] = slots[...]


def scatter_kernel(count, own_ref, out_ref, slots, send_sems, recv_sems):
    me = lax.axis_index("sh")
    across = lax.axis_index("sl")
    inner = lax.axis_index("hd")
    barrier = pltpu.get_barrier_semaphore()

    def peer(index):
        return (index, across, inner)

    def greet(index, carry):
        @pl.when(index != me)
        def _():
            pl.semaphore_signal(
                barrier, inc=1, device_id=peer(index), device_id_type=pl.DeviceIdType.MESH
            )

        return carry

    lax.fori_loop(0, count, greet, 0)
    pl.semaphore_wait(barrier, count - 1)

    def copy_to(index):
        return pltpu.make_async_remote_copy(
            src_ref=own_ref.at[index],
            dst_ref=slots.at[me],
            send_sem=send_sems.at[index],
            recv_sem=recv_sems.at[me],
            device_id=peer(index),
            device_id_type=pl.DeviceIdType.MESH,
        )

    def copy_from(index):
        return pltpu.make_async_remote_copy(
            src_ref=own_ref.at[index],
            dst_ref=slots.at[index],
            send_sem=send_sems.at[index],
            recv_sem=recv_sems.at[index],
            device_id=peer(index),
            device_id_type=pl.DeviceIdType.MESH,
        )

    def send(index, carry):
        @pl.when(index != me)
        def _():
            copy_to(index).start()

        return carry

    lax.fori_loop(0, count, send, 0)
    slots[me] = own_ref[me]

    def finish(index, carry):
        @pl.when(index != me)
        def _():
            copy_to(index).wait_send()
            copy_from(index).wait_recv()

        return carry

    lax.fori_loop(0, count, finish, 0)
    out_ref[...] = jnp.sum(slots[...].astype(jnp.float32), axis=0)


def group_sum_scatter(partial, ident):
    count = lax.axis_size("sh")
    pieces = partial.astype(jnp.bfloat16).reshape((count, partial.shape[0] // count) + partial.shape[1:])
    return pl.pallas_call(
        lambda *refs: scatter_kernel(count, *refs),
        out_shape=jax.ShapeDtypeStruct(pieces.shape[1:], jnp.float32),
        in_specs=[pl.BlockSpec(memory_space=pltpu.VMEM)],
        out_specs=pl.BlockSpec(memory_space=pltpu.VMEM),
        scratch_shapes=[
            pltpu.VMEM(pieces.shape, jnp.bfloat16),
            pltpu.SemaphoreType.DMA((count,)),
            pltpu.SemaphoreType.DMA((count,)),
        ],
        compiler_params=pltpu.CompilerParams(collective_id=ident, has_side_effects=True),
    )(pieces)


def group_maps(block, ident):
    count = lax.axis_size("sh")
    return pl.pallas_call(
        lambda *refs: gather_kernel(count, *refs),
        out_shape=jax.ShapeDtypeStruct((count,) + block.shape, block.dtype),
        in_specs=[pl.BlockSpec(memory_space=pltpu.VMEM)],
        out_specs=pl.BlockSpec(memory_space=pltpu.VMEM),
        scratch_shapes=[
            pltpu.VMEM((count,) + block.shape, block.dtype),
            pltpu.SemaphoreType.DMA((count,)),
            pltpu.SemaphoreType.DMA((count,)),
        ],
        compiler_params=pltpu.CompilerParams(collective_id=ident, has_side_effects=True),
    )(block)


def carried_in(shard, axis, join, neutral, backward):
    count = lax.axis_size(axis)
    place = lax.axis_index(axis)
    ahead = count - 1 - place if backward else place
    both = group_maps(jnp.stack(shard).astype(jnp.bfloat16), 2 if backward else 1)
    gathered = (both[:, 0], both[:, 1])
    state = jax.tree.map(lambda a, e: jnp.zeros_like(a) + jnp.asarray(e, a.dtype), shard, neutral)

    def one(turn, state):
        source = count - 1 - turn if backward else turn
        return join(
            state,
            jax.tree.map(
                lambda a, own: lax.dynamic_index_in_dim(a, source, 0, False).astype(own.dtype),
                gathered,
                shard,
            ),
        )

    return lax.fori_loop(0, ahead, one, state)


def flat_place():
    return (
        lax.axis_index("sh") * lax.axis_size("sl") + lax.axis_index("sl")
    ) * lax.axis_size("hd") + lax.axis_index("hd")


def device_of(index):
    inner = lax.axis_size("sl") * lax.axis_size("hd")
    return (index // inner, (index // lax.axis_size("hd")) % lax.axis_size("sl"), index % lax.axis_size("hd"))


def sum_kernel(count, own_ref, out_ref, slots, send_sems, recv_sems):
    me = flat_place()
    barrier = pltpu.get_barrier_semaphore()

    def greet(index, carry):
        @pl.when(index != me)
        def _():
            pl.semaphore_signal(
                barrier, inc=1, device_id=device_of(index), device_id_type=pl.DeviceIdType.MESH
            )

        return carry

    lax.fori_loop(0, count, greet, 0)
    pl.semaphore_wait(barrier, count - 1)

    def copy_to(index):
        return pltpu.make_async_remote_copy(
            src_ref=own_ref,
            dst_ref=slots.at[me],
            send_sem=send_sems.at[index],
            recv_sem=recv_sems.at[me],
            device_id=device_of(index),
            device_id_type=pl.DeviceIdType.MESH,
        )

    def copy_from(index):
        return pltpu.make_async_remote_copy(
            src_ref=own_ref,
            dst_ref=slots.at[index],
            send_sem=send_sems.at[index],
            recv_sem=recv_sems.at[index],
            device_id=device_of(index),
            device_id_type=pl.DeviceIdType.MESH,
        )

    def send(index, carry):
        @pl.when(index != me)
        def _():
            copy_to(index).start()

        return carry

    lax.fori_loop(0, count, send, 0)
    slots[me] = own_ref[...]

    def finish(index, carry):
        @pl.when(index != me)
        def _():
            copy_to(index).wait_send()
            copy_from(index).wait_recv()

        return carry

    lax.fori_loop(0, count, finish, 0)
    out_ref[...] = jnp.sum(slots[...], axis=0)


def all_sum(vector):
    count = lax.axis_size("sh") * lax.axis_size("sl") * lax.axis_size("hd")
    size = vector.shape[0]
    lanes = 128
    tile = 8 * lanes
    padded = -(-size // tile) * tile
    block = jnp.pad(vector, (0, padded - size)).reshape(padded // lanes, lanes)
    total = pl.pallas_call(
        lambda *refs: sum_kernel(count, *refs),
        out_shape=jax.ShapeDtypeStruct(block.shape, jnp.float32),
        in_specs=[pl.BlockSpec(memory_space=pltpu.VMEM)],
        out_specs=pl.BlockSpec(memory_space=pltpu.VMEM),
        scratch_shapes=[
            pltpu.VMEM((count,) + block.shape, jnp.float32),
            pltpu.SemaphoreType.DMA((count,)),
            pltpu.SemaphoreType.DMA((count,)),
        ],
        compiler_params=pltpu.CompilerParams(collective_id=0, has_side_effects=True),
    )(block)
    return total.reshape(-1)[:size]


def rms_norm(values, scale_gain):
    return values * lax.rsqrt(jnp.mean(values * values, axis=-1, keepdims=True) + EPS) * scale_gain


def unit_norm(values):
    return values * lax.rsqrt(jnp.sum(values * values, axis=-1, keepdims=True) + EPS)


def bf_product(first_mat, second_mat):
    return jnp.dot(first_mat, second_mat, preferred_element_type=jnp.float32)


def hi(spec, *arrays):
    return jnp.einsum(spec, *arrays, precision=HIGH_ACCURACY)


def compose(early_pair, late_pair):
    early_mat, early_add = early_pair
    late_mat, late_add = late_pair
    joined = hi("hij,hjk->hik", late_mat, early_mat)
    shifted = hi("hij,hjk->hik", late_mat, early_add) + late_add
    return (joined, shifted)


def gate_norm(values, out_gate, scale_gain):
    return rms_norm(values, scale_gain) * jax.nn.silu(out_gate)


def swiglu(gate_up):
    half = gate_up.shape[1] // 2
    return jax.nn.silu(gate_up[:, :half]) * gate_up[:, half:]


def owner_pairs(inverse):
    groups = lax.axis_size("sh")
    pairs = [(g * HEADS + t, t * groups + g) for g in range(groups) for t in range(HEADS)]
    return [(b, a) for a, b in pairs] if inverse else pairs


def rows_to_heads(blocks):
    groups = lax.axis_size("sh")
    width = blocks[0].shape[1]
    used = sum(b.shape[0] for b in blocks)
    least = (1 << 20) // (groups * width * 2) + 1
    rows = -(-max(used, least) // 8) * 8
    packed = jnp.concatenate(
        list(blocks) + [jnp.zeros((rows - used, width), blocks[0].dtype)], 0
    )
    moved = lax.ppermute(packed, ALL, owner_pairs(True))
    full = lax.all_gather(moved, "sh", axis=0, tiled=False)
    parts = []
    first = 0
    for block in blocks:
        size = block.shape[0]
        parts.append(full[:, first : first + size].reshape(groups * size, width))
        first += size
    return parts


def heads_to_rows(partials):
    groups = lax.axis_size("sh")
    pieces = [
        p.astype(jnp.bfloat16).reshape((groups, p.shape[0] // groups) + p.shape[1:])
        for p in partials
    ]
    joined = jnp.concatenate(pieces, 1)
    joined = joined.reshape((-1,) + joined.shape[2:])
    summed = lax.psum_scatter(joined, "sh", scatter_dimension=0, tiled=True)
    moved = lax.ppermute(summed, ALL, owner_pairs(False)).astype(jnp.float32)
    parts = []
    first = 0
    for piece in pieces:
        size = piece.shape[1]
        parts.append(moved[first : first + size])
        first += size
    return parts


def columns_to_heads(local_cols):
    per_head = jnp.transpose(local_cols, (1, 0, 2))
    mine = lax.all_to_all(per_head, GROUP, 0, 0, tiled=True)
    mine = mine.reshape(-1, mine.shape[-1])
    return lax.all_gather(mine, "sh", axis=0, tiled=True)


def heads_to_columns(partial, direct=False):
    low = partial.astype(jnp.bfloat16)
    if direct:
        summed = group_sum_scatter(low, 3).astype(jnp.bfloat16)
    else:
        summed = lax.psum_scatter(low, "sh", scatter_dimension=0, tiled=True)
    summed = summed.reshape(HEADS, -1, summed.shape[-1])
    back = lax.all_to_all(summed, GROUP, 0, 0, tiled=True)
    return jnp.transpose(back, (1, 0, 2)).astype(jnp.float32)


def group_gather(rows, direct=False):
    if direct:
        copies = jnp.broadcast_to(rows[None], (HEADS,) + rows.shape)
        moved = lax.all_to_all(copies, GROUP, 0, 0, tiled=True)
        return moved.reshape((-1,) + rows.shape[1:])
    return lax.all_gather(rows, GROUP, axis=0, tiled=True)


def group_scatter(partial, direct=False):
    low = partial.astype(jnp.bfloat16)
    if direct:
        pieces = low.reshape((HEADS, low.shape[0] // HEADS) + low.shape[1:])
        moved = lax.all_to_all(pieces, GROUP, 0, 0, tiled=True)
        return jnp.sum(moved.astype(jnp.float32), 0)
    return lax.psum_scatter(low, GROUP, scatter_dimension=0, tiled=True).astype(jnp.float32)


def masked_power_inverse(system):
    size = system.shape[-1]
    places = jnp.arange(size)
    base = 8
    inside = (places[:, None] // base == places[None, :] // base) & (
        places[:, None] > places[None, :]
    )
    step = -(system * inside.astype(system.dtype))
    eye = jnp.eye(size, dtype=system.dtype)
    result = eye + step
    for _ in range(2):
        step = hi("bij,bjk->bik", step, step)
        result = result + hi("bij,bjk->bik", result, step)
    width = base
    while width < size:
        across = (places[:, None] // (2 * width) == places[None, :] // (2 * width)) & (
            places[:, None] // width != places[None, :] // width
        )
        lower_left = system * across.astype(system.dtype)
        result = result - hi("bij,bjk->bik", result, hi("bij,bjk->bik", lower_left, result))
        width = 2 * width
    return result


@jax.custom_vjp
def unit_lower_inverse(system):
    return masked_power_inverse(system)


def inverse_keep(system):
    inverse = masked_power_inverse(system)
    return inverse, inverse


def inverse_back(inverse, grad):
    turned = jnp.swapaxes(inverse, -1, -2)
    return (-hi("bij,bjk->bik", turned, hi("bij,bjk->bik", grad, turned)),)


unit_lower_inverse.defvjp(inverse_keep, inverse_back)


def block_mixer(query_rows, key_rows, value_rows, beta_rows, log_decay, starts_flag):
    pseudo = key_rows.shape[0]
    span = STEPS * BLOCK
    blocks = pseudo // span
    queries = query_rows.reshape(blocks, BLOCK, DK)
    keys = key_rows.reshape(blocks, span, DK)
    values = value_rows.reshape(blocks, span, DK)
    betas = beta_rows.reshape(blocks, span)
    decays = log_decay.reshape(blocks, span)
    flags = starts_flag.reshape(blocks, span)
    places = jnp.arange(span)
    lower = places[:, None] >= places[None, :]
    strict = (places[:, None] > places[None, :]).astype(jnp.float32)
    identity = jnp.eye(span, dtype=jnp.float32)
    eye_key = jnp.eye(DK, dtype=jnp.float32)

    summed = jnp.cumsum(decays, axis=1)
    segment = jnp.cumsum(flags, axis=1)
    same_doc = (segment[:, :, None] == segment[:, None, :]) & lower
    decay_ratio = jnp.exp(
        jnp.where(same_doc, summed[:, :, None] - summed[:, None, :], 0.0)
    ) * same_doc.astype(jnp.float32)
    from_start = jnp.exp(summed) * (segment == 0.0).astype(jnp.float32)
    key_key = hi("bik,bjk->bij", keys, keys)
    system = identity + betas[:, :, None] * decay_ratio * key_key * strict
    right_side = jnp.concatenate(
        [betas[:, :, None] * values, (betas * from_start)[:, :, None] * keys], 2
    )
    solved = hi("bij,bjk->bik", unit_lower_inverse(system), right_side)
    fresh = solved[:, :, :DK]
    carried = solved[:, :, DK:]
    last_keys = keys * decay_ratio[:, -1, :, None]
    transfer = from_start[:, -1, None, None] * eye_key - hi("bsi,bsj->bij", last_keys, carried)
    offset = hi("bsi,bsj->bij", last_keys, fresh)
    query_key = hi("bqk,bsk->bqs", queries, keys) * decay_ratio[:, STEPS - 1 :: STEPS]
    frame = from_start[:, STEPS - 1 :: STEPS, None] * queries - hi(
        "bqs,bsj->bqj", query_key, carried
    )
    direct = hi("bqs,bsj->bqj", query_key, fresh)

    state = jnp.concatenate([eye_key, jnp.zeros((DK, DK), jnp.float32)], 1)
    states = []
    for index in range(blocks):
        states.append(state)
        state = hi("ij,jk->ik", transfer[index], state) + jnp.concatenate(
            [jnp.zeros((DK, DK), jnp.float32), offset[index]], 1
        )
    states = jnp.stack(states)
    mats = states[:, :, :DK]
    adds = states[:, :, DK:]
    final_mat = state[:, :DK]
    final_add = state[:, DK:]
    query_frame = hi("bqi,bij->bqj", frame, mats)
    partial = hi("bqi,bij->bqj", frame, adds) + direct
    return (
        query_frame.reshape(blocks * BLOCK, DK),
        partial.reshape(blocks * BLOCK, DK),
        final_mat[None],
        final_add[None],
    )


def local(
    tokens_in,
    mixer_norm,
    mix_weight,
    head_gates,
    conv_taps,
    decay_log,
    decay_bias,
    gate_weight,
    out_norm,
    out_weight,
    feed_norm,
    up_weight,
    down_weight,
    doc_lengths,
    out_grad,
):
    row_count = tokens_in.shape[0]
    weight_rows = mix_weight.shape[0]
    head = lax.axis_index("sl") * lax.axis_size("hd") + lax.axis_index("hd")
    length = row_count * HEADS

    head_cols = jnp.concatenate(
        [
            gate_weight.reshape(weight_rows, HEADS, DK),
            mix_weight.reshape(weight_rows, HEADS, PROJ),
            head_gates.reshape(weight_rows, HEADS, STEPS + 1),
            jnp.broadcast_to(mixer_norm[:, None, None], (weight_rows, HEADS, 1)),
        ],
        2,
    )
    head_wide = columns_to_heads(head_cols)
    head_full = head_wide[:, :WIDE]
    gain_one = head_wide[:, WIDE].astype(jnp.float32)
    half = FF // HEADS
    up_cols = jnp.concatenate(
        [
            up_weight[:, :FF].reshape(weight_rows, HEADS, half),
            up_weight[:, FF:].reshape(weight_rows, HEADS, half),
            jnp.broadcast_to(feed_norm[:, None, None], (weight_rows, HEADS, 1)),
        ],
        2,
    )
    up_wide = columns_to_heads(up_cols)
    up_full = up_wide[:, : 2 * half]
    gain_two = up_wide[:, 2 * half].astype(jnp.float32)
    tap_width = conv_taps.shape[1]
    tap_row = jnp.pad(conv_taps.reshape(1, -1), ((0, 0), (0, D - CONV * tap_width)))
    out_full, down_full, tap_rows = rows_to_heads((out_weight, down_weight, tap_row))
    conv_part = jnp.transpose(
        tap_rows[:, : CONV * tap_width].reshape(-1, CONV, tap_width), (1, 0, 2)
    ).reshape(CONV, -1).astype(jnp.float32)

    x_float = tokens_in.astype(jnp.float32)
    normed_float, norm_one_back = jax.vjp(rms_norm, x_float, gain_one)
    normed_one = group_gather(normed_float.astype(jnp.bfloat16), True)
    head_out = bf_product(normed_one, head_full)
    out_gate = head_out[:, :DK]
    proj_head = head_out[:, DK : DK + PROJ].astype(jnp.bfloat16)
    scalar_rows = head_out[:, DK + PROJ :].astype(jnp.bfloat16).astype(jnp.float32)

    rim_rows = from_behind(proj_head[length - (CONV - 1) :], "sh", 1)
    padded = jnp.concatenate([rim_rows, proj_head], 0).astype(jnp.float32)
    starts = jnp.cumsum(doc_lengths) - doc_lengths
    positions = lax.axis_index("sh") * length + jnp.arange(length, dtype=jnp.int32)
    starts_flag = jnp.any(positions[:, None] == starts[None, :], 1).astype(jnp.float32)
    doc_begin = jnp.max(jnp.where(starts[None, :] <= positions[:, None], starts[None, :], 0), 1)
    tap_masks = [
        (positions - (CONV - 1) + tap_index >= doc_begin).astype(jnp.float32)
        for tap_index in range(CONV)
    ]
    pseudo_flag = jnp.concatenate(
        [starts_flag[:, None], jnp.zeros((length, STEPS - 1), jnp.float32)], 1
    ).reshape(-1)
    rate_log = lax.dynamic_index_in_dim(decay_log, head, 0, False)
    bias_part = lax.dynamic_index_in_dim(decay_bias, head, 0, False)

    def mixer_inputs(padded, scalar_rows, conv_part, rate_log, bias_part):
        convolved = jnp.zeros_like(padded[CONV - 1 :])
        for tap_index in range(CONV):
            convolved = (
                convolved
                + conv_part[tap_index]
                * padded[tap_index : tap_index + length]
                * tap_masks[tap_index][:, None]
            )
        activated = jax.nn.silu(convolved).reshape(length, 1 + 2 * STEPS, DK)
        query_rows = unit_norm(activated[:, 0])
        key_rows = unit_norm(activated[:, 1 : 1 + STEPS]).reshape(STEPS * length, DK)
        value_rows = activated[:, 1 + STEPS :].reshape(STEPS * length, DK)
        beta_rows = jax.nn.sigmoid(scalar_rows[:, :STEPS]).reshape(STEPS * length)
        log_rate = -jnp.exp(rate_log) * jax.nn.softplus(scalar_rows[:, STEPS] + bias_part)
        log_decay = jnp.concatenate(
            [log_rate[:, None], jnp.zeros((length, STEPS - 1), jnp.float32)], 1
        ).reshape(STEPS * length)
        return (query_rows, key_rows, value_rows, beta_rows, log_decay)

    def recurrence(query_rows, key_rows, value_rows, beta_rows, log_decay):
        return block_mixer(query_rows, key_rows, value_rows, beta_rows, log_decay, pseudo_flag)

    prepared, inputs_back = jax.vjp(
        mixer_inputs, padded, scalar_rows, conv_part, rate_log, bias_part
    )
    (query_frame, partial_value_rows, transfer, offset), recurrence_back = jax.vjp(
        recurrence, *prepared
    )
    grad_rows = group_gather(out_grad)
    grad_rows, query_frame, partial_value_rows, transfer, offset = lax.optimization_barrier(
        (grad_rows, query_frame, partial_value_rows, transfer, offset)
    )
    identity = jnp.eye(DK, dtype=jnp.float32)[None]
    zeros_state = jnp.zeros((1, DK, DK), jnp.float32)
    prefix_map, incoming_state = carried_in(
        (transfer, offset), "sh", compose, (identity, zeros_state), False
    )
    mixer_result = partial_value_rows + hi("zy,yi->zi", query_frame, incoming_state[0])
    mixer_low = mixer_result.astype(jnp.bfloat16).astype(jnp.float32)
    gated, gate_back = jax.vjp(gate_norm, mixer_low, out_gate, out_norm)
    gated_rows = gated.astype(jnp.bfloat16)
    middle = x_float + group_scatter(bf_product(gated_rows, out_full), True)
    normed_mid, norm_two_back = jax.vjp(rms_norm, middle, gain_two)
    normed_two = group_gather(normed_mid.astype(jnp.bfloat16))
    gate_up = bf_product(normed_two, up_full)
    hidden_float, swiglu_back = jax.vjp(swiglu, gate_up)
    hidden = hidden_float.astype(jnp.bfloat16)
    feed_partial = bf_product(hidden, down_full)

    grad_out = out_grad.astype(jnp.float32)
    grad_hidden = bf_product(grad_rows, down_full.T)
    grad_down_partial = bf_product(hidden.T, grad_rows)
    (grad_gate_up,) = swiglu_back(grad_hidden)
    grad_gate_up = grad_gate_up.astype(jnp.bfloat16)
    grad_normed_two = group_scatter(bf_product(grad_gate_up, up_full.T))
    grad_mid_norm, grad_gain_two = norm_two_back(grad_normed_two)
    grad_up_payload = jnp.concatenate(
        [bf_product(normed_two.T, grad_gate_up), grad_gain_two[:, None]], 1
    )
    grad_middle = grad_out + grad_mid_norm
    feed_partial, grad_up_payload, grad_down_partial, grad_branch_low = lax.optimization_barrier(
        (feed_partial, grad_up_payload, grad_down_partial, grad_middle.astype(jnp.bfloat16))
    )
    grad_up_cols = heads_to_columns(grad_up_payload, True)
    grad_up = jnp.concatenate(
        [
            grad_up_cols[:, :, :half].reshape(weight_rows, FF),
            grad_up_cols[:, :, half : 2 * half].reshape(weight_rows, FF),
        ],
        1,
    )
    grad_branch = group_gather(grad_branch_low)
    feed_partial, grad_down_partial, grad_branch = lax.optimization_barrier(
        (feed_partial, grad_down_partial, grad_branch)
    )
    feed_sum = group_scatter(feed_partial, True)
    grad_gated = bf_product(grad_branch, out_full.T)
    grad_down, grad_outw = heads_to_rows((grad_down_partial, bf_product(gated_rows.T, grad_branch)))
    grad_mixer, grad_gate, grad_out_norm = gate_back(grad_gated)
    grad_gate = grad_gate.astype(jnp.bfloat16)
    head_gradients = grad_mixer.astype(jnp.bfloat16).astype(jnp.float32)
    local_adjoint = hi("dc,dr->cr", query_frame, head_gradients)[None]
    transfer_turned = jnp.transpose(transfer, (0, 2, 1))
    later_map, state_gradient = carried_in(
        (transfer_turned, local_adjoint), "sh", compose, (identity, zeros_state), True
    )
    basis_gradient = hi("nu,wu->nw", head_gradients, incoming_state[0])
    transfer_gradient = hi("tnf,tmf->tnm", state_gradient, incoming_state)
    grad_prepared = recurrence_back(
        (basis_gradient, head_gradients, transfer_gradient, state_gradient)
    )
    grad_prepared, feed_sum, grad_up_cols, grad_down, grad_outw = lax.optimization_barrier(
        (grad_prepared, feed_sum, grad_up_cols, grad_down, grad_outw)
    )
    layer_out = (middle + feed_sum).astype(jnp.bfloat16)
    grad_padded, grad_scalars, grad_conv, grad_rate, grad_bias = inputs_back(grad_prepared)
    rim_grad = from_behind(grad_padded[: CONV - 1], "sh", -1)
    own_grad = grad_padded[CONV - 1 :]
    grad_proj = jnp.concatenate(
        [own_grad[: length - (CONV - 1)], own_grad[length - (CONV - 1) :] + rim_grad], 0
    )
    grad_head = jnp.concatenate(
        [grad_gate, grad_proj.astype(jnp.bfloat16), grad_scalars.astype(jnp.bfloat16)], 1
    )
    grad_normed_one = group_scatter(bf_product(grad_head, head_full.T), True)
    grad_x_norm, grad_gain_one = norm_one_back(grad_normed_one)
    grad_head_cols = heads_to_columns(
        jnp.concatenate([bf_product(normed_one.T, grad_head), grad_gain_one[:, None]], 1)
    )
    grad_gatew = grad_head_cols[:, :, :DK].reshape(weight_rows, D)
    grad_mixw = grad_head_cols[:, :, DK : DK + PROJ].reshape(weight_rows, HEADS * PROJ)
    grad_gatesw = grad_head_cols[:, :, DK + PROJ : WIDE].reshape(
        weight_rows, HEADS * (STEPS + 1)
    )
    grad_tokens = (grad_middle + grad_x_norm).astype(jnp.bfloat16)
    conv_grad = lax.ppermute(
        group_sum_scatter(jnp.transpose(grad_conv), 7), ALL, owner_pairs(False)
    )
    conv_grad = jnp.transpose(conv_grad)
    one_hot = (jnp.arange(HEADS) == head).astype(jnp.float32)
    small_sums = all_sum(
        jnp.concatenate([one_hot * grad_rate, one_hot * grad_bias, grad_out_norm])
    )
    return (
        layer_out,
        grad_tokens,
        jnp.sum(grad_head_cols[:, :, WIDE], 1),
        grad_mixw,
        grad_gatesw,
        conv_grad,
        small_sums[:HEADS],
        small_sums[HEADS : 2 * HEADS],
        grad_gatew,
        small_sums[2 * HEADS :],
        grad_outw,
        jnp.sum(grad_up_cols[:, :, 2 * half], 1),
        grad_up,
        grad_down,
    )


def solution(mesh):
    seq = mesh.shape["seq"]
    across = mesh.shape["head"]
    inner = HEADS // across
    grid = Mesh(
        np.asarray(mesh.devices).reshape(seq // inner, inner, across), ("sh", "sl", "hd")
    )
    rows = P(ALL, None)
    flat = P(ALL)
    return jax.shard_map(
        local,
        mesh=grid,
        in_specs=(
            rows,
            flat,
            rows,
            rows,
            P(None, ALL),
            P(),
            P(),
            rows,
            P(),
            rows,
            flat,
            rows,
            rows,
            P(),
            rows,
        ),
        out_specs=(
            rows,
            rows,
            flat,
            rows,
            rows,
            P(None, ALL),
            P(),
            P(),
            rows,
            P(),
            rows,
            flat,
            rows,
            rows,
        ),
        check_vma=False,
    )
```
